32 devices in a mesh: seq: 8 (over y, x, core), head: 4 (over z).
Axes of the slice: x: 2, y: 2, z: 4, core: 2. Of those that a mesh axis runs over, the one named last changes fastest.
Arguments:
- dna: bfloat16 [6144, 768], P('seq')
- conv_in: bfloat16 [5, 1536, 768], P(None, 'head')
- dilated_kernel_weight: bfloat16 [3, 1536, 1536], P(None, 'head'), may hold values from -0.09375 to 0.09375
- w_query: bfloat16 [1536, 1536], P('head')
- w_key: bfloat16 [1536, 1536], P('head')
- w_value: bfloat16 [1536, 1536], P('head'), may hold values from -0.15625 to 0.15625
- w_out: bfloat16 [1536, 1536], P('head'), may hold values from -0.21875 to 0.21875
Outputs:
- encoded: bfloat16 [3072, 1536], P('seq', 'head')
The draws below stay inside these ranges and needn't reach their ends.
All inputs are finite; a program needn't handle non-finite values.
Results may differ from the reference program's by a relative error of at most 0.007.
Values may be sent and summed in bfloat16 or wider, within the bound.
No kernel may reach another device: no remote copies, remote signals or barrier semaphores. Data moves between devices by JAX's collectives and lax.ppermute only.
A program may use at most 64 MiB of HBM per device.

```python
import math
import jax
import jax.numpy as jnp
from jax import lax

C_IN = 768
C = 1536
HEADS = 24
HEAD_DIM = 64
KW = 5
DILATION_STEP = 4
SAMPLED_SPOTS = 3072
IN_POS = 6144


def draw_dna(key, part):
    rows_key = jax.random.fold_in(key, 21)
    base_key = jax.random.fold_in(key, 22)
    scales = jnp.exp(jax.random.uniform(rows_key, (IN_POS, 1), jnp.float32, math.log(0.3), math.log(3.0)))
    base = jax.random.normal(base_key, (IN_POS, C_IN), jnp.float32)
    return (base * scales).astype(jnp.bfloat16)


def draw_conv_in(key, part):
    jitter_key = jax.random.fold_in(key, 31)
    base_key = jax.random.fold_in(key, 32)
    ramp = jnp.exp(math.log(3.0) * jnp.arange(C, dtype=jnp.float32) / (C - 1)).reshape(1, C, 1)
    jitter = jnp.exp(jax.random.uniform(jitter_key, (1, C, 1), jnp.float32, math.log(0.5), math.log(2.0)))
    base = jax.random.normal(base_key, (KW, C, C_IN), jnp.float32)
    return (base * ramp * jitter / math.sqrt(KW * C_IN)).astype(jnp.bfloat16)


def shared_projection(key, which):
    own = jax.random.normal(jax.random.fold_in(key, 42 + which), (HEADS * HEAD_DIM, C), jnp.float32)
    return own / math.sqrt(C)


def draw_w_query(key, part):
    return shared_projection(key, 0).astype(jnp.bfloat16)


def draw_w_key(key, part):
    return shared_projection(key, 1).astype(jnp.bfloat16)


def strengthened(entries, rng, source, target, blocks, factor):
    def block_of(position):
        return (jnp.arange(entries.shape[position]) // (entries.shape[position] // blocks)).reshape((-1,) + (1,) * (entries.ndim - 1 - position))

    first = jax.random.permutation(rng, blocks)[block_of(target)]
    second = (block_of(target) + blocks // 2) % blocks
    return jnp.where((block_of(source) == first) | (block_of(source) == second), factor * entries, entries)


def block_levels(rng, extent, pieces, least, largest):
    level, own = 1.0, jax.random.fold_in(rng, 6)
    for axis_at, blocks in pieces:
        steps = jnp.exp(jax.random.uniform(jax.random.fold_in(own, axis_at), (blocks,), jnp.float32, least / len(pieces), largest / len(pieces)))
        level = level * jnp.repeat(steps, extent[axis_at] // blocks).reshape([-1 if axis == axis_at else 1 for axis in range(len(extent))])
    return level


def noise(key, shape, deviation, bound, pieces=(), held_as=jnp.bfloat16):
    result = deviation * jax.random.normal(key, shape, jnp.float32)
    if pieces:
        result = result * block_levels(key, shape, pieces, -0.22, 0.18)
    return jnp.clip(result, -bound, bound).astype(held_as)


def gaussian_with(key, shape, width, reach, split, heavy, kind=jnp.bfloat16):
    array = width * jax.random.normal(key, shape, jnp.float32)
    if split:
        array = array * block_levels(key, shape, split, -0.22, 0.18)
    return jnp.clip(strengthened(array, jax.random.fold_in(key, 3), *heavy), -reach, reach).astype(kind)


def setup_inputs(seed: int = 0) -> dict:
    arg_keys = jax.random.split(jax.random.key(seed), 8)
    dna = draw_dna(jax.random.fold_in(arg_keys[7], 71), 0)
    conv_in = draw_conv_in(jax.random.fold_in(arg_keys[7], 71), 0)
    dilated_kernel_weight = noise(arg_keys[2], (3, C, C), (3 * C) ** -0.5, 0.09375, ((1, 4),))
    w_query = draw_w_query(jax.random.fold_in(arg_keys[7], 71), 0)
    w_key = draw_w_key(jax.random.fold_in(arg_keys[7], 71), 0)
    w_value = noise(arg_keys[5], (HEADS * HEAD_DIM, C), C ** -0.5, 0.15625, ((0, 4),))
    w_out = gaussian_with(arg_keys[6], (HEADS * HEAD_DIM, C), (HEADS * HEAD_DIM) ** -0.5, 0.21875, ((0, 4),), (0, 1, 4, 2.0))
    return {"dna": dna, "conv_in": conv_in, "dilated_kernel_weight": dilated_kernel_weight, "w_query": w_query, "w_key": w_key, "w_value": w_value, "w_out": w_out}


def row_scale(h):
    return h * lax.rsqrt(lax.optimization_barrier(jnp.mean(h * h, axis=1, keepdims=True)) + 1e-06)

def reduce_operands(left, right):
    return lax.dot_general(left, right, (((1,), (1,)), ((), ())), preferred_element_type=jnp.float32)

def reference(dna, conv_in, dilated_kernel_weight, w_query, w_key, w_value, w_out):
    half = (KW - 1) // 2
    padded = jnp.pad(dna, ((half, half), (0, 0)))
    h1 = jnp.zeros((SAMPLED_SPOTS, C), jnp.float32)
    for kernel_offset in range(KW):
        rows = padded[kernel_offset:kernel_offset + 2 * SAMPLED_SPOTS:2]
        h1 = h1 + reduce_operands(rows, conv_in[kernel_offset])
    gelu_output = jax.nn.gelu(row_scale(h1), approximate=True).astype(jnp.bfloat16)
    broad_input = jnp.pad(gelu_output, ((DILATION_STEP, DILATION_STEP), (0, 0)))
    second_hidden = h1
    for kernel_offset in range(3):
        second_hidden = second_hidden + reduce_operands(broad_input[DILATION_STEP * kernel_offset:DILATION_STEP * kernel_offset + SAMPLED_SPOTS], dilated_kernel_weight[kernel_offset])
    normed = row_scale(second_hidden).astype(jnp.bfloat16)
    query = reduce_operands(normed, w_query).astype(jnp.bfloat16)
    keys = reduce_operands(normed, w_key).astype(jnp.bfloat16)
    values = reduce_operands(normed, w_value).astype(jnp.bfloat16)
    scale = 1.0 / math.sqrt(HEAD_DIM)

    def split_heads(a):
        return jnp.transpose(a.reshape(SAMPLED_SPOTS, HEADS, HEAD_DIM), (1, 0, 2))

    def one_head(operands):
        q_head, k_head, v_head = operands
        scores = jnp.dot(q_head, k_head.T, preferred_element_type=jnp.float32) * scale
        top = lax.optimization_barrier(jnp.max(scores, axis=1, keepdims=True))
        weights = jnp.exp(scores - top)
        total = lax.optimization_barrier(jnp.sum(weights, axis=1, keepdims=True))
        return jnp.dot(weights.astype(jnp.bfloat16), v_head, preferred_element_type=jnp.float32) / total
    heads_out = lax.map(one_head, (split_heads(query), split_heads(keys), split_heads(values)))
    attended = jnp.transpose(heads_out, (1, 0, 2)).reshape(SAMPLED_SPOTS, HEADS * HEAD_DIM).astype(jnp.bfloat16)
    mixed = jnp.dot(attended, w_out, preferred_element_type=jnp.float32)
    return (second_hidden + mixed).astype(jnp.bfloat16)
```

```python
import functools
import math

import jax
import jax.numpy as jnp
from jax import lax
from jax.experimental import pallas as pl
from jax.experimental.pallas import tpu as pltpu
from jax.sharding import PartitionSpec as P

C = 1536
HEAD_DIM = 64
KW = 5
DILATION_STEP = 4
EPS = 1e-06
EDGE = 16
LOG2E = math.log2(math.e)
MIB = 1 << 20


def padded_2(block, sides, width):
    for axis, dim in sides:
        count = lax.axis_size(axis)
        forward = [(i, i + 1) for i in range(count - 1)]
        backward = [(target, source) for source, target in forward]
        low = lax.ppermute(
            lax.slice_in_dim(block, block.shape[dim] - width, None, axis=dim), axis, forward
        )
        high = lax.ppermute(lax.slice_in_dim(block, 0, width, axis=dim), axis, backward)
        block = jnp.concatenate([low, block, high], axis=dim)
    return block


def row_scale(hidden):
    squares = lax.psum(jnp.sum(hidden * hidden, axis=1), "head")
    return hidden * lax.rsqrt(squares / C + EPS)[:, None]


def reduce_operands(left, right):
    return lax.dot_general(
        left, right, (((1,), (1,)), ((), ())), preferred_element_type=jnp.float32
    )


def general_form(dna, conv_in, dilated_kernel_weight, w_query, w_key, w_value, w_out):
    local_row_count = dna.shape[0] // 2
    half = (KW - 1) // 2
    padded = padded_2(dna, (("seq", 0),), half)
    h1 = jnp.zeros((local_row_count, conv_in.shape[1]), jnp.float32)
    for kernel_offset in range(KW):
        rows = lax.slice(
            padded,
            (kernel_offset, 0),
            (kernel_offset + 2 * local_row_count - 1, padded.shape[1]),
            (2, 1),
        )
        h1 = h1 + reduce_operands(rows, conv_in[kernel_offset])
    gelu_output = jax.nn.gelu(row_scale(h1), approximate=True).astype(jnp.bfloat16)
    complete_output = lax.all_gather(gelu_output, "head", axis=1, tiled=True)
    broad_input = padded_2(complete_output, (("seq", 0),), DILATION_STEP)
    second_hidden = h1
    for kernel_offset in range(3):
        second_hidden = second_hidden + reduce_operands(
            broad_input[
                DILATION_STEP * kernel_offset : DILATION_STEP * kernel_offset + local_row_count
            ],
            dilated_kernel_weight[kernel_offset],
        )
    normed = row_scale(second_hidden).astype(jnp.bfloat16)
    local_width = w_query.shape[0]
    heads_here = local_width // HEAD_DIM
    piece = lax.all_gather(normed, "head", axis=1, tiled=True)
    q_acc, k_acc, v_acc = (reduce_operands(piece, w) for w in (w_query, w_key, w_value))
    query = q_acc.astype(jnp.bfloat16).reshape(local_row_count, heads_here, HEAD_DIM)
    keys = k_acc.astype(jnp.bfloat16)
    values = v_acc.astype(jnp.bfloat16)
    scale = 1.0 / math.sqrt(HEAD_DIM)
    start_state = (
        jnp.full((heads_here, local_row_count), -1e30, jnp.float32),
        jnp.zeros((heads_here, local_row_count), jnp.float32),
        jnp.zeros((local_row_count, heads_here, HEAD_DIM), jnp.float32),
    )
    key_rows = lax.all_gather(keys, "seq", axis=0, tiled=True)
    value_rows = lax.all_gather(values, "seq", axis=0, tiled=True)
    count = key_rows.shape[0]
    width = 512 if count % 512 == 0 else count
    blocks = count // width
    key_blocks = key_rows.reshape(blocks, width, heads_here, HEAD_DIM)
    value_blocks = value_rows.reshape(blocks, width, heads_here, HEAD_DIM)

    def step(state, operands):
        running, total, acc = state
        key_block, value_block = operands
        scores = (
            jnp.einsum("qhd,khd->hqk", query, key_block, preferred_element_type=jnp.float32) * scale
        )
        newest = jnp.maximum(running, jnp.max(scores, axis=2))
        factor = jnp.exp(running - newest)
        weights = jnp.exp(scores - newest[:, :, None])
        total = total * factor + jnp.sum(weights, axis=2)
        update = jnp.einsum(
            "hqk,khd->qhd",
            weights.astype(jnp.bfloat16),
            value_block,
            preferred_element_type=jnp.float32,
        )
        acc = acc * jnp.transpose(factor)[:, :, None] + update
        return ((newest, total, acc), None)

    state, _ = lax.scan(step, start_state, (key_blocks, value_blocks))
    running, total, acc = state
    attended = (
        (acc / jnp.transpose(total)[:, :, None])
        .reshape(local_row_count, local_width)
        .astype(jnp.bfloat16)
    )
    partial_out = jnp.dot(attended, w_out, preferred_element_type=jnp.float32)
    mixed = lax.psum_scatter(
        partial_out.astype(jnp.bfloat16), "head", scatter_dimension=1, tiled=True
    ).astype(jnp.float32)
    return (second_hidden + mixed).astype(jnp.bfloat16)


def whole(shape):
    return pl.BlockSpec(shape, lambda *_: (0,) * len(shape))


def nbytes(*arrays):
    return sum(math.prod(a.shape) * jnp.dtype(a.dtype).itemsize for a in arrays)


def cost(flops, arrays, transcendentals=0):
    return pl.CostEstimate(
        flops=int(flops), bytes_accessed=int(nbytes(*arrays)), transcendentals=int(transcendentals)
    )


def rotate(offset):
    count = lax.axis_size("head")
    return [(i, (i + offset) % count) for i in range(count)]


def shared(block):
    count = lax.axis_size("head")
    return [block] + [lax.ppermute(block, "head", rotate(k)) for k in (1, count - 1, 2)]


def owner(k):
    count = lax.axis_size("head")
    return lax.rem(lax.axis_index("head") + count - k, count)


SHIFTS = (0, 1, 3, 2)


def conv_kernel(dna_ref, low_ref, high_ref, weight_ref, h1_ref, sent_ref, wide):
    rows = dna_ref.shape[0]
    tiles = wide.shape[0]
    for j in range(tiles):
        lanes = pl.ds(128 * j, 128)
        wide[j, pl.ds(0, EDGE), :] = low_ref[:, lanes].astype(jnp.float32)
        wide[j, pl.ds(EDGE, rows), :] = dna_ref[:, lanes].astype(jnp.float32)
        wide[j, pl.ds(EDGE + rows, EDGE), :] = high_ref[:, lanes].astype(jnp.float32)
    count = sent_ref.shape[0]
    first = EDGE - 2 * DILATION_STEP - KW // 2
    total = None
    for tap in range(KW):
        picked = [wide[j, pl.ds(first + tap, count, stride=2), :] for j in range(tiles)]
        taken = jnp.concatenate(picked, axis=1).astype(jnp.bfloat16)
        term = reduce_operands(taken, weight_ref[tap])
        total = term if total is None else total + term
    sent_ref[...] = total.astype(jnp.bfloat16)
    h1_ref[...] = total[DILATION_STEP : DILATION_STEP + rows // 2]


def first_conv(dna, low, high, weight):
    rows, width = dna.shape
    out = weight.shape[1]
    kept = jax.ShapeDtypeStruct((rows // 2, out), jnp.float32)
    sent = jax.ShapeDtypeStruct((rows // 2 + 2 * DILATION_STEP, out), jnp.bfloat16)
    return pl.pallas_call(
        conv_kernel,
        out_shape=(kept, sent),
        scratch_shapes=[pltpu.VMEM((width // 128, rows + 2 * EDGE, 128), jnp.float32)],
        compiler_params=pltpu.CompilerParams(vmem_limit_bytes=32 * MIB),
        cost_estimate=cost(
            2 * sent.shape[0] * out * width * KW, (dna, low, high, weight, kept, sent)
        ),
        name="first_conv",
    )(dna, low, high, weight)


def dilated_kernel(a0, a1, a2, a3, h1_ref, weight_ref, h2_ref, sent_ref, act):
    parts = (a0, a1, a2, a3)
    count, width = a0.shape
    rows = h1_ref.shape[0]
    squares = None
    for part in parts:
        block = part[...].astype(jnp.float32)
        term = jnp.sum(block * block, axis=1, keepdims=True)
        squares = term if squares is None else squares + term
    inverse = lax.rsqrt(squares / C + EPS)
    position = lax.axis_index("seq") * rows - DILATION_STEP + lax.broadcasted_iota(
        jnp.int32, (count, 1), 0
    )
    inside = (position >= 0) & (position < rows * lax.axis_size("seq"))
    inverse = jnp.where(inside, inverse, 0.0)
    total = h1_ref[...]
    for part, shift in zip(parts, SHIFTS):
        act[...] = jax.nn.gelu(part[...].astype(jnp.float32) * inverse, approximate=True)
        columns = pl.ds(pl.multiple_of(owner(shift) * width, 128), width)
        for tap in range(3):
            taken = act[pl.ds(tap * DILATION_STEP, rows), :].astype(jnp.bfloat16)
            total = total + reduce_operands(taken, weight_ref[tap, :, columns])
    h2_ref[...] = total
    sent_ref[...] = total.astype(jnp.bfloat16)


def second_conv(parts, h1, weight):
    count, width = parts[0].shape
    rows, out = h1.shape
    kept = jax.ShapeDtypeStruct((rows, out), jnp.float32)
    sent = jax.ShapeDtypeStruct((rows, out), jnp.bfloat16)
    return pl.pallas_call(
        dilated_kernel,
        out_shape=(kept, sent),
        scratch_shapes=[pltpu.VMEM((count, width), jnp.float32)],
        compiler_params=pltpu.CompilerParams(vmem_limit_bytes=32 * MIB),
        cost_estimate=cost(
            2 * rows * out * weight.shape[2] * 3,
            (*parts, h1, weight, kept, sent),
            count * weight.shape[2],
        ),
        name="second_conv",
    )(*parts, h1, weight)


def project_kernel(a0, a1, a2, a3, wq, wk, wv, q_ref, kv_ref):
    parts = (a0, a1, a2, a3)
    width = a0.shape[1]
    squares = None
    for part in parts:
        block = part[...].astype(jnp.float32)
        term = jnp.sum(block * block, axis=1, keepdims=True)
        squares = term if squares is None else squares + term
    inverse = lax.rsqrt(squares / C + EPS)

    def product(weight_ref):
        total = None
        for part, shift in zip(parts, SHIFTS):
            columns = pl.ds(pl.multiple_of(owner(shift) * width, 128), width)
            term = reduce_operands(part[...], weight_ref[:, columns])
            total = term if total is None else total + term
        return total

    out = wq.shape[0]
    kv_ref[:, :out] = (product(wk) * inverse).astype(jnp.bfloat16)
    kv_ref[:, out:] = (product(wv) * inverse).astype(jnp.bfloat16)
    scale = LOG2E / math.sqrt(HEAD_DIM)
    q_ref[...] = (product(wq) * (inverse * scale)).astype(jnp.bfloat16)


def project(parts, wq, wk, wv):
    rows = parts[0].shape[0]
    out = wq.shape[0]
    q = jax.ShapeDtypeStruct((rows, out), jnp.bfloat16)
    kv = jax.ShapeDtypeStruct((rows, 2 * out), jnp.bfloat16)
    return pl.pallas_call(
        project_kernel,
        out_shape=(q, kv),
        compiler_params=pltpu.CompilerParams(vmem_limit_bytes=32 * MIB),
        cost_estimate=cost(6 * rows * out * wq.shape[1], (*parts, wq, wk, wv, q, kv)),
        name="project",
    )(*parts, wq, wk, wv)


def attend_kernel(count, q_ref, *refs):
    keys, values = refs[:count], refs[count : 2 * count]
    w_ref, h2_ref, own_ref, p1, p2, p3, acc = refs[2 * count :]
    step = pl.program_id(0)
    rows, width = own_ref.shape
    tile = 128
    lane = lax.broadcasted_iota(jnp.int32, (tile, 2 * HEAD_DIM), 1)
    pieces = []
    for start in range(0, rows, tile):
        query = q_ref[pl.ds(start, tile), :]
        results = []
        for head in range(2):
            mine = (lane // HEAD_DIM) == head
            one = jnp.where(mine, query, jnp.zeros_like(query))
            scores = [reduce_operands(one, key[...]) for key in keys]
            top = functools.reduce(jnp.maximum, scores)
            top = jnp.max(top, axis=1, keepdims=True)
            total, out = None, None
            for score, value in zip(scores, values):
                weights = jnp.exp2(score - top)
                total = weights if total is None else total + weights
                term = jnp.dot(
                    weights.astype(jnp.bfloat16), value[...], preferred_element_type=jnp.float32
                )
                out = term if out is None else out + term
            results.append(out / jnp.sum(total, axis=1, keepdims=True))
        pieces.append(jnp.where(lane < HEAD_DIM, results[0], results[1]).astype(jnp.bfloat16))
    attended = jnp.concatenate(pieces, axis=0)
    product = jnp.dot(attended, w_ref[...], preferred_element_type=jnp.float32)

    @pl.when(step == 0)
    def _():
        acc[...] = product

    @pl.when(step > 0)
    def _():
        acc[...] += product

    @pl.when(step == pl.num_programs(0) - 1)
    def _():
        def block(shift):
            return acc[:, pl.ds(pl.multiple_of(owner(shift) * width, 128), width)]

        own_ref[...] = block(0) + h2_ref[...]
        for ref, shift in ((p1, 3), (p2, 1), (p3, 2)):
            ref[...] = block(shift).astype(jnp.bfloat16)


def attend(q, blocks, w_out, h2):
    rows, width = h2.shape
    pairs = width // (2 * HEAD_DIM)
    count = len(blocks)
    seen = blocks[0].shape[0]
    own = jax.ShapeDtypeStruct((rows, width), jnp.float32)
    part = jax.ShapeDtypeStruct((rows, width), jnp.bfloat16)
    lanes = 2 * HEAD_DIM
    return pl.pallas_call(
        functools.partial(attend_kernel, count),
        grid=(pairs,),
        out_shape=(own, part, part, part),
        in_specs=[pl.BlockSpec((rows, lanes), lambda g: (0, g))]
        + [pl.BlockSpec((seen, lanes), lambda g: (0, g))] * count
        + [pl.BlockSpec((seen, lanes), lambda g: (0, g + pairs))] * count
        + [pl.BlockSpec((lanes, w_out.shape[1]), lambda g: (g, 0)), whole(h2.shape)],
        out_specs=[whole((rows, width))] * 4,
        scratch_shapes=[pltpu.VMEM((rows, w_out.shape[1]), jnp.float32)],
        compiler_params=pltpu.CompilerParams(vmem_limit_bytes=40 * MIB),
        cost_estimate=cost(
            4 * rows * width * seen * count + 2 * rows * width * w_out.shape[1],
            (q, *blocks, w_out, h2, own, part, part, part),
            rows * seen * count * width // HEAD_DIM,
        ),
        name="attend",
    )(q, *blocks, *blocks, w_out, h2)


def exchanged(block, mask):
    count = lax.axis_size("seq")
    return lax.ppermute(block, "seq", [(i, i ^ mask) for i in range(count)])


def on_device(dna, conv_in, dilated_kernel_weight, w_query, w_key, w_value, w_out):
    count = lax.axis_size("seq")
    low = lax.ppermute(dna[-EDGE:], "seq", [(i, i + 1) for i in range(count - 1)])
    high = lax.ppermute(dna[:EDGE], "seq", [(i + 1, i) for i in range(count - 1)])
    h1, sent = first_conv(dna, low, high, conv_in)
    h2, sent = second_conv(shared(sent), h1, dilated_kernel_weight)
    q, kv = project(shared(sent), w_query, w_key, w_value)
    far = [exchanged(kv, mask) for mask in range(2, count, 2)]
    near = [kv] + far
    blocks = near + [exchanged(block, 1) for block in near]
    own, p1, p2, p3 = attend(q, blocks, w_out, h2)
    total = own
    for part, shift in ((p1, 1), (p2, 3), (p3, 2)):
        total = total + lax.ppermute(part, "head", rotate(shift)).astype(jnp.float32)
    return total.astype(jnp.bfloat16)


def solution(mesh):
    in_specs = (
        P("seq", None),
        P(None, "head", None),
        P(None, "head", None),
        P("head", None),
        P("head", None),
        P("head", None),
        P("head", None),
    )
    out_specs = P("seq", "head")
    seq, head = mesh.shape["seq"], mesh.shape["head"]
    aligned = (C // head) % 128 == 0
    body = on_device if head == 4 and seq & (seq - 1) == 0 and aligned else general_form
    return jax.shard_map(body, mesh=mesh, in_specs=in_specs, out_specs=out_specs, check_vma=False)
```

```python
import functools
import math

import jax
import jax.numpy as jnp
from jax import lax
from jax.experimental import pallas as pl
from jax.experimental.pallas import tpu as pltpu
from jax.sharding import PartitionSpec as P

C = 1536
HEAD_DIM = 64
KW = 5
DILATION_STEP = 4
EPS = 1e-06
EDGE = 16
LOG2E = math.log2(math.e)
MIB = 1 << 20


def padded_2(block, sides, width):
    for axis, dim in sides:
        count = lax.axis_size(axis)
        forward = [(i, i + 1) for i in range(count - 1)]
        backward = [(target, source) for source, target in forward]
        low = lax.ppermute(
            lax.slice_in_dim(block, block.shape[dim] - width, None, axis=dim), axis, forward
        )
        high = lax.ppermute(lax.slice_in_dim(block, 0, width, axis=dim), axis, backward)
        block = jnp.concatenate([low, block, high], axis=dim)
    return block


def row_scale(hidden):
    squares = lax.psum(jnp.sum(hidden * hidden, axis=1), "head")
    return hidden * lax.rsqrt(squares / C + EPS)[:, None]


def reduce_operands(left, right):
    return lax.dot_general(
        left, right, (((1,), (1,)), ((), ())), preferred_element_type=jnp.float32
    )


def general_form(dna, conv_in, dilated_kernel_weight, w_query, w_key, w_value, w_out):
    local_row_count = dna.shape[0] // 2
    half = (KW - 1) // 2
    padded = padded_2(dna, (("seq", 0),), half)
    h1 = jnp.zeros((local_row_count, conv_in.shape[1]), jnp.float32)
    for kernel_offset in range(KW):
        rows = lax.slice(
            padded,
            (kernel_offset, 0),
            (kernel_offset + 2 * local_row_count - 1, padded.shape[1]),
            (2, 1),
        )
        h1 = h1 + reduce_operands(rows, conv_in[kernel_offset])
    gelu_output = jax.nn.gelu(row_scale(h1), approximate=True).astype(jnp.bfloat16)
    complete_output = lax.all_gather(gelu_output, "head", axis=1, tiled=True)
    broad_input = padded_2(complete_output, (("seq", 0),), DILATION_STEP)
    second_hidden = h1
    for kernel_offset in range(3):
        second_hidden = second_hidden + reduce_operands(
            broad_input[
                DILATION_STEP * kernel_offset : DILATION_STEP * kernel_offset + local_row_count
            ],
            dilated_kernel_weight[kernel_offset],
        )
    normed = row_scale(second_hidden).astype(jnp.bfloat16)
    local_width = w_query.shape[0]
    heads_here = local_width // HEAD_DIM
    piece = lax.all_gather(normed, "head", axis=1, tiled=True)
    q_acc, k_acc, v_acc = (reduce_operands(piece, w) for w in (w_query, w_key, w_value))
    query = q_acc.astype(jnp.bfloat16).reshape(local_row_count, heads_here, HEAD_DIM)
    keys = k_acc.astype(jnp.bfloat16)
    values = v_acc.astype(jnp.bfloat16)
    scale = 1.0 / math.sqrt(HEAD_DIM)
    start_state = (
        jnp.full((heads_here, local_row_count), -1e30, jnp.float32),
        jnp.zeros((heads_here, local_row_count), jnp.float32),
        jnp.zeros((local_row_count, heads_here, HEAD_DIM), jnp.float32),
    )
    key_rows = lax.all_gather(keys, "seq", axis=0, tiled=True)
    value_rows = lax.all_gather(values, "seq", axis=0, tiled=True)
    count = key_rows.shape[0]
    width = 512 if count % 512 == 0 else count
    blocks = count // width
    key_blocks = key_rows.reshape(blocks, width, heads_here, HEAD_DIM)
    value_blocks = value_rows.reshape(blocks, width, heads_here, HEAD_DIM)

    def step(state, operands):
        running, total, acc = state
        key_block, value_block = operands
        scores = (
            jnp.einsum("qhd,khd->hqk", query, key_block, preferred_element_type=jnp.float32) * scale
        )
        newest = jnp.maximum(running, jnp.max(scores, axis=2))
        factor = jnp.exp(running - newest)
        weights = jnp.exp(scores - newest[:, :, None])
        total = total * factor + jnp.sum(weights, axis=2)
        update = jnp.einsum(
            "hqk,khd->qhd",
            weights.astype(jnp.bfloat16),
            value_block,
            preferred_element_type=jnp.float32,
        )
        acc = acc * jnp.transpose(factor)[:, :, None] + update
        return ((newest, total, acc), None)

    state, _ = lax.scan(step, start_state, (key_blocks, value_blocks))
    running, total, acc = state
    attended = (
        (acc / jnp.transpose(total)[:, :, None])
        .reshape(local_row_count, local_width)
        .astype(jnp.bfloat16)
    )
    partial_out = jnp.dot(attended, w_out, preferred_element_type=jnp.float32)
    mixed = lax.psum_scatter(
        partial_out.astype(jnp.bfloat16), "head", scatter_dimension=1, tiled=True
    ).astype(jnp.float32)
    return (second_hidden + mixed).astype(jnp.bfloat16)


def nbytes(*arrays):
    return sum(math.prod(a.shape) * jnp.dtype(a.dtype).itemsize for a in arrays)


def cost(flops, arrays, transcendentals=0):
    return pl.CostEstimate(
        flops=int(flops), bytes_accessed=int(nbytes(*arrays)), transcendentals=int(transcendentals)
    )


def rotate(offset):
    count = lax.axis_size("head")
    return [(i, (i + offset) % count) for i in range(count)]


def shared(block):
    count = lax.axis_size("head")
    return [block] + [lax.ppermute(block, "head", rotate(k)) for k in (1, count - 1, 2)]


def owner(k):
    count = lax.axis_size("head")
    return lax.rem(lax.axis_index("head") + count - k, count)


SHIFTS = (0, 1, 3, 2)


def store_wide(wide, start, block):
    for j in range(wide.shape[0]):
        rows = pl.ds(start, block.shape[0])
        wide[j, rows, :] = block[:, 128 * j : 128 * (j + 1)].astype(jnp.float32)


def taps_sum(wide, weight_ref, groups):
    total = None
    for tap in range(KW):
        picked = []
        for start, count in groups:
            lanes = [
                wide[j, pl.ds(start + tap, count, stride=2), :] for j in range(wide.shape[0])
            ]
            picked.append(jnp.concatenate(lanes, axis=1).astype(jnp.bfloat16))
        taken = picked[0] if len(picked) == 1 else jnp.concatenate(picked, axis=0)
        term = reduce_operands(taken, weight_ref[tap])
        total = term if total is None else total + term
    return total


FIRST = EDGE - KW // 2


def conv_middle_kernel(dna_ref, weight_ref, h1_ref, sent_ref, wide):
    store_wide(wide, 0, dna_ref[pl.ds(0, wide.shape[1]), :])
    total = taps_sum(wide, weight_ref, [(FIRST, sent_ref.shape[0])])
    h1_ref[...] = total
    sent_ref[...] = total.astype(jnp.bfloat16)


def conv_edge_kernel(dna_ref, low_ref, high_ref, weight_ref, h1_ref, sent_ref, wide):
    rows = dna_ref.shape[0]
    upper = sent_ref.shape[0] - EDGE
    first = rows - 2 * upper
    zeros = jnp.zeros((EDGE, dna_ref.shape[1]), jnp.bfloat16)
    store_wide(wide, 0, zeros)
    store_wide(wide, EDGE, low_ref[...])
    store_wide(wide, 2 * EDGE, dna_ref[pl.ds(0, 2 * EDGE), :])
    store_wide(wide, 4 * EDGE, dna_ref[pl.ds(first, rows - first), :])
    store_wide(wide, 4 * EDGE + rows - first, high_ref[...])
    store_wide(wide, 5 * EDGE + rows - first, zeros)
    total = taps_sum(wide, weight_ref, [(FIRST, EDGE), (4 * EDGE + FIRST, upper)])
    h1_ref[...] = total
    sent_ref[...] = total.astype(jnp.bfloat16)


def first_conv(kernel, operands, weight, count, deep, name):
    width, out = weight.shape[2], weight.shape[1]
    kept = jax.ShapeDtypeStruct((count, out), jnp.float32)
    sent = jax.ShapeDtypeStruct((count, out), jnp.bfloat16)
    return pl.pallas_call(
        kernel,
        out_shape=(kept, sent),
        scratch_shapes=[pltpu.VMEM((width // 128, deep, 128), jnp.float32)],
        compiler_params=pltpu.CompilerParams(vmem_limit_bytes=24 * MIB),
        cost_estimate=cost(2 * count * out * width * KW, (*operands, weight, kept, sent)),
        name=name,
    )(*operands, weight)


def inverse_norm(blocks):
    squares = None
    for block in blocks:
        term = jnp.sum(block * block, axis=1, keepdims=True)
        squares = term if squares is None else squares + term
    return lax.rsqrt(squares / C + EPS)


def wide_blocks(parts, start, count):
    return [part[pl.ds(start, count), :].astype(jnp.float32) for part in parts]


def gelu(value):
    return jax.nn.gelu(value, approximate=True)


def columns_of(shift, width):
    return pl.ds(pl.multiple_of(owner(shift) * width, 128), width)


def dilated_middle_kernel(a0, a1, a2, a3, h1_ref, weight_ref, h2_ref, sent_ref, act):
    parts = (a0, a1, a2, a3)
    count, width = a0.shape
    rows = h2_ref.shape[0]
    blocks = wide_blocks(parts, 0, count)
    inverse = inverse_norm(blocks)
    total = h1_ref[pl.ds(8, rows), :]
    for slot, (block, shift) in enumerate(zip(blocks, SHIFTS)):
        act[slot] = gelu(block * inverse)
        for tap in range(3):
            taken = act[slot, pl.ds((tap + 1) * DILATION_STEP, rows), :].astype(jnp.bfloat16)
            total = total + reduce_operands(taken, weight_ref[tap, :, columns_of(shift, width)])
    h2_ref[...] = total
    sent_ref[...] = total.astype(jnp.bfloat16)


def dilated_edge_kernel(
    m0, m1, m2, m3, e0, e1, e2, e3, hm_ref, he_ref, h2m_ref, weight_ref, h2_ref, sent_ref, act
):
    middle, edge = (m0, m1, m2, m3), (e0, e1, e2, e3)
    inner, width = m0.shape
    outer = e0.shape[0]
    rows = h2_ref.shape[0]
    upper = outer - EDGE
    position = lax.axis_index("seq") * rows + lax.broadcasted_iota(jnp.int32, (outer, 1), 0)
    place = lax.broadcasted_iota(jnp.int32, (outer, 1), 0)
    position = position + jnp.where(place < EDGE, -8, inner - 8)
    inside = (position >= 0) & (position < rows * lax.axis_size("seq"))
    outer_blocks = wide_blocks(edge, 0, outer)
    outer_inverse = jnp.where(inside, inverse_norm(outer_blocks), 0.0)
    low_blocks = wide_blocks(middle, 0, EDGE)
    low_inverse = inverse_norm(low_blocks)
    high_blocks = wide_blocks(middle, inner - EDGE, EDGE)
    high_inverse = inverse_norm(high_blocks)
    last = rows - (outer - EDGE)
    total = jnp.concatenate(
        [
            he_ref[pl.ds(8, 8), :],
            hm_ref[pl.ds(0, 8), :],
            hm_ref[pl.ds(inner - 8, 8), :],
            he_ref[pl.ds(EDGE, upper - 8), :],
        ],
        axis=0,
    )
    tail = 2 * EDGE
    for slot, shift in enumerate(SHIFTS):
        full = gelu(outer_blocks[slot] * outer_inverse)
        act[slot, pl.ds(0, EDGE), :] = full[:EDGE]
        act[slot, pl.ds(EDGE, EDGE), :] = gelu(low_blocks[slot] * low_inverse)
        act[slot, pl.ds(tail, EDGE), :] = gelu(high_blocks[slot] * high_inverse)
        act[slot, pl.ds(tail + EDGE, upper), :] = full[EDGE:]
        for tap in range(3):
            shifted = (tap + 1) * DILATION_STEP
            taken = jnp.concatenate(
                [
                    act[slot, pl.ds(shifted, EDGE), :],
                    act[slot, pl.ds(tail + shifted, upper), :],
                ],
                axis=0,
            ).astype(jnp.bfloat16)
            total = total + reduce_operands(taken, weight_ref[tap, :, columns_of(shift, width)])
    h2_ref[pl.ds(0, EDGE), :] = total[:EDGE]
    h2_ref[pl.ds(EDGE, last - EDGE), :] = h2m_ref[...]
    h2_ref[pl.ds(last, rows - last), :] = total[EDGE:]
    sent_ref[...] = total.astype(jnp.bfloat16)


def second_conv(kernel, operands, weight, kept_rows, sent_rows, deep, name):
    out, width = weight.shape[1], operands[0].shape[1]
    kept = jax.ShapeDtypeStruct((kept_rows, out), jnp.float32)
    sent = jax.ShapeDtypeStruct((sent_rows, out), jnp.bfloat16)
    return pl.pallas_call(
        kernel,
        out_shape=(kept, sent),
        scratch_shapes=[pltpu.VMEM((4, deep, width), jnp.float32)],
        compiler_params=pltpu.CompilerParams(vmem_limit_bytes=24 * MIB),
        cost_estimate=cost(
            2 * sent_rows * out * weight.shape[2] * 3,
            (*operands, weight, kept, sent),
            deep * weight.shape[2],
        ),
        name=name,
    )(*operands, weight)


def projections(parts, wq, wk, wv, kv_ref):
    width = parts[0].shape[1]
    inverse = inverse_norm([part[...].astype(jnp.float32) for part in parts])

    def product(weight_ref):
        total = None
        for part, shift in zip(parts, SHIFTS):
            term = reduce_operands(part[...], weight_ref[:, columns_of(shift, width)])
            total = term if total is None else total + term
        return total

    out = wq.shape[0]
    kv_ref[:, :out] = (product(wk) * inverse).astype(jnp.bfloat16)
    kv_ref[:, out:] = (product(wv) * inverse).astype(jnp.bfloat16)
    scale = LOG2E / math.sqrt(HEAD_DIM)
    return (product(wq) * (inverse * scale)).astype(jnp.bfloat16)


def project_middle_kernel(a0, a1, a2, a3, wq, wk, wv, q_ref, kv_ref):
    q_ref[...] = projections((a0, a1, a2, a3), wq, wk, wv, kv_ref)


def project_edge_kernel(a0, a1, a2, a3, qm_ref, wq, wk, wv, q_ref, kv_ref):
    query = projections((a0, a1, a2, a3), wq, wk, wv, kv_ref)
    inner, rows = qm_ref.shape[0], q_ref.shape[0]
    q_ref[pl.ds(0, EDGE), :] = query[:EDGE]
    q_ref[pl.ds(EDGE, inner), :] = qm_ref[...]
    q_ref[pl.ds(EDGE + inner, rows - EDGE - inner), :] = query[EDGE:]


def project(kernel, operands, weights, q_rows, name):
    rows, out = operands[0].shape[0], weights[0].shape[0]
    q = jax.ShapeDtypeStruct((q_rows, out), jnp.bfloat16)
    kv = jax.ShapeDtypeStruct((rows, 2 * out), jnp.bfloat16)
    return pl.pallas_call(
        kernel,
        out_shape=(q, kv),
        compiler_params=pltpu.CompilerParams(vmem_limit_bytes=20 * MIB),
        cost_estimate=cost(6 * rows * out * C, (*operands, *weights, q, kv)),
        name=name,
    )(*operands, *weights)


TILE = 64


def partial_attention(q_ref, blocks, scores, weights, head, lane):
    rows = q_ref.shape[0]
    width = q_ref.shape[1]
    seen = blocks[0].shape[0]
    pair = head // 2
    lanes = pl.ds(pair * 2 * HEAD_DIM, 2 * HEAD_DIM)
    mine = (lane // HEAD_DIM) == head % 2
    query = q_ref[:, lanes]
    query = jnp.where(mine, query, jnp.zeros_like(query))
    for i, block in enumerate(blocks):
        scores[:, pl.ds(i * seen, seen)] = reduce_operands(query, block[:, lanes])
    tops, sums = [], []
    extent = seen * len(blocks)
    for start in range(0, rows, TILE):
        tile = scores[pl.ds(start, TILE), pl.ds(0, extent)]
        top = jnp.max(tile, axis=1, keepdims=True)
        weight = jnp.exp2(tile - top)
        sums.append(jnp.sum(weight, axis=1, keepdims=True))
        tops.append(top)
        weights[pl.ds(start, TILE), pl.ds(0, extent)] = weight.astype(jnp.bfloat16)
    out = None
    for i, block in enumerate(blocks):
        value = block[:, pl.ds(width + pair * 2 * HEAD_DIM, 2 * HEAD_DIM)]
        term = jnp.dot(
            weights[:, pl.ds(i * seen, seen)], value, preferred_element_type=jnp.float32
        )
        out = term if out is None else out + term
    return out, jnp.concatenate(tops, axis=0), jnp.concatenate(sums, axis=0)


def attend_part_kernel(count, q_ref, *refs):
    blocks = refs[:count]
    out_ref, top_ref, sum_ref, scores, weights = refs[count:]
    rows, width = q_ref.shape
    lane = lax.broadcasted_iota(jnp.int32, (rows, 2 * HEAD_DIM), 1)
    tops, sums = jnp.zeros_like(top_ref), jnp.zeros_like(sum_ref)
    for pair in range(width // (2 * HEAD_DIM)):
        halves = []
        for half in range(2):
            head = 2 * pair + half
            out, top, total = partial_attention(
                q_ref, blocks, scores.at[half], weights.at[half], head, lane
            )
            halves.append(out)
            tops = jnp.where(lane == head, top, tops)
            sums = jnp.where(lane == head, total, sums)
        lanes = pl.ds(pair * 2 * HEAD_DIM, 2 * HEAD_DIM)
        out_ref[:, lanes] = jnp.where(lane < HEAD_DIM, halves[0], halves[1])
    top_ref[...] = tops
    sum_ref[...] = sums


def attend_last_kernel(count, earlier, q_ref, *refs):
    blocks = refs[:count]
    states = [refs[count + 3 * i : count + 3 * i + 3] for i in range(earlier)]
    w_ref, h2_ref, own_ref, p1, p2, p3, scores, weights, attended = refs[count + 3 * earlier :]
    rows, width = q_ref.shape
    lane = lax.broadcasted_iota(jnp.int32, (rows, 2 * HEAD_DIM), 1)
    for pair in range(width // (2 * HEAD_DIM)):
        lanes = pl.ds(pair * 2 * HEAD_DIM, 2 * HEAD_DIM)
        halves = []
        for half in range(2):
            head = 2 * pair + half
            out, top, total = partial_attention(
                q_ref, blocks, scores.at[half], weights.at[half], head, lane
            )
            tops = [top] + [state[1][:, head : head + 1] for state in states]
            sums = [total] + [state[2][:, head : head + 1] for state in states]
            outs = [out] + [state[0][:, lanes] for state in states]
            highest = functools.reduce(jnp.maximum, tops)
            factors = [jnp.exp2(one - highest) for one in tops]
            norm = sum(f * one for f, one in zip(factors, sums))
            mixed = sum(f * one for f, one in zip(factors, outs))
            halves.append(mixed / norm)
        merged = jnp.where(lane < HEAD_DIM, halves[0], halves[1])
        attended[:, lanes] = merged.astype(jnp.bfloat16)

    def product(shift):
        return jnp.dot(
            attended[...], w_ref[:, columns_of(shift, width)], preferred_element_type=jnp.float32
        )

    for ref, shift in ((p3, 2), (p1, 3), (p2, 1)):
        ref[...] = product(shift).astype(jnp.bfloat16)
    own_ref[...] = product(0) + h2_ref[...]


def attention_scratch(rows, extent):
    return [
        pltpu.VMEM((2, rows, extent), jnp.float32),
        pltpu.VMEM((2, rows, extent), jnp.bfloat16),
    ]


def attend_part(q, blocks, name):
    rows, width = q.shape
    extent = sum(block.shape[0] for block in blocks)
    state = (
        jax.ShapeDtypeStruct((rows, width), jnp.float32),
        jax.ShapeDtypeStruct((rows, 2 * HEAD_DIM), jnp.float32),
        jax.ShapeDtypeStruct((rows, 2 * HEAD_DIM), jnp.float32),
    )
    return pl.pallas_call(
        functools.partial(attend_part_kernel, len(blocks)),
        out_shape=state,
        scratch_shapes=attention_scratch(rows, extent),
        compiler_params=pltpu.CompilerParams(vmem_limit_bytes=24 * MIB),
        cost_estimate=cost(
            4 * rows * width * extent, (q, *blocks, *state), rows * extent * width // HEAD_DIM
        ),
        name=name,
    )(q, *blocks)


def attend_last(q, blocks, states, w_out, h2, name):
    rows, width = q.shape
    extent = sum(block.shape[0] for block in blocks)
    own = jax.ShapeDtypeStruct((rows, width), jnp.float32)
    part = jax.ShapeDtypeStruct((rows, width), jnp.bfloat16)
    flat = [array for state in states for array in state]
    return pl.pallas_call(
        functools.partial(attend_last_kernel, len(blocks), len(states)),
        out_shape=(own, part, part, part),
        scratch_shapes=attention_scratch(rows, extent) + [pltpu.VMEM((rows, width), jnp.bfloat16)],
        compiler_params=pltpu.CompilerParams(vmem_limit_bytes=24 * MIB),
        cost_estimate=cost(
            4 * rows * width * extent + 2 * rows * width * w_out.shape[1],
            (q, *blocks, *flat, w_out, h2, own, part, part, part),
            rows * extent * width // HEAD_DIM,
        ),
        name=name,
    )(q, *blocks, *flat, w_out, h2)


def exchanged(block, mask):
    count = lax.axis_size("seq")
    return lax.ppermute(block, "seq", [(i, i ^ mask) for i in range(count)])


def on_device(dna, conv_in, dilated_kernel_weight, w_query, w_key, w_value, w_out):
    count = lax.axis_size("seq")
    rows = dna.shape[0] // 2
    inner = rows // 2
    low = lax.ppermute(dna[-EDGE:], "seq", [(i, i + 1) for i in range(count - 1)])
    high = lax.ppermute(dna[:EDGE], "seq", [(i + 1, i) for i in range(count - 1)])
    h1_m, sent = first_conv(
        conv_middle_kernel, (dna,), conv_in, inner + EDGE, rows + 4 * EDGE, "conv_middle"
    )
    wide_m = shared(sent)
    h1_e, sent = first_conv(
        conv_edge_kernel, (dna, low, high), conv_in, inner, rows + 4 * EDGE, "conv_edge"
    )
    wide_e = shared(sent)
    h2_m, sent = second_conv(
        dilated_middle_kernel,
        (*wide_m, h1_m),
        dilated_kernel_weight,
        inner,
        inner,
        inner + EDGE,
        "dilated_middle",
    )
    normed_m = shared(sent)
    h2, sent = second_conv(
        dilated_edge_kernel,
        (*wide_m, *wide_e, h1_m, h1_e, h2_m),
        dilated_kernel_weight,
        rows,
        inner,
        inner + 2 * EDGE,
        "dilated_edge",
    )
    normed_e = shared(sent)
    weights = (w_query, w_key, w_value)
    q_m, kv_m = project(project_middle_kernel, normed_m, weights, inner, "project_middle")
    q, kv_e = project(project_edge_kernel, (*normed_e, q_m), weights, rows, "project_edge")

    def with_near(block):
        return [block, exchanged(block, 1)]

    x_m, y_m = exchanged(kv_m, 2), exchanged(kv_m, 4)
    d_m = exchanged(x_m, 4)
    x_e, y_e = exchanged(kv_e, 2), exchanged(kv_e, 4)
    d_e = exchanged(y_e, 2)
    first = [kv for block in (kv_m, x_m, y_m, d_m) for kv in with_near(block)]
    second = [kv for block in (kv_e, x_e, y_e) for kv in with_near(block)]
    states = [attend_part(q, first, "attend_m"), attend_part(q, second, "attend_e")]
    own, p1, p2, p3 = attend_last(q, with_near(d_e), states, w_out, h2, "attend_last")
    total = own
    for part, shift in ((p1, 1), (p2, 3), (p3, 2)):
        total = total + lax.ppermute(part, "head", rotate(shift)).astype(jnp.float32)
    return total.astype(jnp.bfloat16)


def solution(mesh):
    in_specs = (
        P("seq", None),
        P(None, "head", None),
        P(None, "head", None),
        P("head", None),
        P("head", None),
        P("head", None),
        P("head", None),
    )
    out_specs = P("seq", "head")
    seq, head = mesh.shape["seq"], mesh.shape["head"]
    aligned = (C // head) % 128 == 0
    body = on_device if head == 4 and seq == 8 and aligned else general_form
    return jax.shard_map(body, mesh=mesh, in_specs=in_specs, out_specs=out_specs, check_vma=False)
```

```python
import functools
import math

import jax
import jax.numpy as jnp
from jax import lax
from jax.experimental import pallas as pl
from jax.experimental.pallas import tpu as pltpu
from jax.sharding import PartitionSpec as P

C = 1536
HEAD_DIM = 64
KW = 5
DILATION_STEP = 4
EPS = 1e-06
EDGE = 16
LOG2E = math.log2(math.e)
MIB = 1 << 20
LANES = 128


def padded_2(block, sides, width):
    for axis, dim in sides:
        count = lax.axis_size(axis)
        forward = [(i, i + 1) for i in range(count - 1)]
        backward = [(target, source) for source, target in forward]
        low = lax.ppermute(
            lax.slice_in_dim(block, block.shape[dim] - width, None, axis=dim), axis, forward
        )
        high = lax.ppermute(lax.slice_in_dim(block, 0, width, axis=dim), axis, backward)
        block = jnp.concatenate([low, block, high], axis=dim)
    return block


def row_scale(hidden):
    squares = lax.psum(jnp.sum(hidden * hidden, axis=1), "head")
    return hidden * lax.rsqrt(squares / C + EPS)[:, None]


def reduce_operands(left, right):
    return lax.dot_general(
        left, right, (((1,), (1,)), ((), ())), preferred_element_type=jnp.float32
    )


def general_form(dna, conv_in, dilated_kernel_weight, w_query, w_key, w_value, w_out):
    local_row_count = dna.shape[0] // 2
    half = (KW - 1) // 2
    padded = padded_2(dna, (("seq", 0),), half)
    h1 = jnp.zeros((local_row_count, conv_in.shape[1]), jnp.float32)
    for kernel_offset in range(KW):
        rows = lax.slice(
            padded,
            (kernel_offset, 0),
            (kernel_offset + 2 * local_row_count - 1, padded.shape[1]),
            (2, 1),
        )
        h1 = h1 + reduce_operands(rows, conv_in[kernel_offset])
    gelu_output = jax.nn.gelu(row_scale(h1), approximate=True).astype(jnp.bfloat16)
    complete_output = lax.all_gather(gelu_output, "head", axis=1, tiled=True)
    broad_input = padded_2(complete_output, (("seq", 0),), DILATION_STEP)
    second_hidden = h1
    for kernel_offset in range(3):
        second_hidden = second_hidden + reduce_operands(
            broad_input[
                DILATION_STEP * kernel_offset : DILATION_STEP * kernel_offset + local_row_count
            ],
            dilated_kernel_weight[kernel_offset],
        )
    normed = row_scale(second_hidden).astype(jnp.bfloat16)
    local_width = w_query.shape[0]
    heads_here = local_width // HEAD_DIM
    piece = lax.all_gather(normed, "head", axis=1, tiled=True)
    q_acc, k_acc, v_acc = (reduce_operands(piece, w) for w in (w_query, w_key, w_value))
    query = q_acc.astype(jnp.bfloat16).reshape(local_row_count, heads_here, HEAD_DIM)
    keys = k_acc.astype(jnp.bfloat16)
    values = v_acc.astype(jnp.bfloat16)
    scale = 1.0 / math.sqrt(HEAD_DIM)
    start_state = (
        jnp.full((heads_here, local_row_count), -1e30, jnp.float32),
        jnp.zeros((heads_here, local_row_count), jnp.float32),
        jnp.zeros((local_row_count, heads_here, HEAD_DIM), jnp.float32),
    )
    key_rows = lax.all_gather(keys, "seq", axis=0, tiled=True)
    value_rows = lax.all_gather(values, "seq", axis=0, tiled=True)
    count = key_rows.shape[0]
    width = 512 if count % 512 == 0 else count
    blocks = count // width
    key_blocks = key_rows.reshape(blocks, width, heads_here, HEAD_DIM)
    value_blocks = value_rows.reshape(blocks, width, heads_here, HEAD_DIM)

    def step(state, operands):
        running, total, acc = state
        key_block, value_block = operands
        scores = (
            jnp.einsum("qhd,khd->hqk", query, key_block, preferred_element_type=jnp.float32) * scale
        )
        newest = jnp.maximum(running, jnp.max(scores, axis=2))
        factor = jnp.exp(running - newest)
        weights = jnp.exp(scores - newest[:, :, None])
        total = total * factor + jnp.sum(weights, axis=2)
        update = jnp.einsum(
            "hqk,khd->qhd",
            weights.astype(jnp.bfloat16),
            value_block,
            preferred_element_type=jnp.float32,
        )
        acc = acc * jnp.transpose(factor)[:, :, None] + update
        return ((newest, total, acc), None)

    state, _ = lax.scan(step, start_state, (key_blocks, value_blocks))
    running, total, acc = state
    attended = (
        (acc / jnp.transpose(total)[:, :, None])
        .reshape(local_row_count, local_width)
        .astype(jnp.bfloat16)
    )
    partial_out = jnp.dot(attended, w_out, preferred_element_type=jnp.float32)
    mixed = lax.psum_scatter(
        partial_out.astype(jnp.bfloat16), "head", scatter_dimension=1, tiled=True
    ).astype(jnp.float32)
    return (second_hidden + mixed).astype(jnp.bfloat16)


def nbytes(*arrays):
    return sum(math.prod(a.shape) * jnp.dtype(a.dtype).itemsize for a in arrays)


def cost(flops, arrays, transcendentals=0):
    return pl.CostEstimate(
        flops=int(flops), bytes_accessed=int(nbytes(*arrays)), transcendentals=int(transcendentals)
    )


def rotate(offset):
    count = lax.axis_size("head")
    return [(i, (i + offset) % count) for i in range(count)]


def after(value, *others):
    return lax.optimization_barrier((value, *others))[0]


def shared(block, earlier=(None, None, None)):
    count = lax.axis_size("head")
    moved = []
    for k, previous in zip((1, count - 1, 2), earlier):
        held = block if previous is None else after(block, previous)
        moved.append(lax.ppermute(held, "head", rotate(k)))
    return [block, *moved]


def owner(k):
    count = lax.axis_size("head")
    return lax.rem(lax.axis_index("head") + count - k, count)


SHIFTS = (0, 1, 3, 2)


def store_wide(wide, start, block):
    for j in range(wide.shape[0]):
        rows = pl.ds(start, block.shape[0])
        wide[j, rows, :] = block[:, 128 * j : 128 * (j + 1)].astype(jnp.float32)


def taps_sum(wide, weight_ref, groups):
    total = None
    for tap in range(KW):
        picked = []
        for start, count in groups:
            lanes = [
                wide[j, pl.ds(start + tap, count, stride=2), :] for j in range(wide.shape[0])
            ]
            picked.append(jnp.concatenate(lanes, axis=1).astype(jnp.bfloat16))
        taken = picked[0] if len(picked) == 1 else jnp.concatenate(picked, axis=0)
        term = reduce_operands(taken, weight_ref[tap])
        total = term if total is None else total + term
    return total


FIRST = EDGE - KW // 2


def conv_middle_kernel(dna_ref, weight_ref, h1_ref, sent_ref, wide):
    store_wide(wide, 0, dna_ref[pl.ds(0, wide.shape[1]), :])
    total = taps_sum(wide, weight_ref, [(FIRST, sent_ref.shape[0])])
    h1_ref[...] = total
    sent_ref[...] = total.astype(jnp.bfloat16)


def conv_edge_kernel(dna_ref, low_ref, high_ref, weight_ref, h1_ref, sent_ref, wide):
    rows = dna_ref.shape[0]
    upper = sent_ref.shape[0] - EDGE
    first = rows - 2 * upper
    zeros = jnp.zeros((EDGE, dna_ref.shape[1]), jnp.bfloat16)
    store_wide(wide, 0, zeros)
    store_wide(wide, EDGE, low_ref[...])
    store_wide(wide, 2 * EDGE, dna_ref[pl.ds(0, 2 * EDGE), :])
    store_wide(wide, 4 * EDGE, dna_ref[pl.ds(first, rows - first), :])
    store_wide(wide, 4 * EDGE + rows - first, high_ref[...])
    store_wide(wide, 5 * EDGE + rows - first, zeros)
    total = taps_sum(wide, weight_ref, [(FIRST, EDGE), (4 * EDGE + FIRST, upper)])
    h1_ref[...] = total
    sent_ref[...] = total.astype(jnp.bfloat16)


def first_conv(kernel, operands, weight, count, deep, name):
    width, out = weight.shape[2], weight.shape[1]
    kept = jax.ShapeDtypeStruct((count, out), jnp.float32)
    sent = jax.ShapeDtypeStruct((count, out), jnp.bfloat16)
    return pl.pallas_call(
        kernel,
        out_shape=(kept, sent),
        scratch_shapes=[pltpu.VMEM((width // 128, deep, 128), jnp.float32)],
        compiler_params=pltpu.CompilerParams(vmem_limit_bytes=24 * MIB),
        cost_estimate=cost(2 * count * out * width * KW, (*operands, weight, kept, sent)),
        name=name,
    )(*operands, weight)


def inverse_norm(blocks):
    squares = None
    for block in blocks:
        term = jnp.sum(block * block, axis=1, keepdims=True)
        squares = term if squares is None else squares + term
    return lax.rsqrt(squares / C + EPS)


def wide_blocks(parts, start, count):
    return [part[pl.ds(start, count), :].astype(jnp.float32) for part in parts]


def gelu(value):
    return jax.nn.gelu(value, approximate=True)


def columns_of(shift, width):
    return pl.ds(pl.multiple_of(owner(shift) * width, 128), width)


def dilated_middle_kernel(a0, a1, a2, a3, h1_ref, weight_ref, h2_ref, sent_ref, act):
    parts = (a0, a1, a2, a3)
    count, width = a0.shape
    rows = h2_ref.shape[0]
    blocks = wide_blocks(parts, 0, count)
    inverse = inverse_norm(blocks)
    total = h1_ref[pl.ds(8, rows), :]
    for slot, (block, shift) in enumerate(zip(blocks, SHIFTS)):
        act[slot] = gelu(block * inverse)
        for tap in range(3):
            taken = act[slot, pl.ds((tap + 1) * DILATION_STEP, rows), :].astype(jnp.bfloat16)
            total = total + reduce_operands(taken, weight_ref[tap, :, columns_of(shift, width)])
    h2_ref[...] = total
    sent_ref[...] = total.astype(jnp.bfloat16)


def dilated_edge_kernel(
    m0, m1, m2, m3, e0, e1, e2, e3, hm_ref, he_ref, h2m_ref, weight_ref, h2_ref, sent_ref, act
):
    middle, edge = (m0, m1, m2, m3), (e0, e1, e2, e3)
    inner, width = m0.shape
    outer = e0.shape[0]
    rows = h2_ref.shape[0]
    upper = outer - EDGE
    position = lax.axis_index("seq") * rows + lax.broadcasted_iota(jnp.int32, (outer, 1), 0)
    place = lax.broadcasted_iota(jnp.int32, (outer, 1), 0)
    position = position + jnp.where(place < EDGE, -8, inner - 8)
    inside = (position >= 0) & (position < rows * lax.axis_size("seq"))
    outer_blocks = wide_blocks(edge, 0, outer)
    outer_inverse = jnp.where(inside, inverse_norm(outer_blocks), 0.0)
    low_blocks = wide_blocks(middle, 0, EDGE)
    low_inverse = inverse_norm(low_blocks)
    high_blocks = wide_blocks(middle, inner - EDGE, EDGE)
    high_inverse = inverse_norm(high_blocks)
    last = rows - (outer - EDGE)
    total = jnp.concatenate(
        [
            he_ref[pl.ds(8, 8), :],
            hm_ref[pl.ds(0, 8), :],
            hm_ref[pl.ds(inner - 8, 8), :],
            he_ref[pl.ds(EDGE, upper - 8), :],
        ],
        axis=0,
    )
    tail = 2 * EDGE
    for slot, shift in enumerate(SHIFTS):
        full = gelu(outer_blocks[slot] * outer_inverse)
        act[slot, pl.ds(0, EDGE), :] = full[:EDGE]
        act[slot, pl.ds(EDGE, EDGE), :] = gelu(low_blocks[slot] * low_inverse)
        act[slot, pl.ds(tail, EDGE), :] = gelu(high_blocks[slot] * high_inverse)
        act[slot, pl.ds(tail + EDGE, upper), :] = full[EDGE:]
        for tap in range(3):
            shifted = (tap + 1) * DILATION_STEP
            taken = jnp.concatenate(
                [
                    act[slot, pl.ds(shifted, EDGE), :],
                    act[slot, pl.ds(tail + shifted, upper), :],
                ],
                axis=0,
            ).astype(jnp.bfloat16)
            total = total + reduce_operands(taken, weight_ref[tap, :, columns_of(shift, width)])
    h2_ref[pl.ds(0, EDGE), :] = total[:EDGE]
    h2_ref[pl.ds(EDGE, last - EDGE), :] = h2m_ref[...]
    h2_ref[pl.ds(last, rows - last), :] = total[EDGE:]
    sent_ref[...] = total.astype(jnp.bfloat16)


def second_conv(kernel, operands, weight, kept_rows, sent_rows, deep, name):
    out, width = weight.shape[1], operands[0].shape[1]
    kept = jax.ShapeDtypeStruct((kept_rows, out), jnp.float32)
    sent = jax.ShapeDtypeStruct((sent_rows, out), jnp.bfloat16)
    return pl.pallas_call(
        kernel,
        out_shape=(kept, sent),
        scratch_shapes=[pltpu.VMEM((4, deep, width), jnp.float32)],
        compiler_params=pltpu.CompilerParams(vmem_limit_bytes=24 * MIB),
        cost_estimate=cost(
            2 * sent_rows * out * weight.shape[2] * 3,
            (*operands, weight, kept, sent),
            deep * weight.shape[2],
        ),
        name=name,
    )(*operands, weight)


def projections(parts, wq, wk, wv, kv_ref):
    width = parts[0].shape[1]
    rows, out = parts[0].shape[0], wq.shape[0]
    blocks = [part[...].astype(jnp.float32) for part in parts]
    inverse = inverse_norm(blocks)
    normed = [(block * inverse).astype(jnp.bfloat16) for block in blocks]

    def product(weight_ref, weight_first):
        total = None
        for part, shift in zip(normed, SHIFTS):
            weight = weight_ref[:, columns_of(shift, width)]
            pair = (weight, part) if weight_first else (part, weight)
            term = reduce_operands(*pair)
            total = term if total is None else total + term
        return total

    kv_ref[:, :out] = product(wk, False).astype(jnp.bfloat16)
    value = product(wv, True).astype(jnp.bfloat16)
    for row in range(0, rows, LANES):
        for lane in range(0, out, LANES):
            kv_ref[pl.ds(row, LANES), pl.ds(out + lane, LANES)] = value[
                lane : lane + LANES, row : row + LANES
            ]
    scale = LOG2E / math.sqrt(HEAD_DIM)
    return (product(wq, False) * scale).astype(jnp.bfloat16)


def project_middle_kernel(a0, a1, a2, a3, wq, wk, wv, q_ref, kv_ref):
    q_ref[...] = projections((a0, a1, a2, a3), wq, wk, wv, kv_ref)


def project_edge_kernel(a0, a1, a2, a3, qm_ref, wq, wk, wv, q_ref, kv_ref):
    query = projections((a0, a1, a2, a3), wq, wk, wv, kv_ref)
    inner, rows = qm_ref.shape[0], q_ref.shape[0]
    q_ref[pl.ds(0, EDGE), :] = query[:EDGE]
    q_ref[pl.ds(EDGE, inner), :] = qm_ref[...]
    q_ref[pl.ds(EDGE + inner, rows - EDGE - inner), :] = query[EDGE:]


def project(kernel, operands, weights, q_rows, name):
    rows, out = operands[0].shape[0], weights[0].shape[0]
    q = jax.ShapeDtypeStruct((q_rows, out), jnp.bfloat16)
    kv = jax.ShapeDtypeStruct((rows, 2 * out), jnp.bfloat16)
    return pl.pallas_call(
        kernel,
        out_shape=(q, kv),
        compiler_params=pltpu.CompilerParams(vmem_limit_bytes=20 * MIB),
        cost_estimate=cost(6 * rows * out * C, (*operands, *weights, q, kv)),
        name=name,
    )(*operands, *weights)


TILE = 64


def partial_attention(query, blocks, scores, weights, head, lane):
    width = query.shape[1]
    pair, half = divmod(head, 2)
    lanes = slice(pair * LANES, (pair + 1) * LANES)
    mine = query[:, lanes]
    mine = jnp.where((lane // HEAD_DIM) == half, mine, jnp.zeros_like(mine))
    keys = jnp.concatenate([block[:, lanes] for block in blocks], axis=0)
    scores[...] = reduce_operands(keys, mine)
    columns = scores.shape[1]
    top = None
    for start in range(0, scores.shape[0], TILE):
        tile = jnp.max(scores[pl.ds(start, TILE), :].reshape(-1, 8, columns), axis=0)
        top = tile if top is None else jnp.maximum(top, tile)
    top = jnp.max(top, axis=0, keepdims=True)
    total = None
    for start in range(0, scores.shape[0], TILE):
        weight = jnp.exp2(scores[pl.ds(start, TILE), :] - top)
        tile = jnp.sum(weight.reshape(-1, 8, columns), axis=0)
        total = tile if total is None else total + tile
        weights[pl.ds(start, TILE), :] = weight.astype(jnp.bfloat16)
    values = [
        block[pl.ds(row + half * HEAD_DIM, HEAD_DIM), pl.ds(width + pair * LANES, LANES)]
        for block in blocks
        for row in range(0, block.shape[0], LANES)
    ]
    values = jnp.concatenate(values, axis=1)
    out = jnp.dot(values, weights[...], preferred_element_type=jnp.float32)
    return out, top, jnp.sum(total, axis=0, keepdims=True)


def state_parts(state, head, width, columns):
    return (
        state[pl.ds(head * HEAD_DIM, HEAD_DIM), columns],
        state[pl.ds(width + head, 1), columns],
        state[pl.ds(width + 8 + head, 1), columns],
    )


def merged_parts(one, other):
    top = jnp.maximum(one[1], other[1])
    first, second = jnp.exp2(one[1] - top), jnp.exp2(other[1] - top)
    return first * one[0] + second * other[0], top, first * one[2] + second * other[2]


def attend_kernel(first_column, q_refs, blocks, state, out_ref, scores, weights):
    width = q_refs[0].shape[1]
    query = jnp.concatenate([ref[...] for ref in q_refs], axis=0)
    columns = query.shape[0]
    lane = lax.broadcasted_iota(jnp.int32, (columns, LANES), 1)
    out_ref[pl.ds(width, 16), :] = jnp.zeros((16, columns), jnp.float32)
    for head in range(width // HEAD_DIM):
        part = partial_attention(
            query, blocks, scores.at[head % 2], weights.at[head % 2], head, lane
        )
        if state is not None:
            part = merged_parts(
                part, state_parts(state, head, width, pl.ds(first_column, columns))
            )
        out_ref[pl.ds(head * HEAD_DIM, HEAD_DIM), :] = part[0]
        out_ref[pl.ds(width + head, 1), :] = part[1]
        out_ref[pl.ds(width + 8 + head, 1), :] = part[2]


def attend(queries, blocks, state, first_column, name):
    rows, width = queries[0].shape
    columns = rows * len(queries)
    extent = sum(block.shape[0] for block in blocks)
    out = jax.ShapeDtypeStruct((width + 16, columns), jnp.float32)
    operands = (*queries, *blocks) + (() if state is None else (state,))

    def kernel(*refs):
        q_refs, block_refs = refs[: len(queries)], refs[len(queries) :][: len(blocks)]
        state_ref = None if state is None else refs[len(operands) - 1]
        attend_kernel(
            first_column, q_refs, block_refs, state_ref, *refs[len(operands) :]
        )

    return pl.pallas_call(
        kernel,
        out_shape=out,
        scratch_shapes=[
            pltpu.VMEM((2, extent, columns), jnp.float32),
            pltpu.VMEM((2, extent, columns), jnp.bfloat16),
        ],
        compiler_params=pltpu.CompilerParams(vmem_limit_bytes=24 * MIB),
        cost_estimate=cost(
            4 * columns * width * extent, (*operands, out), columns * extent * width // HEAD_DIM
        ),
        name=name,
    )(*operands)


def mix_kernel(own_state, other_state, w_ref, h2_ref, own_ref, p1, p2, p3, attended):
    rows, width = h2_ref.shape
    for pair in range(width // LANES):
        halves = []
        for head in (2 * pair, 2 * pair + 1):
            out, _, total = merged_parts(
                state_parts(own_state, head, width, pl.ds(0, rows)),
                state_parts(other_state, head, width, pl.ds(0, rows)),
            )
            halves.append(out / total)
        merged = jnp.transpose(jnp.concatenate(halves, axis=0))
        attended[:, pl.ds(pair * LANES, LANES)] = merged.astype(jnp.bfloat16)

    def product(shift):
        return jnp.dot(
            attended[...], w_ref[:, columns_of(shift, width)], preferred_element_type=jnp.float32
        )

    for ref, shift in ((p3, 2), (p1, 3), (p2, 1)):
        ref[...] = product(shift).astype(jnp.bfloat16)
    own_ref[...] = product(0) + h2_ref[...]


def mix(own_state, other_state, w_out, h2):
    rows, width = h2.shape
    own = jax.ShapeDtypeStruct((rows, width), jnp.float32)
    part = jax.ShapeDtypeStruct((rows, width), jnp.bfloat16)
    operands = (own_state, other_state, w_out, h2)
    return pl.pallas_call(
        mix_kernel,
        out_shape=(own, part, part, part),
        scratch_shapes=[pltpu.VMEM((rows, width), jnp.bfloat16)],
        compiler_params=pltpu.CompilerParams(vmem_limit_bytes=16 * MIB),
        cost_estimate=cost(
            2 * rows * width * w_out.shape[1], (*operands, own, part, part, part)
        ),
        name="mix",
    )(*operands)


def exchanged(block, mask):
    count = lax.axis_size("seq")
    return lax.ppermute(block, "seq", [(i, i ^ mask) for i in range(count)])


def on_device(dna, conv_in, dilated_kernel_weight, w_query, w_key, w_value, w_out):
    count = lax.axis_size("seq")
    rows = dna.shape[0] // 2
    inner = 2 * LANES
    outer = rows - inner
    low = lax.ppermute(dna[-EDGE:], "seq", [(i, i + 1) for i in range(count - 1)])
    high = lax.ppermute(dna[:EDGE], "seq", [(i + 1, i) for i in range(count - 1)])
    h1_m, sent = first_conv(
        conv_middle_kernel, (dna,), conv_in, inner + EDGE, 2 * (inner + 2 * EDGE), "conv_middle"
    )
    wide_m = shared(sent)
    h1_e, sent = first_conv(
        conv_edge_kernel, (dna, low, high), conv_in, outer, 2 * (outer + 2 * EDGE), "conv_edge"
    )
    wide_e = shared(sent, (None, None, wide_m[1]))
    h2_m, sent = second_conv(
        dilated_middle_kernel,
        (*wide_m, after(h1_m, sent)),
        dilated_kernel_weight,
        inner,
        inner,
        inner + EDGE,
        "dilated_middle",
    )
    normed_m = shared(sent, wide_e[1:])
    h2, sent = second_conv(
        dilated_edge_kernel,
        (*wide_m, *wide_e, h1_m, h1_e, h2_m),
        dilated_kernel_weight,
        rows,
        outer,
        outer + 2 * EDGE,
        "dilated_edge",
    )
    normed_e = shared(sent, normed_m[1:])
    normed_m[0] = after(normed_m[0], sent)
    weights = (w_query, w_key, w_value)
    q_m, kv_m = project(project_middle_kernel, normed_m, weights, inner, "project_middle")
    x_m, y_m = exchanged(kv_m, 2), exchanged(kv_m, 4)
    normed_e[0] = after(normed_e[0], x_m)
    d_m = exchanged(x_m, 4)
    q, kv_e = project(project_edge_kernel, (*normed_e, q_m), weights, rows, "project_edge")
    x_e, y_e, q_other = exchanged(kv_e, 2), exchanged(kv_e, 4), exchanged(q, 1)
    d_e = exchanged(y_e, 2)
    state = attend((q, q_other), (kv_m, x_m, y_m, d_m), None, 0, "attend_m")
    late = (kv_e, x_e, y_e, d_e)
    state_other = attend((q_other,), late, state, rows, "attend_other")
    given = exchanged(state_other, 1)
    state_own = attend((q,), late, state, 0, "attend_own")
    own, p1, p2, p3 = mix(state_own, given, w_out, h2)
    total = own
    for part, shift in ((p1, 1), (p2, 3), (p3, 2)):
        total = total + lax.ppermute(part, "head", rotate(shift)).astype(jnp.float32)
    return total.astype(jnp.bfloat16)


def solution(mesh):
    in_specs = (
        P("seq", None),
        P(None, "head", None),
        P(None, "head", None),
        P("head", None),
        P("head", None),
        P("head", None),
        P("head", None),
    )
    out_specs = P("seq", "head")
    seq, head = mesh.shape["seq"], mesh.shape["head"]
    aligned = (C // head) % 128 == 0
    body = on_device if head == 4 and seq == 8 and aligned else general_form
    return jax.shard_map(body, mesh=mesh, in_specs=in_specs, out_specs=out_specs, check_vma=False)
```

```python
import functools
import math

import jax
import jax.numpy as jnp
from jax import lax
from jax.experimental import pallas as pl
from jax.experimental.pallas import tpu as pltpu
from jax.sharding import PartitionSpec as P

C = 1536
HEAD_DIM = 64
KW = 5
DILATION_STEP = 4
EPS = 1e-06
EDGE = 16
LOG2E = math.log2(math.e)
MIB = 1 << 20
LANES = 128


def padded_2(block, sides, width):
    for axis, dim in sides:
        count = lax.axis_size(axis)
        forward = [(i, i + 1) for i in range(count - 1)]
        backward = [(target, source) for source, target in forward]
        low = lax.ppermute(
            lax.slice_in_dim(block, block.shape[dim] - width, None, axis=dim), axis, forward
        )
        high = lax.ppermute(lax.slice_in_dim(block, 0, width, axis=dim), axis, backward)
        block = jnp.concatenate([low, block, high], axis=dim)
    return block


def row_scale(hidden):
    squares = lax.psum(jnp.sum(hidden * hidden, axis=1), "head")
    return hidden * lax.rsqrt(squares / C + EPS)[:, None]


def reduce_operands(left, right):
    return lax.dot_general(
        left, right, (((1,), (1,)), ((), ())), preferred_element_type=jnp.float32
    )


def general_form(dna, conv_in, dilated_kernel_weight, w_query, w_key, w_value, w_out):
    local_row_count = dna.shape[0] // 2
    half = (KW - 1) // 2
    padded = padded_2(dna, (("seq", 0),), half)
    h1 = jnp.zeros((local_row_count, conv_in.shape[1]), jnp.float32)
    for kernel_offset in range(KW):
        rows = lax.slice(
            padded,
            (kernel_offset, 0),
            (kernel_offset + 2 * local_row_count - 1, padded.shape[1]),
            (2, 1),
        )
        h1 = h1 + reduce_operands(rows, conv_in[kernel_offset])
    gelu_output = jax.nn.gelu(row_scale(h1), approximate=True).astype(jnp.bfloat16)
    complete_output = lax.all_gather(gelu_output, "head", axis=1, tiled=True)
    broad_input = padded_2(complete_output, (("seq", 0),), DILATION_STEP)
    second_hidden = h1
    for kernel_offset in range(3):
        second_hidden = second_hidden + reduce_operands(
            broad_input[
                DILATION_STEP * kernel_offset : DILATION_STEP * kernel_offset + local_row_count
            ],
            dilated_kernel_weight[kernel_offset],
        )
    normed = row_scale(second_hidden).astype(jnp.bfloat16)
    local_width = w_query.shape[0]
    heads_here = local_width // HEAD_DIM
    piece = lax.all_gather(normed, "head", axis=1, tiled=True)
    q_acc, k_acc, v_acc = (reduce_operands(piece, w) for w in (w_query, w_key, w_value))
    query = q_acc.astype(jnp.bfloat16).reshape(local_row_count, heads_here, HEAD_DIM)
    keys = k_acc.astype(jnp.bfloat16)
    values = v_acc.astype(jnp.bfloat16)
    scale = 1.0 / math.sqrt(HEAD_DIM)
    start_state = (
        jnp.full((heads_here, local_row_count), -1e30, jnp.float32),
        jnp.zeros((heads_here, local_row_count), jnp.float32),
        jnp.zeros((local_row_count, heads_here, HEAD_DIM), jnp.float32),
    )
    key_rows = lax.all_gather(keys, "seq", axis=0, tiled=True)
    value_rows = lax.all_gather(values, "seq", axis=0, tiled=True)
    count = key_rows.shape[0]
    width = 512 if count % 512 == 0 else count
    blocks = count // width
    key_blocks = key_rows.reshape(blocks, width, heads_here, HEAD_DIM)
    value_blocks = value_rows.reshape(blocks, width, heads_here, HEAD_DIM)

    def step(state, operands):
        running, total, acc = state
        key_block, value_block = operands
        scores = (
            jnp.einsum("qhd,khd->hqk", query, key_block, preferred_element_type=jnp.float32) * scale
        )
        newest = jnp.maximum(running, jnp.max(scores, axis=2))
        factor = jnp.exp(running - newest)
        weights = jnp.exp(scores - newest[:, :, None])
        total = total * factor + jnp.sum(weights, axis=2)
        update = jnp.einsum(
            "hqk,khd->qhd",
            weights.astype(jnp.bfloat16),
            value_block,
            preferred_element_type=jnp.float32,
        )
        acc = acc * jnp.transpose(factor)[:, :, None] + update
        return ((newest, total, acc), None)

    state, _ = lax.scan(step, start_state, (key_blocks, value_blocks))
    running, total, acc = state
    attended = (
        (acc / jnp.transpose(total)[:, :, None])
        .reshape(local_row_count, local_width)
        .astype(jnp.bfloat16)
    )
    partial_out = jnp.dot(attended, w_out, preferred_element_type=jnp.float32)
    mixed = lax.psum_scatter(
        partial_out.astype(jnp.bfloat16), "head", scatter_dimension=1, tiled=True
    ).astype(jnp.float32)
    return (second_hidden + mixed).astype(jnp.bfloat16)


def nbytes(*arrays):
    return sum(math.prod(a.shape) * jnp.dtype(a.dtype).itemsize for a in arrays)


def cost(flops, arrays, transcendentals=0):
    return pl.CostEstimate(
        flops=int(flops), bytes_accessed=int(nbytes(*arrays)), transcendentals=int(transcendentals)
    )


def rotate(offset):
    count = lax.axis_size("head")
    return [(i, (i + offset) % count) for i in range(count)]


def after(value, *others):
    return lax.optimization_barrier((value, *others))[0]


def shared(block):
    count = lax.axis_size("head")
    return [block] + [lax.ppermute(block, "head", rotate(k)) for k in (1, count - 1, 2)]


def owner(k):
    count = lax.axis_size("head")
    return lax.rem(lax.axis_index("head") + count - k, count)


SHIFTS = (0, 1, 3, 2)


def gathered(block):
    return lax.all_gather(block, "head", axis=0, tiled=True)


def pieces(ref):
    count = ref.shape[0] // len(SHIFTS)
    starts = [pl.multiple_of(owner(shift) * count, 16) for shift in SHIFTS]
    return tuple(ref.at[pl.ds(start, count), :] for start in starts)


def store_wide(wide, start, block):
    for j in range(wide.shape[0]):
        rows = pl.ds(start, block.shape[0])
        wide[j, rows, :] = block[:, 128 * j : 128 * (j + 1)].astype(jnp.float32)


def taps_sum(wide, weight_ref, groups):
    total = None
    for tap in range(KW):
        picked = []
        for start, count in groups:
            lanes = [
                wide[j, pl.ds(start + tap, count, stride=2), :] for j in range(wide.shape[0])
            ]
            picked.append(jnp.concatenate(lanes, axis=1).astype(jnp.bfloat16))
        taken = picked[0] if len(picked) == 1 else jnp.concatenate(picked, axis=0)
        term = reduce_operands(taken, weight_ref[tap])
        total = term if total is None else total + term
    return total


FIRST = EDGE - KW // 2


def conv_middle_kernel(dna_ref, weight_ref, h1_ref, sent_ref, wide):
    store_wide(wide, 0, dna_ref[pl.ds(0, wide.shape[1]), :])
    total = taps_sum(wide, weight_ref, [(FIRST, sent_ref.shape[0])])
    h1_ref[...] = total
    sent_ref[...] = total.astype(jnp.bfloat16)


def conv_edge_kernel(dna_ref, low_ref, high_ref, weight_ref, h1_ref, sent_ref, wide):
    rows = dna_ref.shape[0]
    upper = sent_ref.shape[0] - EDGE
    first = rows - 2 * upper
    zeros = jnp.zeros((EDGE, dna_ref.shape[1]), jnp.bfloat16)
    store_wide(wide, 0, zeros)
    store_wide(wide, EDGE, low_ref[...])
    store_wide(wide, 2 * EDGE, dna_ref[pl.ds(0, 2 * EDGE), :])
    store_wide(wide, 4 * EDGE, dna_ref[pl.ds(first, rows - first), :])
    store_wide(wide, 4 * EDGE + rows - first, high_ref[...])
    store_wide(wide, 5 * EDGE + rows - first, zeros)
    total = taps_sum(wide, weight_ref, [(FIRST, EDGE), (4 * EDGE + FIRST, upper)])
    h1_ref[...] = total
    sent_ref[...] = total.astype(jnp.bfloat16)


def first_conv(kernel, operands, weight, count, deep, name):
    width, out = weight.shape[2], weight.shape[1]
    kept = jax.ShapeDtypeStruct((count, out), jnp.float32)
    sent = jax.ShapeDtypeStruct((count, out), jnp.bfloat16)
    return pl.pallas_call(
        kernel,
        out_shape=(kept, sent),
        scratch_shapes=[pltpu.VMEM((width // 128, deep, 128), jnp.float32)],
        compiler_params=pltpu.CompilerParams(vmem_limit_bytes=24 * MIB),
        cost_estimate=cost(2 * count * out * width * KW, (*operands, weight, kept, sent)),
        name=name,
    )(*operands, weight)


def inverse_norm(blocks):
    squares = None
    for block in blocks:
        term = jnp.sum(block * block, axis=1, keepdims=True)
        squares = term if squares is None else squares + term
    return lax.rsqrt(squares / C + EPS)


def wide_blocks(parts, start, count):
    return [part[pl.ds(start, count), :].astype(jnp.float32) for part in parts]


def gelu(value):
    return jax.nn.gelu(value, approximate=True)


def columns_of(shift, width):
    return pl.ds(pl.multiple_of(owner(shift) * width, 128), width)


def dilated_middle_kernel(a_ref, h1_ref, weight_ref, h2_ref, sent_ref, act):
    parts = pieces(a_ref)
    count, width = parts[0].shape
    rows = h2_ref.shape[0]
    blocks = wide_blocks(parts, 0, count)
    inverse = inverse_norm(blocks)
    total = h1_ref[pl.ds(8, rows), :]
    for slot, (block, shift) in enumerate(zip(blocks, SHIFTS)):
        act[slot] = gelu(block * inverse)
        for tap in range(3):
            taken = act[slot, pl.ds((tap + 1) * DILATION_STEP, rows), :].astype(jnp.bfloat16)
            total = total + reduce_operands(taken, weight_ref[tap, :, columns_of(shift, width)])
    h2_ref[...] = total
    sent_ref[...] = total.astype(jnp.bfloat16)


def dilated_edge_kernel(
    m_ref, e0, e1, e2, e3, hm_ref, he_ref, h2m_ref, weight_ref, h2_ref, sent_ref, act
):
    middle, edge = pieces(m_ref), (e0, e1, e2, e3)
    inner, width = middle[0].shape
    outer = e0.shape[0]
    rows = h2_ref.shape[0]
    upper = outer - EDGE
    position = lax.axis_index("seq") * rows + lax.broadcasted_iota(jnp.int32, (outer, 1), 0)
    place = lax.broadcasted_iota(jnp.int32, (outer, 1), 0)
    position = position + jnp.where(place < EDGE, -8, inner - 8)
    inside = (position >= 0) & (position < rows * lax.axis_size("seq"))
    outer_blocks = wide_blocks(edge, 0, outer)
    outer_inverse = jnp.where(inside, inverse_norm(outer_blocks), 0.0)
    low_blocks = wide_blocks(middle, 0, EDGE)
    low_inverse = inverse_norm(low_blocks)
    high_blocks = wide_blocks(middle, inner - EDGE, EDGE)
    high_inverse = inverse_norm(high_blocks)
    last = rows - (outer - EDGE)
    total = jnp.concatenate(
        [
            he_ref[pl.ds(8, 8), :],
            hm_ref[pl.ds(0, 8), :],
            hm_ref[pl.ds(inner - 8, 8), :],
            he_ref[pl.ds(EDGE, upper - 8), :],
        ],
        axis=0,
    )
    tail = 2 * EDGE
    for slot, shift in enumerate(SHIFTS):
        full = gelu(outer_blocks[slot] * outer_inverse)
        act[slot, pl.ds(0, EDGE), :] = full[:EDGE]
        act[slot, pl.ds(EDGE, EDGE), :] = gelu(low_blocks[slot] * low_inverse)
        act[slot, pl.ds(tail, EDGE), :] = gelu(high_blocks[slot] * high_inverse)
        act[slot, pl.ds(tail + EDGE, upper), :] = full[EDGE:]
        for tap in range(3):
            shifted = (tap + 1) * DILATION_STEP
            taken = jnp.concatenate(
                [
                    act[slot, pl.ds(shifted, EDGE), :],
                    act[slot, pl.ds(tail + shifted, upper), :],
                ],
                axis=0,
            ).astype(jnp.bfloat16)
            total = total + reduce_operands(taken, weight_ref[tap, :, columns_of(shift, width)])
    h2_ref[pl.ds(0, EDGE), :] = total[:EDGE]
    h2_ref[pl.ds(EDGE, last - EDGE), :] = h2m_ref[...]
    h2_ref[pl.ds(last, rows - last), :] = total[EDGE:]
    sent_ref[...] = total.astype(jnp.bfloat16)


def second_conv(kernel, operands, weight, kept_rows, sent_rows, deep, name):
    out, width = weight.shape[1], operands[0].shape[1]
    kept = jax.ShapeDtypeStruct((kept_rows, out), jnp.float32)
    sent = jax.ShapeDtypeStruct((sent_rows, out), jnp.bfloat16)
    return pl.pallas_call(
        kernel,
        out_shape=(kept, sent),
        scratch_shapes=[pltpu.VMEM((4, deep, width), jnp.float32)],
        compiler_params=pltpu.CompilerParams(vmem_limit_bytes=24 * MIB),
        cost_estimate=cost(
            2 * sent_rows * out * weight.shape[2] * 3,
            (*operands, weight, kept, sent),
            deep * weight.shape[2],
        ),
        name=name,
    )(*operands, weight)


def projections(parts, wq, wk, wv, kv_ref):
    width = parts[0].shape[1]
    rows, out = parts[0].shape[0], wq.shape[0]
    blocks = [part[...].astype(jnp.float32) for part in parts]
    inverse = inverse_norm(blocks)
    normed = [(block * inverse).astype(jnp.bfloat16) for block in blocks]

    def product(weight_ref, weight_first):
        total = None
        for part, shift in zip(normed, SHIFTS):
            weight = weight_ref[:, columns_of(shift, width)]
            pair = (weight, part) if weight_first else (part, weight)
            term = reduce_operands(*pair)
            total = term if total is None else total + term
        return total

    kv_ref[:, :out] = product(wk, False).astype(jnp.bfloat16)
    value = product(wv, True).astype(jnp.bfloat16)
    for row in range(0, rows, LANES):
        for lane in range(0, out, LANES):
            kv_ref[pl.ds(row, LANES), pl.ds(out + lane, LANES)] = value[
                lane : lane + LANES, row : row + LANES
            ]
    scale = LOG2E / math.sqrt(HEAD_DIM)
    return (product(wq, False) * scale).astype(jnp.bfloat16)


def project_middle_kernel(a_ref, wq, wk, wv, q_ref, kv_ref):
    q_ref[...] = projections(pieces(a_ref), wq, wk, wv, kv_ref)


def project_edge_kernel(a0, a1, a2, a3, qm_ref, wq, wk, wv, q_ref, kv_ref):
    query = projections((a0, a1, a2, a3), wq, wk, wv, kv_ref)
    inner, rows = qm_ref.shape[0], q_ref.shape[0]
    q_ref[pl.ds(0, EDGE), :] = query[:EDGE]
    q_ref[pl.ds(EDGE, inner), :] = qm_ref[...]
    q_ref[pl.ds(EDGE + inner, rows - EDGE - inner), :] = query[EDGE:]


def project(kernel, operands, weights, rows, q_rows, name):
    out = weights[0].shape[0]
    q = jax.ShapeDtypeStruct((q_rows, out), jnp.bfloat16)
    kv = jax.ShapeDtypeStruct((rows, 2 * out), jnp.bfloat16)
    return pl.pallas_call(
        kernel,
        out_shape=(q, kv),
        compiler_params=pltpu.CompilerParams(vmem_limit_bytes=20 * MIB),
        cost_estimate=cost(6 * rows * out * C, (*operands, *weights, q, kv)),
        name=name,
    )(*operands, *weights)


TILE = 64


def partial_attention(query, blocks, scores, weights, head, lane):
    width = query.shape[1]
    pair, half = divmod(head, 2)
    lanes = slice(pair * LANES, (pair + 1) * LANES)
    mine = query[:, lanes]
    mine = jnp.where((lane // HEAD_DIM) == half, mine, jnp.zeros_like(mine))
    keys = jnp.concatenate([block[:, lanes] for block in blocks], axis=0)
    scores[...] = reduce_operands(keys, mine)
    columns = scores.shape[1]
    top = None
    for start in range(0, scores.shape[0], TILE):
        tile = jnp.max(scores[pl.ds(start, TILE), :].reshape(-1, 8, columns), axis=0)
        top = tile if top is None else jnp.maximum(top, tile)
    top = jnp.max(top, axis=0, keepdims=True)
    total = None
    for start in range(0, scores.shape[0], TILE):
        weight = jnp.exp2(scores[pl.ds(start, TILE), :] - top)
        tile = jnp.sum(weight.reshape(-1, 8, columns), axis=0)
        total = tile if total is None else total + tile
        weights[pl.ds(start, TILE), :] = weight.astype(jnp.bfloat16)
    values = [
        block[pl.ds(row + half * HEAD_DIM, HEAD_DIM), pl.ds(width + pair * LANES, LANES)]
        for block in blocks
        for row in range(0, block.shape[0], LANES)
    ]
    values = jnp.concatenate(values, axis=1)
    out = jnp.dot(values, weights[...], preferred_element_type=jnp.float32)
    return out, top, jnp.sum(total, axis=0, keepdims=True)


def state_parts(state, head, width, columns):
    return (
        state[pl.ds(head * HEAD_DIM, HEAD_DIM), columns],
        state[pl.ds(width + head, 1), columns],
        state[pl.ds(width + 8 + head, 1), columns],
    )


def merged_parts(one, other):
    top = jnp.maximum(one[1], other[1])
    first, second = jnp.exp2(one[1] - top), jnp.exp2(other[1] - top)
    return first * one[0] + second * other[0], top, first * one[2] + second * other[2]


def attend_kernel(first_column, q_refs, blocks, state, out_ref, scores, weights):
    width = q_refs[0].shape[1]
    query = jnp.concatenate([ref[...] for ref in q_refs], axis=0)
    columns = query.shape[0]
    lane = lax.broadcasted_iota(jnp.int32, (columns, LANES), 1)
    out_ref[pl.ds(width, 16), :] = jnp.zeros((16, columns), jnp.float32)
    for head in range(width // HEAD_DIM):
        part = partial_attention(
            query, blocks, scores.at[head % 2], weights.at[head % 2], head, lane
        )
        if state is not None:
            part = merged_parts(
                part, state_parts(state, head, width, pl.ds(first_column, columns))
            )
        out_ref[pl.ds(head * HEAD_DIM, HEAD_DIM), :] = part[0]
        out_ref[pl.ds(width + head, 1), :] = part[1]
        out_ref[pl.ds(width + 8 + head, 1), :] = part[2]


def attend(queries, blocks, state, first_column, name):
    rows, width = queries[0].shape
    columns = rows * len(queries)
    extent = sum(block.shape[0] for block in blocks)
    out = jax.ShapeDtypeStruct((width + 16, columns), jnp.float32)
    operands = (*queries, *blocks) + (() if state is None else (state,))

    def kernel(*refs):
        q_refs, block_refs = refs[: len(queries)], refs[len(queries) :][: len(blocks)]
        state_ref = None if state is None else refs[len(operands) - 1]
        attend_kernel(
            first_column, q_refs, block_refs, state_ref, *refs[len(operands) :]
        )

    return pl.pallas_call(
        kernel,
        out_shape=out,
        scratch_shapes=[
            pltpu.VMEM((2, extent, columns), jnp.float32),
            pltpu.VMEM((2, extent, columns), jnp.bfloat16),
        ],
        compiler_params=pltpu.CompilerParams(vmem_limit_bytes=24 * MIB),
        cost_estimate=cost(
            4 * columns * width * extent, (*operands, out), columns * extent * width // HEAD_DIM
        ),
        name=name,
    )(*operands)


def mix_kernel(own_state, other_state, w_ref, h2_ref, own_ref, p1, p2, p3, attended):
    rows, width = h2_ref.shape
    for pair in range(width // LANES):
        halves = []
        for head in (2 * pair, 2 * pair + 1):
            out, _, total = merged_parts(
                state_parts(own_state, head, width, pl.ds(0, rows)),
                state_parts(other_state, head, width, pl.ds(0, rows)),
            )
            halves.append(out / total)
        merged = jnp.transpose(jnp.concatenate(halves, axis=0))
        attended[:, pl.ds(pair * LANES, LANES)] = merged.astype(jnp.bfloat16)

    def product(shift):
        return jnp.dot(
            attended[...], w_ref[:, columns_of(shift, width)], preferred_element_type=jnp.float32
        )

    for ref, shift in ((p3, 2), (p1, 3), (p2, 1)):
        ref[...] = product(shift).astype(jnp.bfloat16)
    own_ref[...] = product(0) + h2_ref[...]


def mix(own_state, other_state, w_out, h2):
    rows, width = h2.shape
    own = jax.ShapeDtypeStruct((rows, width), jnp.float32)
    part = jax.ShapeDtypeStruct((rows, width), jnp.bfloat16)
    operands = (own_state, other_state, w_out, h2)
    return pl.pallas_call(
        mix_kernel,
        out_shape=(own, part, part, part),
        scratch_shapes=[pltpu.VMEM((rows, width), jnp.bfloat16)],
        compiler_params=pltpu.CompilerParams(vmem_limit_bytes=16 * MIB),
        cost_estimate=cost(
            2 * rows * width * w_out.shape[1], (*operands, own, part, part, part)
        ),
        name="mix",
    )(*operands)


def exchanged(block, mask):
    count = lax.axis_size("seq")
    return lax.ppermute(block, "seq", [(i, i ^ mask) for i in range(count)])


def on_device(dna, conv_in, dilated_kernel_weight, w_query, w_key, w_value, w_out):
    count = lax.axis_size("seq")
    rows = dna.shape[0] // 2
    inner = 2 * LANES
    outer = rows - inner
    low = lax.ppermute(dna[-EDGE:], "seq", [(i, i + 1) for i in range(count - 1)])
    high = lax.ppermute(dna[:EDGE], "seq", [(i + 1, i) for i in range(count - 1)])
    h1_m, sent = first_conv(
        conv_middle_kernel, (dna,), conv_in, inner + EDGE, 2 * (inner + 2 * EDGE), "conv_middle"
    )
    wide_m = gathered(sent)
    h1_e, sent = first_conv(
        conv_edge_kernel, (dna, low, high), conv_in, outer, 2 * (outer + 2 * EDGE), "conv_edge"
    )
    wide_e = shared(sent)
    h2_m, sent = second_conv(
        dilated_middle_kernel,
        (wide_m, after(h1_m, sent)),
        dilated_kernel_weight,
        inner,
        inner,
        inner + EDGE,
        "dilated_middle",
    )
    normed_m = gathered(sent)
    h2, sent = second_conv(
        dilated_edge_kernel,
        (wide_m, *wide_e, h1_m, h1_e, h2_m),
        dilated_kernel_weight,
        rows,
        outer,
        outer + 2 * EDGE,
        "dilated_edge",
    )
    normed_e = shared(sent)
    normed_m = after(normed_m, sent)
    weights = (w_query, w_key, w_value)
    q_m, kv_m = project(
        project_middle_kernel, (normed_m,), weights, inner, inner, "project_middle"
    )
    x_m, y_m, d_m = (exchanged(kv_m, mask) for mask in (2, 4, 6))
    q, kv_e = project(
        project_edge_kernel, (*normed_e, q_m), weights, outer, rows, "project_edge"
    )
    q_other, x_e, y_e, d_e = exchanged(q, 1), *(exchanged(kv_e, mask) for mask in (2, 4, 6))
    state = attend((q, q_other), (kv_m, x_m, y_m, d_m), None, 0, "attend_m")
    late = (kv_e, x_e, y_e, d_e)
    state_other = attend((q_other,), late, state, rows, "attend_other")
    given = exchanged(state_other, 1)
    state_own = attend((q,), late, state, 0, "attend_own")
    own, p1, p2, p3 = mix(state_own, given, w_out, h2)
    total = own
    for part, shift in ((p1, 1), (p2, 3), (p3, 2)):
        total = total + lax.ppermute(part, "head", rotate(shift)).astype(jnp.float32)
    return total.astype(jnp.bfloat16)


def solution(mesh):
    in_specs = (
        P("seq", None),
        P(None, "head", None),
        P(None, "head", None),
        P("head", None),
        P("head", None),
        P("head", None),
        P("head", None),
    )
    out_specs = P("seq", "head")
    seq, head = mesh.shape["seq"], mesh.shape["head"]
    aligned = (C // head) % 128 == 0
    body = on_device if head == 4 and seq == 8 and aligned else general_form
    return jax.shard_map(body, mesh=mesh, in_specs=in_specs, out_specs=out_specs, check_vma=False)
```

```python
import functools
import math

import jax
import jax.numpy as jnp
from jax import lax
from jax.experimental import pallas as pl
from jax.experimental.pallas import tpu as pltpu
from jax.sharding import PartitionSpec as P

C = 1536
HEAD_DIM = 64
KW = 5
DILATION_STEP = 4
EPS = 1e-06
EDGE = 16
LOG2E = math.log2(math.e)
MIB = 1 << 20
LANES = 128


def padded_2(block, sides, width):
    for axis, dim in sides:
        count = lax.axis_size(axis)
        forward = [(i, i + 1) for i in range(count - 1)]
        backward = [(target, source) for source, target in forward]
        low = lax.ppermute(
            lax.slice_in_dim(block, block.shape[dim] - width, None, axis=dim), axis, forward
        )
        high = lax.ppermute(lax.slice_in_dim(block, 0, width, axis=dim), axis, backward)
        block = jnp.concatenate([low, block, high], axis=dim)
    return block


def row_scale(hidden):
    squares = lax.psum(jnp.sum(hidden * hidden, axis=1), "head")
    return hidden * lax.rsqrt(squares / C + EPS)[:, None]


def reduce_operands(left, right):
    return lax.dot_general(
        left, right, (((1,), (1,)), ((), ())), preferred_element_type=jnp.float32
    )


def general_form(dna, conv_in, dilated_kernel_weight, w_query, w_key, w_value, w_out):
    local_row_count = dna.shape[0] // 2
    half = (KW - 1) // 2
    padded = padded_2(dna, (("seq", 0),), half)
    h1 = jnp.zeros((local_row_count, conv_in.shape[1]), jnp.float32)
    for kernel_offset in range(KW):
        rows = lax.slice(
            padded,
            (kernel_offset, 0),
            (kernel_offset + 2 * local_row_count - 1, padded.shape[1]),
            (2, 1),
        )
        h1 = h1 + reduce_operands(rows, conv_in[kernel_offset])
    gelu_output = jax.nn.gelu(row_scale(h1), approximate=True).astype(jnp.bfloat16)
    complete_output = lax.all_gather(gelu_output, "head", axis=1, tiled=True)
    broad_input = padded_2(complete_output, (("seq", 0),), DILATION_STEP)
    second_hidden = h1
    for kernel_offset in range(3):
        second_hidden = second_hidden + reduce_operands(
            broad_input[
                DILATION_STEP * kernel_offset : DILATION_STEP * kernel_offset + local_row_count
            ],
            dilated_kernel_weight[kernel_offset],
        )
    normed = row_scale(second_hidden).astype(jnp.bfloat16)
    local_width = w_query.shape[0]
    heads_here = local_width // HEAD_DIM
    piece = lax.all_gather(normed, "head", axis=1, tiled=True)
    q_acc, k_acc, v_acc = (reduce_operands(piece, w) for w in (w_query, w_key, w_value))
    query = q_acc.astype(jnp.bfloat16).reshape(local_row_count, heads_here, HEAD_DIM)
    keys = k_acc.astype(jnp.bfloat16)
    values = v_acc.astype(jnp.bfloat16)
    scale = 1.0 / math.sqrt(HEAD_DIM)
    start_state = (
        jnp.full((heads_here, local_row_count), -1e30, jnp.float32),
        jnp.zeros((heads_here, local_row_count), jnp.float32),
        jnp.zeros((local_row_count, heads_here, HEAD_DIM), jnp.float32),
    )
    key_rows = lax.all_gather(keys, "seq", axis=0, tiled=True)
    value_rows = lax.all_gather(values, "seq", axis=0, tiled=True)
    count = key_rows.shape[0]
    width = 512 if count % 512 == 0 else count
    blocks = count // width
    key_blocks = key_rows.reshape(blocks, width, heads_here, HEAD_DIM)
    value_blocks = value_rows.reshape(blocks, width, heads_here, HEAD_DIM)

    def step(state, operands):
        running, total, acc = state
        key_block, value_block = operands
        scores = (
            jnp.einsum("qhd,khd->hqk", query, key_block, preferred_element_type=jnp.float32) * scale
        )
        newest = jnp.maximum(running, jnp.max(scores, axis=2))
        factor = jnp.exp(running - newest)
        weights = jnp.exp(scores - newest[:, :, None])
        total = total * factor + jnp.sum(weights, axis=2)
        update = jnp.einsum(
            "hqk,khd->qhd",
            weights.astype(jnp.bfloat16),
            value_block,
            preferred_element_type=jnp.float32,
        )
        acc = acc * jnp.transpose(factor)[:, :, None] + update
        return ((newest, total, acc), None)

    state, _ = lax.scan(step, start_state, (key_blocks, value_blocks))
    running, total, acc = state
    attended = (
        (acc / jnp.transpose(total)[:, :, None])
        .reshape(local_row_count, local_width)
        .astype(jnp.bfloat16)
    )
    partial_out = jnp.dot(attended, w_out, preferred_element_type=jnp.float32)
    mixed = lax.psum_scatter(
        partial_out.astype(jnp.bfloat16), "head", scatter_dimension=1, tiled=True
    ).astype(jnp.float32)
    return (second_hidden + mixed).astype(jnp.bfloat16)


def nbytes(*arrays):
    return sum(math.prod(a.shape) * jnp.dtype(a.dtype).itemsize for a in arrays)


def cost(flops, arrays, transcendentals=0):
    return pl.CostEstimate(
        flops=int(flops), bytes_accessed=int(nbytes(*arrays)), transcendentals=int(transcendentals)
    )


def rotate(offset):
    count = lax.axis_size("head")
    return [(i, (i + offset) % count) for i in range(count)]


def after(value, *others):
    return lax.optimization_barrier((value, *others))[0]


def shared(block, earlier=(None, None, None)):
    count = lax.axis_size("head")
    moved = []
    for k, previous in zip((1, count - 1, 2), earlier):
        held = block if previous is None else after(block, previous)
        moved.append(lax.ppermute(held, "head", rotate(k)))
    return [block, *moved]


def owner(k):
    count = lax.axis_size("head")
    return lax.rem(lax.axis_index("head") + count - k, count)


SHIFTS = (0, 1, 3, 2)


def store_wide(wide, start, block):
    for j in range(wide.shape[0]):
        rows = pl.ds(start, block.shape[0])
        wide[j, rows, :] = block[:, 128 * j : 128 * (j + 1)].astype(jnp.float32)


def taps_sum(wide, weight_ref, groups):
    total = None
    for tap in range(KW):
        picked = []
        for start, count in groups:
            lanes = [
                wide[j, pl.ds(start + tap, count, stride=2), :] for j in range(wide.shape[0])
            ]
            picked.append(jnp.concatenate(lanes, axis=1).astype(jnp.bfloat16))
        taken = picked[0] if len(picked) == 1 else jnp.concatenate(picked, axis=0)
        term = reduce_operands(taken, weight_ref[tap])
        total = term if total is None else total + term
    return total


FIRST = EDGE - KW // 2


def conv_middle_kernel(dna_ref, weight_ref, h1_ref, sent_ref, wide):
    store_wide(wide, 0, dna_ref[pl.ds(0, wide.shape[1]), :])
    total = taps_sum(wide, weight_ref, [(FIRST, sent_ref.shape[0])])
    h1_ref[...] = total
    sent_ref[...] = total.astype(jnp.bfloat16)


def conv_edge_kernel(dna_ref, low_ref, high_ref, weight_ref, h1_ref, sent_ref, wide):
    rows = dna_ref.shape[0]
    upper = sent_ref.shape[0] - EDGE
    first = rows - 2 * upper
    zeros = jnp.zeros((EDGE, dna_ref.shape[1]), jnp.bfloat16)
    store_wide(wide, 0, zeros)
    store_wide(wide, EDGE, low_ref[...])
    store_wide(wide, 2 * EDGE, dna_ref[pl.ds(0, 2 * EDGE), :])
    store_wide(wide, 4 * EDGE, dna_ref[pl.ds(first, rows - first), :])
    store_wide(wide, 4 * EDGE + rows - first, high_ref[...])
    store_wide(wide, 5 * EDGE + rows - first, zeros)
    total = taps_sum(wide, weight_ref, [(FIRST, EDGE), (4 * EDGE + FIRST, upper)])
    h1_ref[...] = total
    sent_ref[...] = total.astype(jnp.bfloat16)


def first_conv(kernel, operands, weight, count, deep, name):
    width, out = weight.shape[2], weight.shape[1]
    kept = jax.ShapeDtypeStruct((count, out), jnp.float32)
    sent = jax.ShapeDtypeStruct((count, out), jnp.bfloat16)
    return pl.pallas_call(
        kernel,
        out_shape=(kept, sent),
        scratch_shapes=[pltpu.VMEM((width // 128, deep, 128), jnp.float32)],
        compiler_params=pltpu.CompilerParams(vmem_limit_bytes=24 * MIB),
        cost_estimate=cost(2 * count * out * width * KW, (*operands, weight, kept, sent)),
        name=name,
    )(*operands, weight)


def inverse_norm(blocks):
    squares = None
    for block in blocks:
        term = jnp.sum(block * block, axis=1, keepdims=True)
        squares = term if squares is None else squares + term
    return lax.rsqrt(squares / C + EPS)


def wide_blocks(parts, start, count):
    return [part[pl.ds(start, count), :].astype(jnp.float32) for part in parts]


def gelu(value):
    return jax.nn.gelu(value, approximate=True)


def columns_of(shift, width):
    return pl.ds(pl.multiple_of(owner(shift) * width, 128), width)


def dilated_middle_kernel(a0, a1, a2, a3, h1_ref, weight_ref, h2_ref, sent_ref, act):
    parts = (a0, a1, a2, a3)
    count, width = a0.shape
    rows = h2_ref.shape[0]
    blocks = wide_blocks(parts, 0, count)
    inverse = inverse_norm(blocks)
    total = h1_ref[pl.ds(8, rows), :]
    for slot, (block, shift) in enumerate(zip(blocks, SHIFTS)):
        act[slot] = gelu(block * inverse)
        for tap in range(3):
            taken = act[slot, pl.ds((tap + 1) * DILATION_STEP, rows), :].astype(jnp.bfloat16)
            total = total + reduce_operands(taken, weight_ref[tap, :, columns_of(shift, width)])
    h2_ref[...] = total
    sent_ref[...] = total.astype(jnp.bfloat16)


def dilated_edge_kernel(
    m0, m1, m2, m3, e0, e1, e2, e3, hm_ref, he_ref, h2m_ref, weight_ref, h2_ref, sent_ref, act
):
    middle, edge = (m0, m1, m2, m3), (e0, e1, e2, e3)
    inner, width = m0.shape
    outer = e0.shape[0]
    rows = h2_ref.shape[0]
    upper = outer - EDGE
    position = lax.axis_index("seq") * rows + lax.broadcasted_iota(jnp.int32, (outer, 1), 0)
    place = lax.broadcasted_iota(jnp.int32, (outer, 1), 0)
    position = position + jnp.where(place < EDGE, -8, inner - 8)
    inside = (position >= 0) & (position < rows * lax.axis_size("seq"))
    outer_blocks = wide_blocks(edge, 0, outer)
    outer_inverse = jnp.where(inside, inverse_norm(outer_blocks), 0.0)
    low_blocks = wide_blocks(middle, 0, EDGE)
    low_inverse = inverse_norm(low_blocks)
    high_blocks = wide_blocks(middle, inner - EDGE, EDGE)
    high_inverse = inverse_norm(high_blocks)
    last = rows - (outer - EDGE)
    total = jnp.concatenate(
        [
            he_ref[pl.ds(8, 8), :],
            hm_ref[pl.ds(0, 8), :],
            hm_ref[pl.ds(inner - 8, 8), :],
            he_ref[pl.ds(EDGE, upper - 8), :],
        ],
        axis=0,
    )
    tail = 2 * EDGE
    for slot, shift in enumerate(SHIFTS):
        full = gelu(outer_blocks[slot] * outer_inverse)
        act[slot, pl.ds(0, EDGE), :] = full[:EDGE]
        act[slot, pl.ds(EDGE, EDGE), :] = gelu(low_blocks[slot] * low_inverse)
        act[slot, pl.ds(tail, EDGE), :] = gelu(high_blocks[slot] * high_inverse)
        act[slot, pl.ds(tail + EDGE, upper), :] = full[EDGE:]
        for tap in range(3):
            shifted = (tap + 1) * DILATION_STEP
            taken = jnp.concatenate(
                [
                    act[slot, pl.ds(shifted, EDGE), :],
                    act[slot, pl.ds(tail + shifted, upper), :],
                ],
                axis=0,
            ).astype(jnp.bfloat16)
            total = total + reduce_operands(taken, weight_ref[tap, :, columns_of(shift, width)])
    h2_ref[pl.ds(0, EDGE), :] = total[:EDGE]
    h2_ref[pl.ds(EDGE, last - EDGE), :] = h2m_ref[...]
    h2_ref[pl.ds(last, rows - last), :] = total[EDGE:]
    sent_ref[...] = total.astype(jnp.bfloat16)


def second_conv(kernel, operands, weight, kept_rows, sent_rows, deep, name):
    out, width = weight.shape[1], operands[0].shape[1]
    kept = jax.ShapeDtypeStruct((kept_rows, out), jnp.float32)
    sent = jax.ShapeDtypeStruct((sent_rows, out), jnp.bfloat16)
    return pl.pallas_call(
        kernel,
        out_shape=(kept, sent),
        scratch_shapes=[pltpu.VMEM((4, deep, width), jnp.float32)],
        compiler_params=pltpu.CompilerParams(vmem_limit_bytes=24 * MIB),
        cost_estimate=cost(
            2 * sent_rows * out * weight.shape[2] * 3,
            (*operands, weight, kept, sent),
            deep * weight.shape[2],
        ),
        name=name,
    )(*operands, weight)


def projections(parts, wq, wk, wv, kv_ref):
    width = parts[0].shape[1]
    rows, out = parts[0].shape[0], wq.shape[0]
    blocks = [part[...].astype(jnp.float32) for part in parts]
    inverse = inverse_norm(blocks)
    normed = [(block * inverse).astype(jnp.bfloat16) for block in blocks]

    def product(weight_ref, weight_first):
        total = None
        for part, shift in zip(normed, SHIFTS):
            weight = weight_ref[:, columns_of(shift, width)]
            pair = (weight, part) if weight_first else (part, weight)
            term = reduce_operands(*pair)
            total = term if total is None else total + term
        return total

    kv_ref[:, :out] = product(wk, False).astype(jnp.bfloat16)
    value = product(wv, True).astype(jnp.bfloat16)
    for row in range(0, rows, LANES):
        for lane in range(0, out, LANES):
            kv_ref[pl.ds(row, LANES), pl.ds(out + lane, LANES)] = value[
                lane : lane + LANES, row : row + LANES
            ]
    scale = LOG2E / math.sqrt(HEAD_DIM)
    return (product(wq, False) * scale).astype(jnp.bfloat16)


def project_middle_kernel(a0, a1, a2, a3, wq, wk, wv, q_ref, kv_ref):
    q_ref[...] = projections((a0, a1, a2, a3), wq, wk, wv, kv_ref)


def project_edge_kernel(a0, a1, a2, a3, qm_ref, wq, wk, wv, q_ref, kv_ref):
    query = projections((a0, a1, a2, a3), wq, wk, wv, kv_ref)
    inner, rows = qm_ref.shape[0], q_ref.shape[0]
    q_ref[pl.ds(0, EDGE), :] = query[:EDGE]
    q_ref[pl.ds(EDGE, inner), :] = qm_ref[...]
    q_ref[pl.ds(EDGE + inner, rows - EDGE - inner), :] = query[EDGE:]


def project(kernel, operands, weights, q_rows, name):
    rows, out = operands[0].shape[0], weights[0].shape[0]
    q = jax.ShapeDtypeStruct((q_rows, out), jnp.bfloat16)
    kv = jax.ShapeDtypeStruct((rows, 2 * out), jnp.bfloat16)
    return pl.pallas_call(
        kernel,
        out_shape=(q, kv),
        compiler_params=pltpu.CompilerParams(vmem_limit_bytes=20 * MIB),
        cost_estimate=cost(6 * rows * out * C, (*operands, *weights, q, kv)),
        name=name,
    )(*operands, *weights)


TILE = 64


def partial_attention(query, blocks, scores, weights, head, lane):
    width = query.shape[1]
    pair, half = divmod(head, 2)
    lanes = slice(pair * LANES, (pair + 1) * LANES)
    mine = query[:, lanes]
    mine = jnp.where((lane // HEAD_DIM) == half, mine, jnp.zeros_like(mine))
    keys = jnp.concatenate([block[:, lanes] for block in blocks], axis=0)
    scores[...] = reduce_operands(keys, mine)
    columns = scores.shape[1]
    top = None
    for start in range(0, scores.shape[0], TILE):
        tile = jnp.max(scores[pl.ds(start, TILE), :].reshape(-1, 8, columns), axis=0)
        top = tile if top is None else jnp.maximum(top, tile)
    top = jnp.max(top, axis=0, keepdims=True)
    total = None
    for start in range(0, scores.shape[0], TILE):
        weight = jnp.exp2(scores[pl.ds(start, TILE), :] - top)
        tile = jnp.sum(weight.reshape(-1, 8, columns), axis=0)
        total = tile if total is None else total + tile
        weights[pl.ds(start, TILE), :] = weight.astype(jnp.bfloat16)
    values = [
        block[pl.ds(row + half * HEAD_DIM, HEAD_DIM), pl.ds(width + pair * LANES, LANES)]
        for block in blocks
        for row in range(0, block.shape[0], LANES)
    ]
    values = jnp.concatenate(values, axis=1)
    out = jnp.dot(values, weights[...], preferred_element_type=jnp.float32)
    return out, top, jnp.sum(total, axis=0, keepdims=True)


def state_parts(state, head, width, columns):
    return (
        state[pl.ds(head * HEAD_DIM, HEAD_DIM), columns],
        state[pl.ds(width + head, 1), columns],
        state[pl.ds(width + 8 + head, 1), columns],
    )


def merged_parts(one, other):
    top = jnp.maximum(one[1], other[1])
    first, second = jnp.exp2(one[1] - top), jnp.exp2(other[1] - top)
    return first * one[0] + second * other[0], top, first * one[2] + second * other[2]


def attend_kernel(first_column, q_refs, blocks, state, out_ref, scores, weights):
    width = q_refs[0].shape[1]
    query = jnp.concatenate([ref[...] for ref in q_refs], axis=0)
    columns = query.shape[0]
    lane = lax.broadcasted_iota(jnp.int32, (columns, LANES), 1)
    out_ref[pl.ds(width, 16), :] = jnp.zeros((16, columns), jnp.float32)
    for head in range(width // HEAD_DIM):
        part = partial_attention(
            query, blocks, scores.at[head % 2], weights.at[head % 2], head, lane
        )
        if state is not None:
            part = merged_parts(
                part, state_parts(state, head, width, pl.ds(first_column, columns))
            )
        out_ref[pl.ds(head * HEAD_DIM, HEAD_DIM), :] = part[0]
        out_ref[pl.ds(width + head, 1), :] = part[1]
        out_ref[pl.ds(width + 8 + head, 1), :] = part[2]


def attend(queries, blocks, state, first_column, name):
    rows, width = queries[0].shape
    columns = rows * len(queries)
    extent = sum(block.shape[0] for block in blocks)
    out = jax.ShapeDtypeStruct((width + 16, columns), jnp.float32)
    operands = (*queries, *blocks) + (() if state is None else (state,))

    def kernel(*refs):
        q_refs, block_refs = refs[: len(queries)], refs[len(queries) :][: len(blocks)]
        state_ref = None if state is None else refs[len(operands) - 1]
        attend_kernel(
            first_column, q_refs, block_refs, state_ref, *refs[len(operands) :]
        )

    return pl.pallas_call(
        kernel,
        out_shape=out,
        scratch_shapes=[
            pltpu.VMEM((2, extent, columns), jnp.float32),
            pltpu.VMEM((2, extent, columns), jnp.bfloat16),
        ],
        compiler_params=pltpu.CompilerParams(vmem_limit_bytes=24 * MIB),
        cost_estimate=cost(
            4 * columns * width * extent, (*operands, out), columns * extent * width // HEAD_DIM
        ),
        name=name,
    )(*operands)


def mix_kernel(own_state, other_state, w_ref, h2_ref, own_ref, p1, p2, p3, attended):
    rows, width = h2_ref.shape
    for pair in range(width // LANES):
        halves = []
        for head in (2 * pair, 2 * pair + 1):
            out, _, total = merged_parts(
                state_parts(own_state, head, width, pl.ds(0, rows)),
                state_parts(other_state, head, width, pl.ds(0, rows)),
            )
            halves.append(out / total)
        merged = jnp.transpose(jnp.concatenate(halves, axis=0))
        attended[:, pl.ds(pair * LANES, LANES)] = merged.astype(jnp.bfloat16)

    def product(shift):
        return jnp.dot(
            attended[...], w_ref[:, columns_of(shift, width)], preferred_element_type=jnp.float32
        )

    for ref, shift in ((p3, 2), (p1, 3), (p2, 1)):
        ref[...] = product(shift).astype(jnp.bfloat16)
    own_ref[...] = product(0) + h2_ref[...]


def mix(own_state, other_state, w_out, h2):
    rows, width = h2.shape
    own = jax.ShapeDtypeStruct((rows, width), jnp.float32)
    part = jax.ShapeDtypeStruct((rows, width), jnp.bfloat16)
    operands = (own_state, other_state, w_out, h2)
    return pl.pallas_call(
        mix_kernel,
        out_shape=(own, part, part, part),
        scratch_shapes=[pltpu.VMEM((rows, width), jnp.bfloat16)],
        compiler_params=pltpu.CompilerParams(vmem_limit_bytes=16 * MIB),
        cost_estimate=cost(
            2 * rows * width * w_out.shape[1], (*operands, own, part, part, part)
        ),
        name="mix",
    )(*operands)


def exchanged(block, mask):
    count = lax.axis_size("seq")
    return lax.ppermute(block, "seq", [(i, i ^ mask) for i in range(count)])


def on_device(dna, conv_in, dilated_kernel_weight, w_query, w_key, w_value, w_out):
    count = lax.axis_size("seq")
    rows = dna.shape[0] // 2
    inner = 2 * LANES
    outer = rows - inner
    low = lax.ppermute(dna[-EDGE:], "seq", [(i, i + 1) for i in range(count - 1)])
    high = lax.ppermute(dna[:EDGE], "seq", [(i + 1, i) for i in range(count - 1)])
    h1_m, sent = first_conv(
        conv_middle_kernel, (dna,), conv_in, inner + EDGE, 2 * (inner + 2 * EDGE), "conv_middle"
    )
    wide_m = shared(sent)
    h1_e, sent = first_conv(
        conv_edge_kernel, (dna, low, high), conv_in, outer, 2 * (outer + 2 * EDGE), "conv_edge"
    )
    wide_e = shared(sent, (None, None, wide_m[1]))
    h2_m, sent = second_conv(
        dilated_middle_kernel,
        (*wide_m, after(h1_m, sent)),
        dilated_kernel_weight,
        inner,
        inner,
        inner + EDGE,
        "dilated_middle",
    )
    normed_m = shared(sent, wide_e[1:])
    h2, sent = second_conv(
        dilated_edge_kernel,
        (*wide_m, *wide_e, h1_m, h1_e, h2_m),
        dilated_kernel_weight,
        rows,
        outer,
        outer + 2 * EDGE,
        "dilated_edge",
    )
    normed_e = shared(sent, normed_m[1:])
    normed_m[0] = after(normed_m[0], sent)
    weights = (w_query, w_key, w_value)
    q_m, kv_m = project(project_middle_kernel, normed_m, weights, inner, "project_middle")
    x_m, y_m, d_m = (exchanged(kv_m, mask) for mask in (2, 4, 6))
    q, kv_e = project(project_edge_kernel, (*normed_e, q_m), weights, rows, "project_edge")
    q_other, x_e, y_e, d_e = exchanged(q, 1), *(exchanged(kv_e, mask) for mask in (2, 4, 6))
    state = attend((q, q_other), (kv_m, kv_e, x_m, y_m, d_m), None, 0, "attend_m")
    late = (x_e, y_e, d_e)
    state_other = attend((q_other,), late, state, rows, "attend_other")
    given = exchanged(state_other, 1)
    state_own = attend((q,), late, state, 0, "attend_own")
    own, p1, p2, p3 = mix(state_own, given, w_out, h2)
    total = own
    for part, shift in ((p1, 1), (p2, 3), (p3, 2)):
        total = total + lax.ppermute(part, "head", rotate(shift)).astype(jnp.float32)
    return total.astype(jnp.bfloat16)


def solution(mesh):
    in_specs = (
        P("seq", None),
        P(None, "head", None),
        P(None, "head", None),
        P("head", None),
        P("head", None),
        P("head", None),
        P("head", None),
    )
    out_specs = P("seq", "head")
    seq, head = mesh.shape["seq"], mesh.shape["head"]
    aligned = (C // head) % 128 == 0
    body = on_device if head == 4 and seq == 8 and aligned else general_form
    return jax.shard_map(body, mesh=mesh, in_specs=in_specs, out_specs=out_specs, check_vma=False)
```

```python
import functools
import math

import jax
import jax.numpy as jnp
from jax import lax
from jax.experimental import pallas as pl
from jax.experimental.pallas import tpu as pltpu
from jax.sharding import PartitionSpec as P

C = 1536
HEAD_DIM = 64
KW = 5
DILATION_STEP = 4
EPS = 1e-06
EDGE = 16
LOG2E = math.log2(math.e)
MIB = 1 << 20
LANES = 128


def padded_2(block, sides, width):
    for axis, dim in sides:
        count = lax.axis_size(axis)
        forward = [(i, i + 1) for i in range(count - 1)]
        backward = [(target, source) for source, target in forward]
        low = lax.ppermute(
            lax.slice_in_dim(block, block.shape[dim] - width, None, axis=dim), axis, forward
        )
        high = lax.ppermute(lax.slice_in_dim(block, 0, width, axis=dim), axis, backward)
        block = jnp.concatenate([low, block, high], axis=dim)
    return block


def row_scale(hidden):
    squares = lax.psum(jnp.sum(hidden * hidden, axis=1), "head")
    return hidden * lax.rsqrt(squares / C + EPS)[:, None]


def reduce_operands(left, right):
    return lax.dot_general(
        left, right, (((1,), (1,)), ((), ())), preferred_element_type=jnp.float32
    )


def general_form(dna, conv_in, dilated_kernel_weight, w_query, w_key, w_value, w_out):
    local_row_count = dna.shape[0] // 2
    half = (KW - 1) // 2
    padded = padded_2(dna, (("seq", 0),), half)
    h1 = jnp.zeros((local_row_count, conv_in.shape[1]), jnp.float32)
    for kernel_offset in range(KW):
        rows = lax.slice(
            padded,
            (kernel_offset, 0),
            (kernel_offset + 2 * local_row_count - 1, padded.shape[1]),
            (2, 1),
        )
        h1 = h1 + reduce_operands(rows, conv_in[kernel_offset])
    gelu_output = jax.nn.gelu(row_scale(h1), approximate=True).astype(jnp.bfloat16)
    complete_output = lax.all_gather(gelu_output, "head", axis=1, tiled=True)
    broad_input = padded_2(complete_output, (("seq", 0),), DILATION_STEP)
    second_hidden = h1
    for kernel_offset in range(3):
        second_hidden = second_hidden + reduce_operands(
            broad_input[
                DILATION_STEP * kernel_offset : DILATION_STEP * kernel_offset + local_row_count
            ],
            dilated_kernel_weight[kernel_offset],
        )
    normed = row_scale(second_hidden).astype(jnp.bfloat16)
    local_width = w_query.shape[0]
    heads_here = local_width // HEAD_DIM
    piece = lax.all_gather(normed, "head", axis=1, tiled=True)
    q_acc, k_acc, v_acc = (reduce_operands(piece, w) for w in (w_query, w_key, w_value))
    query = q_acc.astype(jnp.bfloat16).reshape(local_row_count, heads_here, HEAD_DIM)
    keys = k_acc.astype(jnp.bfloat16)
    values = v_acc.astype(jnp.bfloat16)
    scale = 1.0 / math.sqrt(HEAD_DIM)
    start_state = (
        jnp.full((heads_here, local_row_count), -1e30, jnp.float32),
        jnp.zeros((heads_here, local_row_count), jnp.float32),
        jnp.zeros((local_row_count, heads_here, HEAD_DIM), jnp.float32),
    )
    key_rows = lax.all_gather(keys, "seq", axis=0, tiled=True)
    value_rows = lax.all_gather(values, "seq", axis=0, tiled=True)
    count = key_rows.shape[0]
    width = 512 if count % 512 == 0 else count
    blocks = count // width
    key_blocks = key_rows.reshape(blocks, width, heads_here, HEAD_DIM)
    value_blocks = value_rows.reshape(blocks, width, heads_here, HEAD_DIM)

    def step(state, operands):
        running, total, acc = state
        key_block, value_block = operands
        scores = (
            jnp.einsum("qhd,khd->hqk", query, key_block, preferred_element_type=jnp.float32) * scale
        )
        newest = jnp.maximum(running, jnp.max(scores, axis=2))
        factor = jnp.exp(running - newest)
        weights = jnp.exp(scores - newest[:, :, None])
        total = total * factor + jnp.sum(weights, axis=2)
        update = jnp.einsum(
            "hqk,khd->qhd",
            weights.astype(jnp.bfloat16),
            value_block,
            preferred_element_type=jnp.float32,
        )
        acc = acc * jnp.transpose(factor)[:, :, None] + update
        return ((newest, total, acc), None)

    state, _ = lax.scan(step, start_state, (key_blocks, value_blocks))
    running, total, acc = state
    attended = (
        (acc / jnp.transpose(total)[:, :, None])
        .reshape(local_row_count, local_width)
        .astype(jnp.bfloat16)
    )
    partial_out = jnp.dot(attended, w_out, preferred_element_type=jnp.float32)
    mixed = lax.psum_scatter(
        partial_out.astype(jnp.bfloat16), "head", scatter_dimension=1, tiled=True
    ).astype(jnp.float32)
    return (second_hidden + mixed).astype(jnp.bfloat16)


def nbytes(*arrays):
    return sum(math.prod(a.shape) * jnp.dtype(a.dtype).itemsize for a in arrays)


def cost(flops, arrays, transcendentals=0):
    return pl.CostEstimate(
        flops=int(flops), bytes_accessed=int(nbytes(*arrays)), transcendentals=int(transcendentals)
    )


def rotate(offset):
    count = lax.axis_size("head")
    return [(i, (i + offset) % count) for i in range(count)]


def after(value, *others):
    return lax.optimization_barrier((value, *others))[0]


def shared(block, earlier=(None, None, None)):
    count = lax.axis_size("head")
    moved = []
    for k, previous in zip((1, count - 1, 2), earlier):
        held = block if previous is None else after(block, previous)
        moved.append(lax.ppermute(held, "head", rotate(k)))
    return [block, *moved]


def owner(k):
    count = lax.axis_size("head")
    return lax.rem(lax.axis_index("head") + count - k, count)


SHIFTS = (0, 1, 3, 2)


def store_wide(wide, start, block):
    for j in range(wide.shape[0]):
        rows = pl.ds(start, block.shape[0])
        wide[j, rows, :] = block[:, 128 * j : 128 * (j + 1)].astype(jnp.float32)


def taps_sum(wide, weight_ref, groups):
    total = None
    for tap in range(KW):
        picked = []
        for start, count in groups:
            lanes = [
                wide[j, pl.ds(start + tap, count, stride=2), :] for j in range(wide.shape[0])
            ]
            picked.append(jnp.concatenate(lanes, axis=1).astype(jnp.bfloat16))
        taken = picked[0] if len(picked) == 1 else jnp.concatenate(picked, axis=0)
        term = reduce_operands(taken, weight_ref[tap])
        total = term if total is None else total + term
    return total


FIRST = EDGE - KW // 2


def conv_middle_kernel(dna_ref, weight_ref, h1_ref, sent_ref, wide):
    store_wide(wide, 0, dna_ref[pl.ds(0, wide.shape[1]), :])
    total = taps_sum(wide, weight_ref, [(FIRST, sent_ref.shape[0])])
    h1_ref[...] = total
    sent_ref[...] = total.astype(jnp.bfloat16)


def conv_edge_kernel(dna_ref, low_ref, high_ref, weight_ref, h1_ref, sent_ref, wide):
    rows = dna_ref.shape[0]
    upper = sent_ref.shape[0] - EDGE
    first = rows - 2 * upper
    zeros = jnp.zeros((EDGE, dna_ref.shape[1]), jnp.bfloat16)
    store_wide(wide, 0, zeros)
    store_wide(wide, EDGE, low_ref[...])
    store_wide(wide, 2 * EDGE, dna_ref[pl.ds(0, 2 * EDGE), :])
    store_wide(wide, 4 * EDGE, dna_ref[pl.ds(first, rows - first), :])
    store_wide(wide, 4 * EDGE + rows - first, high_ref[...])
    store_wide(wide, 5 * EDGE + rows - first, zeros)
    total = taps_sum(wide, weight_ref, [(FIRST, EDGE), (4 * EDGE + FIRST, upper)])
    h1_ref[...] = total
    sent_ref[...] = total.astype(jnp.bfloat16)


def first_conv(kernel, operands, weight, count, deep, name):
    width, out = weight.shape[2], weight.shape[1]
    kept = jax.ShapeDtypeStruct((count, out), jnp.float32)
    sent = jax.ShapeDtypeStruct((count, out), jnp.bfloat16)
    return pl.pallas_call(
        kernel,
        out_shape=(kept, sent),
        scratch_shapes=[pltpu.VMEM((width // 128, deep, 128), jnp.float32)],
        compiler_params=pltpu.CompilerParams(vmem_limit_bytes=24 * MIB),
        cost_estimate=cost(2 * count * out * width * KW, (*operands, weight, kept, sent)),
        name=name,
    )(*operands, weight)


def inverse_norm(blocks):
    squares = None
    for block in blocks:
        term = jnp.sum(block * block, axis=1, keepdims=True)
        squares = term if squares is None else squares + term
    return lax.rsqrt(squares / C + EPS)


def wide_blocks(parts, start, count):
    return [part[pl.ds(start, count), :].astype(jnp.float32) for part in parts]


def gelu(value):
    return jax.nn.gelu(value, approximate=True)


def columns_of(shift, width):
    return pl.ds(pl.multiple_of(owner(shift) * width, 128), width)


def dilated_middle_kernel(a0, a1, a2, a3, h1_ref, weight_ref, h2_ref, sent_ref, act):
    parts = (a0, a1, a2, a3)
    count, width = a0.shape
    rows = h2_ref.shape[0]
    blocks = wide_blocks(parts, 0, count)
    inverse = inverse_norm(blocks)
    total = h1_ref[pl.ds(8, rows), :]
    for slot, (block, shift) in enumerate(zip(blocks, SHIFTS)):
        act[slot] = gelu(block * inverse)
        for tap in range(3):
            taken = act[slot, pl.ds((tap + 1) * DILATION_STEP, rows), :].astype(jnp.bfloat16)
            total = total + reduce_operands(taken, weight_ref[tap, :, columns_of(shift, width)])
    h2_ref[...] = total
    sent_ref[...] = total.astype(jnp.bfloat16)


def dilated_edge_kernel(
    m0, m1, m2, m3, e0, e1, e2, e3, hm_ref, he_ref, h2m_ref, weight_ref, h2_ref, sent_ref, act
):
    middle, edge = (m0, m1, m2, m3), (e0, e1, e2, e3)
    inner, width = m0.shape
    outer = e0.shape[0]
    rows = h2_ref.shape[0]
    upper = outer - EDGE
    position = lax.axis_index("seq") * rows + lax.broadcasted_iota(jnp.int32, (outer, 1), 0)
    place = lax.broadcasted_iota(jnp.int32, (outer, 1), 0)
    position = position + jnp.where(place < EDGE, -8, inner - 8)
    inside = (position >= 0) & (position < rows * lax.axis_size("seq"))
    outer_blocks = wide_blocks(edge, 0, outer)
    outer_inverse = jnp.where(inside, inverse_norm(outer_blocks), 0.0)
    low_blocks = wide_blocks(middle, 0, EDGE)
    low_inverse = inverse_norm(low_blocks)
    high_blocks = wide_blocks(middle, inner - EDGE, EDGE)
    high_inverse = inverse_norm(high_blocks)
    last = rows - (outer - EDGE)
    total = jnp.concatenate(
        [
            he_ref[pl.ds(8, 8), :],
            hm_ref[pl.ds(0, 8), :],
            hm_ref[pl.ds(inner - 8, 8), :],
            he_ref[pl.ds(EDGE, upper - 8), :],
        ],
        axis=0,
    )
    tail = 2 * EDGE
    for slot, shift in enumerate(SHIFTS):
        full = gelu(outer_blocks[slot] * outer_inverse)
        act[slot, pl.ds(0, EDGE), :] = full[:EDGE]
        act[slot, pl.ds(EDGE, EDGE), :] = gelu(low_blocks[slot] * low_inverse)
        act[slot, pl.ds(tail, EDGE), :] = gelu(high_blocks[slot] * high_inverse)
        act[slot, pl.ds(tail + EDGE, upper), :] = full[EDGE:]
        for tap in range(3):
            shifted = (tap + 1) * DILATION_STEP
            taken = jnp.concatenate(
                [
                    act[slot, pl.ds(shifted, EDGE), :],
                    act[slot, pl.ds(tail + shifted, upper), :],
                ],
                axis=0,
            ).astype(jnp.bfloat16)
            total = total + reduce_operands(taken, weight_ref[tap, :, columns_of(shift, width)])
    h2_ref[pl.ds(0, EDGE), :] = total[:EDGE]
    h2_ref[pl.ds(EDGE, last - EDGE), :] = h2m_ref[...]
    h2_ref[pl.ds(last, rows - last), :] = total[EDGE:]
    sent_ref[...] = total.astype(jnp.bfloat16)


def second_conv(kernel, operands, weight, kept_rows, sent_rows, deep, name):
    out, width = weight.shape[1], operands[0].shape[1]
    kept = jax.ShapeDtypeStruct((kept_rows, out), jnp.float32)
    sent = jax.ShapeDtypeStruct((sent_rows, out), jnp.bfloat16)
    return pl.pallas_call(
        kernel,
        out_shape=(kept, sent),
        scratch_shapes=[pltpu.VMEM((4, deep, width), jnp.float32)],
        compiler_params=pltpu.CompilerParams(vmem_limit_bytes=24 * MIB),
        cost_estimate=cost(
            2 * sent_rows * out * weight.shape[2] * 3,
            (*operands, weight, kept, sent),
            deep * weight.shape[2],
        ),
        name=name,
    )(*operands, weight)


def projections(parts, wq, wk, wv, kv_ref):
    width = parts[0].shape[1]
    rows, out = parts[0].shape[0], wq.shape[0]
    blocks = [part[...].astype(jnp.float32) for part in parts]
    inverse = inverse_norm(blocks)
    normed = [(block * inverse).astype(jnp.bfloat16) for block in blocks]

    def product(weight_ref, start=0, stop=rows, weight_first=False):
        total = None
        for part, shift in zip(normed, SHIFTS):
            weight = weight_ref[:, columns_of(shift, width)]
            taken = part[start:stop]
            pair = (weight, taken) if weight_first else (taken, weight)
            term = reduce_operands(*pair)
            total = term if total is None else total + term
        return total

    kv_ref[:, :out] = product(wk).astype(jnp.bfloat16)
    turned = rows - rows % LANES
    value = product(wv, 0, turned, True).astype(jnp.bfloat16)
    for row in range(0, turned, LANES):
        for lane in range(0, out, LANES):
            kv_ref[pl.ds(row, LANES), pl.ds(out + lane, LANES)] = value[
                lane : lane + LANES, row : row + LANES
            ]
    if turned < rows:
        value = product(wv, turned, rows)
        kv_ref[pl.ds(turned, rows - turned), out:] = value.astype(jnp.bfloat16)
    scale = LOG2E / math.sqrt(HEAD_DIM)
    return (product(wq) * scale).astype(jnp.bfloat16)


def project_middle_kernel(a0, a1, a2, a3, wq, wk, wv, q_ref, kv_ref):
    q_ref[...] = projections((a0, a1, a2, a3), wq, wk, wv, kv_ref)


def project_edge_kernel(a0, a1, a2, a3, qm_ref, wq, wk, wv, q_ref, kv_ref):
    query = projections((a0, a1, a2, a3), wq, wk, wv, kv_ref)
    inner, rows = qm_ref.shape[0], q_ref.shape[0]
    q_ref[pl.ds(0, EDGE), :] = query[:EDGE]
    q_ref[pl.ds(EDGE, inner), :] = qm_ref[...]
    q_ref[pl.ds(EDGE + inner, rows - EDGE - inner), :] = query[EDGE:]


def project(kernel, operands, weights, q_rows, name):
    rows, out = operands[0].shape[0], weights[0].shape[0]
    q = jax.ShapeDtypeStruct((q_rows, out), jnp.bfloat16)
    kv = jax.ShapeDtypeStruct((rows, 2 * out), jnp.bfloat16)
    return pl.pallas_call(
        kernel,
        out_shape=(q, kv),
        compiler_params=pltpu.CompilerParams(vmem_limit_bytes=20 * MIB),
        cost_estimate=cost(6 * rows * out * C, (*operands, *weights, q, kv)),
        name=name,
    )(*operands, *weights)


TILE = 64


def split_rows(block):
    turned = block.shape[0] - block.shape[0] % LANES
    return turned, block.shape[0] - turned


def turned_values(blocks, width, pair):
    lanes = pl.ds(width + pair * LANES, LANES)
    values = []
    for block in blocks:
        for row in range(0, split_rows(block)[0], LANES):
            values.append(block[pl.ds(row, LANES), lanes])
    rest = []
    for block in blocks:
        start, count = split_rows(block)
        if count:
            rest.append(block[pl.ds(start, count), lanes].astype(jnp.float32))
    if rest:
        values.append(jnp.transpose(jnp.concatenate(rest, axis=0)).astype(jnp.bfloat16))
    return jnp.concatenate(values, axis=1)


def ordered_keys(blocks, pair):
    lanes = pl.ds(pair * LANES, LANES)
    keys = [block[pl.ds(0, split_rows(block)[0]), lanes] for block in blocks]
    for block in blocks:
        start, count = split_rows(block)
        if count:
            keys.append(block[pl.ds(start, count), lanes])
    return jnp.concatenate(keys, axis=0)


def partial_attention(query, keys, values, scores, weights, head, lane):
    pair, half = divmod(head, 2)
    mine = query[:, pair * LANES : (pair + 1) * LANES]
    mine = jnp.where((lane // HEAD_DIM) == half, mine, jnp.zeros_like(mine))
    scores[...] = reduce_operands(keys, mine)
    columns = scores.shape[1]
    top = None
    for start in range(0, scores.shape[0], TILE):
        tile = jnp.max(scores[pl.ds(start, TILE), :].reshape(-1, 8, columns), axis=0)
        top = tile if top is None else jnp.maximum(top, tile)
    top = jnp.max(top, axis=0, keepdims=True)
    total = None
    for start in range(0, scores.shape[0], TILE):
        weight = jnp.exp2(scores[pl.ds(start, TILE), :] - top)
        tile = jnp.sum(weight.reshape(-1, 8, columns), axis=0)
        total = tile if total is None else total + tile
        weights[pl.ds(start, TILE), :] = weight.astype(jnp.bfloat16)
    values = values[half * HEAD_DIM : (half + 1) * HEAD_DIM]
    out = jnp.dot(values, weights[...], preferred_element_type=jnp.float32)
    return out, top, jnp.sum(total, axis=0, keepdims=True)


def state_parts(state, head, width, columns):
    return (
        state[pl.ds(head * HEAD_DIM, HEAD_DIM), columns],
        state[pl.ds(width + head, 1), columns],
        state[pl.ds(width + 8 + head, 1), columns],
    )


def merged_parts(one, other):
    top = jnp.maximum(one[1], other[1])
    first, second = jnp.exp2(one[1] - top), jnp.exp2(other[1] - top)
    return first * one[0] + second * other[0], top, first * one[2] + second * other[2]


def attend_kernel(first_column, q_refs, blocks, state, out_ref, scores, weights):
    width = q_refs[0].shape[1]
    query = jnp.concatenate([ref[...] for ref in q_refs], axis=0)
    columns = query.shape[0]
    lane = lax.broadcasted_iota(jnp.int32, (columns, LANES), 1)
    out_ref[pl.ds(width, 16), :] = jnp.zeros((16, columns), jnp.float32)
    for head in range(width // HEAD_DIM):
        if head % 2 == 0:
            keys = ordered_keys(blocks, head // 2)
            values = turned_values(blocks, width, head // 2)
        part = partial_attention(
            query, keys, values, scores.at[head % 2], weights.at[head % 2], head, lane
        )
        if state is not None:
            part = merged_parts(
                part, state_parts(state, head, width, pl.ds(first_column, columns))
            )
        out_ref[pl.ds(head * HEAD_DIM, HEAD_DIM), :] = part[0]
        out_ref[pl.ds(width + head, 1), :] = part[1]
        out_ref[pl.ds(width + 8 + head, 1), :] = part[2]


def attend(queries, blocks, state, first_column, name):
    rows, width = queries[0].shape
    columns = rows * len(queries)
    extent = sum(block.shape[0] for block in blocks)
    out = jax.ShapeDtypeStruct((width + 16, columns), jnp.float32)
    operands = (*queries, *blocks) + (() if state is None else (state,))

    def kernel(*refs):
        q_refs, block_refs = refs[: len(queries)], refs[len(queries) :][: len(blocks)]
        state_ref = None if state is None else refs[len(operands) - 1]
        attend_kernel(
            first_column, q_refs, block_refs, state_ref, *refs[len(operands) :]
        )

    return pl.pallas_call(
        kernel,
        out_shape=out,
        scratch_shapes=[
            pltpu.VMEM((2, extent, columns), jnp.float32),
            pltpu.VMEM((2, extent, columns), jnp.bfloat16),
        ],
        compiler_params=pltpu.CompilerParams(vmem_limit_bytes=24 * MIB),
        cost_estimate=cost(
            4 * columns * width * extent, (*operands, out), columns * extent * width // HEAD_DIM
        ),
        name=name,
    )(*operands)


def mix_kernel(own_state, other_state, w_ref, h2_ref, own_ref, p1, p2, p3, attended):
    rows, width = h2_ref.shape
    for pair in range(width // LANES):
        halves = []
        for head in (2 * pair, 2 * pair + 1):
            out, _, total = merged_parts(
                state_parts(own_state, head, width, pl.ds(0, rows)),
                state_parts(other_state, head, width, pl.ds(0, rows)),
            )
            halves.append(out / total)
        merged = jnp.transpose(jnp.concatenate(halves, axis=0))
        attended[:, pl.ds(pair * LANES, LANES)] = merged.astype(jnp.bfloat16)

    def product(shift):
        return jnp.dot(
            attended[...], w_ref[:, columns_of(shift, width)], preferred_element_type=jnp.float32
        )

    for ref, shift in ((p3, 2), (p1, 3), (p2, 1)):
        ref[...] = product(shift).astype(jnp.bfloat16)
    own_ref[...] = product(0) + h2_ref[...]


def mix(own_state, other_state, w_out, h2):
    rows, width = h2.shape
    own = jax.ShapeDtypeStruct((rows, width), jnp.float32)
    part = jax.ShapeDtypeStruct((rows, width), jnp.bfloat16)
    operands = (own_state, other_state, w_out, h2)
    return pl.pallas_call(
        mix_kernel,
        out_shape=(own, part, part, part),
        scratch_shapes=[pltpu.VMEM((rows, width), jnp.bfloat16)],
        compiler_params=pltpu.CompilerParams(vmem_limit_bytes=16 * MIB),
        cost_estimate=cost(
            2 * rows * width * w_out.shape[1], (*operands, own, part, part, part)
        ),
        name="mix",
    )(*operands)


def exchanged(block, mask):
    count = lax.axis_size("seq")
    return lax.ppermute(block, "seq", [(i, i ^ mask) for i in range(count)])


def on_device(dna, conv_in, dilated_kernel_weight, w_query, w_key, w_value, w_out):
    count = lax.axis_size("seq")
    rows = dna.shape[0] // 2
    inner = rows // 2
    outer = rows - inner
    low = lax.ppermute(dna[-EDGE:], "seq", [(i, i + 1) for i in range(count - 1)])
    high = lax.ppermute(dna[:EDGE], "seq", [(i + 1, i) for i in range(count - 1)])
    h1_m, sent = first_conv(
        conv_middle_kernel, (dna,), conv_in, inner + EDGE, 2 * (inner + 2 * EDGE), "conv_middle"
    )
    wide_m = shared(sent)
    h1_e, sent = first_conv(
        conv_edge_kernel, (dna, low, high), conv_in, outer, 2 * (outer + 2 * EDGE), "conv_edge"
    )
    wide_e = shared(sent, (None, None, wide_m[1]))
    h2_m, sent = second_conv(
        dilated_middle_kernel,
        (*wide_m, after(h1_m, sent)),
        dilated_kernel_weight,
        inner,
        inner,
        inner + EDGE,
        "dilated_middle",
    )
    normed_m = shared(sent, wide_e[1:])
    h2, sent = second_conv(
        dilated_edge_kernel,
        (*wide_m, *wide_e, h1_m, h1_e, h2_m),
        dilated_kernel_weight,
        rows,
        outer,
        outer + 2 * EDGE,
        "dilated_edge",
    )
    normed_e = shared(sent, normed_m[1:])
    normed_m[0] = after(normed_m[0], sent)
    weights = (w_query, w_key, w_value)
    q_m, kv_m = project(project_middle_kernel, normed_m, weights, inner, "project_middle")
    x_m, y_m, d_m = (exchanged(kv_m, mask) for mask in (2, 4, 6))
    q, kv_e = project(project_edge_kernel, (*normed_e, q_m), weights, rows, "project_edge")
    q_other, x_e, y_e, d_e = exchanged(q, 1), *(exchanged(kv_e, mask) for mask in (2, 4, 6))
    state = attend((q, q_other), (kv_m, kv_e, x_m, y_m, d_m), None, 0, "attend_m")
    late = (x_e, y_e, d_e)
    state_other = attend((q_other,), late, state, rows, "attend_other")
    given = exchanged(state_other, 1)
    state_own = attend((q,), late, state, 0, "attend_own")
    own, p1, p2, p3 = mix(state_own, given, w_out, h2)
    total = own
    for part, shift in ((p1, 1), (p2, 3), (p3, 2)):
        total = total + lax.ppermute(part, "head", rotate(shift)).astype(jnp.float32)
    return total.astype(jnp.bfloat16)


def solution(mesh):
    in_specs = (
        P("seq", None),
        P(None, "head", None),
        P(None, "head", None),
        P("head", None),
        P("head", None),
        P("head", None),
        P("head", None),
    )
    out_specs = P("seq", "head")
    seq, head = mesh.shape["seq"], mesh.shape["head"]
    aligned = (C // head) % 128 == 0
    body = on_device if head == 4 and seq == 8 and aligned else general_form
    return jax.shard_map(body, mesh=mesh, in_specs=in_specs, out_specs=out_specs, check_vma=False)
```

```python
import functools
import math

import jax
import jax.numpy as jnp
from jax import lax
from jax.experimental import pallas as pl
from jax.experimental.pallas import tpu as pltpu
from jax.sharding import PartitionSpec as P

C = 1536
HEAD_DIM = 64
KW = 5
DILATION_STEP = 4
EPS = 1e-06
EDGE = 16
LOG2E = math.log2(math.e)
MIB = 1 << 20
LANES = 128


def padded_2(block, sides, width):
    for axis, dim in sides:
        count = lax.axis_size(axis)
        forward = [(i, i + 1) for i in range(count - 1)]
        backward = [(target, source) for source, target in forward]
        low = lax.ppermute(
            lax.slice_in_dim(block, block.shape[dim] - width, None, axis=dim), axis, forward
        )
        high = lax.ppermute(lax.slice_in_dim(block, 0, width, axis=dim), axis, backward)
        block = jnp.concatenate([low, block, high], axis=dim)
    return block


def row_scale(hidden):
    squares = lax.psum(jnp.sum(hidden * hidden, axis=1), "head")
    return hidden * lax.rsqrt(squares / C + EPS)[:, None]


def reduce_operands(left, right):
    return lax.dot_general(
        left, right, (((1,), (1,)), ((), ())), preferred_element_type=jnp.float32
    )


def general_form(dna, conv_in, dilated_kernel_weight, w_query, w_key, w_value, w_out):
    local_row_count = dna.shape[0] // 2
    half = (KW - 1) // 2
    padded = padded_2(dna, (("seq", 0),), half)
    h1 = jnp.zeros((local_row_count, conv_in.shape[1]), jnp.float32)
    for kernel_offset in range(KW):
        rows = lax.slice(
            padded,
            (kernel_offset, 0),
            (kernel_offset + 2 * local_row_count - 1, padded.shape[1]),
            (2, 1),
        )
        h1 = h1 + reduce_operands(rows, conv_in[kernel_offset])
    gelu_output = jax.nn.gelu(row_scale(h1), approximate=True).astype(jnp.bfloat16)
    complete_output = lax.all_gather(gelu_output, "head", axis=1, tiled=True)
    broad_input = padded_2(complete_output, (("seq", 0),), DILATION_STEP)
    second_hidden = h1
    for kernel_offset in range(3):
        second_hidden = second_hidden + reduce_operands(
            broad_input[
                DILATION_STEP * kernel_offset : DILATION_STEP * kernel_offset + local_row_count
            ],
            dilated_kernel_weight[kernel_offset],
        )
    normed = row_scale(second_hidden).astype(jnp.bfloat16)
    local_width = w_query.shape[0]
    heads_here = local_width // HEAD_DIM
    piece = lax.all_gather(normed, "head", axis=1, tiled=True)
    q_acc, k_acc, v_acc = (reduce_operands(piece, w) for w in (w_query, w_key, w_value))
    query = q_acc.astype(jnp.bfloat16).reshape(local_row_count, heads_here, HEAD_DIM)
    keys = k_acc.astype(jnp.bfloat16)
    values = v_acc.astype(jnp.bfloat16)
    scale = 1.0 / math.sqrt(HEAD_DIM)
    start_state = (
        jnp.full((heads_here, local_row_count), -1e30, jnp.float32),
        jnp.zeros((heads_here, local_row_count), jnp.float32),
        jnp.zeros((local_row_count, heads_here, HEAD_DIM), jnp.float32),
    )
    key_rows = lax.all_gather(keys, "seq", axis=0, tiled=True)
    value_rows = lax.all_gather(values, "seq", axis=0, tiled=True)
    count = key_rows.shape[0]
    width = 512 if count % 512 == 0 else count
    blocks = count // width
    key_blocks = key_rows.reshape(blocks, width, heads_here, HEAD_DIM)
    value_blocks = value_rows.reshape(blocks, width, heads_here, HEAD_DIM)

    def step(state, operands):
        running, total, acc = state
        key_block, value_block = operands
        scores = (
            jnp.einsum("qhd,khd->hqk", query, key_block, preferred_element_type=jnp.float32) * scale
        )
        newest = jnp.maximum(running, jnp.max(scores, axis=2))
        factor = jnp.exp(running - newest)
        weights = jnp.exp(scores - newest[:, :, None])
        total = total * factor + jnp.sum(weights, axis=2)
        update = jnp.einsum(
            "hqk,khd->qhd",
            weights.astype(jnp.bfloat16),
            value_block,
            preferred_element_type=jnp.float32,
        )
        acc = acc * jnp.transpose(factor)[:, :, None] + update
        return ((newest, total, acc), None)

    state, _ = lax.scan(step, start_state, (key_blocks, value_blocks))
    running, total, acc = state
    attended = (
        (acc / jnp.transpose(total)[:, :, None])
        .reshape(local_row_count, local_width)
        .astype(jnp.bfloat16)
    )
    partial_out = jnp.dot(attended, w_out, preferred_element_type=jnp.float32)
    mixed = lax.psum_scatter(
        partial_out.astype(jnp.bfloat16), "head", scatter_dimension=1, tiled=True
    ).astype(jnp.float32)
    return (second_hidden + mixed).astype(jnp.bfloat16)


def nbytes(*arrays):
    return sum(math.prod(a.shape) * jnp.dtype(a.dtype).itemsize for a in arrays)


def cost(flops, arrays, transcendentals=0):
    return pl.CostEstimate(
        flops=int(flops), bytes_accessed=int(nbytes(*arrays)), transcendentals=int(transcendentals)
    )


def rotate(offset):
    count = lax.axis_size("head")
    return [(i, (i + offset) % count) for i in range(count)]


def after(value, *others):
    return lax.optimization_barrier((value, *others))[0]


def shared(block, earlier=(None, None, None)):
    count = lax.axis_size("head")
    moved = []
    for k, previous in zip((1, count - 1, 2), earlier):
        held = block if previous is None else after(block, *previous)
        moved.append(lax.ppermute(held, "head", rotate(k)))
    return [block, *moved]


def owner(k):
    count = lax.axis_size("head")
    return lax.rem(lax.axis_index("head") + count - k, count)


SHIFTS = (0, 1, 3, 2)


def store_wide(wide, start, block):
    for j in range(wide.shape[0]):
        rows = pl.ds(start, block.shape[0])
        wide[j, rows, :] = block[:, 128 * j : 128 * (j + 1)].astype(jnp.float32)


def taps_sum(wide, weight_ref, groups):
    total = None
    for tap in range(KW):
        picked = []
        for start, count in groups:
            lanes = [
                wide[j, pl.ds(start + tap, count, stride=2), :] for j in range(wide.shape[0])
            ]
            picked.append(jnp.concatenate(lanes, axis=1).astype(jnp.bfloat16))
        taken = picked[0] if len(picked) == 1 else jnp.concatenate(picked, axis=0)
        term = reduce_operands(taken, weight_ref[tap])
        total = term if total is None else total + term
    return total


FIRST = EDGE - KW // 2


def conv_middle_kernel(dna_ref, weight_ref, h1_ref, sent_ref, wide):
    store_wide(wide, 0, dna_ref[pl.ds(0, wide.shape[1]), :])
    total = taps_sum(wide, weight_ref, [(FIRST, sent_ref.shape[0])])
    h1_ref[...] = total
    sent_ref[...] = total.astype(jnp.bfloat16)


def conv_edge_kernel(dna_ref, low_ref, high_ref, weight_ref, h1_ref, sent_ref, wide):
    rows = dna_ref.shape[0]
    upper = sent_ref.shape[0] - EDGE
    first = rows - 2 * upper
    zeros = jnp.zeros((EDGE, dna_ref.shape[1]), jnp.bfloat16)
    store_wide(wide, 0, zeros)
    store_wide(wide, EDGE, low_ref[...])
    store_wide(wide, 2 * EDGE, dna_ref[pl.ds(0, 2 * EDGE), :])
    store_wide(wide, 4 * EDGE, dna_ref[pl.ds(first, rows - first), :])
    store_wide(wide, 4 * EDGE + rows - first, high_ref[...])
    store_wide(wide, 5 * EDGE + rows - first, zeros)
    total = taps_sum(wide, weight_ref, [(FIRST, EDGE), (4 * EDGE + FIRST, upper)])
    h1_ref[...] = total
    sent_ref[...] = total.astype(jnp.bfloat16)


def first_conv(kernel, operands, weight, count, deep, name):
    width, out = weight.shape[2], weight.shape[1]
    kept = jax.ShapeDtypeStruct((count, out), jnp.float32)
    sent = jax.ShapeDtypeStruct((count, out), jnp.bfloat16)
    return pl.pallas_call(
        kernel,
        out_shape=(kept, sent),
        scratch_shapes=[pltpu.VMEM((width // 128, deep, 128), jnp.float32)],
        compiler_params=pltpu.CompilerParams(vmem_limit_bytes=24 * MIB),
        cost_estimate=cost(2 * count * out * width * KW, (*operands, weight, kept, sent)),
        name=name,
    )(*operands, weight)


def inverse_norm(blocks):
    squares = None
    for block in blocks:
        term = jnp.sum(block * block, axis=1, keepdims=True)
        squares = term if squares is None else squares + term
    return lax.rsqrt(squares / C + EPS)


def wide_blocks(parts, start, count):
    return [part[pl.ds(start, count), :].astype(jnp.float32) for part in parts]


def gelu(value):
    return jax.nn.gelu(value, approximate=True)


def columns_of(shift, width):
    return pl.ds(pl.multiple_of(owner(shift) * width, 128), width)


def dilated_middle_kernel(a0, a1, a2, a3, h1_ref, weight_ref, h2_ref, sent_ref, act):
    parts = (a0, a1, a2, a3)
    count, width = a0.shape
    rows = h2_ref.shape[0]
    blocks = wide_blocks(parts, 0, count)
    inverse = inverse_norm(blocks)
    total = h1_ref[pl.ds(8, rows), :]
    for slot, (block, shift) in enumerate(zip(blocks, SHIFTS)):
        act[slot] = gelu(block * inverse)
        for tap in range(3):
            taken = act[slot, pl.ds((tap + 1) * DILATION_STEP, rows), :].astype(jnp.bfloat16)
            total = total + reduce_operands(taken, weight_ref[tap, :, columns_of(shift, width)])
    h2_ref[...] = total
    sent_ref[...] = total.astype(jnp.bfloat16)


def dilated_edge_kernel(
    m0, m1, m2, m3, e0, e1, e2, e3, hm_ref, he_ref, h2m_ref, weight_ref, h2_ref, sent_ref, act
):
    middle, edge = (m0, m1, m2, m3), (e0, e1, e2, e3)
    inner, width = m0.shape
    outer = e0.shape[0]
    rows = h2_ref.shape[0]
    upper = outer - EDGE
    position = lax.axis_index("seq") * rows + lax.broadcasted_iota(jnp.int32, (outer, 1), 0)
    place = lax.broadcasted_iota(jnp.int32, (outer, 1), 0)
    position = position + jnp.where(place < EDGE, -8, inner - 8)
    inside = (position >= 0) & (position < rows * lax.axis_size("seq"))
    outer_blocks = wide_blocks(edge, 0, outer)
    outer_inverse = jnp.where(inside, inverse_norm(outer_blocks), 0.0)
    low_blocks = wide_blocks(middle, 0, EDGE)
    low_inverse = inverse_norm(low_blocks)
    high_blocks = wide_blocks(middle, inner - EDGE, EDGE)
    high_inverse = inverse_norm(high_blocks)
    last = rows - (outer - EDGE)
    total = jnp.concatenate(
        [
            he_ref[pl.ds(8, 8), :],
            hm_ref[pl.ds(0, 8), :],
            hm_ref[pl.ds(inner - 8, 8), :],
            he_ref[pl.ds(EDGE, upper - 8), :],
        ],
        axis=0,
    )
    tail = 2 * EDGE
    for slot, shift in enumerate(SHIFTS):
        full = gelu(outer_blocks[slot] * outer_inverse)
        act[slot, pl.ds(0, EDGE), :] = full[:EDGE]
        act[slot, pl.ds(EDGE, EDGE), :] = gelu(low_blocks[slot] * low_inverse)
        act[slot, pl.ds(tail, EDGE), :] = gelu(high_blocks[slot] * high_inverse)
        act[slot, pl.ds(tail + EDGE, upper), :] = full[EDGE:]
        for tap in range(3):
            shifted = (tap + 1) * DILATION_STEP
            taken = jnp.concatenate(
                [
                    act[slot, pl.ds(shifted, EDGE), :],
                    act[slot, pl.ds(tail + shifted, upper), :],
                ],
                axis=0,
            ).astype(jnp.bfloat16)
            total = total + reduce_operands(taken, weight_ref[tap, :, columns_of(shift, width)])
    h2_ref[pl.ds(0, EDGE), :] = total[:EDGE]
    h2_ref[pl.ds(EDGE, last - EDGE), :] = h2m_ref[...]
    h2_ref[pl.ds(last, rows - last), :] = total[EDGE:]
    sent_ref[...] = total.astype(jnp.bfloat16)


def second_conv(kernel, operands, weight, kept_rows, sent_rows, deep, name):
    out, width = weight.shape[1], operands[0].shape[1]
    kept = jax.ShapeDtypeStruct((kept_rows, out), jnp.float32)
    sent = jax.ShapeDtypeStruct((sent_rows, out), jnp.bfloat16)
    return pl.pallas_call(
        kernel,
        out_shape=(kept, sent),
        scratch_shapes=[pltpu.VMEM((4, deep, width), jnp.float32)],
        compiler_params=pltpu.CompilerParams(vmem_limit_bytes=24 * MIB),
        cost_estimate=cost(
            2 * sent_rows * out * weight.shape[2] * 3,
            (*operands, weight, kept, sent),
            deep * weight.shape[2],
        ),
        name=name,
    )(*operands, weight)


def projections(parts, wq, wk, wv, kv_ref):
    width = parts[0].shape[1]
    rows, out = parts[0].shape[0], wq.shape[0]
    blocks = [part[...].astype(jnp.float32) for part in parts]
    inverse = inverse_norm(blocks)
    normed = [(block * inverse).astype(jnp.bfloat16) for block in blocks]

    def product(weight_ref, start=0, stop=rows, weight_first=False):
        total = None
        for part, shift in zip(normed, SHIFTS):
            weight = weight_ref[:, columns_of(shift, width)]
            taken = part[start:stop]
            pair = (weight, taken) if weight_first else (taken, weight)
            term = reduce_operands(*pair)
            total = term if total is None else total + term
        return total

    kv_ref[:, :out] = product(wk).astype(jnp.bfloat16)
    turned = rows - rows % LANES
    value = product(wv, 0, turned, True).astype(jnp.bfloat16)
    for row in range(0, turned, LANES):
        for lane in range(0, out, LANES):
            kv_ref[pl.ds(row, LANES), pl.ds(out + lane, LANES)] = value[
                lane : lane + LANES, row : row + LANES
            ]
    if turned < rows:
        value = product(wv, turned, rows)
        kv_ref[pl.ds(turned, rows - turned), out:] = value.astype(jnp.bfloat16)
    scale = LOG2E / math.sqrt(HEAD_DIM)
    return (product(wq) * scale).astype(jnp.bfloat16)


def project_middle_kernel(a0, a1, a2, a3, wq, wk, wv, q_ref, kv_ref):
    q_ref[...] = projections((a0, a1, a2, a3), wq, wk, wv, kv_ref)


def project_edge_kernel(a0, a1, a2, a3, qm_ref, wq, wk, wv, q_ref, kv_ref):
    query = projections((a0, a1, a2, a3), wq, wk, wv, kv_ref)
    inner, rows = qm_ref.shape[0], q_ref.shape[0]
    q_ref[pl.ds(0, EDGE), :] = query[:EDGE]
    q_ref[pl.ds(EDGE, inner), :] = qm_ref[...]
    q_ref[pl.ds(EDGE + inner, rows - EDGE - inner), :] = query[EDGE:]


def project(kernel, operands, weights, q_rows, name):
    rows, out = operands[0].shape[0], weights[0].shape[0]
    q = jax.ShapeDtypeStruct((q_rows, out), jnp.bfloat16)
    kv = jax.ShapeDtypeStruct((rows, 2 * out), jnp.bfloat16)
    return pl.pallas_call(
        kernel,
        out_shape=(q, kv),
        compiler_params=pltpu.CompilerParams(vmem_limit_bytes=20 * MIB),
        cost_estimate=cost(6 * rows * out * C, (*operands, *weights, q, kv)),
        name=name,
    )(*operands, *weights)


TILE = 64


def split_rows(block):
    turned = block.shape[0] - block.shape[0] % LANES
    return turned, block.shape[0] - turned


def turned_values(blocks, width, pair):
    lanes = pl.ds(width + pair * LANES, LANES)
    values = []
    for block in blocks:
        for row in range(0, split_rows(block)[0], LANES):
            values.append(block[pl.ds(row, LANES), lanes])
    rest = []
    for block in blocks:
        start, count = split_rows(block)
        if count:
            rest.append(block[pl.ds(start, count), lanes].astype(jnp.float32))
    if rest:
        values.append(jnp.transpose(jnp.concatenate(rest, axis=0)).astype(jnp.bfloat16))
    return jnp.concatenate(values, axis=1)


def ordered_keys(blocks, pair):
    lanes = pl.ds(pair * LANES, LANES)
    keys = [block[pl.ds(0, split_rows(block)[0]), lanes] for block in blocks]
    for block in blocks:
        start, count = split_rows(block)
        if count:
            keys.append(block[pl.ds(start, count), lanes])
    return jnp.concatenate(keys, axis=0)


def partial_attention(query, keys, values, scores, weights, head, lane):
    pair, half = divmod(head, 2)
    mine = query[:, pair * LANES : (pair + 1) * LANES]
    mine = jnp.where((lane // HEAD_DIM) == half, mine, jnp.zeros_like(mine))
    scores[...] = reduce_operands(keys, mine)
    columns = scores.shape[1]
    top = None
    for start in range(0, scores.shape[0], TILE):
        tile = jnp.max(scores[pl.ds(start, TILE), :].reshape(-1, 8, columns), axis=0)
        top = tile if top is None else jnp.maximum(top, tile)
    top = jnp.max(top, axis=0, keepdims=True)
    total = None
    for start in range(0, scores.shape[0], TILE):
        weight = jnp.exp2(scores[pl.ds(start, TILE), :] - top)
        tile = jnp.sum(weight.reshape(-1, 8, columns), axis=0)
        total = tile if total is None else total + tile
        weights[pl.ds(start, TILE), :] = weight.astype(jnp.bfloat16)
    values = values[half * HEAD_DIM : (half + 1) * HEAD_DIM]
    out = jnp.dot(values, weights[...], preferred_element_type=jnp.float32)
    return out, top, jnp.sum(total, axis=0, keepdims=True)


def state_parts(state, head, width, columns):
    return (
        state[pl.ds(head * HEAD_DIM, HEAD_DIM), columns],
        state[pl.ds(width + head, 1), columns],
        state[pl.ds(width + 8 + head, 1), columns],
    )


def merged_parts(one, other):
    top = jnp.maximum(one[1], other[1])
    first, second = jnp.exp2(one[1] - top), jnp.exp2(other[1] - top)
    return first * one[0] + second * other[0], top, first * one[2] + second * other[2]


def attend_kernel(first_column, q_refs, blocks, state, out_ref, scores, weights):
    width = q_refs[0].shape[1]
    query = jnp.concatenate([ref[...] for ref in q_refs], axis=0)
    columns = query.shape[0]
    lane = lax.broadcasted_iota(jnp.int32, (columns, LANES), 1)
    out_ref[pl.ds(width, 16), :] = jnp.zeros((16, columns), jnp.float32)
    for head in range(width // HEAD_DIM):
        if head % 2 == 0:
            keys = ordered_keys(blocks, head // 2)
            values = turned_values(blocks, width, head // 2)
        part = partial_attention(
            query, keys, values, scores.at[head % 2], weights.at[head % 2], head, lane
        )
        if state is not None:
            part = merged_parts(
                part, state_parts(state, head, width, pl.ds(first_column, columns))
            )
        out_ref[pl.ds(head * HEAD_DIM, HEAD_DIM), :] = part[0]
        out_ref[pl.ds(width + head, 1), :] = part[1]
        out_ref[pl.ds(width + 8 + head, 1), :] = part[2]


def attend(queries, blocks, state, first_column, name):
    rows, width = queries[0].shape
    columns = rows * len(queries)
    extent = sum(block.shape[0] for block in blocks)
    out = jax.ShapeDtypeStruct((width + 16, columns), jnp.float32)
    operands = (*queries, *blocks) + (() if state is None else (state,))

    def kernel(*refs):
        q_refs, block_refs = refs[: len(queries)], refs[len(queries) :][: len(blocks)]
        state_ref = None if state is None else refs[len(operands) - 1]
        attend_kernel(
            first_column, q_refs, block_refs, state_ref, *refs[len(operands) :]
        )

    return pl.pallas_call(
        kernel,
        out_shape=out,
        scratch_shapes=[
            pltpu.VMEM((2, extent, columns), jnp.float32),
            pltpu.VMEM((2, extent, columns), jnp.bfloat16),
        ],
        compiler_params=pltpu.CompilerParams(vmem_limit_bytes=24 * MIB),
        cost_estimate=cost(
            4 * columns * width * extent, (*operands, out), columns * extent * width // HEAD_DIM
        ),
        name=name,
    )(*operands)


def mix_kernel(own_state, other_state, w_ref, h2_ref, own_ref, p1, p2, p3, attended):
    rows, width = h2_ref.shape
    for pair in range(width // LANES):
        halves = []
        for head in (2 * pair, 2 * pair + 1):
            out, _, total = merged_parts(
                state_parts(own_state, head, width, pl.ds(0, rows)),
                state_parts(other_state, head, width, pl.ds(0, rows)),
            )
            halves.append(out / total)
        merged = jnp.transpose(jnp.concatenate(halves, axis=0))
        attended[:, pl.ds(pair * LANES, LANES)] = merged.astype(jnp.bfloat16)

    def product(mask):
        target = jnp.bitwise_xor(lax.axis_index("head"), mask)
        columns = pl.ds(pl.multiple_of(target * width, LANES), width)
        return jnp.dot(attended[...], w_ref[:, columns], preferred_element_type=jnp.float32)

    for ref, mask in ((p3, 3), (p2, 2), (p1, 1)):
        ref[...] = product(mask).astype(jnp.bfloat16)
    own_ref[...] = product(0) + h2_ref[...]


def mix(own_state, other_state, w_out, h2):
    rows, width = h2.shape
    own = jax.ShapeDtypeStruct((rows, width), jnp.float32)
    part = jax.ShapeDtypeStruct((rows, width), jnp.bfloat16)
    operands = (own_state, other_state, w_out, h2)
    return pl.pallas_call(
        mix_kernel,
        out_shape=(own, part, part, part),
        scratch_shapes=[pltpu.VMEM((rows, width), jnp.bfloat16)],
        compiler_params=pltpu.CompilerParams(vmem_limit_bytes=16 * MIB),
        cost_estimate=cost(
            2 * rows * width * w_out.shape[1], (*operands, own, part, part, part)
        ),
        name="mix",
    )(*operands)


def exchanged(block, mask):
    count = lax.axis_size("seq")
    return lax.ppermute(block, "seq", [(i, i ^ mask) for i in range(count)])


def on_device(dna, conv_in, dilated_kernel_weight, w_query, w_key, w_value, w_out):
    count = lax.axis_size("seq")
    rows = dna.shape[0] // 2
    inner = rows // 2
    outer = rows - inner
    low = lax.ppermute(dna[-EDGE:], "seq", [(i, i + 1) for i in range(count - 1)])
    high = lax.ppermute(dna[:EDGE], "seq", [(i + 1, i) for i in range(count - 1)])
    h1_m, sent = first_conv(
        conv_middle_kernel, (dna,), conv_in, inner + EDGE, 2 * (inner + 2 * EDGE), "conv_middle"
    )
    wide_m = shared(sent)
    h1_e, sent = first_conv(
        conv_edge_kernel, (dna, low, high), conv_in, outer, 2 * (outer + 2 * EDGE), "conv_edge"
    )
    wide_e = shared(sent, (None, None, wide_m[1:2]))
    h2_m, sent = second_conv(
        dilated_middle_kernel,
        (*wide_m, after(h1_m, sent)),
        dilated_kernel_weight,
        inner,
        inner,
        inner + EDGE,
        "dilated_middle",
    )
    normed_m = shared(sent, [[part] for part in wide_e[1:]])
    h2, sent = second_conv(
        dilated_edge_kernel,
        (*wide_m, *wide_e, h1_m, h1_e, h2_m),
        dilated_kernel_weight,
        rows,
        outer,
        outer + 2 * EDGE,
        "dilated_edge",
    )
    normed_e = shared(sent, [normed_m[1:]] * 3)
    normed_m[0] = after(normed_m[0], sent)
    weights = (w_query, w_key, w_value)
    q_m, kv_m = project(project_middle_kernel, normed_m, weights, inner, "project_middle")
    x_m, y_m, d_m = (exchanged(kv_m, mask) for mask in (2, 4, 6))
    q, kv_e = project(project_edge_kernel, (*normed_e, q_m), weights, rows, "project_edge")
    q_other, x_e, y_e, d_e = exchanged(q, 1), *(exchanged(kv_e, mask) for mask in (2, 4, 6))
    state = attend((q, q_other), (kv_m, kv_e, x_m, y_m, d_m), None, 0, "attend_m")
    late = (x_e, y_e, d_e)
    state_other = attend((q_other,), late, state, rows, "attend_other")
    given = exchanged(state_other, 1)
    state_own = attend((q,), late, state, 0, "attend_own")
    own, p1, p2, p3 = mix(state_own, given, w_out, h2)
    inward = lax.ppermute(p3, "head", [(0, 1), (3, 2)])
    across = lax.ppermute(p3, "head", [(1, 2), (2, 1)])
    joined = (p2.astype(jnp.float32) + inward.astype(jnp.float32)).astype(jnp.bfloat16)
    skipped = lax.ppermute(joined, "head", [(i, i ^ 2) for i in range(4)])
    beside = lax.ppermute(after(p1, inward), "head", [(i, i ^ 1) for i in range(4)])
    total = own
    for part in (across, beside, skipped):
        total = total + part.astype(jnp.float32)
    return total.astype(jnp.bfloat16)


def solution(mesh):
    in_specs = (
        P("seq", None),
        P(None, "head", None),
        P(None, "head", None),
        P("head", None),
        P("head", None),
        P("head", None),
        P("head", None),
    )
    out_specs = P("seq", "head")
    seq, head = mesh.shape["seq"], mesh.shape["head"]
    aligned = (C // head) % 128 == 0
    body = on_device if head == 4 and seq == 8 and aligned else general_form
    return jax.shard_map(body, mesh=mesh, in_specs=in_specs, out_specs=out_specs, check_vma=False)
```

```python
import functools
import math

import jax
import jax.numpy as jnp
from jax import lax
from jax.experimental import pallas as pl
from jax.experimental.pallas import tpu as pltpu
from jax.sharding import PartitionSpec as P

C = 1536
HEAD_DIM = 64
KW = 5
DILATION_STEP = 4
EPS = 1e-06
EDGE = 16
LOG2E = math.log2(math.e)
MIB = 1 << 20
LANES = 128


def padded_2(block, sides, width):
    for axis, dim in sides:
        count = lax.axis_size(axis)
        forward = [(i, i + 1) for i in range(count - 1)]
        backward = [(target, source) for source, target in forward]
        low = lax.ppermute(
            lax.slice_in_dim(block, block.shape[dim] - width, None, axis=dim), axis, forward
        )
        high = lax.ppermute(lax.slice_in_dim(block, 0, width, axis=dim), axis, backward)
        block = jnp.concatenate([low, block, high], axis=dim)
    return block


def row_scale(hidden):
    squares = lax.psum(jnp.sum(hidden * hidden, axis=1), "head")
    return hidden * lax.rsqrt(squares / C + EPS)[:, None]


def reduce_operands(left, right):
    return lax.dot_general(
        left, right, (((1,), (1,)), ((), ())), preferred_element_type=jnp.float32
    )


def general_form(dna, conv_in, dilated_kernel_weight, w_query, w_key, w_value, w_out):
    local_row_count = dna.shape[0] // 2
    half = (KW - 1) // 2
    padded = padded_2(dna, (("seq", 0),), half)
    h1 = jnp.zeros((local_row_count, conv_in.shape[1]), jnp.float32)
    for kernel_offset in range(KW):
        rows = lax.slice(
            padded,
            (kernel_offset, 0),
            (kernel_offset + 2 * local_row_count - 1, padded.shape[1]),
            (2, 1),
        )
        h1 = h1 + reduce_operands(rows, conv_in[kernel_offset])
    gelu_output = jax.nn.gelu(row_scale(h1), approximate=True).astype(jnp.bfloat16)
    complete_output = lax.all_gather(gelu_output, "head", axis=1, tiled=True)
    broad_input = padded_2(complete_output, (("seq", 0),), DILATION_STEP)
    second_hidden = h1
    for kernel_offset in range(3):
        second_hidden = second_hidden + reduce_operands(
            broad_input[
                DILATION_STEP * kernel_offset : DILATION_STEP * kernel_offset + local_row_count
            ],
            dilated_kernel_weight[kernel_offset],
        )
    normed = row_scale(second_hidden).astype(jnp.bfloat16)
    local_width = w_query.shape[0]
    heads_here = local_width // HEAD_DIM
    piece = lax.all_gather(normed, "head", axis=1, tiled=True)
    q_acc, k_acc, v_acc = (reduce_operands(piece, w) for w in (w_query, w_key, w_value))
    query = q_acc.astype(jnp.bfloat16).reshape(local_row_count, heads_here, HEAD_DIM)
    keys = k_acc.astype(jnp.bfloat16)
    values = v_acc.astype(jnp.bfloat16)
    scale = 1.0 / math.sqrt(HEAD_DIM)
    start_state = (
        jnp.full((heads_here, local_row_count), -1e30, jnp.float32),
        jnp.zeros((heads_here, local_row_count), jnp.float32),
        jnp.zeros((local_row_count, heads_here, HEAD_DIM), jnp.float32),
    )
    key_rows = lax.all_gather(keys, "seq", axis=0, tiled=True)
    value_rows = lax.all_gather(values, "seq", axis=0, tiled=True)
    count = key_rows.shape[0]
    width = 512 if count % 512 == 0 else count
    blocks = count // width
    key_blocks = key_rows.reshape(blocks, width, heads_here, HEAD_DIM)
    value_blocks = value_rows.reshape(blocks, width, heads_here, HEAD_DIM)

    def step(state, operands):
        running, total, acc = state
        key_block, value_block = operands
        scores = (
            jnp.einsum("qhd,khd->hqk", query, key_block, preferred_element_type=jnp.float32) * scale
        )
        newest = jnp.maximum(running, jnp.max(scores, axis=2))
        factor = jnp.exp(running - newest)
        weights = jnp.exp(scores - newest[:, :, None])
        total = total * factor + jnp.sum(weights, axis=2)
        update = jnp.einsum(
            "hqk,khd->qhd",
            weights.astype(jnp.bfloat16),
            value_block,
            preferred_element_type=jnp.float32,
        )
        acc = acc * jnp.transpose(factor)[:, :, None] + update
        return ((newest, total, acc), None)

    state, _ = lax.scan(step, start_state, (key_blocks, value_blocks))
    running, total, acc = state
    attended = (
        (acc / jnp.transpose(total)[:, :, None])
        .reshape(local_row_count, local_width)
        .astype(jnp.bfloat16)
    )
    partial_out = jnp.dot(attended, w_out, preferred_element_type=jnp.float32)
    mixed = lax.psum_scatter(
        partial_out.astype(jnp.bfloat16), "head", scatter_dimension=1, tiled=True
    ).astype(jnp.float32)
    return (second_hidden + mixed).astype(jnp.bfloat16)


def nbytes(*arrays):
    return sum(math.prod(a.shape) * jnp.dtype(a.dtype).itemsize for a in arrays)


def cost(flops, arrays, transcendentals=0):
    return pl.CostEstimate(
        flops=int(flops), bytes_accessed=int(nbytes(*arrays)), transcendentals=int(transcendentals)
    )


def after(value, *others):
    return lax.optimization_barrier((value, *others))[0]


def swapped(block, mask):
    count = lax.axis_size("head")
    return lax.ppermute(block, "head", [(i, i ^ mask) for i in range(count)])


def shared(block, earlier=None):
    near = far = block
    if earlier is not None:
        near, far = after(block, earlier[1]), after(block, earlier[2])
    far = swapped(far, 2)
    near = swapped(near, 1)
    return [block, near, far]


def forwarded(parts, gate=None):
    far = parts[2] if gate is None else after(parts[2], gate)
    return [*parts, swapped(far, 1)]


def owner(mask):
    return jnp.bitwise_xor(lax.axis_index("head"), mask)


MASKS = (0, 1, 2, 3)


def store_wide(wide, start, block):
    for j in range(wide.shape[0]):
        rows = pl.ds(start, block.shape[0])
        wide[j, rows, :] = block[:, 128 * j : 128 * (j + 1)].astype(jnp.float32)


def taps_sum(wide, weight_ref, groups):
    total = None
    for tap in range(KW):
        picked = []
        for start, count in groups:
            lanes = [
                wide[j, pl.ds(start + tap, count, stride=2), :] for j in range(wide.shape[0])
            ]
            picked.append(jnp.concatenate(lanes, axis=1).astype(jnp.bfloat16))
        taken = picked[0] if len(picked) == 1 else jnp.concatenate(picked, axis=0)
        term = reduce_operands(taken, weight_ref[tap])
        total = term if total is None else total + term
    return total


FIRST = EDGE - KW // 2


def conv_middle_kernel(dna_ref, weight_ref, h1_ref, sent_ref, wide):
    store_wide(wide, 0, dna_ref[pl.ds(0, wide.shape[1]), :])
    total = taps_sum(wide, weight_ref, [(FIRST, sent_ref.shape[0])])
    h1_ref[...] = total
    sent_ref[...] = total.astype(jnp.bfloat16)


def conv_edge_kernel(dna_ref, low_ref, high_ref, weight_ref, h1_ref, sent_ref, wide):
    rows = dna_ref.shape[0]
    upper = sent_ref.shape[0] - EDGE
    first = rows - 2 * upper
    zeros = jnp.zeros((EDGE, dna_ref.shape[1]), jnp.bfloat16)
    store_wide(wide, 0, zeros)
    store_wide(wide, EDGE, low_ref[...])
    store_wide(wide, 2 * EDGE, dna_ref[pl.ds(0, 2 * EDGE), :])
    store_wide(wide, 4 * EDGE, dna_ref[pl.ds(first, rows - first), :])
    store_wide(wide, 4 * EDGE + rows - first, high_ref[...])
    store_wide(wide, 5 * EDGE + rows - first, zeros)
    total = taps_sum(wide, weight_ref, [(FIRST, EDGE), (4 * EDGE + FIRST, upper)])
    h1_ref[...] = total
    sent_ref[...] = total.astype(jnp.bfloat16)


def first_conv(kernel, operands, weight, count, deep, name):
    width, out = weight.shape[2], weight.shape[1]
    kept = jax.ShapeDtypeStruct((count, out), jnp.float32)
    sent = jax.ShapeDtypeStruct((count, out), jnp.bfloat16)
    return pl.pallas_call(
        kernel,
        out_shape=(kept, sent),
        scratch_shapes=[pltpu.VMEM((width // 128, deep, 128), jnp.float32)],
        compiler_params=pltpu.CompilerParams(vmem_limit_bytes=24 * MIB),
        cost_estimate=cost(2 * count * out * width * KW, (*operands, weight, kept, sent)),
        name=name,
    )(*operands, weight)


def inverse_norm(blocks):
    squares = None
    for block in blocks:
        term = jnp.sum(block * block, axis=1, keepdims=True)
        squares = term if squares is None else squares + term
    return lax.rsqrt(squares / C + EPS)


def wide_blocks(parts, start, count):
    return [part[pl.ds(start, count), :].astype(jnp.float32) for part in parts]


def gelu(value):
    return jax.nn.gelu(value, approximate=True)


def columns_of(mask, width):
    return pl.ds(pl.multiple_of(owner(mask) * width, LANES), width)


def dilated_middle_kernel(a0, a1, a2, a3, h1_ref, weight_ref, h2_ref, sent_ref, act):
    parts = (a0, a1, a2, a3)
    count, width = a0.shape
    rows = h2_ref.shape[0]
    blocks = wide_blocks(parts, 0, count)
    inverse = inverse_norm(blocks)
    total = h1_ref[pl.ds(8, rows), :]
    for slot, (block, mask) in enumerate(zip(blocks, MASKS)):
        act[slot] = gelu(block * inverse)
        for tap in range(3):
            taken = act[slot, pl.ds((tap + 1) * DILATION_STEP, rows), :].astype(jnp.bfloat16)
            total = total + reduce_operands(taken, weight_ref[tap, :, columns_of(mask, width)])
    h2_ref[...] = total
    sent_ref[...] = total.astype(jnp.bfloat16)


def dilated_edge_kernel(
    m0, m1, m2, m3, e0, e1, e2, e3, hm_ref, he_ref, h2m_ref, weight_ref, h2_ref, sent_ref, act
):
    middle, edge = (m0, m1, m2, m3), (e0, e1, e2, e3)
    inner, width = m0.shape
    outer = e0.shape[0]
    rows = h2_ref.shape[0]
    upper = outer - EDGE
    position = lax.axis_index("seq") * rows + lax.broadcasted_iota(jnp.int32, (outer, 1), 0)
    place = lax.broadcasted_iota(jnp.int32, (outer, 1), 0)
    position = position + jnp.where(place < EDGE, -8, inner - 8)
    inside = (position >= 0) & (position < rows * lax.axis_size("seq"))
    outer_blocks = wide_blocks(edge, 0, outer)
    outer_inverse = jnp.where(inside, inverse_norm(outer_blocks), 0.0)
    low_blocks = wide_blocks(middle, 0, EDGE)
    low_inverse = inverse_norm(low_blocks)
    high_blocks = wide_blocks(middle, inner - EDGE, EDGE)
    high_inverse = inverse_norm(high_blocks)
    last = rows - (outer - EDGE)
    total = jnp.concatenate(
        [
            he_ref[pl.ds(8, 8), :],
            hm_ref[pl.ds(0, 8), :],
            hm_ref[pl.ds(inner - 8, 8), :],
            he_ref[pl.ds(EDGE, upper - 8), :],
        ],
        axis=0,
    )
    tail = 2 * EDGE
    for slot, mask in enumerate(MASKS):
        full = gelu(outer_blocks[slot] * outer_inverse)
        act[slot, pl.ds(0, EDGE), :] = full[:EDGE]
        act[slot, pl.ds(EDGE, EDGE), :] = gelu(low_blocks[slot] * low_inverse)
        act[slot, pl.ds(tail, EDGE), :] = gelu(high_blocks[slot] * high_inverse)
        act[slot, pl.ds(tail + EDGE, upper), :] = full[EDGE:]
        for tap in range(3):
            shifted = (tap + 1) * DILATION_STEP
            taken = jnp.concatenate(
                [
                    act[slot, pl.ds(shifted, EDGE), :],
                    act[slot, pl.ds(tail + shifted, upper), :],
                ],
                axis=0,
            ).astype(jnp.bfloat16)
            total = total + reduce_operands(taken, weight_ref[tap, :, columns_of(mask, width)])
    h2_ref[pl.ds(0, EDGE), :] = total[:EDGE]
    h2_ref[pl.ds(EDGE, last - EDGE), :] = h2m_ref[...]
    h2_ref[pl.ds(last, rows - last), :] = total[EDGE:]
    sent_ref[...] = total.astype(jnp.bfloat16)


def second_conv(kernel, operands, weight, kept_rows, sent_rows, deep, name):
    out, width = weight.shape[1], operands[0].shape[1]
    kept = jax.ShapeDtypeStruct((kept_rows, out), jnp.float32)
    sent = jax.ShapeDtypeStruct((sent_rows, out), jnp.bfloat16)
    return pl.pallas_call(
        kernel,
        out_shape=(kept, sent),
        scratch_shapes=[pltpu.VMEM((4, deep, width), jnp.float32)],
        compiler_params=pltpu.CompilerParams(vmem_limit_bytes=24 * MIB),
        cost_estimate=cost(
            2 * sent_rows * out * weight.shape[2] * 3,
            (*operands, weight, kept, sent),
            deep * weight.shape[2],
        ),
        name=name,
    )(*operands, weight)


def projections(parts, wq, wk, wv, kv_ref):
    width = parts[0].shape[1]
    rows, out = parts[0].shape[0], wq.shape[0]
    blocks = [part[...].astype(jnp.float32) for part in parts]
    inverse = inverse_norm(blocks)
    normed = [(block * inverse).astype(jnp.bfloat16) for block in blocks]

    def product(weight_ref, start=0, stop=rows, weight_first=False):
        total = None
        for part, mask in zip(normed, MASKS):
            weight = weight_ref[:, columns_of(mask, width)]
            taken = part[start:stop]
            pair = (weight, taken) if weight_first else (taken, weight)
            term = reduce_operands(*pair)
            total = term if total is None else total + term
        return total

    kv_ref[:, :out] = product(wk).astype(jnp.bfloat16)
    turned = rows - rows % LANES
    value = product(wv, 0, turned, True).astype(jnp.bfloat16)
    for row in range(0, turned, LANES):
        for lane in range(0, out, LANES):
            kv_ref[pl.ds(row, LANES), pl.ds(out + lane, LANES)] = value[
                lane : lane + LANES, row : row + LANES
            ]
    if turned < rows:
        value = product(wv, turned, rows)
        kv_ref[pl.ds(turned, rows - turned), out:] = value.astype(jnp.bfloat16)
    scale = LOG2E / math.sqrt(HEAD_DIM)
    return (product(wq) * scale).astype(jnp.bfloat16)


def project_middle_kernel(a0, a1, a2, a3, wq, wk, wv, q_ref, kv_ref):
    q_ref[...] = projections((a0, a1, a2, a3), wq, wk, wv, kv_ref)


def project_edge_kernel(a0, a1, a2, a3, qm_ref, wq, wk, wv, q_ref, kv_ref):
    query = projections((a0, a1, a2, a3), wq, wk, wv, kv_ref)
    inner, rows = qm_ref.shape[0], q_ref.shape[0]
    q_ref[pl.ds(0, EDGE), :] = query[:EDGE]
    q_ref[pl.ds(EDGE, inner), :] = qm_ref[...]
    q_ref[pl.ds(EDGE + inner, rows - EDGE - inner), :] = query[EDGE:]


def project(kernel, operands, weights, q_rows, name):
    rows, out = operands[0].shape[0], weights[0].shape[0]
    q = jax.ShapeDtypeStruct((q_rows, out), jnp.bfloat16)
    kv = jax.ShapeDtypeStruct((rows, 2 * out), jnp.bfloat16)
    return pl.pallas_call(
        kernel,
        out_shape=(q, kv),
        compiler_params=pltpu.CompilerParams(vmem_limit_bytes=20 * MIB),
        cost_estimate=cost(6 * rows * out * C, (*operands, *weights, q, kv)),
        name=name,
    )(*operands, *weights)


TILE = 64


def split_rows(block):
    turned = block.shape[0] - block.shape[0] % LANES
    return turned, block.shape[0] - turned


def turned_values(blocks, width, pair):
    lanes = pl.ds(width + pair * LANES, LANES)
    values = []
    for block in blocks:
        for row in range(0, split_rows(block)[0], LANES):
            values.append(block[pl.ds(row, LANES), lanes])
    rest = []
    for block in blocks:
        start, count = split_rows(block)
        if count:
            rest.append(block[pl.ds(start, count), lanes].astype(jnp.float32))
    if rest:
        values.append(jnp.transpose(jnp.concatenate(rest, axis=0)).astype(jnp.bfloat16))
    return jnp.concatenate(values, axis=1)


def ordered_keys(blocks, pair):
    lanes = pl.ds(pair * LANES, LANES)
    keys = [block[pl.ds(0, split_rows(block)[0]), lanes] for block in blocks]
    for block in blocks:
        start, count = split_rows(block)
        if count:
            keys.append(block[pl.ds(start, count), lanes])
    return jnp.concatenate(keys, axis=0)


def partial_attention(query, keys, values, scores, weights, head, lane):
    pair, half = divmod(head, 2)
    mine = query[:, pair * LANES : (pair + 1) * LANES]
    mine = jnp.where((lane // HEAD_DIM) == half, mine, jnp.zeros_like(mine))
    scores[...] = reduce_operands(keys, mine)
    columns = scores.shape[1]
    top = None
    for start in range(0, scores.shape[0], TILE):
        tile = jnp.max(scores[pl.ds(start, TILE), :].reshape(-1, 8, columns), axis=0)
        top = tile if top is None else jnp.maximum(top, tile)
    top = jnp.max(top, axis=0, keepdims=True)
    total = None
    for start in range(0, scores.shape[0], TILE):
        weight = jnp.exp2(scores[pl.ds(start, TILE), :] - top)
        tile = jnp.sum(weight.reshape(-1, 8, columns), axis=0)
        total = tile if total is None else total + tile
        weights[pl.ds(start, TILE), :] = weight.astype(jnp.bfloat16)
    values = values[half * HEAD_DIM : (half + 1) * HEAD_DIM]
    out = jnp.dot(values, weights[...], preferred_element_type=jnp.float32)
    return out, top, jnp.sum(total, axis=0, keepdims=True)


def state_parts(state, head, width, columns):
    return (
        state[pl.ds(head * HEAD_DIM, HEAD_DIM), columns],
        state[pl.ds(width + head, 1), columns],
        state[pl.ds(width + 8 + head, 1), columns],
    )


def merged_parts(one, other):
    top = jnp.maximum(one[1], other[1])
    first, second = jnp.exp2(one[1] - top), jnp.exp2(other[1] - top)
    return first * one[0] + second * other[0], top, first * one[2] + second * other[2]


def attend_kernel(first_column, q_refs, blocks, state, out_ref, scores, weights):
    width = q_refs[0].shape[1]
    query = jnp.concatenate([ref[...] for ref in q_refs], axis=0)
    columns = query.shape[0]
    lane = lax.broadcasted_iota(jnp.int32, (columns, LANES), 1)
    out_ref[pl.ds(width, 16), :] = jnp.zeros((16, columns), jnp.float32)
    for head in range(width // HEAD_DIM):
        if head % 2 == 0:
            keys = ordered_keys(blocks, head // 2)
            values = turned_values(blocks, width, head // 2)
        part = partial_attention(
            query, keys, values, scores.at[head % 2], weights.at[head % 2], head, lane
        )
        if state is not None:
            part = merged_parts(
                part, state_parts(state, head, width, pl.ds(first_column, columns))
            )
        out_ref[pl.ds(head * HEAD_DIM, HEAD_DIM), :] = part[0]
        out_ref[pl.ds(width + head, 1), :] = part[1]
        out_ref[pl.ds(width + 8 + head, 1), :] = part[2]


def attend(queries, blocks, state, first_column, name):
    rows, width = queries[0].shape
    columns = rows * len(queries)
    extent = sum(block.shape[0] for block in blocks)
    out = jax.ShapeDtypeStruct((width + 16, columns), jnp.float32)
    operands = (*queries, *blocks) + (() if state is None else (state,))

    def kernel(*refs):
        q_refs, block_refs = refs[: len(queries)], refs[len(queries) :][: len(blocks)]
        state_ref = None if state is None else refs[len(operands) - 1]
        attend_kernel(
            first_column, q_refs, block_refs, state_ref, *refs[len(operands) :]
        )

    return pl.pallas_call(
        kernel,
        out_shape=out,
        scratch_shapes=[
            pltpu.VMEM((2, extent, columns), jnp.float32),
            pltpu.VMEM((2, extent, columns), jnp.bfloat16),
        ],
        compiler_params=pltpu.CompilerParams(vmem_limit_bytes=24 * MIB),
        cost_estimate=cost(
            4 * columns * width * extent, (*operands, out), columns * extent * width // HEAD_DIM
        ),
        name=name,
    )(*operands)


def mix_kernel(own_state, other_state, w_ref, h2_ref, own_ref, p1, p2, p3, attended):
    rows, width = h2_ref.shape
    for pair in range(width // LANES):
        halves = []
        for head in (2 * pair, 2 * pair + 1):
            out, _, total = merged_parts(
                state_parts(own_state, head, width, pl.ds(0, rows)),
                state_parts(other_state, head, width, pl.ds(0, rows)),
            )
            halves.append(out / total)
        merged = jnp.transpose(jnp.concatenate(halves, axis=0))
        attended[:, pl.ds(pair * LANES, LANES)] = merged.astype(jnp.bfloat16)

    def product(mask):
        return jnp.dot(
            attended[...], w_ref[:, columns_of(mask, width)], preferred_element_type=jnp.float32
        )

    for ref, mask in ((p3, 3), (p2, 2), (p1, 1)):
        ref[...] = product(mask).astype(jnp.bfloat16)
    own_ref[...] = product(0) + h2_ref[...]


def mix(own_state, other_state, w_out, h2):
    rows, width = h2.shape
    own = jax.ShapeDtypeStruct((rows, width), jnp.float32)
    part = jax.ShapeDtypeStruct((rows, width), jnp.bfloat16)
    operands = (own_state, other_state, w_out, h2)
    return pl.pallas_call(
        mix_kernel,
        out_shape=(own, part, part, part),
        scratch_shapes=[pltpu.VMEM((rows, width), jnp.bfloat16)],
        compiler_params=pltpu.CompilerParams(vmem_limit_bytes=16 * MIB),
        cost_estimate=cost(
            2 * rows * width * w_out.shape[1], (*operands, own, part, part, part)
        ),
        name="mix",
    )(*operands)


def exchanged(block, mask):
    count = lax.axis_size("seq")
    return lax.ppermute(block, "seq", [(i, i ^ mask) for i in range(count)])


def on_device(dna, conv_in, dilated_kernel_weight, w_query, w_key, w_value, w_out):
    count = lax.axis_size("seq")
    rows = dna.shape[0] // 2
    inner = rows // 2
    outer = rows - inner
    low = lax.ppermute(dna[-EDGE:], "seq", [(i, i + 1) for i in range(count - 1)])
    high = lax.ppermute(dna[:EDGE], "seq", [(i + 1, i) for i in range(count - 1)])
    h1_m, sent = first_conv(
        conv_middle_kernel, (dna,), conv_in, inner + EDGE, 2 * (inner + 2 * EDGE), "conv_middle"
    )
    wide_m = forwarded(shared(sent))
    h1_e, sent = first_conv(
        conv_edge_kernel, (dna, after(low, wide_m[2]), high), conv_in, outer, 2 * (outer + 2 * EDGE), "conv_edge"
    )
    wide_e = shared(sent)
    h2_m, sent = second_conv(
        dilated_middle_kernel,
        (*wide_m, after(h1_m, sent)),
        dilated_kernel_weight,
        inner,
        inner,
        inner + EDGE,
        "dilated_middle",
    )
    normed_m = forwarded(shared(sent, wide_e))
    wide_e = forwarded(wide_e, sent)
    h2, sent = second_conv(
        dilated_edge_kernel,
        (*wide_m, *wide_e, h1_m, h1_e, h2_m),
        dilated_kernel_weight,
        rows,
        outer,
        outer + 2 * EDGE,
        "dilated_edge",
    )
    normed_e = shared(sent, normed_m)
    normed_m[0] = after(normed_m[0], sent)
    weights = (w_query, w_key, w_value)
    q_m, kv_m = project(project_middle_kernel, normed_m, weights, inner, "project_middle")
    x_m, y_m, d_m = (exchanged(kv_m, mask) for mask in (2, 4, 6))
    normed_e = forwarded(normed_e, kv_m)
    q, kv_e = project(project_edge_kernel, (*normed_e, q_m), weights, rows, "project_edge")
    q_other, x_e, y_e, d_e = exchanged(q, 1), *(exchanged(kv_e, mask) for mask in (2, 4, 6))
    state = attend((q, q_other), (kv_m, kv_e, x_m, y_m, d_m), None, 0, "attend_m")
    late = (x_e, y_e, d_e)
    state_other = attend((q_other,), late, state, rows, "attend_other")
    given = exchanged(state_other, 1)
    state_own = attend((q,), late, state, 0, "attend_own")
    own, p1, p2, p3 = mix(state_own, given, w_out, h2)
    inward = swapped(p3, 1)
    joined = (p2.astype(jnp.float32) + inward.astype(jnp.float32)).astype(jnp.bfloat16)
    total = own
    for part in (swapped(after(p1, joined), 1), swapped(joined, 2)):
        total = total + part.astype(jnp.float32)
    return total.astype(jnp.bfloat16)


def solution(mesh):
    in_specs = (
        P("seq", None),
        P(None, "head", None),
        P(None, "head", None),
        P("head", None),
        P("head", None),
        P("head", None),
        P("head", None),
    )
    out_specs = P("seq", "head")
    seq, head = mesh.shape["seq"], mesh.shape["head"]
    aligned = (C // head) % 128 == 0
    body = on_device if head == 4 and seq == 8 and aligned else general_form
    return jax.shard_map(body, mesh=mesh, in_specs=in_specs, out_specs=out_specs, check_vma=False)
```

```python
import functools
import math

import jax
import jax.numpy as jnp
from jax import lax
from jax.experimental import pallas as pl
from jax.experimental.pallas import tpu as pltpu
from jax.sharding import PartitionSpec as P

C = 1536
HEAD_DIM = 64
KW = 5
DILATION_STEP = 4
EPS = 1e-06
EDGE = 16
LOG2E = math.log2(math.e)
MIB = 1 << 20
LANES = 128


def padded_2(block, sides, width):
    for axis, dim in sides:
        count = lax.axis_size(axis)
        forward = [(i, i + 1) for i in range(count - 1)]
        backward = [(target, source) for source, target in forward]
        low = lax.ppermute(
            lax.slice_in_dim(block, block.shape[dim] - width, None, axis=dim), axis, forward
        )
        high = lax.ppermute(lax.slice_in_dim(block, 0, width, axis=dim), axis, backward)
        block = jnp.concatenate([low, block, high], axis=dim)
    return block


def row_scale(hidden):
    squares = lax.psum(jnp.sum(hidden * hidden, axis=1), "head")
    return hidden * lax.rsqrt(squares / C + EPS)[:, None]


def reduce_operands(left, right):
    return lax.dot_general(
        left, right, (((1,), (1,)), ((), ())), preferred_element_type=jnp.float32
    )


def general_form(dna, conv_in, dilated_kernel_weight, w_query, w_key, w_value, w_out):
    local_row_count = dna.shape[0] // 2
    half = (KW - 1) // 2
    padded = padded_2(dna, (("seq", 0),), half)
    h1 = jnp.zeros((local_row_count, conv_in.shape[1]), jnp.float32)
    for kernel_offset in range(KW):
        rows = lax.slice(
            padded,
            (kernel_offset, 0),
            (kernel_offset + 2 * local_row_count - 1, padded.shape[1]),
            (2, 1),
        )
        h1 = h1 + reduce_operands(rows, conv_in[kernel_offset])
    gelu_output = jax.nn.gelu(row_scale(h1), approximate=True).astype(jnp.bfloat16)
    complete_output = lax.all_gather(gelu_output, "head", axis=1, tiled=True)
    broad_input = padded_2(complete_output, (("seq", 0),), DILATION_STEP)
    second_hidden = h1
    for kernel_offset in range(3):
        second_hidden = second_hidden + reduce_operands(
            broad_input[
                DILATION_STEP * kernel_offset : DILATION_STEP * kernel_offset + local_row_count
            ],
            dilated_kernel_weight[kernel_offset],
        )
    normed = row_scale(second_hidden).astype(jnp.bfloat16)
    local_width = w_query.shape[0]
    heads_here = local_width // HEAD_DIM
    piece = lax.all_gather(normed, "head", axis=1, tiled=True)
    q_acc, k_acc, v_acc = (reduce_operands(piece, w) for w in (w_query, w_key, w_value))
    query = q_acc.astype(jnp.bfloat16).reshape(local_row_count, heads_here, HEAD_DIM)
    keys = k_acc.astype(jnp.bfloat16)
    values = v_acc.astype(jnp.bfloat16)
    scale = 1.0 / math.sqrt(HEAD_DIM)
    start_state = (
        jnp.full((heads_here, local_row_count), -1e30, jnp.float32),
        jnp.zeros((heads_here, local_row_count), jnp.float32),
        jnp.zeros((local_row_count, heads_here, HEAD_DIM), jnp.float32),
    )
    key_rows = lax.all_gather(keys, "seq", axis=0, tiled=True)
    value_rows = lax.all_gather(values, "seq", axis=0, tiled=True)
    count = key_rows.shape[0]
    width = 512 if count % 512 == 0 else count
    blocks = count // width
    key_blocks = key_rows.reshape(blocks, width, heads_here, HEAD_DIM)
    value_blocks = value_rows.reshape(blocks, width, heads_here, HEAD_DIM)

    def step(state, operands):
        running, total, acc = state
        key_block, value_block = operands
        scores = (
            jnp.einsum("qhd,khd->hqk", query, key_block, preferred_element_type=jnp.float32) * scale
        )
        newest = jnp.maximum(running, jnp.max(scores, axis=2))
        factor = jnp.exp(running - newest)
        weights = jnp.exp(scores - newest[:, :, None])
        total = total * factor + jnp.sum(weights, axis=2)
        update = jnp.einsum(
            "hqk,khd->qhd",
            weights.astype(jnp.bfloat16),
            value_block,
            preferred_element_type=jnp.float32,
        )
        acc = acc * jnp.transpose(factor)[:, :, None] + update
        return ((newest, total, acc), None)

    state, _ = lax.scan(step, start_state, (key_blocks, value_blocks))
    running, total, acc = state
    attended = (
        (acc / jnp.transpose(total)[:, :, None])
        .reshape(local_row_count, local_width)
        .astype(jnp.bfloat16)
    )
    partial_out = jnp.dot(attended, w_out, preferred_element_type=jnp.float32)
    mixed = lax.psum_scatter(
        partial_out.astype(jnp.bfloat16), "head", scatter_dimension=1, tiled=True
    ).astype(jnp.float32)
    return (second_hidden + mixed).astype(jnp.bfloat16)


def nbytes(*arrays):
    return sum(math.prod(a.shape) * jnp.dtype(a.dtype).itemsize for a in arrays)


def cost(flops, arrays, transcendentals=0):
    return pl.CostEstimate(
        flops=int(flops), bytes_accessed=int(nbytes(*arrays)), transcendentals=int(transcendentals)
    )


def after(value, *others):
    return lax.optimization_barrier((value, *others))[0]


def swapped(block, mask):
    count = lax.axis_size("head")
    return lax.ppermute(block, "head", [(i, i ^ mask) for i in range(count)])


def shared(block, earlier=None):
    near = far = block
    if earlier is not None:
        near, far = after(block, earlier[1]), after(block, earlier[2])
    far = swapped(far, 2)
    near = swapped(near, 1)
    return [block, near, far]


def forwarded(parts, gate=None):
    far = parts[2] if gate is None else after(parts[2], gate)
    return [*parts, swapped(far, 1)]


def owner(mask):
    return jnp.bitwise_xor(lax.axis_index("head"), mask)


MASKS = (0, 1, 2, 3)


def store_wide(wide, start, block):
    for j in range(wide.shape[0]):
        rows = pl.ds(start, block.shape[0])
        wide[j, rows, :] = block[:, 128 * j : 128 * (j + 1)].astype(jnp.float32)


def taps_sum(wide, weight_ref, groups):
    total = None
    for tap in range(KW):
        picked = []
        for start, count in groups:
            lanes = [
                wide[j, pl.ds(start + tap, count, stride=2), :] for j in range(wide.shape[0])
            ]
            picked.append(jnp.concatenate(lanes, axis=1).astype(jnp.bfloat16))
        taken = picked[0] if len(picked) == 1 else jnp.concatenate(picked, axis=0)
        term = reduce_operands(taken, weight_ref[tap])
        total = term if total is None else total + term
    return total


FIRST = EDGE - KW // 2


def conv_middle_kernel(dna_ref, weight_ref, h1_ref, sent_ref, wide):
    store_wide(wide, 0, dna_ref[pl.ds(0, wide.shape[1]), :])
    total = taps_sum(wide, weight_ref, [(FIRST, sent_ref.shape[0])])
    h1_ref[...] = total
    sent_ref[...] = total.astype(jnp.bfloat16)


def conv_edge_kernel(dna_ref, low_ref, high_ref, weight_ref, h1_ref, sent_ref, wide):
    rows = dna_ref.shape[0]
    upper = sent_ref.shape[0] - EDGE
    first = rows - 2 * upper
    zeros = jnp.zeros((EDGE, dna_ref.shape[1]), jnp.bfloat16)
    store_wide(wide, 0, zeros)
    store_wide(wide, EDGE, low_ref[...])
    store_wide(wide, 2 * EDGE, dna_ref[pl.ds(0, 2 * EDGE), :])
    store_wide(wide, 4 * EDGE, dna_ref[pl.ds(first, rows - first), :])
    store_wide(wide, 4 * EDGE + rows - first, high_ref[...])
    store_wide(wide, 5 * EDGE + rows - first, zeros)
    total = taps_sum(wide, weight_ref, [(FIRST, EDGE), (4 * EDGE + FIRST, upper)])
    h1_ref[...] = total
    sent_ref[...] = total.astype(jnp.bfloat16)


def first_conv(kernel, operands, weight, count, deep, name):
    width, out = weight.shape[2], weight.shape[1]
    kept = jax.ShapeDtypeStruct((count, out), jnp.float32)
    sent = jax.ShapeDtypeStruct((count, out), jnp.bfloat16)
    return pl.pallas_call(
        kernel,
        out_shape=(kept, sent),
        scratch_shapes=[pltpu.VMEM((width // 128, deep, 128), jnp.float32)],
        compiler_params=pltpu.CompilerParams(vmem_limit_bytes=24 * MIB),
        cost_estimate=cost(2 * count * out * width * KW, (*operands, weight, kept, sent)),
        name=name,
    )(*operands, weight)


def inverse_norm(blocks):
    squares = None
    for block in blocks:
        term = jnp.sum(block * block, axis=1, keepdims=True)
        squares = term if squares is None else squares + term
    return lax.rsqrt(squares / C + EPS)


def wide_blocks(parts, start, count):
    return [part[pl.ds(start, count), :].astype(jnp.float32) for part in parts]


def gelu(value):
    return jax.nn.gelu(value, approximate=True)


def columns_of(mask, width):
    return pl.ds(pl.multiple_of(owner(mask) * width, LANES), width)


def dilated_middle_kernel(a0, a1, a2, a3, h1_ref, weight_ref, h2_ref, sent_ref, act):
    parts = (a0, a1, a2, a3)
    count, width = a0.shape
    rows = h2_ref.shape[0]
    blocks = wide_blocks(parts, 0, count)
    inverse = inverse_norm(blocks)
    total = h1_ref[pl.ds(8, rows), :]
    for slot, (block, mask) in enumerate(zip(blocks, MASKS)):
        act[slot] = gelu(block * inverse)
        for tap in range(3):
            taken = act[slot, pl.ds((tap + 1) * DILATION_STEP, rows), :].astype(jnp.bfloat16)
            total = total + reduce_operands(taken, weight_ref[tap, :, columns_of(mask, width)])
    h2_ref[...] = total
    sent_ref[...] = total.astype(jnp.bfloat16)


def dilated_edge_kernel(
    m0, m1, m2, m3, e0, e1, e2, e3, hm_ref, he_ref, h2m_ref, weight_ref, h2_ref, sent_ref, act
):
    middle, edge = (m0, m1, m2, m3), (e0, e1, e2, e3)
    inner, width = m0.shape
    outer = e0.shape[0]
    rows = h2_ref.shape[0]
    upper = outer - EDGE
    position = lax.axis_index("seq") * rows + lax.broadcasted_iota(jnp.int32, (outer, 1), 0)
    place = lax.broadcasted_iota(jnp.int32, (outer, 1), 0)
    position = position + jnp.where(place < EDGE, -8, inner - 8)
    inside = (position >= 0) & (position < rows * lax.axis_size("seq"))
    outer_blocks = wide_blocks(edge, 0, outer)
    outer_inverse = jnp.where(inside, inverse_norm(outer_blocks), 0.0)
    low_blocks = wide_blocks(middle, 0, EDGE)
    low_inverse = inverse_norm(low_blocks)
    high_blocks = wide_blocks(middle, inner - EDGE, EDGE)
    high_inverse = inverse_norm(high_blocks)
    last = rows - (outer - EDGE)
    total = jnp.concatenate(
        [
            he_ref[pl.ds(8, 8), :],
            hm_ref[pl.ds(0, 8), :],
            hm_ref[pl.ds(inner - 8, 8), :],
            he_ref[pl.ds(EDGE, upper - 8), :],
        ],
        axis=0,
    )
    tail = 2 * EDGE
    for slot, mask in enumerate(MASKS):
        full = gelu(outer_blocks[slot] * outer_inverse)
        act[slot, pl.ds(0, EDGE), :] = full[:EDGE]
        act[slot, pl.ds(EDGE, EDGE), :] = gelu(low_blocks[slot] * low_inverse)
        act[slot, pl.ds(tail, EDGE), :] = gelu(high_blocks[slot] * high_inverse)
        act[slot, pl.ds(tail + EDGE, upper), :] = full[EDGE:]
        for tap in range(3):
            shifted = (tap + 1) * DILATION_STEP
            taken = jnp.concatenate(
                [
                    act[slot, pl.ds(shifted, EDGE), :],
                    act[slot, pl.ds(tail + shifted, upper), :],
                ],
                axis=0,
            ).astype(jnp.bfloat16)
            total = total + reduce_operands(taken, weight_ref[tap, :, columns_of(mask, width)])
    h2_ref[pl.ds(0, EDGE), :] = total[:EDGE]
    h2_ref[pl.ds(EDGE, last - EDGE), :] = h2m_ref[...]
    h2_ref[pl.ds(last, rows - last), :] = total[EDGE:]
    sent_ref[...] = total.astype(jnp.bfloat16)


def second_conv(kernel, operands, weight, kept_rows, sent_rows, deep, name):
    out, width = weight.shape[1], operands[0].shape[1]
    kept = jax.ShapeDtypeStruct((kept_rows, out), jnp.float32)
    sent = jax.ShapeDtypeStruct((sent_rows, out), jnp.bfloat16)
    return pl.pallas_call(
        kernel,
        out_shape=(kept, sent),
        scratch_shapes=[pltpu.VMEM((4, deep, width), jnp.float32)],
        compiler_params=pltpu.CompilerParams(vmem_limit_bytes=24 * MIB),
        cost_estimate=cost(
            2 * sent_rows * out * weight.shape[2] * 3,
            (*operands, weight, kept, sent),
            deep * weight.shape[2],
        ),
        name=name,
    )(*operands, weight)


def projections(parts, wq, wk, wv, kv_ref):
    width = parts[0].shape[1]
    rows, out = parts[0].shape[0], wq.shape[0]
    blocks = [part[...].astype(jnp.float32) for part in parts]
    inverse = inverse_norm(blocks)
    normed = [(block * inverse).astype(jnp.bfloat16) for block in blocks]

    def product(weight_ref, start=0, stop=rows, weight_first=False):
        total = None
        for part, mask in zip(normed, MASKS):
            weight = weight_ref[:, columns_of(mask, width)]
            taken = part[start:stop]
            pair = (weight, taken) if weight_first else (taken, weight)
            term = reduce_operands(*pair)
            total = term if total is None else total + term
        return total

    kv_ref[:, :out] = product(wk).astype(jnp.bfloat16)
    turned = rows - rows % LANES
    value = product(wv, 0, turned, True).astype(jnp.bfloat16)
    for row in range(0, turned, LANES):
        for lane in range(0, out, LANES):
            kv_ref[pl.ds(row, LANES), pl.ds(out + lane, LANES)] = value[
                lane : lane + LANES, row : row + LANES
            ]
    if turned < rows:
        value = product(wv, turned, rows)
        kv_ref[pl.ds(turned, rows - turned), out:] = value.astype(jnp.bfloat16)
    scale = LOG2E / math.sqrt(HEAD_DIM)
    return (product(wq) * scale).astype(jnp.bfloat16)


def project_middle_kernel(a0, a1, a2, a3, wq, wk, wv, q_ref, kv_ref):
    q_ref[...] = projections((a0, a1, a2, a3), wq, wk, wv, kv_ref)


def project_edge_kernel(a0, a1, a2, a3, qm_ref, wq, wk, wv, q_ref, kv_ref):
    query = projections((a0, a1, a2, a3), wq, wk, wv, kv_ref)
    inner, rows = qm_ref.shape[0], q_ref.shape[0]
    q_ref[pl.ds(0, EDGE), :] = query[:EDGE]
    q_ref[pl.ds(EDGE, inner), :] = qm_ref[...]
    q_ref[pl.ds(EDGE + inner, rows - EDGE - inner), :] = query[EDGE:]


def project(kernel, operands, weights, q_rows, name):
    rows, out = operands[0].shape[0], weights[0].shape[0]
    q = jax.ShapeDtypeStruct((q_rows, out), jnp.bfloat16)
    kv = jax.ShapeDtypeStruct((rows, 2 * out), jnp.bfloat16)
    return pl.pallas_call(
        kernel,
        out_shape=(q, kv),
        compiler_params=pltpu.CompilerParams(vmem_limit_bytes=20 * MIB),
        cost_estimate=cost(6 * rows * out * C, (*operands, *weights, q, kv)),
        name=name,
    )(*operands, *weights)


TILE = 64


def split_rows(block):
    turned = block.shape[0] - block.shape[0] % LANES
    return turned, block.shape[0] - turned


def turned_values(blocks, width, pair):
    lanes = pl.ds(width + pair * LANES, LANES)
    values = []
    for block in blocks:
        for row in range(0, split_rows(block)[0], LANES):
            values.append(block[pl.ds(row, LANES), lanes])
    rest = []
    for block in blocks:
        start, count = split_rows(block)
        if count:
            rest.append(block[pl.ds(start, count), lanes].astype(jnp.float32))
    if rest:
        values.append(jnp.transpose(jnp.concatenate(rest, axis=0)).astype(jnp.bfloat16))
    return jnp.concatenate(values, axis=1)


def ordered_keys(blocks, pair):
    lanes = pl.ds(pair * LANES, LANES)
    keys = [block[pl.ds(0, split_rows(block)[0]), lanes] for block in blocks]
    for block in blocks:
        start, count = split_rows(block)
        if count:
            keys.append(block[pl.ds(start, count), lanes])
    return jnp.concatenate(keys, axis=0)


def partial_attention(query, keys, values, scores, weights, head, lane):
    pair, half = divmod(head, 2)
    mine = query[:, pair * LANES : (pair + 1) * LANES]
    mine = jnp.where((lane // HEAD_DIM) == half, mine, jnp.zeros_like(mine))
    scores[...] = reduce_operands(keys, mine)
    columns = scores.shape[1]
    top = None
    for start in range(0, scores.shape[0], TILE):
        tile = jnp.max(scores[pl.ds(start, TILE), :].reshape(-1, 8, columns), axis=0)
        top = tile if top is None else jnp.maximum(top, tile)
    top = jnp.max(top, axis=0, keepdims=True)
    total = None
    for start in range(0, scores.shape[0], TILE):
        weight = jnp.exp2(scores[pl.ds(start, TILE), :] - top)
        tile = jnp.sum(weight.reshape(-1, 8, columns), axis=0)
        total = tile if total is None else total + tile
        weights[pl.ds(start, TILE), :] = weight.astype(jnp.bfloat16)
    values = values[half * HEAD_DIM : (half + 1) * HEAD_DIM]
    out = jnp.dot(values, weights[...], preferred_element_type=jnp.float32)
    return out, top, jnp.sum(total, axis=0, keepdims=True)


def state_parts(state, head, width, columns):
    return (
        state[pl.ds(head * HEAD_DIM, HEAD_DIM), columns],
        state[pl.ds(width + head, 1), columns],
        state[pl.ds(width + 8 + head, 1), columns],
    )


def merged_parts(one, other):
    top = jnp.maximum(one[1], other[1])
    first, second = jnp.exp2(one[1] - top), jnp.exp2(other[1] - top)
    return first * one[0] + second * other[0], top, first * one[2] + second * other[2]


def attend_kernel(first_column, q_refs, blocks, state, out_ref, scores, weights):
    width = q_refs[0].shape[1]
    query = jnp.concatenate([ref[...] for ref in q_refs], axis=0)
    columns = query.shape[0]
    lane = lax.broadcasted_iota(jnp.int32, (columns, LANES), 1)
    out_ref[pl.ds(width, 16), :] = jnp.zeros((16, columns), jnp.float32)
    for head in range(width // HEAD_DIM):
        if head % 2 == 0:
            keys = ordered_keys(blocks, head // 2)
            values = turned_values(blocks, width, head // 2)
        part = partial_attention(
            query, keys, values, scores.at[head % 2], weights.at[head % 2], head, lane
        )
        if state is not None:
            part = merged_parts(
                part, state_parts(state, head, width, pl.ds(first_column, columns))
            )
        out_ref[pl.ds(head * HEAD_DIM, HEAD_DIM), :] = part[0]
        out_ref[pl.ds(width + head, 1), :] = part[1]
        out_ref[pl.ds(width + 8 + head, 1), :] = part[2]


def attend(queries, blocks, state, first_column, name):
    rows, width = queries[0].shape
    columns = rows * len(queries)
    extent = sum(block.shape[0] for block in blocks)
    out = jax.ShapeDtypeStruct((width + 16, columns), jnp.float32)
    operands = (*queries, *blocks) + (() if state is None else (state,))

    def kernel(*refs):
        q_refs, block_refs = refs[: len(queries)], refs[len(queries) :][: len(blocks)]
        state_ref = None if state is None else refs[len(operands) - 1]
        attend_kernel(
            first_column, q_refs, block_refs, state_ref, *refs[len(operands) :]
        )

    return pl.pallas_call(
        kernel,
        out_shape=out,
        scratch_shapes=[
            pltpu.VMEM((2, extent, columns), jnp.float32),
            pltpu.VMEM((2, extent, columns), jnp.bfloat16),
        ],
        compiler_params=pltpu.CompilerParams(vmem_limit_bytes=24 * MIB),
        cost_estimate=cost(
            4 * columns * width * extent, (*operands, out), columns * extent * width // HEAD_DIM
        ),
        name=name,
    )(*operands)


def mix_kernel(own_state, other_state, w_ref, h2_ref, own_ref, p1, p2, p3, attended):
    rows, width = h2_ref.shape
    for pair in range(width // LANES):
        halves = []
        for head in (2 * pair, 2 * pair + 1):
            out, _, total = merged_parts(
                state_parts(own_state, head, width, pl.ds(0, rows)),
                state_parts(other_state, head, width, pl.ds(0, rows)),
            )
            halves.append(out / total)
        merged = jnp.transpose(jnp.concatenate(halves, axis=0))
        attended[:, pl.ds(pair * LANES, LANES)] = merged.astype(jnp.bfloat16)

    def product(mask):
        return jnp.dot(
            attended[...], w_ref[:, columns_of(mask, width)], preferred_element_type=jnp.float32
        )

    for ref, mask in ((p3, 3), (p2, 2), (p1, 1)):
        ref[...] = product(mask).astype(jnp.bfloat16)
    own_ref[...] = product(0) + h2_ref[...]


def mix(own_state, other_state, w_out, h2):
    rows, width = h2.shape
    own = jax.ShapeDtypeStruct((rows, width), jnp.float32)
    part = jax.ShapeDtypeStruct((rows, width), jnp.bfloat16)
    operands = (own_state, other_state, w_out, h2)
    return pl.pallas_call(
        mix_kernel,
        out_shape=(own, part, part, part),
        scratch_shapes=[pltpu.VMEM((rows, width), jnp.bfloat16)],
        compiler_params=pltpu.CompilerParams(vmem_limit_bytes=16 * MIB),
        cost_estimate=cost(
            2 * rows * width * w_out.shape[1], (*operands, own, part, part, part)
        ),
        name="mix",
    )(*operands)


def exchanged(block, mask):
    count = lax.axis_size("seq")
    return lax.ppermute(block, "seq", [(i, i ^ mask) for i in range(count)])


def on_device(dna, conv_in, dilated_kernel_weight, w_query, w_key, w_value, w_out):
    count = lax.axis_size("seq")
    rows = dna.shape[0] // 2
    inner = rows // 2
    outer = rows - inner
    low = lax.ppermute(dna[-EDGE:], "seq", [(i, i + 1) for i in range(count - 1)])
    high = lax.ppermute(dna[:EDGE], "seq", [(i + 1, i) for i in range(count - 1)])
    h1_m, sent = first_conv(
        conv_middle_kernel, (dna,), conv_in, inner + EDGE, 2 * (inner + 2 * EDGE), "conv_middle"
    )
    wide_m = forwarded(shared(sent))
    h1_e, sent = first_conv(
        conv_edge_kernel, (dna, after(low, *wide_m[1:3]), high), conv_in, outer, 2 * (outer + 2 * EDGE), "conv_edge"
    )
    wide_e = shared(sent)
    h2_m, sent = second_conv(
        dilated_middle_kernel,
        (*wide_m, after(h1_m, sent)),
        dilated_kernel_weight,
        inner,
        inner,
        inner + EDGE,
        "dilated_middle",
    )
    normed_m = shared(sent, wide_e)
    wide_e = forwarded(wide_e, sent)
    h2, sent = second_conv(
        dilated_edge_kernel,
        (*wide_m, *wide_e, h1_m, h1_e, h2_m),
        dilated_kernel_weight,
        rows,
        outer,
        outer + 2 * EDGE,
        "dilated_edge",
    )
    normed_e = shared(sent, normed_m)
    normed_m = forwarded(normed_m, sent)
    weights = (w_query, w_key, w_value)
    q_m, kv_m = project(project_middle_kernel, normed_m, weights, inner, "project_middle")
    x_m, y_m, d_m = (exchanged(kv_m, mask) for mask in (2, 4, 6))
    normed_e = forwarded(normed_e, kv_m)
    q, kv_e = project(project_edge_kernel, (*normed_e, q_m), weights, rows, "project_edge")
    q_other, x_e, y_e, d_e = exchanged(q, 1), *(exchanged(kv_e, mask) for mask in (2, 4, 6))
    state = attend((q, q_other), (kv_m, kv_e, x_m, y_m, d_m), None, 0, "attend_m")
    late = (x_e, y_e, d_e)
    state_other = attend((q_other,), late, state, rows, "attend_other")
    given = exchanged(state_other, 1)
    state_own = attend((q,), late, state, 0, "attend_own")
    own, p1, p2, p3 = mix(state_own, given, w_out, h2)
    inward = swapped(p3, 1)
    joined = (p2.astype(jnp.float32) + inward.astype(jnp.float32)).astype(jnp.bfloat16)
    total = own
    for part in (swapped(after(p1, joined), 1), swapped(joined, 2)):
        total = total + part.astype(jnp.float32)
    return total.astype(jnp.bfloat16)


def solution(mesh):
    in_specs = (
        P("seq", None),
        P(None, "head", None),
        P(None, "head", None),
        P("head", None),
        P("head", None),
        P("head", None),
        P("head", None),
    )
    out_specs = P("seq", "head")
    seq, head = mesh.shape["seq"], mesh.shape["head"]
    aligned = (C // head) % 128 == 0
    body = on_device if head == 4 and seq == 8 and aligned else general_form
    return jax.shard_map(body, mesh=mesh, in_specs=in_specs, out_specs=out_specs, check_vma=False)
```

```python
import functools
import math

import jax
import jax.numpy as jnp
from jax import lax
from jax.experimental import pallas as pl
from jax.experimental.pallas import tpu as pltpu
from jax.sharding import PartitionSpec as P

C = 1536
HEAD_DIM = 64
KW = 5
DILATION_STEP = 4
EPS = 1e-06
EDGE = 16
LOG2E = math.log2(math.e)
MIB = 1 << 20
LANES = 128


def padded_2(block, sides, width):
    for axis, dim in sides:
        count = lax.axis_size(axis)
        forward = [(i, i + 1) for i in range(count - 1)]
        backward = [(target, source) for source, target in forward]
        low = lax.ppermute(
            lax.slice_in_dim(block, block.shape[dim] - width, None, axis=dim), axis, forward
        )
        high = lax.ppermute(lax.slice_in_dim(block, 0, width, axis=dim), axis, backward)
        block = jnp.concatenate([low, block, high], axis=dim)
    return block


def row_scale(hidden):
    squares = lax.psum(jnp.sum(hidden * hidden, axis=1), "head")
    return hidden * lax.rsqrt(squares / C + EPS)[:, None]


def reduce_operands(left, right):
    return lax.dot_general(
        left, right, (((1,), (1,)), ((), ())), preferred_element_type=jnp.float32
    )


def general_form(dna, conv_in, dilated_kernel_weight, w_query, w_key, w_value, w_out):
    local_row_count = dna.shape[0] // 2
    half = (KW - 1) // 2
    padded = padded_2(dna, (("seq", 0),), half)
    h1 = jnp.zeros((local_row_count, conv_in.shape[1]), jnp.float32)
    for kernel_offset in range(KW):
        rows = lax.slice(
            padded,
            (kernel_offset, 0),
            (kernel_offset + 2 * local_row_count - 1, padded.shape[1]),
            (2, 1),
        )
        h1 = h1 + reduce_operands(rows, conv_in[kernel_offset])
    gelu_output = jax.nn.gelu(row_scale(h1), approximate=True).astype(jnp.bfloat16)
    complete_output = lax.all_gather(gelu_output, "head", axis=1, tiled=True)
    broad_input = padded_2(complete_output, (("seq", 0),), DILATION_STEP)
    second_hidden = h1
    for kernel_offset in range(3):
        second_hidden = second_hidden + reduce_operands(
            broad_input[
                DILATION_STEP * kernel_offset : DILATION_STEP * kernel_offset + local_row_count
            ],
            dilated_kernel_weight[kernel_offset],
        )
    normed = row_scale(second_hidden).astype(jnp.bfloat16)
    local_width = w_query.shape[0]
    heads_here = local_width // HEAD_DIM
    piece = lax.all_gather(normed, "head", axis=1, tiled=True)
    q_acc, k_acc, v_acc = (reduce_operands(piece, w) for w in (w_query, w_key, w_value))
    query = q_acc.astype(jnp.bfloat16).reshape(local_row_count, heads_here, HEAD_DIM)
    keys = k_acc.astype(jnp.bfloat16)
    values = v_acc.astype(jnp.bfloat16)
    scale = 1.0 / math.sqrt(HEAD_DIM)
    start_state = (
        jnp.full((heads_here, local_row_count), -1e30, jnp.float32),
        jnp.zeros((heads_here, local_row_count), jnp.float32),
        jnp.zeros((local_row_count, heads_here, HEAD_DIM), jnp.float32),
    )
    key_rows = lax.all_gather(keys, "seq", axis=0, tiled=True)
    value_rows = lax.all_gather(values, "seq", axis=0, tiled=True)
    count = key_rows.shape[0]
    width = 512 if count % 512 == 0 else count
    blocks = count // width
    key_blocks = key_rows.reshape(blocks, width, heads_here, HEAD_DIM)
    value_blocks = value_rows.reshape(blocks, width, heads_here, HEAD_DIM)

    def step(state, operands):
        running, total, acc = state
        key_block, value_block = operands
        scores = (
            jnp.einsum("qhd,khd->hqk", query, key_block, preferred_element_type=jnp.float32) * scale
        )
        newest = jnp.maximum(running, jnp.max(scores, axis=2))
        factor = jnp.exp(running - newest)
        weights = jnp.exp(scores - newest[:, :, None])
        total = total * factor + jnp.sum(weights, axis=2)
        update = jnp.einsum(
            "hqk,khd->qhd",
            weights.astype(jnp.bfloat16),
            value_block,
            preferred_element_type=jnp.float32,
        )
        acc = acc * jnp.transpose(factor)[:, :, None] + update
        return ((newest, total, acc), None)

    state, _ = lax.scan(step, start_state, (key_blocks, value_blocks))
    running, total, acc = state
    attended = (
        (acc / jnp.transpose(total)[:, :, None])
        .reshape(local_row_count, local_width)
        .astype(jnp.bfloat16)
    )
    partial_out = jnp.dot(attended, w_out, preferred_element_type=jnp.float32)
    mixed = lax.psum_scatter(
        partial_out.astype(jnp.bfloat16), "head", scatter_dimension=1, tiled=True
    ).astype(jnp.float32)
    return (second_hidden + mixed).astype(jnp.bfloat16)


def nbytes(*arrays):
    return sum(math.prod(a.shape) * jnp.dtype(a.dtype).itemsize for a in arrays)


def cost(flops, arrays, transcendentals=0):
    return pl.CostEstimate(
        flops=int(flops), bytes_accessed=int(nbytes(*arrays)), transcendentals=int(transcendentals)
    )


def after(value, *others):
    return lax.optimization_barrier((value, *others))[0]


def swapped(block, mask):
    count = lax.axis_size("head")
    return lax.ppermute(block, "head", [(i, i ^ mask) for i in range(count)])


def shared(block, earlier=None):
    near = far = block
    if earlier is not None:
        near, far = after(block, earlier[1]), after(block, earlier[2])
    far = swapped(far, 2)
    near = swapped(near, 1)
    return [block, near, far]


def forwarded(parts, gate=None):
    far = parts[2] if gate is None else after(parts[2], gate)
    return [*parts, swapped(far, 1)]


def owner(mask):
    return jnp.bitwise_xor(lax.axis_index("head"), mask)


MASKS = (0, 1, 2, 3)


def store_wide(wide, start, block):
    for j in range(wide.shape[0]):
        rows = pl.ds(start, block.shape[0])
        wide[j, rows, :] = block[:, 128 * j : 128 * (j + 1)].astype(jnp.float32)


def taps_sum(wide, weight_ref, groups, copies=None):
    total = None
    for tap in range(KW):
        if copies is not None:
            copies[tap].wait()
        picked = []
        for start, count in groups:
            lanes = [
                wide[j, pl.ds(start + tap, count, stride=2), :] for j in range(wide.shape[0])
            ]
            picked.append(jnp.concatenate(lanes, axis=1).astype(jnp.bfloat16))
        taken = picked[0] if len(picked) == 1 else jnp.concatenate(picked, axis=0)
        term = reduce_operands(taken, weight_ref[tap])
        total = term if total is None else total + term
    return total


FIRST = EDGE - KW // 2


def conv_middle_kernel(dna_ref, weight_ref, h1_ref, sent_ref, wide, rows, weights, sems):
    first = pltpu.make_async_copy(dna_ref.at[pl.ds(0, rows.shape[0]), :], rows, sems.at[KW])
    copies = [
        pltpu.make_async_copy(weight_ref.at[tap], weights.at[tap], sems.at[tap])
        for tap in range(KW)
    ]
    for copy in (first, *copies):
        copy.start()
    first.wait()
    store_wide(wide, 0, rows[...])
    total = taps_sum(wide, weights, [(FIRST, sent_ref.shape[0])], copies)
    h1_ref[...] = total
    sent_ref[...] = total.astype(jnp.bfloat16)


def conv_edge_kernel(dna_ref, low_ref, high_ref, weight_ref, h1_ref, sent_ref, wide):
    rows = dna_ref.shape[0]
    upper = sent_ref.shape[0] - EDGE
    first = rows - 2 * upper
    zeros = jnp.zeros((EDGE, dna_ref.shape[1]), jnp.bfloat16)
    store_wide(wide, 0, zeros)
    store_wide(wide, EDGE, low_ref[...])
    store_wide(wide, 2 * EDGE, dna_ref[pl.ds(0, 2 * EDGE), :])
    store_wide(wide, 4 * EDGE, dna_ref[pl.ds(first, rows - first), :])
    store_wide(wide, 4 * EDGE + rows - first, high_ref[...])
    store_wide(wide, 5 * EDGE + rows - first, zeros)
    total = taps_sum(wide, weight_ref, [(FIRST, EDGE), (4 * EDGE + FIRST, upper)])
    h1_ref[...] = total
    sent_ref[...] = total.astype(jnp.bfloat16)


def first_conv(kernel, operands, weight, count, deep, name, streamed=False):
    width, out = weight.shape[2], weight.shape[1]
    kept = jax.ShapeDtypeStruct((count, out), jnp.float32)
    sent = jax.ShapeDtypeStruct((count, out), jnp.bfloat16)
    scratch = [pltpu.VMEM((width // 128, deep, 128), jnp.float32)]
    place = pltpu.VMEM
    if streamed:
        place = pltpu.HBM
        operands = [pltpu.with_memory_space_constraint(a, place) for a in operands]
        weight = pltpu.with_memory_space_constraint(weight, place)
        scratch += [
            pltpu.VMEM((deep, width), jnp.bfloat16),
            pltpu.VMEM(weight.shape, jnp.bfloat16),
            pltpu.SemaphoreType.DMA((KW + 1,)),
        ]
    return pl.pallas_call(
        kernel,
        out_shape=(kept, sent),
        in_specs=[pl.BlockSpec(memory_space=place)] * (len(operands) + 1),
        scratch_shapes=scratch,
        compiler_params=pltpu.CompilerParams(vmem_limit_bytes=24 * MIB),
        cost_estimate=cost(2 * count * out * width * KW, (*operands, weight, kept, sent)),
        name=name,
    )(*operands, weight)


def inverse_norm(blocks):
    squares = None
    for block in blocks:
        term = jnp.sum(block * block, axis=1, keepdims=True)
        squares = term if squares is None else squares + term
    return lax.rsqrt(squares / C + EPS)


def wide_blocks(parts, start, count):
    return [part[pl.ds(start, count), :].astype(jnp.float32) for part in parts]


def gelu(value):
    return jax.nn.gelu(value, approximate=True)


def columns_of(mask, width):
    return pl.ds(pl.multiple_of(owner(mask) * width, LANES), width)


def dilated_middle_kernel(a0, a1, a2, a3, h1_ref, weight_ref, h2_ref, sent_ref, act):
    parts = (a0, a1, a2, a3)
    count, width = a0.shape
    rows = h2_ref.shape[0]
    blocks = wide_blocks(parts, 0, count)
    inverse = inverse_norm(blocks)
    total = h1_ref[pl.ds(8, rows), :]
    for slot, (block, mask) in enumerate(zip(blocks, MASKS)):
        act[slot] = gelu(block * inverse)
        for tap in range(3):
            taken = act[slot, pl.ds((tap + 1) * DILATION_STEP, rows), :].astype(jnp.bfloat16)
            total = total + reduce_operands(taken, weight_ref[tap, :, columns_of(mask, width)])
    h2_ref[...] = total
    sent_ref[...] = total.astype(jnp.bfloat16)


def dilated_edge_kernel(
    m0, m1, m2, m3, e0, e1, e2, e3, hm_ref, he_ref, h2m_ref, weight_ref, h2_ref, sent_ref, act
):
    middle, edge = (m0, m1, m2, m3), (e0, e1, e2, e3)
    inner, width = m0.shape
    outer = e0.shape[0]
    rows = h2_ref.shape[0]
    upper = outer - EDGE
    position = lax.axis_index("seq") * rows + lax.broadcasted_iota(jnp.int32, (outer, 1), 0)
    place = lax.broadcasted_iota(jnp.int32, (outer, 1), 0)
    position = position + jnp.where(place < EDGE, -8, inner - 8)
    inside = (position >= 0) & (position < rows * lax.axis_size("seq"))
    outer_blocks = wide_blocks(edge, 0, outer)
    outer_inverse = jnp.where(inside, inverse_norm(outer_blocks), 0.0)
    low_blocks = wide_blocks(middle, 0, EDGE)
    low_inverse = inverse_norm(low_blocks)
    high_blocks = wide_blocks(middle, inner - EDGE, EDGE)
    high_inverse = inverse_norm(high_blocks)
    last = rows - (outer - EDGE)
    total = jnp.concatenate(
        [
            he_ref[pl.ds(8, 8), :],
            hm_ref[pl.ds(0, 8), :],
            hm_ref[pl.ds(inner - 8, 8), :],
            he_ref[pl.ds(EDGE, upper - 8), :],
        ],
        axis=0,
    )
    tail = 2 * EDGE
    for slot, mask in enumerate(MASKS):
        full = gelu(outer_blocks[slot] * outer_inverse)
        act[slot, pl.ds(0, EDGE), :] = full[:EDGE]
        act[slot, pl.ds(EDGE, EDGE), :] = gelu(low_blocks[slot] * low_inverse)
        act[slot, pl.ds(tail, EDGE), :] = gelu(high_blocks[slot] * high_inverse)
        act[slot, pl.ds(tail + EDGE, upper), :] = full[EDGE:]
        for tap in range(3):
            shifted = (tap + 1) * DILATION_STEP
            taken = jnp.concatenate(
                [
                    act[slot, pl.ds(shifted, EDGE), :],
                    act[slot, pl.ds(tail + shifted, upper), :],
                ],
                axis=0,
            ).astype(jnp.bfloat16)
            total = total + reduce_operands(taken, weight_ref[tap, :, columns_of(mask, width)])
    h2_ref[pl.ds(0, EDGE), :] = total[:EDGE]
    h2_ref[pl.ds(EDGE, last - EDGE), :] = h2m_ref[...]
    h2_ref[pl.ds(last, rows - last), :] = total[EDGE:]
    sent_ref[...] = total.astype(jnp.bfloat16)


def second_conv(kernel, operands, weight, kept_rows, sent_rows, deep, name):
    out, width = weight.shape[1], operands[0].shape[1]
    kept = jax.ShapeDtypeStruct((kept_rows, out), jnp.float32)
    sent = jax.ShapeDtypeStruct((sent_rows, out), jnp.bfloat16)
    return pl.pallas_call(
        kernel,
        out_shape=(kept, sent),
        scratch_shapes=[pltpu.VMEM((4, deep, width), jnp.float32)],
        compiler_params=pltpu.CompilerParams(vmem_limit_bytes=24 * MIB),
        cost_estimate=cost(
            2 * sent_rows * out * weight.shape[2] * 3,
            (*operands, weight, kept, sent),
            deep * weight.shape[2],
        ),
        name=name,
    )(*operands, weight)


def projections(parts, wq, wk, wv, kv_ref):
    width = parts[0].shape[1]
    rows, out = parts[0].shape[0], wq.shape[0]
    blocks = [part[...].astype(jnp.float32) for part in parts]
    inverse = inverse_norm(blocks)
    normed = [(block * inverse).astype(jnp.bfloat16) for block in blocks]

    def product(weight_ref, start=0, stop=rows, weight_first=False):
        total = None
        for part, mask in zip(normed, MASKS):
            weight = weight_ref[:, columns_of(mask, width)]
            taken = part[start:stop]
            pair = (weight, taken) if weight_first else (taken, weight)
            term = reduce_operands(*pair)
            total = term if total is None else total + term
        return total

    kv_ref[:, :out] = product(wk).astype(jnp.bfloat16)
    turned = rows - rows % LANES
    value = product(wv, 0, turned, True).astype(jnp.bfloat16)
    for row in range(0, turned, LANES):
        for lane in range(0, out, LANES):
            kv_ref[pl.ds(row, LANES), pl.ds(out + lane, LANES)] = value[
                lane : lane + LANES, row : row + LANES
            ]
    if turned < rows:
        value = product(wv, turned, rows)
        kv_ref[pl.ds(turned, rows - turned), out:] = value.astype(jnp.bfloat16)
    scale = LOG2E / math.sqrt(HEAD_DIM)
    return (product(wq) * scale).astype(jnp.bfloat16)


def project_middle_kernel(a0, a1, a2, a3, wq, wk, wv, q_ref, kv_ref):
    q_ref[...] = projections((a0, a1, a2, a3), wq, wk, wv, kv_ref)


def project_edge_kernel(a0, a1, a2, a3, qm_ref, wq, wk, wv, q_ref, kv_ref):
    query = projections((a0, a1, a2, a3), wq, wk, wv, kv_ref)
    inner, rows = qm_ref.shape[0], q_ref.shape[0]
    q_ref[pl.ds(0, EDGE), :] = query[:EDGE]
    q_ref[pl.ds(EDGE, inner), :] = qm_ref[...]
    q_ref[pl.ds(EDGE + inner, rows - EDGE - inner), :] = query[EDGE:]


def project(kernel, operands, weights, q_rows, name):
    rows, out = operands[0].shape[0], weights[0].shape[0]
    q = jax.ShapeDtypeStruct((q_rows, out), jnp.bfloat16)
    kv = jax.ShapeDtypeStruct((rows, 2 * out), jnp.bfloat16)
    return pl.pallas_call(
        kernel,
        out_shape=(q, kv),
        compiler_params=pltpu.CompilerParams(vmem_limit_bytes=20 * MIB),
        cost_estimate=cost(6 * rows * out * C, (*operands, *weights, q, kv)),
        name=name,
    )(*operands, *weights)


TILE = 64


def split_rows(block):
    turned = block.shape[0] - block.shape[0] % LANES
    return turned, block.shape[0] - turned


def turned_values(blocks, width, pair):
    lanes = pl.ds(width + pair * LANES, LANES)
    values = []
    for block in blocks:
        for row in range(0, split_rows(block)[0], LANES):
            values.append(block[pl.ds(row, LANES), lanes])
    rest = []
    for block in blocks:
        start, count = split_rows(block)
        if count:
            rest.append(block[pl.ds(start, count), lanes].astype(jnp.float32))
    if rest:
        values.append(jnp.transpose(jnp.concatenate(rest, axis=0)).astype(jnp.bfloat16))
    return jnp.concatenate(values, axis=1)


def ordered_keys(blocks, pair):
    lanes = pl.ds(pair * LANES, LANES)
    keys = [block[pl.ds(0, split_rows(block)[0]), lanes] for block in blocks]
    for block in blocks:
        start, count = split_rows(block)
        if count:
            keys.append(block[pl.ds(start, count), lanes])
    return jnp.concatenate(keys, axis=0)


def partial_attention(query, keys, values, scores, weights, head, lane):
    pair, half = divmod(head, 2)
    mine = query[:, pair * LANES : (pair + 1) * LANES]
    mine = jnp.where((lane // HEAD_DIM) == half, mine, jnp.zeros_like(mine))
    scores[...] = reduce_operands(keys, mine)
    columns = scores.shape[1]
    top = None
    for start in range(0, scores.shape[0], TILE):
        tile = jnp.max(scores[pl.ds(start, TILE), :].reshape(-1, 8, columns), axis=0)
        top = tile if top is None else jnp.maximum(top, tile)
    top = jnp.max(top, axis=0, keepdims=True)
    total = None
    for start in range(0, scores.shape[0], TILE):
        weight = jnp.exp2(scores[pl.ds(start, TILE), :] - top)
        tile = jnp.sum(weight.reshape(-1, 8, columns), axis=0)
        total = tile if total is None else total + tile
        weights[pl.ds(start, TILE), :] = weight.astype(jnp.bfloat16)
    values = values[half * HEAD_DIM : (half + 1) * HEAD_DIM]
    out = jnp.dot(values, weights[...], preferred_element_type=jnp.float32)
    return out, top, jnp.sum(total, axis=0, keepdims=True)


def state_parts(state, head, width, columns):
    return (
        state[pl.ds(head * HEAD_DIM, HEAD_DIM), columns],
        state[pl.ds(width + head, 1), columns],
        state[pl.ds(width + 8 + head, 1), columns],
    )


def merged_parts(one, other):
    top = jnp.maximum(one[1], other[1])
    first, second = jnp.exp2(one[1] - top), jnp.exp2(other[1] - top)
    return first * one[0] + second * other[0], top, first * one[2] + second * other[2]


def attend_kernel(first_column, q_refs, blocks, state, out_ref, scores, weights):
    width = q_refs[0].shape[1]
    query = jnp.concatenate([ref[...] for ref in q_refs], axis=0)
    columns = query.shape[0]
    lane = lax.broadcasted_iota(jnp.int32, (columns, LANES), 1)
    out_ref[pl.ds(width, 16), :] = jnp.zeros((16, columns), jnp.float32)
    for head in range(width // HEAD_DIM):
        if head % 2 == 0:
            keys = ordered_keys(blocks, head // 2)
            values = turned_values(blocks, width, head // 2)
        part = partial_attention(
            query, keys, values, scores.at[head % 2], weights.at[head % 2], head, lane
        )
        if state is not None:
            part = merged_parts(
                part, state_parts(state, head, width, pl.ds(first_column, columns))
            )
        out_ref[pl.ds(head * HEAD_DIM, HEAD_DIM), :] = part[0]
        out_ref[pl.ds(width + head, 1), :] = part[1]
        out_ref[pl.ds(width + 8 + head, 1), :] = part[2]


def attend(queries, blocks, state, first_column, name):
    rows, width = queries[0].shape
    columns = rows * len(queries)
    extent = sum(block.shape[0] for block in blocks)
    out = jax.ShapeDtypeStruct((width + 16, columns), jnp.float32)
    operands = (*queries, *blocks) + (() if state is None else (state,))

    def kernel(*refs):
        q_refs, block_refs = refs[: len(queries)], refs[len(queries) :][: len(blocks)]
        state_ref = None if state is None else refs[len(operands) - 1]
        attend_kernel(
            first_column, q_refs, block_refs, state_ref, *refs[len(operands) :]
        )

    return pl.pallas_call(
        kernel,
        out_shape=out,
        scratch_shapes=[
            pltpu.VMEM((2, extent, columns), jnp.float32),
            pltpu.VMEM((2, extent, columns), jnp.bfloat16),
        ],
        compiler_params=pltpu.CompilerParams(vmem_limit_bytes=24 * MIB),
        cost_estimate=cost(
            4 * columns * width * extent, (*operands, out), columns * extent * width // HEAD_DIM
        ),
        name=name,
    )(*operands)


def mix_kernel(own_state, other_state, w_ref, h2_ref, own_ref, p1, p2, p3, attended):
    rows, width = h2_ref.shape
    for pair in range(width // LANES):
        halves = []
        for head in (2 * pair, 2 * pair + 1):
            out, _, total = merged_parts(
                state_parts(own_state, head, width, pl.ds(0, rows)),
                state_parts(other_state, head, width, pl.ds(0, rows)),
            )
            halves.append(out / total)
        merged = jnp.transpose(jnp.concatenate(halves, axis=0))
        attended[:, pl.ds(pair * LANES, LANES)] = merged.astype(jnp.bfloat16)

    def product(mask):
        return jnp.dot(
            attended[...], w_ref[:, columns_of(mask, width)], preferred_element_type=jnp.float32
        )

    for ref, mask in ((p3, 3), (p2, 2), (p1, 1)):
        ref[...] = product(mask).astype(jnp.bfloat16)
    own_ref[...] = product(0) + h2_ref[...]


def mix(own_state, other_state, w_out, h2):
    rows, width = h2.shape
    own = jax.ShapeDtypeStruct((rows, width), jnp.float32)
    part = jax.ShapeDtypeStruct((rows, width), jnp.bfloat16)
    operands = (own_state, other_state, w_out, h2)
    return pl.pallas_call(
        mix_kernel,
        out_shape=(own, part, part, part),
        scratch_shapes=[pltpu.VMEM((rows, width), jnp.bfloat16)],
        compiler_params=pltpu.CompilerParams(vmem_limit_bytes=16 * MIB),
        cost_estimate=cost(
            2 * rows * width * w_out.shape[1], (*operands, own, part, part, part)
        ),
        name="mix",
    )(*operands)


def exchanged(block, mask):
    count = lax.axis_size("seq")
    return lax.ppermute(block, "seq", [(i, i ^ mask) for i in range(count)])


def on_device(dna, conv_in, dilated_kernel_weight, w_query, w_key, w_value, w_out):
    count = lax.axis_size("seq")
    rows = dna.shape[0] // 2
    inner = rows // 2
    outer = rows - inner
    low = lax.ppermute(dna[-EDGE:], "seq", [(i, i + 1) for i in range(count - 1)])
    high = lax.ppermute(dna[:EDGE], "seq", [(i + 1, i) for i in range(count - 1)])
    h1_m, sent = first_conv(
        conv_middle_kernel,
        (dna,),
        conv_in,
        inner + EDGE,
        2 * (inner + 2 * EDGE),
        "conv_middle",
        True,
    )
    wide_m = forwarded(shared(sent))
    h1_e, sent = first_conv(
        conv_edge_kernel, (dna, after(low, *wide_m[1:3]), high), conv_in, outer, 2 * (outer + 2 * EDGE), "conv_edge"
    )
    wide_e = shared(sent)
    h2_m, sent = second_conv(
        dilated_middle_kernel,
        (*wide_m, after(h1_m, sent)),
        dilated_kernel_weight,
        inner,
        inner,
        inner + EDGE,
        "dilated_middle",
    )
    normed_m = forwarded(shared(sent, wide_e))
    wide_e = forwarded(wide_e, sent)
    h2, sent = second_conv(
        dilated_edge_kernel,
        (*wide_m, *wide_e, h1_m, h1_e, h2_m),
        dilated_kernel_weight,
        rows,
        outer,
        outer + 2 * EDGE,
        "dilated_edge",
    )
    normed_e = shared(sent, normed_m)
    normed_m[0] = after(normed_m[0], sent)
    weights = (w_query, w_key, w_value)
    q_m, kv_m = project(project_middle_kernel, normed_m, weights, inner, "project_middle")
    x_m, y_m, d_m = (exchanged(kv_m, mask) for mask in (2, 4, 6))
    normed_e = forwarded(normed_e, kv_m)
    q, kv_e = project(project_edge_kernel, (*normed_e, q_m), weights, rows, "project_edge")
    q_other, x_e, y_e, d_e = exchanged(q, 1), *(exchanged(kv_e, mask) for mask in (2, 4, 6))
    state = attend((q, q_other), (kv_m, kv_e, x_m, y_m, d_m), None, 0, "attend_m")
    late = (x_e, y_e, d_e)
    state_other = attend((q_other,), late, state, rows, "attend_other")
    given = exchanged(state_other, 1)
    state_own = attend((q,), late, state, 0, "attend_own")
    own, p1, p2, p3 = mix(state_own, given, w_out, h2)
    inward = swapped(p3, 1)
    joined = (p2.astype(jnp.float32) + inward.astype(jnp.float32)).astype(jnp.bfloat16)
    total = own
    for part in (swapped(joined, 2), swapped(after(p1, joined), 1)):
        total = total + part.astype(jnp.float32)
    return total.astype(jnp.bfloat16)


def solution(mesh):
    in_specs = (
        P("seq", None),
        P(None, "head", None),
        P(None, "head", None),
        P("head", None),
        P("head", None),
        P("head", None),
        P("head", None),
    )
    out_specs = P("seq", "head")
    seq, head = mesh.shape["seq"], mesh.shape["head"]
    aligned = (C // head) % 128 == 0
    body = on_device if head == 4 and seq == 8 and aligned else general_form
    return jax.shard_map(body, mesh=mesh, in_specs=in_specs, out_specs=out_specs, check_vma=False)
```

```python
import functools
import math

import jax
import jax.numpy as jnp
from jax import lax
from jax.experimental import pallas as pl
from jax.experimental.pallas import tpu as pltpu
from jax.sharding import PartitionSpec as P

C = 1536
HEAD_DIM = 64
KW = 5
DILATION_STEP = 4
EPS = 1e-06
EDGE = 16
LOG2E = math.log2(math.e)
MIB = 1 << 20
LANES = 128


def padded_2(block, sides, width):
    for axis, dim in sides:
        count = lax.axis_size(axis)
        forward = [(i, i + 1) for i in range(count - 1)]
        backward = [(target, source) for source, target in forward]
        low = lax.ppermute(
            lax.slice_in_dim(block, block.shape[dim] - width, None, axis=dim), axis, forward
        )
        high = lax.ppermute(lax.slice_in_dim(block, 0, width, axis=dim), axis, backward)
        block = jnp.concatenate([low, block, high], axis=dim)
    return block


def row_scale(hidden):
    squares = lax.psum(jnp.sum(hidden * hidden, axis=1), "head")
    return hidden * lax.rsqrt(squares / C + EPS)[:, None]


def reduce_operands(left, right):
    return lax.dot_general(
        left, right, (((1,), (1,)), ((), ())), preferred_element_type=jnp.float32
    )


def general_form(dna, conv_in, dilated_kernel_weight, w_query, w_key, w_value, w_out):
    local_row_count = dna.shape[0] // 2
    half = (KW - 1) // 2
    padded = padded_2(dna, (("seq", 0),), half)
    h1 = jnp.zeros((local_row_count, conv_in.shape[1]), jnp.float32)
    for kernel_offset in range(KW):
        rows = lax.slice(
            padded,
            (kernel_offset, 0),
            (kernel_offset + 2 * local_row_count - 1, padded.shape[1]),
            (2, 1),
        )
        h1 = h1 + reduce_operands(rows, conv_in[kernel_offset])
    gelu_output = jax.nn.gelu(row_scale(h1), approximate=True).astype(jnp.bfloat16)
    complete_output = lax.all_gather(gelu_output, "head", axis=1, tiled=True)
    broad_input = padded_2(complete_output, (("seq", 0),), DILATION_STEP)
    second_hidden = h1
    for kernel_offset in range(3):
        second_hidden = second_hidden + reduce_operands(
            broad_input[
                DILATION_STEP * kernel_offset : DILATION_STEP * kernel_offset + local_row_count
            ],
            dilated_kernel_weight[kernel_offset],
        )
    normed = row_scale(second_hidden).astype(jnp.bfloat16)
    local_width = w_query.shape[0]
    heads_here = local_width // HEAD_DIM
    piece = lax.all_gather(normed, "head", axis=1, tiled=True)
    q_acc, k_acc, v_acc = (reduce_operands(piece, w) for w in (w_query, w_key, w_value))
    query = q_acc.astype(jnp.bfloat16).reshape(local_row_count, heads_here, HEAD_DIM)
    keys = k_acc.astype(jnp.bfloat16)
    values = v_acc.astype(jnp.bfloat16)
    scale = 1.0 / math.sqrt(HEAD_DIM)
    start_state = (
        jnp.full((heads_here, local_row_count), -1e30, jnp.float32),
        jnp.zeros((heads_here, local_row_count), jnp.float32),
        jnp.zeros((local_row_count, heads_here, HEAD_DIM), jnp.float32),
    )
    key_rows = lax.all_gather(keys, "seq", axis=0, tiled=True)
    value_rows = lax.all_gather(values, "seq", axis=0, tiled=True)
    count = key_rows.shape[0]
    width = 512 if count % 512 == 0 else count
    blocks = count // width
    key_blocks = key_rows.reshape(blocks, width, heads_here, HEAD_DIM)
    value_blocks = value_rows.reshape(blocks, width, heads_here, HEAD_DIM)

    def step(state, operands):
        running, total, acc = state
        key_block, value_block = operands
        scores = (
            jnp.einsum("qhd,khd->hqk", query, key_block, preferred_element_type=jnp.float32) * scale
        )
        newest = jnp.maximum(running, jnp.max(scores, axis=2))
        factor = jnp.exp(running - newest)
        weights = jnp.exp(scores - newest[:, :, None])
        total = total * factor + jnp.sum(weights, axis=2)
        update = jnp.einsum(
            "hqk,khd->qhd",
            weights.astype(jnp.bfloat16),
            value_block,
            preferred_element_type=jnp.float32,
        )
        acc = acc * jnp.transpose(factor)[:, :, None] + update
        return ((newest, total, acc), None)

    state, _ = lax.scan(step, start_state, (key_blocks, value_blocks))
    running, total, acc = state
    attended = (
        (acc / jnp.transpose(total)[:, :, None])
        .reshape(local_row_count, local_width)
        .astype(jnp.bfloat16)
    )
    partial_out = jnp.dot(attended, w_out, preferred_element_type=jnp.float32)
    mixed = lax.psum_scatter(
        partial_out.astype(jnp.bfloat16), "head", scatter_dimension=1, tiled=True
    ).astype(jnp.float32)
    return (second_hidden + mixed).astype(jnp.bfloat16)


def nbytes(*arrays):
    return sum(math.prod(a.shape) * jnp.dtype(a.dtype).itemsize for a in arrays)


def cost(flops, arrays, transcendentals=0):
    return pl.CostEstimate(
        flops=int(flops), bytes_accessed=int(nbytes(*arrays)), transcendentals=int(transcendentals)
    )


def after(value, *others):
    return lax.optimization_barrier((value, *others))[0]


def swapped(block, mask):
    count = lax.axis_size("head")
    return lax.ppermute(block, "head", [(i, i ^ mask) for i in range(count)])


def shared(block, earlier=None):
    near = far = block
    if earlier is not None:
        near, far = after(block, earlier[1]), after(block, earlier[2])
    far = swapped(far, 2)
    near = swapped(near, 1)
    return [block, near, far]


def forwarded(parts, gate=None):
    far = parts[2] if gate is None else after(parts[2], gate)
    return [*parts, swapped(far, 1)]


def owner(mask):
    return jnp.bitwise_xor(lax.axis_index("head"), mask)


MASKS = (0, 1, 2, 3)


def store_wide(wide, start, block):
    for j in range(wide.shape[0]):
        rows = pl.ds(start, block.shape[0])
        wide[j, rows, :] = block[:, 128 * j : 128 * (j + 1)].astype(jnp.float32)


def taps_sum(wide, weight_ref, groups, copies=None):
    total = None
    for tap in range(KW):
        if copies is not None:
            copies[tap].wait()
        picked = []
        for start, count in groups:
            lanes = [
                wide[j, pl.ds(start + tap, count, stride=2), :] for j in range(wide.shape[0])
            ]
            picked.append(jnp.concatenate(lanes, axis=1).astype(jnp.bfloat16))
        taken = picked[0] if len(picked) == 1 else jnp.concatenate(picked, axis=0)
        term = reduce_operands(taken, weight_ref[tap])
        total = term if total is None else total + term
    return total


FIRST = EDGE - KW // 2


def conv_middle_kernel(dna_ref, weight_ref, h1_ref, sent_ref, wide, rows, weights, sems):
    first = pltpu.make_async_copy(dna_ref.at[pl.ds(0, rows.shape[0]), :], rows, sems.at[KW])
    copies = [
        pltpu.make_async_copy(weight_ref.at[tap], weights.at[tap], sems.at[tap])
        for tap in range(KW)
    ]
    for copy in (first, *copies):
        copy.start()
    first.wait()
    store_wide(wide, 0, rows[...])
    total = taps_sum(wide, weights, [(FIRST, sent_ref.shape[0])], copies)
    h1_ref[...] = total
    sent_ref[...] = total.astype(jnp.bfloat16)


def conv_edge_kernel(dna_ref, low_ref, high_ref, weight_ref, h1_ref, sent_ref, wide):
    rows = dna_ref.shape[0]
    upper = sent_ref.shape[0] - EDGE
    first = rows - 2 * upper
    zeros = jnp.zeros((EDGE, dna_ref.shape[1]), jnp.bfloat16)
    store_wide(wide, 0, zeros)
    store_wide(wide, EDGE, low_ref[...])
    store_wide(wide, 2 * EDGE, dna_ref[pl.ds(0, 2 * EDGE), :])
    store_wide(wide, 4 * EDGE, dna_ref[pl.ds(first, rows - first), :])
    store_wide(wide, 4 * EDGE + rows - first, high_ref[...])
    store_wide(wide, 5 * EDGE + rows - first, zeros)
    total = taps_sum(wide, weight_ref, [(FIRST, EDGE), (4 * EDGE + FIRST, upper)])
    h1_ref[...] = total
    sent_ref[...] = total.astype(jnp.bfloat16)


def first_conv(kernel, operands, weight, count, deep, name, streamed=False):
    width, out = weight.shape[2], weight.shape[1]
    kept = jax.ShapeDtypeStruct((count, out), jnp.float32)
    sent = jax.ShapeDtypeStruct((count, out), jnp.bfloat16)
    scratch = [pltpu.VMEM((width // 128, deep, 128), jnp.float32)]
    place = pltpu.VMEM
    if streamed:
        place = pltpu.HBM
        operands = [pltpu.with_memory_space_constraint(a, place) for a in operands]
        weight = pltpu.with_memory_space_constraint(weight, place)
        scratch += [
            pltpu.VMEM((deep, width), jnp.bfloat16),
            pltpu.VMEM(weight.shape, jnp.bfloat16),
            pltpu.SemaphoreType.DMA((KW + 1,)),
        ]
    return pl.pallas_call(
        kernel,
        out_shape=(kept, sent),
        in_specs=[pl.BlockSpec(memory_space=place)] * (len(operands) + 1),
        scratch_shapes=scratch,
        compiler_params=pltpu.CompilerParams(vmem_limit_bytes=24 * MIB),
        cost_estimate=cost(2 * count * out * width * KW, (*operands, weight, kept, sent)),
        name=name,
    )(*operands, weight)


def inverse_norm(blocks):
    squares = None
    for block in blocks:
        term = jnp.sum(block * block, axis=1, keepdims=True)
        squares = term if squares is None else squares + term
    return lax.rsqrt(squares / C + EPS)


def wide_blocks(parts, start, count):
    return [part[pl.ds(start, count), :].astype(jnp.float32) for part in parts]


def gelu(value):
    return jax.nn.gelu(value, approximate=True)


def columns_of(mask, width):
    return pl.ds(pl.multiple_of(owner(mask) * width, LANES), width)


def dilated_middle_kernel(a0, a1, a2, a3, h1_ref, weight_ref, h2_ref, sent_ref, act):
    parts = (a0, a1, a2, a3)
    count, width = a0.shape
    rows = h2_ref.shape[0]
    blocks = wide_blocks(parts, 0, count)
    inverse = inverse_norm(blocks)
    total = h1_ref[pl.ds(8, rows), :]
    for slot, (block, mask) in enumerate(zip(blocks, MASKS)):
        act[slot] = gelu(block * inverse)
        for tap in range(3):
            taken = act[slot, pl.ds((tap + 1) * DILATION_STEP, rows), :].astype(jnp.bfloat16)
            total = total + reduce_operands(taken, weight_ref[tap, :, columns_of(mask, width)])
    h2_ref[...] = total
    sent_ref[...] = total.astype(jnp.bfloat16)


def dilated_edge_kernel(
    m0, m1, m2, m3, e0, e1, e2, e3, hm_ref, he_ref, h2m_ref, weight_ref, h2_ref, sent_ref, act
):
    middle, edge = (m0, m1, m2, m3), (e0, e1, e2, e3)
    inner, width = m0.shape
    outer = e0.shape[0]
    rows = h2_ref.shape[0]
    upper = outer - EDGE
    position = lax.axis_index("seq") * rows + lax.broadcasted_iota(jnp.int32, (outer, 1), 0)
    place = lax.broadcasted_iota(jnp.int32, (outer, 1), 0)
    position = position + jnp.where(place < EDGE, -8, inner - 8)
    inside = (position >= 0) & (position < rows * lax.axis_size("seq"))
    outer_blocks = wide_blocks(edge, 0, outer)
    outer_inverse = jnp.where(inside, inverse_norm(outer_blocks), 0.0)
    low_blocks = wide_blocks(middle, 0, EDGE)
    low_inverse = inverse_norm(low_blocks)
    high_blocks = wide_blocks(middle, inner - EDGE, EDGE)
    high_inverse = inverse_norm(high_blocks)
    last = rows - (outer - EDGE)
    total = jnp.concatenate(
        [
            he_ref[pl.ds(8, 8), :],
            hm_ref[pl.ds(0, 8), :],
            hm_ref[pl.ds(inner - 8, 8), :],
            he_ref[pl.ds(EDGE, upper - 8), :],
        ],
        axis=0,
    )
    tail = 2 * EDGE
    for slot, mask in enumerate(MASKS):
        full = gelu(outer_blocks[slot] * outer_inverse)
        act[slot, pl.ds(0, EDGE), :] = full[:EDGE]
        act[slot, pl.ds(EDGE, EDGE), :] = gelu(low_blocks[slot] * low_inverse)
        act[slot, pl.ds(tail, EDGE), :] = gelu(high_blocks[slot] * high_inverse)
        act[slot, pl.ds(tail + EDGE, upper), :] = full[EDGE:]
        for tap in range(3):
            shifted = (tap + 1) * DILATION_STEP
            taken = jnp.concatenate(
                [
                    act[slot, pl.ds(shifted, EDGE), :],
                    act[slot, pl.ds(tail + shifted, upper), :],
                ],
                axis=0,
            ).astype(jnp.bfloat16)
            total = total + reduce_operands(taken, weight_ref[tap, :, columns_of(mask, width)])
    h2_ref[pl.ds(0, EDGE), :] = total[:EDGE]
    h2_ref[pl.ds(EDGE, last - EDGE), :] = h2m_ref[...]
    h2_ref[pl.ds(last, rows - last), :] = total[EDGE:]
    sent_ref[...] = total.astype(jnp.bfloat16)


def second_conv(kernel, operands, weight, kept_rows, sent_rows, deep, name):
    out, width = weight.shape[1], operands[0].shape[1]
    kept = jax.ShapeDtypeStruct((kept_rows, out), jnp.float32)
    sent = jax.ShapeDtypeStruct((sent_rows, out), jnp.bfloat16)
    return pl.pallas_call(
        kernel,
        out_shape=(kept, sent),
        scratch_shapes=[pltpu.VMEM((4, deep, width), jnp.float32)],
        compiler_params=pltpu.CompilerParams(vmem_limit_bytes=24 * MIB),
        cost_estimate=cost(
            2 * sent_rows * out * weight.shape[2] * 3,
            (*operands, weight, kept, sent),
            deep * weight.shape[2],
        ),
        name=name,
    )(*operands, weight)


def projections(parts, wq, wk, wv, kv_ref):
    width = parts[0].shape[1]
    rows, out = parts[0].shape[0], wq.shape[0]
    blocks = [part[...].astype(jnp.float32) for part in parts]
    inverse = inverse_norm(blocks)
    normed = [(block * inverse).astype(jnp.bfloat16) for block in blocks]

    def product(weight_ref, start=0, stop=rows, weight_first=False):
        total = None
        for part, mask in zip(normed, MASKS):
            weight = weight_ref[:, columns_of(mask, width)]
            taken = part[start:stop]
            pair = (weight, taken) if weight_first else (taken, weight)
            term = reduce_operands(*pair)
            total = term if total is None else total + term
        return total

    kv_ref[:, :out] = product(wk).astype(jnp.bfloat16)
    turned = rows - rows % LANES
    value = product(wv, 0, turned, True).astype(jnp.bfloat16)
    for row in range(0, turned, LANES):
        for lane in range(0, out, LANES):
            kv_ref[pl.ds(row, LANES), pl.ds(out + lane, LANES)] = value[
                lane : lane + LANES, row : row + LANES
            ]
    if turned < rows:
        value = product(wv, turned, rows)
        kv_ref[pl.ds(turned, rows - turned), out:] = value.astype(jnp.bfloat16)
    scale = LOG2E / math.sqrt(HEAD_DIM)
    return (product(wq) * scale).astype(jnp.bfloat16)


def project_middle_kernel(a0, a1, a2, a3, wq, wk, wv, q_ref, kv_ref):
    q_ref[...] = projections((a0, a1, a2, a3), wq, wk, wv, kv_ref)


def project_edge_kernel(a0, a1, a2, a3, qm_ref, wq, wk, wv, q_ref, kv_ref):
    query = projections((a0, a1, a2, a3), wq, wk, wv, kv_ref)
    inner, rows = qm_ref.shape[0], q_ref.shape[0]
    q_ref[pl.ds(0, EDGE), :] = query[:EDGE]
    q_ref[pl.ds(EDGE, inner), :] = qm_ref[...]
    q_ref[pl.ds(EDGE + inner, rows - EDGE - inner), :] = query[EDGE:]


def project(kernel, operands, weights, q_rows, name):
    rows, out = operands[0].shape[0], weights[0].shape[0]
    q = jax.ShapeDtypeStruct((q_rows, out), jnp.bfloat16)
    kv = jax.ShapeDtypeStruct((rows, 2 * out), jnp.bfloat16)
    return pl.pallas_call(
        kernel,
        out_shape=(q, kv),
        compiler_params=pltpu.CompilerParams(vmem_limit_bytes=20 * MIB),
        cost_estimate=cost(6 * rows * out * C, (*operands, *weights, q, kv)),
        name=name,
    )(*operands, *weights)


TILE = 64


def split_rows(block):
    turned = block.shape[0] - block.shape[0] % LANES
    return turned, block.shape[0] - turned


def turned_values(blocks, pair):
    lanes = pl.ds(pair * LANES, LANES)
    values = []
    for _, block in blocks:
        for row in range(0, split_rows(block)[0], LANES):
            values.append(block[pl.ds(row, LANES), lanes])
    rest = []
    for _, block in blocks:
        start, count = split_rows(block)
        if count:
            rest.append(block[pl.ds(start, count), lanes].astype(jnp.float32))
    if rest:
        values.append(jnp.transpose(jnp.concatenate(rest, axis=0)).astype(jnp.bfloat16))
    return jnp.concatenate(values, axis=1)


def ordered_keys(blocks, pair):
    lanes = pl.ds(pair * LANES, LANES)
    keys = [block[pl.ds(0, split_rows(block)[0]), lanes] for block, _ in blocks]
    for block, _ in blocks:
        start, count = split_rows(block)
        if count:
            keys.append(block[pl.ds(start, count), lanes])
    return jnp.concatenate(keys, axis=0)


def partial_attention(query, keys, values, scores, weights, head, lane):
    pair, half = divmod(head, 2)
    mine = query[:, pair * LANES : (pair + 1) * LANES]
    mine = jnp.where((lane // HEAD_DIM) == half, mine, jnp.zeros_like(mine))
    scores[...] = reduce_operands(keys, mine)
    columns = scores.shape[1]
    top = None
    for start in range(0, scores.shape[0], TILE):
        tile = jnp.max(scores[pl.ds(start, TILE), :].reshape(-1, 8, columns), axis=0)
        top = tile if top is None else jnp.maximum(top, tile)
    top = jnp.max(top, axis=0, keepdims=True)
    total = None
    for start in range(0, scores.shape[0], TILE):
        weight = jnp.exp2(scores[pl.ds(start, TILE), :] - top)
        tile = jnp.sum(weight.reshape(-1, 8, columns), axis=0)
        total = tile if total is None else total + tile
        weights[pl.ds(start, TILE), :] = weight.astype(jnp.bfloat16)
    values = values[half * HEAD_DIM : (half + 1) * HEAD_DIM]
    out = jnp.dot(values, weights[...], preferred_element_type=jnp.float32)
    return out, top, jnp.sum(total, axis=0, keepdims=True)


def state_parts(state, head, width, columns):
    return (
        state[pl.ds(head * HEAD_DIM, HEAD_DIM), columns],
        state[pl.ds(width + head, 1), columns],
        state[pl.ds(width + 8 + head, 1), columns],
    )


def merged_parts(one, other):
    top = jnp.maximum(one[1], other[1])
    first, second = jnp.exp2(one[1] - top), jnp.exp2(other[1] - top)
    return first * one[0] + second * other[0], top, first * one[2] + second * other[2]


def attend_kernel(first_column, q_refs, blocks, state, out_ref, scores, weights):
    width = q_refs[0].shape[1]
    query = jnp.concatenate([ref[...] for ref in q_refs], axis=0)
    columns = query.shape[0]
    lane = lax.broadcasted_iota(jnp.int32, (columns, LANES), 1)
    out_ref[pl.ds(width, 16), :] = jnp.zeros((16, columns), jnp.float32)
    for head in range(width // HEAD_DIM):
        if head % 2 == 0:
            keys = ordered_keys(blocks, head // 2)
            values = turned_values(blocks, head // 2)
        part = partial_attention(
            query, keys, values, scores.at[head % 2], weights.at[head % 2], head, lane
        )
        if state is not None:
            part = merged_parts(
                part, state_parts(state, head, width, pl.ds(first_column, columns))
            )
        out_ref[pl.ds(head * HEAD_DIM, HEAD_DIM), :] = part[0]
        out_ref[pl.ds(width + head, 1), :] = part[1]
        out_ref[pl.ds(width + 8 + head, 1), :] = part[2]


def attend(queries, blocks, state, first_column, name):
    rows, width = queries[0].shape
    columns = rows * len(queries)
    extent = sum(block[0].shape[0] for block in blocks)
    out = jax.ShapeDtypeStruct((width + 16, columns), jnp.float32)
    flat = [array for block in blocks for array in block]
    operands = (*queries, *flat) + (() if state is None else (state,))

    def kernel(*refs):
        q_refs, rest = refs[: len(queries)], list(refs[len(queries) :])
        block_refs = []
        for block in blocks:
            first = rest.pop(0)
            if len(block) == 2:
                block_refs.append((first, rest.pop(0)))
            else:
                block_refs.append((first.at[:, pl.ds(0, width)], first.at[:, pl.ds(width, width)]))
        state_ref = None if state is None else refs[len(operands) - 1]
        attend_kernel(
            first_column, q_refs, block_refs, state_ref, *refs[len(operands) :]
        )

    return pl.pallas_call(
        kernel,
        out_shape=out,
        scratch_shapes=[
            pltpu.VMEM((2, extent, columns), jnp.float32),
            pltpu.VMEM((2, extent, columns), jnp.bfloat16),
        ],
        compiler_params=pltpu.CompilerParams(vmem_limit_bytes=24 * MIB),
        cost_estimate=cost(
            4 * columns * width * extent, (*operands, out), columns * extent * width // HEAD_DIM
        ),
        name=name,
    )(*operands)


def mix_kernel(own_state, other_state, w_ref, h2_ref, own_ref, p1, p2, p3, attended):
    rows, width = h2_ref.shape
    for pair in range(width // LANES):
        halves = []
        for head in (2 * pair, 2 * pair + 1):
            out, _, total = merged_parts(
                state_parts(own_state, head, width, pl.ds(0, rows)),
                state_parts(other_state, head, width, pl.ds(0, rows)),
            )
            halves.append(out / total)
        merged = jnp.transpose(jnp.concatenate(halves, axis=0))
        attended[:, pl.ds(pair * LANES, LANES)] = merged.astype(jnp.bfloat16)

    def product(mask):
        return jnp.dot(
            attended[...], w_ref[:, columns_of(mask, width)], preferred_element_type=jnp.float32
        )

    for ref, mask in ((p3, 3), (p2, 2), (p1, 1)):
        ref[...] = product(mask).astype(jnp.bfloat16)
    own_ref[...] = product(0) + h2_ref[...]


def mix(own_state, other_state, w_out, h2):
    rows, width = h2.shape
    own = jax.ShapeDtypeStruct((rows, width), jnp.float32)
    part = jax.ShapeDtypeStruct((rows, width), jnp.bfloat16)
    operands = (own_state, other_state, w_out, h2)
    return pl.pallas_call(
        mix_kernel,
        out_shape=(own, part, part, part),
        scratch_shapes=[pltpu.VMEM((rows, width), jnp.bfloat16)],
        compiler_params=pltpu.CompilerParams(vmem_limit_bytes=16 * MIB),
        cost_estimate=cost(
            2 * rows * width * w_out.shape[1], (*operands, own, part, part, part)
        ),
        name="mix",
    )(*operands)


def exchanged(block, mask):
    count = lax.axis_size("seq")
    return lax.ppermute(block, "seq", [(i, i ^ mask) for i in range(count)])


def on_device(dna, conv_in, dilated_kernel_weight, w_query, w_key, w_value, w_out):
    count = lax.axis_size("seq")
    rows = dna.shape[0] // 2
    inner = rows // 2
    outer = rows - inner
    low = lax.ppermute(dna[-EDGE:], "seq", [(i, i + 1) for i in range(count - 1)])
    high = lax.ppermute(dna[:EDGE], "seq", [(i + 1, i) for i in range(count - 1)])
    h1_m, sent = first_conv(
        conv_middle_kernel,
        (dna,),
        conv_in,
        inner + EDGE,
        2 * (inner + 2 * EDGE),
        "conv_middle",
        True,
    )
    wide_m = forwarded(shared(sent))
    h1_e, sent = first_conv(
        conv_edge_kernel, (dna, after(low, *wide_m[1:3]), high), conv_in, outer, 2 * (outer + 2 * EDGE), "conv_edge"
    )
    wide_e = shared(sent)
    h2_m, sent = second_conv(
        dilated_middle_kernel,
        (*wide_m, after(h1_m, sent)),
        dilated_kernel_weight,
        inner,
        inner,
        inner + EDGE,
        "dilated_middle",
    )
    normed_m = forwarded(shared(sent, wide_e))
    wide_e = forwarded(wide_e, sent)
    h2, sent = second_conv(
        dilated_edge_kernel,
        (*wide_m, *wide_e, h1_m, h1_e, h2_m),
        dilated_kernel_weight,
        rows,
        outer,
        outer + 2 * EDGE,
        "dilated_edge",
    )
    normed_e = shared(sent, normed_m)
    normed_m[0] = after(normed_m[0], sent)
    weights = (w_query, w_key, w_value)
    q_m, kv_m = project(project_middle_kernel, normed_m, weights, inner, "project_middle")
    x_m, y_m = exchanged(kv_m, 2), exchanged(kv_m, 4)
    width = q_m.shape[1]
    d_m = (exchanged(x_m[:, :width], 4), exchanged(y_m[:, width:], 2))
    normed_e = forwarded(normed_e, kv_m)
    q, kv_e = project(project_edge_kernel, (*normed_e, q_m), weights, rows, "project_edge")
    q_other, x_e, y_e, d_e = exchanged(q, 1), *(exchanged(kv_e, mask) for mask in (2, 4, 6))
    state = attend((q, q_other), ((kv_m,), (kv_e,), (x_m,), (y_m,), d_m), None, 0, "attend_m")
    late = ((x_e,), (y_e,), (d_e,))
    state_other = attend((q_other,), late, state, rows, "attend_other")
    given = exchanged(state_other, 1)
    state_own = attend((q,), late, state, 0, "attend_own")
    own, p1, p2, p3 = mix(state_own, given, w_out, h2)
    inward = swapped(p3, 1)
    joined = (p2.astype(jnp.float32) + inward.astype(jnp.float32)).astype(jnp.bfloat16)
    total = own
    for part in (swapped(joined, 2), swapped(after(p1, joined), 1)):
        total = total + part.astype(jnp.float32)
    return total.astype(jnp.bfloat16)


def solution(mesh):
    in_specs = (
        P("seq", None),
        P(None, "head", None),
        P(None, "head", None),
        P("head", None),
        P("head", None),
        P("head", None),
        P("head", None),
    )
    out_specs = P("seq", "head")
    seq, head = mesh.shape["seq"], mesh.shape["head"]
    aligned = (C // head) % 128 == 0
    body = on_device if head == 4 and seq == 8 and aligned else general_form
    return jax.shard_map(body, mesh=mesh, in_specs=in_specs, out_specs=out_specs, check_vma=False)
```

```python
import functools
import math

import jax
import jax.numpy as jnp
from jax import lax
from jax.experimental import pallas as pl
from jax.experimental.pallas import tpu as pltpu
from jax.sharding import PartitionSpec as P

C = 1536
HEAD_DIM = 64
KW = 5
DILATION_STEP = 4
EPS = 1e-06
EDGE = 16
LOG2E = math.log2(math.e)
MIB = 1 << 20
LANES = 128


def padded_2(block, sides, width):
    for axis, dim in sides:
        count = lax.axis_size(axis)
        forward = [(i, i + 1) for i in range(count - 1)]
        backward = [(target, source) for source, target in forward]
        low = lax.ppermute(
            lax.slice_in_dim(block, block.shape[dim] - width, None, axis=dim), axis, forward
        )
        high = lax.ppermute(lax.slice_in_dim(block, 0, width, axis=dim), axis, backward)
        block = jnp.concatenate([low, block, high], axis=dim)
    return block


def row_scale(hidden):
    squares = lax.psum(jnp.sum(hidden * hidden, axis=1), "head")
    return hidden * lax.rsqrt(squares / C + EPS)[:, None]


def reduce_operands(left, right):
    return lax.dot_general(
        left, right, (((1,), (1,)), ((), ())), preferred_element_type=jnp.float32
    )


def general_form(dna, conv_in, dilated_kernel_weight, w_query, w_key, w_value, w_out):
    local_row_count = dna.shape[0] // 2
    half = (KW - 1) // 2
    padded = padded_2(dna, (("seq", 0),), half)
    h1 = jnp.zeros((local_row_count, conv_in.shape[1]), jnp.float32)
    for kernel_offset in range(KW):
        rows = lax.slice(
            padded,
            (kernel_offset, 0),
            (kernel_offset + 2 * local_row_count - 1, padded.shape[1]),
            (2, 1),
        )
        h1 = h1 + reduce_operands(rows, conv_in[kernel_offset])
    gelu_output = jax.nn.gelu(row_scale(h1), approximate=True).astype(jnp.bfloat16)
    complete_output = lax.all_gather(gelu_output, "head", axis=1, tiled=True)
    broad_input = padded_2(complete_output, (("seq", 0),), DILATION_STEP)
    second_hidden = h1
    for kernel_offset in range(3):
        second_hidden = second_hidden + reduce_operands(
            broad_input[
                DILATION_STEP * kernel_offset : DILATION_STEP * kernel_offset + local_row_count
            ],
            dilated_kernel_weight[kernel_offset],
        )
    normed = row_scale(second_hidden).astype(jnp.bfloat16)
    local_width = w_query.shape[0]
    heads_here = local_width // HEAD_DIM
    piece = lax.all_gather(normed, "head", axis=1, tiled=True)
    q_acc, k_acc, v_acc = (reduce_operands(piece, w) for w in (w_query, w_key, w_value))
    query = q_acc.astype(jnp.bfloat16).reshape(local_row_count, heads_here, HEAD_DIM)
    keys = k_acc.astype(jnp.bfloat16)
    values = v_acc.astype(jnp.bfloat16)
    scale = 1.0 / math.sqrt(HEAD_DIM)
    start_state = (
        jnp.full((heads_here, local_row_count), -1e30, jnp.float32),
        jnp.zeros((heads_here, local_row_count), jnp.float32),
        jnp.zeros((local_row_count, heads_here, HEAD_DIM), jnp.float32),
    )
    key_rows = lax.all_gather(keys, "seq", axis=0, tiled=True)
    value_rows = lax.all_gather(values, "seq", axis=0, tiled=True)
    count = key_rows.shape[0]
    width = 512 if count % 512 == 0 else count
    blocks = count // width
    key_blocks = key_rows.reshape(blocks, width, heads_here, HEAD_DIM)
    value_blocks = value_rows.reshape(blocks, width, heads_here, HEAD_DIM)

    def step(state, operands):
        running, total, acc = state
        key_block, value_block = operands
        scores = (
            jnp.einsum("qhd,khd->hqk", query, key_block, preferred_element_type=jnp.float32) * scale
        )
        newest = jnp.maximum(running, jnp.max(scores, axis=2))
        factor = jnp.exp(running - newest)
        weights = jnp.exp(scores - newest[:, :, None])
        total = total * factor + jnp.sum(weights, axis=2)
        update = jnp.einsum(
            "hqk,khd->qhd",
            weights.astype(jnp.bfloat16),
            value_block,
            preferred_element_type=jnp.float32,
        )
        acc = acc * jnp.transpose(factor)[:, :, None] + update
        return ((newest, total, acc), None)

    state, _ = lax.scan(step, start_state, (key_blocks, value_blocks))
    running, total, acc = state
    attended = (
        (acc / jnp.transpose(total)[:, :, None])
        .reshape(local_row_count, local_width)
        .astype(jnp.bfloat16)
    )
    partial_out = jnp.dot(attended, w_out, preferred_element_type=jnp.float32)
    mixed = lax.psum_scatter(
        partial_out.astype(jnp.bfloat16), "head", scatter_dimension=1, tiled=True
    ).astype(jnp.float32)
    return (second_hidden + mixed).astype(jnp.bfloat16)


def nbytes(*arrays):
    return sum(math.prod(a.shape) * jnp.dtype(a.dtype).itemsize for a in arrays)


def cost(flops, arrays, transcendentals=0):
    return pl.CostEstimate(
        flops=int(flops), bytes_accessed=int(nbytes(*arrays)), transcendentals=int(transcendentals)
    )


def after(value, *others):
    return lax.optimization_barrier((value, *others))[0]


def swapped(block, mask):
    count = lax.axis_size("head")
    return lax.ppermute(block, "head", [(i, i ^ mask) for i in range(count)])


def shared(block, earlier=None):
    near = far = block
    if earlier is not None:
        near, far = after(block, earlier[1]), after(block, earlier[2])
    far = swapped(far, 2)
    near = swapped(near, 1)
    return [block, near, far]


def forwarded(parts, gate=None):
    far = parts[2] if gate is None else after(parts[2], gate)
    return [*parts, swapped(far, 1)]


def owner(mask):
    return jnp.bitwise_xor(lax.axis_index("head"), mask)


MASKS = (0, 1, 2, 3)


def store_wide(wide, start, block):
    for j in range(wide.shape[0]):
        rows = pl.ds(start, block.shape[0])
        wide[j, rows, :] = block[:, 128 * j : 128 * (j + 1)].astype(jnp.float32)


def taps_sum(wide, weight_ref, groups, copies=None):
    total = None
    for tap in range(KW):
        if copies is not None:
            copies[tap].wait()
        picked = []
        for start, count in groups:
            lanes = [
                wide[j, pl.ds(start + tap, count, stride=2), :] for j in range(wide.shape[0])
            ]
            picked.append(jnp.concatenate(lanes, axis=1).astype(jnp.bfloat16))
        taken = picked[0] if len(picked) == 1 else jnp.concatenate(picked, axis=0)
        term = reduce_operands(taken, weight_ref[tap])
        total = term if total is None else total + term
    return total


FIRST = EDGE - KW // 2


def conv_middle_kernel(dna_ref, weight_ref, h1_ref, sent_ref, wide, rows, weights, sems):
    first = pltpu.make_async_copy(dna_ref.at[pl.ds(0, rows.shape[0]), :], rows, sems.at[KW])
    copies = [
        pltpu.make_async_copy(weight_ref.at[tap], weights.at[tap], sems.at[tap])
        for tap in range(KW)
    ]
    for copy in (first, *copies):
        copy.start()
    first.wait()
    store_wide(wide, 0, rows[...])
    total = taps_sum(wide, weights, [(FIRST, sent_ref.shape[0])], copies)
    h1_ref[...] = total
    sent_ref[...] = total.astype(jnp.bfloat16)


def conv_edge_kernel(dna_ref, low_ref, high_ref, weight_ref, h1_ref, sent_ref, wide):
    rows = dna_ref.shape[0]
    upper = sent_ref.shape[0] - EDGE
    first = rows - 2 * upper
    zeros = jnp.zeros((EDGE, dna_ref.shape[1]), jnp.bfloat16)
    store_wide(wide, 0, zeros)
    store_wide(wide, EDGE, low_ref[...])
    store_wide(wide, 2 * EDGE, dna_ref[pl.ds(0, 2 * EDGE), :])
    store_wide(wide, 4 * EDGE, dna_ref[pl.ds(first, rows - first), :])
    store_wide(wide, 4 * EDGE + rows - first, high_ref[...])
    store_wide(wide, 5 * EDGE + rows - first, zeros)
    total = taps_sum(wide, weight_ref, [(FIRST, EDGE), (4 * EDGE + FIRST, upper)])
    h1_ref[...] = total
    sent_ref[...] = total.astype(jnp.bfloat16)


def first_conv(kernel, operands, weight, count, deep, name, streamed=False):
    width, out = weight.shape[2], weight.shape[1]
    kept = jax.ShapeDtypeStruct((count, out), jnp.float32)
    sent = jax.ShapeDtypeStruct((count, out), jnp.bfloat16)
    scratch = [pltpu.VMEM((width // 128, deep, 128), jnp.float32)]
    place = pltpu.VMEM
    if streamed:
        place = pltpu.HBM
        operands = [pltpu.with_memory_space_constraint(a, place) for a in operands]
        weight = pltpu.with_memory_space_constraint(weight, place)
        scratch += [
            pltpu.VMEM((deep, width), jnp.bfloat16),
            pltpu.VMEM(weight.shape, jnp.bfloat16),
            pltpu.SemaphoreType.DMA((KW + 1,)),
        ]
    return pl.pallas_call(
        kernel,
        out_shape=(kept, sent),
        in_specs=[pl.BlockSpec(memory_space=place)] * (len(operands) + 1),
        scratch_shapes=scratch,
        compiler_params=pltpu.CompilerParams(vmem_limit_bytes=24 * MIB),
        cost_estimate=cost(2 * count * out * width * KW, (*operands, weight, kept, sent)),
        name=name,
    )(*operands, weight)


def inverse_norm(blocks):
    squares = None
    for block in blocks:
        term = jnp.sum(block * block, axis=1, keepdims=True)
        squares = term if squares is None else squares + term
    return lax.rsqrt(squares / C + EPS)


def wide_blocks(parts, start, count):
    return [part[pl.ds(start, count), :].astype(jnp.float32) for part in parts]


def gelu(value):
    return jax.nn.gelu(value, approximate=True)


def columns_of(mask, width):
    return pl.ds(pl.multiple_of(owner(mask) * width, LANES), width)


def dilated_middle_kernel(a0, a1, a2, a3, h1_ref, weight_ref, h2_ref, sent_ref, act):
    parts = (a0, a1, a2, a3)
    count, width = a0.shape
    rows = h2_ref.shape[0]
    blocks = wide_blocks(parts, 0, count)
    inverse = inverse_norm(blocks)
    total = h1_ref[pl.ds(8, rows), :]
    for slot, (block, mask) in enumerate(zip(blocks, MASKS)):
        act[slot] = gelu(block * inverse)
        for tap in range(3):
            taken = act[slot, pl.ds((tap + 1) * DILATION_STEP, rows), :].astype(jnp.bfloat16)
            total = total + reduce_operands(taken, weight_ref[tap, :, columns_of(mask, width)])
    h2_ref[...] = total
    sent_ref[...] = total.astype(jnp.bfloat16)


def dilated_edge_kernel(
    m0, m1, m2, m3, e0, e1, e2, e3, hm_ref, he_ref, h2m_ref, weight_ref, h2_ref, sent_ref, act
):
    middle, edge = (m0, m1, m2, m3), (e0, e1, e2, e3)
    inner, width = m0.shape
    outer = e0.shape[0]
    rows = h2_ref.shape[0]
    upper = outer - EDGE
    position = lax.axis_index("seq") * rows + lax.broadcasted_iota(jnp.int32, (outer, 1), 0)
    place = lax.broadcasted_iota(jnp.int32, (outer, 1), 0)
    position = position + jnp.where(place < EDGE, -8, inner - 8)
    inside = (position >= 0) & (position < rows * lax.axis_size("seq"))
    outer_blocks = wide_blocks(edge, 0, outer)
    outer_inverse = jnp.where(inside, inverse_norm(outer_blocks), 0.0)
    low_blocks = wide_blocks(middle, 0, EDGE)
    low_inverse = inverse_norm(low_blocks)
    high_blocks = wide_blocks(middle, inner - EDGE, EDGE)
    high_inverse = inverse_norm(high_blocks)
    last = rows - (outer - EDGE)
    total = jnp.concatenate(
        [
            he_ref[pl.ds(8, 8), :],
            hm_ref[pl.ds(0, 8), :],
            hm_ref[pl.ds(inner - 8, 8), :],
            he_ref[pl.ds(EDGE, upper - 8), :],
        ],
        axis=0,
    )
    tail = 2 * EDGE
    for slot, mask in enumerate(MASKS):
        full = gelu(outer_blocks[slot] * outer_inverse)
        act[slot, pl.ds(0, EDGE), :] = full[:EDGE]
        act[slot, pl.ds(EDGE, EDGE), :] = gelu(low_blocks[slot] * low_inverse)
        act[slot, pl.ds(tail, EDGE), :] = gelu(high_blocks[slot] * high_inverse)
        act[slot, pl.ds(tail + EDGE, upper), :] = full[EDGE:]
        for tap in range(3):
            shifted = (tap + 1) * DILATION_STEP
            taken = jnp.concatenate(
                [
                    act[slot, pl.ds(shifted, EDGE), :],
                    act[slot, pl.ds(tail + shifted, upper), :],
                ],
                axis=0,
            ).astype(jnp.bfloat16)
            total = total + reduce_operands(taken, weight_ref[tap, :, columns_of(mask, width)])
    h2_ref[pl.ds(0, EDGE), :] = total[:EDGE]
    h2_ref[pl.ds(EDGE, last - EDGE), :] = h2m_ref[...]
    h2_ref[pl.ds(last, rows - last), :] = total[EDGE:]
    sent_ref[...] = total.astype(jnp.bfloat16)


def second_conv(kernel, operands, weight, kept_rows, sent_rows, deep, name):
    out, width = weight.shape[1], operands[0].shape[1]
    kept = jax.ShapeDtypeStruct((kept_rows, out), jnp.float32)
    sent = jax.ShapeDtypeStruct((sent_rows, out), jnp.bfloat16)
    return pl.pallas_call(
        kernel,
        out_shape=(kept, sent),
        scratch_shapes=[pltpu.VMEM((4, deep, width), jnp.float32)],
        compiler_params=pltpu.CompilerParams(vmem_limit_bytes=24 * MIB),
        cost_estimate=cost(
            2 * sent_rows * out * weight.shape[2] * 3,
            (*operands, weight, kept, sent),
            deep * weight.shape[2],
        ),
        name=name,
    )(*operands, weight)


def projections(parts, wq, wk, wv, kv_ref):
    width = parts[0].shape[1]
    rows, out = parts[0].shape[0], wq.shape[0]
    blocks = [part[...].astype(jnp.float32) for part in parts]
    inverse = inverse_norm(blocks)
    normed = [(block * inverse).astype(jnp.bfloat16) for block in blocks]

    def product(weight_ref, start=0, stop=rows, weight_first=False):
        total = None
        for part, mask in zip(normed, MASKS):
            weight = weight_ref[:, columns_of(mask, width)]
            taken = part[start:stop]
            pair = (weight, taken) if weight_first else (taken, weight)
            term = reduce_operands(*pair)
            total = term if total is None else total + term
        return total

    kv_ref[:, :out] = product(wk).astype(jnp.bfloat16)
    turned = rows - rows % LANES
    value = product(wv, 0, turned, True).astype(jnp.bfloat16)
    for row in range(0, turned, LANES):
        for lane in range(0, out, LANES):
            kv_ref[pl.ds(row, LANES), pl.ds(out + lane, LANES)] = value[
                lane : lane + LANES, row : row + LANES
            ]
    if turned < rows:
        value = product(wv, turned, rows)
        kv_ref[pl.ds(turned, rows - turned), out:] = value.astype(jnp.bfloat16)
    scale = LOG2E / math.sqrt(HEAD_DIM)
    return (product(wq) * scale).astype(jnp.bfloat16)


def project_middle_kernel(a0, a1, a2, a3, wq, wk, wv, q_ref, kv_ref):
    q_ref[...] = projections((a0, a1, a2, a3), wq, wk, wv, kv_ref)


def project_edge_kernel(a0, a1, a2, a3, qm_ref, wq, wk, wv, q_ref, kv_ref):
    query = projections((a0, a1, a2, a3), wq, wk, wv, kv_ref)
    inner, rows = qm_ref.shape[0], q_ref.shape[0]
    q_ref[pl.ds(0, EDGE), :] = query[:EDGE]
    q_ref[pl.ds(EDGE, inner), :] = qm_ref[...]
    q_ref[pl.ds(EDGE + inner, rows - EDGE - inner), :] = query[EDGE:]


def project(kernel, operands, weights, q_rows, name):
    rows, out = operands[0].shape[0], weights[0].shape[0]
    q = jax.ShapeDtypeStruct((q_rows, out), jnp.bfloat16)
    kv = jax.ShapeDtypeStruct((rows, 2 * out), jnp.bfloat16)
    return pl.pallas_call(
        kernel,
        out_shape=(q, kv),
        compiler_params=pltpu.CompilerParams(vmem_limit_bytes=20 * MIB),
        cost_estimate=cost(6 * rows * out * C, (*operands, *weights, q, kv)),
        name=name,
    )(*operands, *weights)


TILE = 64


def split_rows(block):
    turned = block.shape[0] - block.shape[0] % LANES
    return turned, block.shape[0] - turned


def turned_values(blocks, width, pair):
    lanes = pl.ds(width + pair * LANES, LANES)
    values = []
    for block in blocks:
        for row in range(0, split_rows(block)[0], LANES):
            values.append(block[pl.ds(row, LANES), lanes])
    rest = []
    for block in blocks:
        start, count = split_rows(block)
        if count:
            rest.append(block[pl.ds(start, count), lanes].astype(jnp.float32))
    if rest:
        values.append(jnp.transpose(jnp.concatenate(rest, axis=0)).astype(jnp.bfloat16))
    return jnp.concatenate(values, axis=1)


def ordered_keys(blocks, pair):
    lanes = pl.ds(pair * LANES, LANES)
    keys = [block[pl.ds(0, split_rows(block)[0]), lanes] for block in blocks]
    for block in blocks:
        start, count = split_rows(block)
        if count:
            keys.append(block[pl.ds(start, count), lanes])
    return jnp.concatenate(keys, axis=0)


def partial_attention(query, keys, values, scores, weights, head, lane):
    pair, half = divmod(head, 2)
    mine = query[:, pair * LANES : (pair + 1) * LANES]
    mine = jnp.where((lane // HEAD_DIM) == half, mine, jnp.zeros_like(mine))
    scores[...] = reduce_operands(keys, mine)
    columns = scores.shape[1]
    top = None
    for start in range(0, scores.shape[0], TILE):
        tile = jnp.max(scores[pl.ds(start, TILE), :].reshape(-1, 8, columns), axis=0)
        top = tile if top is None else jnp.maximum(top, tile)
    top = jnp.max(top, axis=0, keepdims=True)
    total = None
    for start in range(0, scores.shape[0], TILE):
        weight = jnp.exp2(scores[pl.ds(start, TILE), :] - top)
        tile = jnp.sum(weight.reshape(-1, 8, columns), axis=0)
        total = tile if total is None else total + tile
        weights[pl.ds(start, TILE), :] = weight.astype(jnp.bfloat16)
    values = values[half * HEAD_DIM : (half + 1) * HEAD_DIM]
    out = jnp.dot(values, weights[...], preferred_element_type=jnp.float32)
    return out, top, jnp.sum(total, axis=0, keepdims=True)


def state_parts(state, head, width, columns):
    return (
        state[pl.ds(head * HEAD_DIM, HEAD_DIM), columns],
        state[pl.ds(width + head, 1), columns],
        state[pl.ds(width + 8 + head, 1), columns],
    )


def merged_parts(one, other):
    top = jnp.maximum(one[1], other[1])
    first, second = jnp.exp2(one[1] - top), jnp.exp2(other[1] - top)
    return first * one[0] + second * other[0], top, first * one[2] + second * other[2]


def attend_kernel(first_column, q_refs, blocks, state, out_ref, scores, weights):
    width = q_refs[0].shape[1]
    query = jnp.concatenate([ref[...] for ref in q_refs], axis=0)
    columns = query.shape[0]
    lane = lax.broadcasted_iota(jnp.int32, (columns, LANES), 1)
    out_ref[pl.ds(width, 16), :] = jnp.zeros((16, columns), jnp.float32)
    for head in range(width // HEAD_DIM):
        if head % 2 == 0:
            keys = ordered_keys(blocks, head // 2)
            values = turned_values(blocks, width, head // 2)
        part = partial_attention(
            query, keys, values, scores.at[head % 2], weights.at[head % 2], head, lane
        )
        if state is not None:
            part = merged_parts(
                part, state_parts(state, head, width, pl.ds(first_column, columns))
            )
        out_ref[pl.ds(head * HEAD_DIM, HEAD_DIM), :] = part[0]
        out_ref[pl.ds(width + head, 1), :] = part[1]
        out_ref[pl.ds(width + 8 + head, 1), :] = part[2]


def attend(queries, blocks, state, first_column, name):
    rows, width = queries[0].shape
    columns = rows * len(queries)
    extent = sum(block.shape[0] for block in blocks)
    out = jax.ShapeDtypeStruct((width + 16, columns), jnp.float32)
    operands = (*queries, *blocks) + (() if state is None else (state,))

    def kernel(*refs):
        q_refs, block_refs = refs[: len(queries)], refs[len(queries) :][: len(blocks)]
        state_ref = None if state is None else refs[len(operands) - 1]
        attend_kernel(
            first_column, q_refs, block_refs, state_ref, *refs[len(operands) :]
        )

    return pl.pallas_call(
        kernel,
        out_shape=out,
        scratch_shapes=[
            pltpu.VMEM((2, extent, columns), jnp.float32),
            pltpu.VMEM((2, extent, columns), jnp.bfloat16),
        ],
        compiler_params=pltpu.CompilerParams(vmem_limit_bytes=24 * MIB),
        cost_estimate=cost(
            4 * columns * width * extent, (*operands, out), columns * extent * width // HEAD_DIM
        ),
        name=name,
    )(*operands)


def mix_kernel(own_state, other_state, w_ref, h2_ref, own_ref, p1, p2, p3, attended):
    rows, width = h2_ref.shape
    for pair in range(width // LANES):
        halves = []
        for head in (2 * pair, 2 * pair + 1):
            out, _, total = merged_parts(
                state_parts(own_state, head, width, pl.ds(0, rows)),
                state_parts(other_state, head, width, pl.ds(0, rows)),
            )
            halves.append(out / total)
        merged = jnp.transpose(jnp.concatenate(halves, axis=0))
        attended[:, pl.ds(pair * LANES, LANES)] = merged.astype(jnp.bfloat16)

    def product(mask):
        return jnp.dot(
            attended[...], w_ref[:, columns_of(mask, width)], preferred_element_type=jnp.float32
        )

    for ref, mask in ((p3, 3), (p2, 2), (p1, 1)):
        ref[...] = product(mask).astype(jnp.bfloat16)
    own_ref[...] = product(0) + h2_ref[...]


def mix(own_state, other_state, w_out, h2):
    rows, width = h2.shape
    own = jax.ShapeDtypeStruct((rows, width), jnp.float32)
    part = jax.ShapeDtypeStruct((rows, width), jnp.bfloat16)
    operands = (own_state, other_state, w_out, h2)
    return pl.pallas_call(
        mix_kernel,
        out_shape=(own, part, part, part),
        scratch_shapes=[pltpu.VMEM((rows, width), jnp.bfloat16)],
        compiler_params=pltpu.CompilerParams(vmem_limit_bytes=16 * MIB),
        cost_estimate=cost(
            2 * rows * width * w_out.shape[1], (*operands, own, part, part, part)
        ),
        name="mix",
    )(*operands)


def exchanged(block, mask):
    count = lax.axis_size("seq")
    return lax.ppermute(block, "seq", [(i, i ^ mask) for i in range(count)])


def on_device(dna, conv_in, dilated_kernel_weight, w_query, w_key, w_value, w_out):
    count = lax.axis_size("seq")
    rows = dna.shape[0] // 2
    inner = rows // 2
    outer = rows - inner
    low = lax.ppermute(dna[-EDGE:], "seq", [(i, i + 1) for i in range(count - 1)])
    high = lax.ppermute(dna[:EDGE], "seq", [(i + 1, i) for i in range(count - 1)])
    h1_m, sent = first_conv(
        conv_middle_kernel,
        (dna,),
        conv_in,
        inner + EDGE,
        2 * (inner + 2 * EDGE),
        "conv_middle",
        True,
    )
    wide_m = forwarded(shared(sent))
    h1_e, sent = first_conv(
        conv_edge_kernel, (dna, after(low, *wide_m[1:3]), high), conv_in, outer, 2 * (outer + 2 * EDGE), "conv_edge"
    )
    wide_e = shared(sent)
    h2_m, sent = second_conv(
        dilated_middle_kernel,
        (*wide_m, after(h1_m, sent)),
        dilated_kernel_weight,
        inner,
        inner,
        inner + EDGE,
        "dilated_middle",
    )
    normed_m = forwarded(shared(sent, wide_e))
    wide_e = forwarded(wide_e, sent)
    h2, sent = second_conv(
        dilated_edge_kernel,
        (*wide_m, *wide_e, h1_m, h1_e, h2_m),
        dilated_kernel_weight,
        rows,
        outer,
        outer + 2 * EDGE,
        "dilated_edge",
    )
    normed_e = shared(sent, normed_m)
    normed_m[0] = after(normed_m[0], sent)
    weights = (w_query, w_key, w_value)
    q_m, kv_m = project(project_middle_kernel, normed_m, weights, inner, "project_middle")
    x_m, y_m, d_m = (exchanged(kv_m, mask) for mask in (2, 4, 6))
    normed_e = forwarded(normed_e, kv_m)
    q, kv_e = project(project_edge_kernel, (*normed_e, q_m), weights, rows, "project_edge")
    q_other, x_e, y_e, d_e = exchanged(q, 1), *(exchanged(kv_e, mask) for mask in (2, 4, 6))
    state = attend((q, q_other), (kv_m, kv_e, x_m, y_m, d_m), None, 0, "attend_m")
    late = (x_e, y_e, d_e)
    state_other = attend((q_other,), late, state, rows, "attend_other")
    given = exchanged(state_other, 1)
    state_own = attend((q,), late, state, 0, "attend_own")
    own, p1, p2, p3 = mix(state_own, given, w_out, h2)
    inward = swapped(p3, 1)
    joined = (p2.astype(jnp.float32) + inward.astype(jnp.float32)).astype(jnp.bfloat16)
    beside = swapped(after(p1, joined), 1)
    total = own + swapped(joined, 2).astype(jnp.float32)
    total = after(total) + beside.astype(jnp.float32)
    return total.astype(jnp.bfloat16)


def solution(mesh):
    in_specs = (
        P("seq", None),
        P(None, "head", None),
        P(None, "head", None),
        P("head", None),
        P("head", None),
        P("head", None),
        P("head", None),
    )
    out_specs = P("seq", "head")
    seq, head = mesh.shape["seq"], mesh.shape["head"]
    aligned = (C // head) % 128 == 0
    body = on_device if head == 4 and seq == 8 and aligned else general_form
    return jax.shard_map(body, mesh=mesh, in_specs=in_specs, out_specs=out_specs, check_vma=False)
```

```python
import functools
import math

import jax
import jax.numpy as jnp
from jax import lax
from jax.experimental import pallas as pl
from jax.experimental.pallas import tpu as pltpu
from jax.sharding import PartitionSpec as P

C = 1536
HEAD_DIM = 64
KW = 5
DILATION_STEP = 4
EPS = 1e-06
EDGE = 16
LOG2E = math.log2(math.e)
MIB = 1 << 20
LANES = 128


def padded_2(block, sides, width):
    for axis, dim in sides:
        count = lax.axis_size(axis)
        forward = [(i, i + 1) for i in range(count - 1)]
        backward = [(target, source) for source, target in forward]
        low = lax.ppermute(
            lax.slice_in_dim(block, block.shape[dim] - width, None, axis=dim), axis, forward
        )
        high = lax.ppermute(lax.slice_in_dim(block, 0, width, axis=dim), axis, backward)
        block = jnp.concatenate([low, block, high], axis=dim)
    return block


def row_scale(hidden):
    squares = lax.psum(jnp.sum(hidden * hidden, axis=1), "head")
    return hidden * lax.rsqrt(squares / C + EPS)[:, None]


def reduce_operands(left, right):
    return lax.dot_general(
        left, right, (((1,), (1,)), ((), ())), preferred_element_type=jnp.float32
    )


def general_form(dna, conv_in, dilated_kernel_weight, w_query, w_key, w_value, w_out):
    local_row_count = dna.shape[0] // 2
    half = (KW - 1) // 2
    padded = padded_2(dna, (("seq", 0),), half)
    h1 = jnp.zeros((local_row_count, conv_in.shape[1]), jnp.float32)
    for kernel_offset in range(KW):
        rows = lax.slice(
            padded,
            (kernel_offset, 0),
            (kernel_offset + 2 * local_row_count - 1, padded.shape[1]),
            (2, 1),
        )
        h1 = h1 + reduce_operands(rows, conv_in[kernel_offset])
    gelu_output = jax.nn.gelu(row_scale(h1), approximate=True).astype(jnp.bfloat16)
    complete_output = lax.all_gather(gelu_output, "head", axis=1, tiled=True)
    broad_input = padded_2(complete_output, (("seq", 0),), DILATION_STEP)
    second_hidden = h1
    for kernel_offset in range(3):
        second_hidden = second_hidden + reduce_operands(
            broad_input[
                DILATION_STEP * kernel_offset : DILATION_STEP * kernel_offset + local_row_count
            ],
            dilated_kernel_weight[kernel_offset],
        )
    normed = row_scale(second_hidden).astype(jnp.bfloat16)
    local_width = w_query.shape[0]
    heads_here = local_width // HEAD_DIM
    piece = lax.all_gather(normed, "head", axis=1, tiled=True)
    q_acc, k_acc, v_acc = (reduce_operands(piece, w) for w in (w_query, w_key, w_value))
    query = q_acc.astype(jnp.bfloat16).reshape(local_row_count, heads_here, HEAD_DIM)
    keys = k_acc.astype(jnp.bfloat16)
    values = v_acc.astype(jnp.bfloat16)
    scale = 1.0 / math.sqrt(HEAD_DIM)
    start_state = (
        jnp.full((heads_here, local_row_count), -1e30, jnp.float32),
        jnp.zeros((heads_here, local_row_count), jnp.float32),
        jnp.zeros((local_row_count, heads_here, HEAD_DIM), jnp.float32),
    )
    key_rows = lax.all_gather(keys, "seq", axis=0, tiled=True)
    value_rows = lax.all_gather(values, "seq", axis=0, tiled=True)
    count = key_rows.shape[0]
    width = 512 if count % 512 == 0 else count
    blocks = count // width
    key_blocks = key_rows.reshape(blocks, width, heads_here, HEAD_DIM)
    value_blocks = value_rows.reshape(blocks, width, heads_here, HEAD_DIM)

    def step(state, operands):
        running, total, acc = state
        key_block, value_block = operands
        scores = (
            jnp.einsum("qhd,khd->hqk", query, key_block, preferred_element_type=jnp.float32) * scale
        )
        newest = jnp.maximum(running, jnp.max(scores, axis=2))
        factor = jnp.exp(running - newest)
        weights = jnp.exp(scores - newest[:, :, None])
        total = total * factor + jnp.sum(weights, axis=2)
        update = jnp.einsum(
            "hqk,khd->qhd",
            weights.astype(jnp.bfloat16),
            value_block,
            preferred_element_type=jnp.float32,
        )
        acc = acc * jnp.transpose(factor)[:, :, None] + update
        return ((newest, total, acc), None)

    state, _ = lax.scan(step, start_state, (key_blocks, value_blocks))
    running, total, acc = state
    attended = (
        (acc / jnp.transpose(total)[:, :, None])
        .reshape(local_row_count, local_width)
        .astype(jnp.bfloat16)
    )
    partial_out = jnp.dot(attended, w_out, preferred_element_type=jnp.float32)
    mixed = lax.psum_scatter(
        partial_out.astype(jnp.bfloat16), "head", scatter_dimension=1, tiled=True
    ).astype(jnp.float32)
    return (second_hidden + mixed).astype(jnp.bfloat16)


def nbytes(*arrays):
    return sum(math.prod(a.shape) * jnp.dtype(a.dtype).itemsize for a in arrays)


def cost(flops, arrays, transcendentals=0):
    return pl.CostEstimate(
        flops=int(flops), bytes_accessed=int(nbytes(*arrays)), transcendentals=int(transcendentals)
    )


def after(value, *others):
    return lax.optimization_barrier((value, *others))[0]


def swapped(block, mask):
    count = lax.axis_size("head")
    return lax.ppermute(block, "head", [(i, i ^ mask) for i in range(count)])


def shared(block, earlier=None):
    near = far = block
    if earlier is not None:
        near, far = after(block, earlier[1]), after(block, earlier[2])
    far = swapped(far, 2)
    near = swapped(near, 1)
    return [block, near, far]


def forwarded(parts, gate=None):
    far = parts[2] if gate is None else after(parts[2], gate)
    return [*parts, swapped(far, 1)]


def owner(mask):
    return jnp.bitwise_xor(lax.axis_index("head"), mask)


MASKS = (0, 1, 2, 3)


def store_wide(wide, start, block):
    for j in range(wide.shape[0]):
        rows = pl.ds(start, block.shape[0])
        wide[j, rows, :] = block[:, 128 * j : 128 * (j + 1)].astype(jnp.float32)


def taps_sum(wide, weight_ref, groups, copies=None):
    total = None
    for tap in range(KW):
        if copies is not None:
            copies[tap].wait()
        picked = []
        for start, count in groups:
            lanes = [
                wide[j, pl.ds(start + tap, count, stride=2), :] for j in range(wide.shape[0])
            ]
            picked.append(jnp.concatenate(lanes, axis=1).astype(jnp.bfloat16))
        taken = picked[0] if len(picked) == 1 else jnp.concatenate(picked, axis=0)
        term = reduce_operands(taken, weight_ref[tap])
        total = term if total is None else total + term
    return total


FIRST = EDGE - KW // 2


def conv_middle_kernel(dna_ref, weight_ref, h1_ref, sent_ref, wide, rows, weights, sems):
    first = pltpu.make_async_copy(dna_ref.at[pl.ds(0, rows.shape[0]), :], rows, sems.at[KW])
    copies = [
        pltpu.make_async_copy(weight_ref.at[tap], weights.at[tap], sems.at[tap])
        for tap in range(KW)
    ]
    for copy in (first, *copies):
        copy.start()
    first.wait()
    store_wide(wide, 0, rows[...])
    total = taps_sum(wide, weights, [(FIRST, sent_ref.shape[0])], copies)
    h1_ref[...] = total
    sent_ref[...] = total.astype(jnp.bfloat16)


def conv_edge_kernel(dna_ref, low_ref, high_ref, weight_ref, h1_ref, sent_ref, wide):
    rows = dna_ref.shape[0]
    upper = sent_ref.shape[0] - EDGE
    first = rows - 2 * upper
    zeros = jnp.zeros((EDGE, dna_ref.shape[1]), jnp.bfloat16)
    store_wide(wide, 0, zeros)
    store_wide(wide, EDGE, low_ref[...])
    store_wide(wide, 2 * EDGE, dna_ref[pl.ds(0, 2 * EDGE), :])
    store_wide(wide, 4 * EDGE, dna_ref[pl.ds(first, rows - first), :])
    store_wide(wide, 4 * EDGE + rows - first, high_ref[...])
    store_wide(wide, 5 * EDGE + rows - first, zeros)
    total = taps_sum(wide, weight_ref, [(FIRST, EDGE), (4 * EDGE + FIRST, upper)])
    h1_ref[...] = total
    sent_ref[...] = total.astype(jnp.bfloat16)


def first_conv(kernel, operands, weight, count, deep, name, streamed=False):
    width, out = weight.shape[2], weight.shape[1]
    kept = jax.ShapeDtypeStruct((count, out), jnp.float32)
    sent = jax.ShapeDtypeStruct((count, out), jnp.bfloat16)
    scratch = [pltpu.VMEM((width // 128, deep, 128), jnp.float32)]
    place = pltpu.VMEM
    if streamed:
        place = pltpu.HBM
        operands = [pltpu.with_memory_space_constraint(a, place) for a in operands]
        weight = pltpu.with_memory_space_constraint(weight, place)
        scratch += [
            pltpu.VMEM((deep, width), jnp.bfloat16),
            pltpu.VMEM(weight.shape, jnp.bfloat16),
            pltpu.SemaphoreType.DMA((KW + 1,)),
        ]
    return pl.pallas_call(
        kernel,
        out_shape=(kept, sent),
        in_specs=[pl.BlockSpec(memory_space=place)] * (len(operands) + 1),
        scratch_shapes=scratch,
        compiler_params=pltpu.CompilerParams(vmem_limit_bytes=24 * MIB),
        cost_estimate=cost(2 * count * out * width * KW, (*operands, weight, kept, sent)),
        name=name,
    )(*operands, weight)


def inverse_norm(blocks):
    squares = None
    for block in blocks:
        term = jnp.sum(block * block, axis=1, keepdims=True)
        squares = term if squares is None else squares + term
    return lax.rsqrt(squares / C + EPS)


def wide_blocks(parts, start, count):
    return [part[pl.ds(start, count), :].astype(jnp.float32) for part in parts]


def gelu(value):
    return jax.nn.gelu(value, approximate=True)


def columns_of(mask, width):
    return pl.ds(pl.multiple_of(owner(mask) * width, LANES), width)


def dilated_middle_kernel(a0, a1, a2, a3, h1_ref, weight_ref, h2_ref, sent_ref, act):
    parts = (a0, a1, a2, a3)
    count, width = a0.shape
    rows = h2_ref.shape[0]
    blocks = wide_blocks(parts, 0, count)
    inverse = inverse_norm(blocks)
    total = h1_ref[pl.ds(8, rows), :]
    for slot, (block, mask) in enumerate(zip(blocks, MASKS)):
        act[slot] = gelu(block * inverse)
        for tap in range(3):
            taken = act[slot, pl.ds((tap + 1) * DILATION_STEP, rows), :].astype(jnp.bfloat16)
            total = total + reduce_operands(taken, weight_ref[tap, :, columns_of(mask, width)])
    h2_ref[...] = total
    sent_ref[...] = total.astype(jnp.bfloat16)


def dilated_edge_kernel(
    m0, m1, m2, m3, e0, e1, e2, e3, hm_ref, he_ref, h2m_ref, weight_ref, h2_ref, sent_ref, act
):
    middle, edge = (m0, m1, m2, m3), (e0, e1, e2, e3)
    inner, width = m0.shape
    outer = e0.shape[0]
    rows = h2_ref.shape[0]
    upper = outer - EDGE
    position = lax.axis_index("seq") * rows + lax.broadcasted_iota(jnp.int32, (outer, 1), 0)
    place = lax.broadcasted_iota(jnp.int32, (outer, 1), 0)
    position = position + jnp.where(place < EDGE, -8, inner - 8)
    inside = (position >= 0) & (position < rows * lax.axis_size("seq"))
    outer_blocks = wide_blocks(edge, 0, outer)
    outer_inverse = jnp.where(inside, inverse_norm(outer_blocks), 0.0)
    low_blocks = wide_blocks(middle, 0, EDGE)
    low_inverse = inverse_norm(low_blocks)
    high_blocks = wide_blocks(middle, inner - EDGE, EDGE)
    high_inverse = inverse_norm(high_blocks)
    last = rows - (outer - EDGE)
    total = jnp.concatenate(
        [
            he_ref[pl.ds(8, 8), :],
            hm_ref[pl.ds(0, 8), :],
            hm_ref[pl.ds(inner - 8, 8), :],
            he_ref[pl.ds(EDGE, upper - 8), :],
        ],
        axis=0,
    )
    tail = 2 * EDGE
    for slot, mask in enumerate(MASKS):
        full = gelu(outer_blocks[slot] * outer_inverse)
        act[slot, pl.ds(0, EDGE), :] = full[:EDGE]
        act[slot, pl.ds(EDGE, EDGE), :] = gelu(low_blocks[slot] * low_inverse)
        act[slot, pl.ds(tail, EDGE), :] = gelu(high_blocks[slot] * high_inverse)
        act[slot, pl.ds(tail + EDGE, upper), :] = full[EDGE:]
        for tap in range(3):
            shifted = (tap + 1) * DILATION_STEP
            taken = jnp.concatenate(
                [
                    act[slot, pl.ds(shifted, EDGE), :],
                    act[slot, pl.ds(tail + shifted, upper), :],
                ],
                axis=0,
            ).astype(jnp.bfloat16)
            total = total + reduce_operands(taken, weight_ref[tap, :, columns_of(mask, width)])
    h2_ref[pl.ds(0, EDGE), :] = total[:EDGE]
    h2_ref[pl.ds(EDGE, last - EDGE), :] = h2m_ref[...]
    h2_ref[pl.ds(last, rows - last), :] = total[EDGE:]
    sent_ref[...] = total.astype(jnp.bfloat16)


def second_conv(kernel, operands, weight, kept_rows, sent_rows, deep, name):
    out, width = weight.shape[1], operands[0].shape[1]
    kept = jax.ShapeDtypeStruct((kept_rows, out), jnp.float32)
    sent = jax.ShapeDtypeStruct((sent_rows, out), jnp.bfloat16)
    return pl.pallas_call(
        kernel,
        out_shape=(kept, sent),
        scratch_shapes=[pltpu.VMEM((4, deep, width), jnp.float32)],
        compiler_params=pltpu.CompilerParams(vmem_limit_bytes=24 * MIB),
        cost_estimate=cost(
            2 * sent_rows * out * weight.shape[2] * 3,
            (*operands, weight, kept, sent),
            deep * weight.shape[2],
        ),
        name=name,
    )(*operands, weight)


def projections(parts, wq, wk, wv, kv_ref):
    width = parts[0].shape[1]
    rows, out = parts[0].shape[0], wq.shape[0]
    blocks = [part[...].astype(jnp.float32) for part in parts]
    inverse = inverse_norm(blocks)
    normed = [(block * inverse).astype(jnp.bfloat16) for block in blocks]

    def product(weight_ref, start=0, stop=rows, weight_first=False):
        total = None
        for part, mask in zip(normed, MASKS):
            weight = weight_ref[:, columns_of(mask, width)]
            taken = part[start:stop]
            pair = (weight, taken) if weight_first else (taken, weight)
            term = reduce_operands(*pair)
            total = term if total is None else total + term
        return total

    kv_ref[:, :out] = product(wk).astype(jnp.bfloat16)
    turned = rows - rows % LANES
    value = product(wv, 0, turned, True).astype(jnp.bfloat16)
    for row in range(0, turned, LANES):
        for lane in range(0, out, LANES):
            kv_ref[pl.ds(row, LANES), pl.ds(out + lane, LANES)] = value[
                lane : lane + LANES, row : row + LANES
            ]
    if turned < rows:
        value = product(wv, turned, rows)
        kv_ref[pl.ds(turned, rows - turned), out:] = value.astype(jnp.bfloat16)
    scale = LOG2E / math.sqrt(HEAD_DIM)
    return (product(wq) * scale).astype(jnp.bfloat16)


def project_middle_kernel(a0, a1, a2, a3, wq, wk, wv, q_ref, kv_ref):
    q_ref[...] = projections((a0, a1, a2, a3), wq, wk, wv, kv_ref)


def project_edge_kernel(a0, a1, a2, a3, qm_ref, wq, wk, wv, q_ref, kv_ref):
    query = projections((a0, a1, a2, a3), wq, wk, wv, kv_ref)
    inner, rows = qm_ref.shape[0], q_ref.shape[0]
    q_ref[pl.ds(0, EDGE), :] = query[:EDGE]
    q_ref[pl.ds(EDGE, inner), :] = qm_ref[...]
    q_ref[pl.ds(EDGE + inner, rows - EDGE - inner), :] = query[EDGE:]


def project(kernel, operands, weights, q_rows, name):
    rows, out = operands[0].shape[0], weights[0].shape[0]
    q = jax.ShapeDtypeStruct((q_rows, out), jnp.bfloat16)
    kv = jax.ShapeDtypeStruct((rows, 2 * out), jnp.bfloat16)
    return pl.pallas_call(
        kernel,
        out_shape=(q, kv),
        compiler_params=pltpu.CompilerParams(vmem_limit_bytes=20 * MIB),
        cost_estimate=cost(6 * rows * out * C, (*operands, *weights, q, kv)),
        name=name,
    )(*operands, *weights)


TILE = 64


def split_rows(block):
    turned = block.shape[0] - block.shape[0] % LANES
    return turned, block.shape[0] - turned


def turned_values(blocks, width, pair):
    lanes = pl.ds(width + pair * LANES, LANES)
    values = []
    for block in blocks:
        for row in range(0, split_rows(block)[0], LANES):
            values.append(block[pl.ds(row, LANES), lanes])
    rest = []
    for block in blocks:
        start, count = split_rows(block)
        if count:
            rest.append(block[pl.ds(start, count), lanes].astype(jnp.float32))
    if rest:
        values.append(jnp.transpose(jnp.concatenate(rest, axis=0)).astype(jnp.bfloat16))
    return jnp.concatenate(values, axis=1)


def ordered_keys(blocks, pair):
    lanes = pl.ds(pair * LANES, LANES)
    keys = [block[pl.ds(0, split_rows(block)[0]), lanes] for block in blocks]
    for block in blocks:
        start, count = split_rows(block)
        if count:
            keys.append(block[pl.ds(start, count), lanes])
    return jnp.concatenate(keys, axis=0)


def partial_attention(query, keys, values, scores, weights, head, lane):
    pair, half = divmod(head, 2)
    mine = query[:, pair * LANES : (pair + 1) * LANES]
    mine = jnp.where((lane // HEAD_DIM) == half, mine, jnp.zeros_like(mine))
    scores[...] = reduce_operands(keys, mine)
    columns = scores.shape[1]
    top = None
    for start in range(0, scores.shape[0], TILE):
        tile = jnp.max(scores[pl.ds(start, TILE), :].reshape(-1, 8, columns), axis=0)
        top = tile if top is None else jnp.maximum(top, tile)
    top = jnp.max(top, axis=0, keepdims=True)
    total = None
    for start in range(0, scores.shape[0], TILE):
        weight = jnp.exp2(scores[pl.ds(start, TILE), :] - top)
        tile = jnp.sum(weight.reshape(-1, 8, columns), axis=0)
        total = tile if total is None else total + tile
        weights[pl.ds(start, TILE), :] = weight.astype(jnp.bfloat16)
    values = values[half * HEAD_DIM : (half + 1) * HEAD_DIM]
    out = jnp.dot(values, weights[...], preferred_element_type=jnp.float32)
    return out, top, jnp.sum(total, axis=0, keepdims=True)


def state_parts(state, head, width, columns):
    return (
        state[pl.ds(head * HEAD_DIM, HEAD_DIM), columns],
        state[pl.ds(width + head, 1), columns],
        state[pl.ds(width + 8 + head, 1), columns],
    )


def merged_parts(one, other):
    top = jnp.maximum(one[1], other[1])
    first, second = jnp.exp2(one[1] - top), jnp.exp2(other[1] - top)
    return first * one[0] + second * other[0], top, first * one[2] + second * other[2]


def attend_kernel(first_column, q_refs, blocks, state, out_ref, scores, weights):
    width = q_refs[0].shape[1]
    query = jnp.concatenate([ref[...] for ref in q_refs], axis=0)
    columns = query.shape[0]
    lane = lax.broadcasted_iota(jnp.int32, (columns, LANES), 1)
    out_ref[pl.ds(width, 16), :] = jnp.zeros((16, columns), jnp.float32)
    for head in range(width // HEAD_DIM):
        if head % 2 == 0:
            keys = ordered_keys(blocks, head // 2)
            values = turned_values(blocks, width, head // 2)
        part = partial_attention(
            query, keys, values, scores.at[head % 2], weights.at[head % 2], head, lane
        )
        if state is not None:
            part = merged_parts(
                part, state_parts(state, head, width, pl.ds(first_column, columns))
            )
        out_ref[pl.ds(head * HEAD_DIM, HEAD_DIM), :] = part[0]
        out_ref[pl.ds(width + head, 1), :] = part[1]
        out_ref[pl.ds(width + 8 + head, 1), :] = part[2]


def attend(queries, blocks, state, first_column, name):
    rows, width = queries[0].shape
    columns = rows * len(queries)
    extent = sum(block.shape[0] for block in blocks)
    out = jax.ShapeDtypeStruct((width + 16, columns), jnp.float32)
    operands = (*queries, *blocks) + (() if state is None else (state,))

    def kernel(*refs):
        q_refs, block_refs = refs[: len(queries)], refs[len(queries) :][: len(blocks)]
        state_ref = None if state is None else refs[len(operands) - 1]
        attend_kernel(
            first_column, q_refs, block_refs, state_ref, *refs[len(operands) :]
        )

    return pl.pallas_call(
        kernel,
        out_shape=out,
        scratch_shapes=[
            pltpu.VMEM((2, extent, columns), jnp.float32),
            pltpu.VMEM((2, extent, columns), jnp.bfloat16),
        ],
        compiler_params=pltpu.CompilerParams(vmem_limit_bytes=24 * MIB),
        cost_estimate=cost(
            4 * columns * width * extent, (*operands, out), columns * extent * width // HEAD_DIM
        ),
        name=name,
    )(*operands)


def mix_kernel(own_state, other_state, w_ref, h2_ref, own_ref, p1, p2, p3, attended):
    rows, width = h2_ref.shape
    for pair in range(width // LANES):
        halves = []
        for head in (2 * pair, 2 * pair + 1):
            out, _, total = merged_parts(
                state_parts(own_state, head, width, pl.ds(0, rows)),
                state_parts(other_state, head, width, pl.ds(0, rows)),
            )
            halves.append(out / total)
        merged = jnp.transpose(jnp.concatenate(halves, axis=0))
        attended[:, pl.ds(pair * LANES, LANES)] = merged.astype(jnp.bfloat16)

    def product(mask):
        return jnp.dot(
            attended[...], w_ref[:, columns_of(mask, width)], preferred_element_type=jnp.float32
        )

    for ref, mask in ((p3, 3), (p2, 2), (p1, 1)):
        ref[...] = product(mask).astype(jnp.bfloat16)
    own_ref[...] = product(0) + h2_ref[...]


def mix(own_state, other_state, w_out, h2):
    rows, width = h2.shape
    own = jax.ShapeDtypeStruct((rows, width), jnp.float32)
    part = jax.ShapeDtypeStruct((rows, width), jnp.bfloat16)
    operands = (own_state, other_state, w_out, h2)
    return pl.pallas_call(
        mix_kernel,
        out_shape=(own, part, part, part),
        scratch_shapes=[pltpu.VMEM((rows, width), jnp.bfloat16)],
        compiler_params=pltpu.CompilerParams(vmem_limit_bytes=16 * MIB),
        cost_estimate=cost(
            2 * rows * width * w_out.shape[1], (*operands, own, part, part, part)
        ),
        name="mix",
    )(*operands)


def exchanged(block, mask):
    count = lax.axis_size("seq")
    return lax.ppermute(block, "seq", [(i, i ^ mask) for i in range(count)])


def on_device(dna, conv_in, dilated_kernel_weight, w_query, w_key, w_value, w_out):
    count = lax.axis_size("seq")
    rows = dna.shape[0] // 2
    inner = rows // 2
    outer = rows - inner
    low = lax.ppermute(dna[-EDGE:], "seq", [(i, i + 1) for i in range(count - 1)])
    high = lax.ppermute(dna[:EDGE], "seq", [(i + 1, i) for i in range(count - 1)])
    h1_m, sent = first_conv(
        conv_middle_kernel,
        (dna,),
        conv_in,
        inner + EDGE,
        2 * (inner + 2 * EDGE),
        "conv_middle",
        True,
    )
    wide_m = forwarded(shared(sent))
    h1_e, sent = first_conv(
        conv_edge_kernel, (dna, after(low, *wide_m[1:3]), high), conv_in, outer, 2 * (outer + 2 * EDGE), "conv_edge"
    )
    wide_e = shared(sent)
    h2_m, sent = second_conv(
        dilated_middle_kernel,
        (*wide_m, after(h1_m, sent)),
        dilated_kernel_weight,
        inner,
        inner,
        inner + EDGE,
        "dilated_middle",
    )
    normed_m = forwarded(shared(sent, wide_e))
    wide_e = forwarded(wide_e, sent)
    h2, sent = second_conv(
        dilated_edge_kernel,
        (*wide_m, *wide_e, h1_m, h1_e, h2_m),
        dilated_kernel_weight,
        rows,
        outer,
        outer + 2 * EDGE,
        "dilated_edge",
    )
    normed_e = shared(sent, normed_m)
    normed_m[0] = after(normed_m[0], sent)
    weights = (w_query, w_key, w_value)
    q_m, kv_m = project(project_middle_kernel, normed_m, weights, inner, "project_middle")
    x_m, y_m, d_m = (exchanged(kv_m, mask) for mask in (2, 4, 6))
    normed_e = forwarded(normed_e, kv_m)
    q, kv_e = project(project_edge_kernel, (*normed_e, q_m), weights, rows, "project_edge")
    q_other, x_e, y_e, d_e = exchanged(q, 1), *(exchanged(kv_e, mask) for mask in (2, 4, 6))
    state = attend((q, q_other), (kv_m, kv_e, x_m, y_m, d_m), None, 0, "attend_m")
    state = attend((q, q_other), (x_e,), state, 0, "attend_x")
    late = (y_e, d_e)
    state_other = attend((q_other,), late, state, rows, "attend_other")
    given = exchanged(state_other, 1)
    state_own = attend((q,), late, state, 0, "attend_own")
    own, p1, p2, p3 = mix(state_own, given, w_out, h2)
    inward = swapped(p3, 1)
    joined = (p2.astype(jnp.float32) + inward.astype(jnp.float32)).astype(jnp.bfloat16)
    beside = swapped(after(p1, joined), 1)
    total = own + swapped(joined, 2).astype(jnp.float32)
    total = after(total) + beside.astype(jnp.float32)
    return total.astype(jnp.bfloat16)


def solution(mesh):
    in_specs = (
        P("seq", None),
        P(None, "head", None),
        P(None, "head", None),
        P("head", None),
        P("head", None),
        P("head", None),
        P("head", None),
    )
    out_specs = P("seq", "head")
    seq, head = mesh.shape["seq"], mesh.shape["head"]
    aligned = (C // head) % 128 == 0
    body = on_device if head == 4 and seq == 8 and aligned else general_form
    return jax.shard_map(body, mesh=mesh, in_specs=in_specs, out_specs=out_specs, check_vma=False)
```

```python
import functools
import math

import jax
import jax.numpy as jnp
from jax import lax
from jax.experimental import pallas as pl
from jax.experimental.pallas import tpu as pltpu
from jax.sharding import PartitionSpec as P

C = 1536
HEAD_DIM = 64
KW = 5
DILATION_STEP = 4
EPS = 1e-06
EDGE = 16
LOG2E = math.log2(math.e)
MIB = 1 << 20
LANES = 128


def padded_2(block, sides, width):
    for axis, dim in sides:
        count = lax.axis_size(axis)
        forward = [(i, i + 1) for i in range(count - 1)]
        backward = [(target, source) for source, target in forward]
        low = lax.ppermute(
            lax.slice_in_dim(block, block.shape[dim] - width, None, axis=dim), axis, forward
        )
        high = lax.ppermute(lax.slice_in_dim(block, 0, width, axis=dim), axis, backward)
        block = jnp.concatenate([low, block, high], axis=dim)
    return block


def row_scale(hidden):
    squares = lax.psum(jnp.sum(hidden * hidden, axis=1), "head")
    return hidden * lax.rsqrt(squares / C + EPS)[:, None]


def reduce_operands(left, right):
    return lax.dot_general(
        left, right, (((1,), (1,)), ((), ())), preferred_element_type=jnp.float32
    )


def general_form(dna, conv_in, dilated_kernel_weight, w_query, w_key, w_value, w_out):
    local_row_count = dna.shape[0] // 2
    half = (KW - 1) // 2
    padded = padded_2(dna, (("seq", 0),), half)
    h1 = jnp.zeros((local_row_count, conv_in.shape[1]), jnp.float32)
    for kernel_offset in range(KW):
        rows = lax.slice(
            padded,
            (kernel_offset, 0),
            (kernel_offset + 2 * local_row_count - 1, padded.shape[1]),
            (2, 1),
        )
        h1 = h1 + reduce_operands(rows, conv_in[kernel_offset])
    gelu_output = jax.nn.gelu(row_scale(h1), approximate=True).astype(jnp.bfloat16)
    complete_output = lax.all_gather(gelu_output, "head", axis=1, tiled=True)
    broad_input = padded_2(complete_output, (("seq", 0),), DILATION_STEP)
    second_hidden = h1
    for kernel_offset in range(3):
        second_hidden = second_hidden + reduce_operands(
            broad_input[
                DILATION_STEP * kernel_offset : DILATION_STEP * kernel_offset + local_row_count
            ],
            dilated_kernel_weight[kernel_offset],
        )
    normed = row_scale(second_hidden).astype(jnp.bfloat16)
    local_width = w_query.shape[0]
    heads_here = local_width // HEAD_DIM
    piece = lax.all_gather(normed, "head", axis=1, tiled=True)
    q_acc, k_acc, v_acc = (reduce_operands(piece, w) for w in (w_query, w_key, w_value))
    query = q_acc.astype(jnp.bfloat16).reshape(local_row_count, heads_here, HEAD_DIM)
    keys = k_acc.astype(jnp.bfloat16)
    values = v_acc.astype(jnp.bfloat16)
    scale = 1.0 / math.sqrt(HEAD_DIM)
    start_state = (
        jnp.full((heads_here, local_row_count), -1e30, jnp.float32),
        jnp.zeros((heads_here, local_row_count), jnp.float32),
        jnp.zeros((local_row_count, heads_here, HEAD_DIM), jnp.float32),
    )
    key_rows = lax.all_gather(keys, "seq", axis=0, tiled=True)
    value_rows = lax.all_gather(values, "seq", axis=0, tiled=True)
    count = key_rows.shape[0]
    width = 512 if count % 512 == 0 else count
    blocks = count // width
    key_blocks = key_rows.reshape(blocks, width, heads_here, HEAD_DIM)
    value_blocks = value_rows.reshape(blocks, width, heads_here, HEAD_DIM)

    def step(state, operands):
        running, total, acc = state
        key_block, value_block = operands
        scores = (
            jnp.einsum("qhd,khd->hqk", query, key_block, preferred_element_type=jnp.float32) * scale
        )
        newest = jnp.maximum(running, jnp.max(scores, axis=2))
        factor = jnp.exp(running - newest)
        weights = jnp.exp(scores - newest[:, :, None])
        total = total * factor + jnp.sum(weights, axis=2)
        update = jnp.einsum(
            "hqk,khd->qhd",
            weights.astype(jnp.bfloat16),
            value_block,
            preferred_element_type=jnp.float32,
        )
        acc = acc * jnp.transpose(factor)[:, :, None] + update
        return ((newest, total, acc), None)

    state, _ = lax.scan(step, start_state, (key_blocks, value_blocks))
    running, total, acc = state
    attended = (
        (acc / jnp.transpose(total)[:, :, None])
        .reshape(local_row_count, local_width)
        .astype(jnp.bfloat16)
    )
    partial_out = jnp.dot(attended, w_out, preferred_element_type=jnp.float32)
    mixed = lax.psum_scatter(
        partial_out.astype(jnp.bfloat16), "head", scatter_dimension=1, tiled=True
    ).astype(jnp.float32)
    return (second_hidden + mixed).astype(jnp.bfloat16)


def nbytes(*arrays):
    return sum(math.prod(a.shape) * jnp.dtype(a.dtype).itemsize for a in arrays)


def cost(flops, arrays, transcendentals=0):
    return pl.CostEstimate(
        flops=int(flops), bytes_accessed=int(nbytes(*arrays)), transcendentals=int(transcendentals)
    )


def after(value, *others):
    return lax.optimization_barrier((value, *others))[0]


def swapped(block, mask):
    count = lax.axis_size("head")
    return lax.ppermute(block, "head", [(i, i ^ mask) for i in range(count)])


def shared(block, earlier=None):
    near = far = block
    if earlier is not None:
        near, far = after(block, earlier[1]), after(block, earlier[2])
    far = swapped(far, 2)
    near = swapped(near, 1)
    return [block, near, far]


def forwarded(parts, gate=None):
    far = parts[2] if gate is None else after(parts[2], gate)
    return [*parts, swapped(far, 1)]


def owner(mask):
    return jnp.bitwise_xor(lax.axis_index("head"), mask)


MASKS = (0, 1, 2, 3)


def store_wide(wide, start, block):
    for j in range(wide.shape[0]):
        rows = pl.ds(start, block.shape[0])
        wide[j, rows, :] = block[:, 128 * j : 128 * (j + 1)].astype(jnp.float32)


def taps_sum(wide, weight_ref, groups, copies=None):
    total = None
    for tap in range(KW):
        if copies is not None:
            copies[tap].wait()
        picked = []
        for start, count in groups:
            lanes = [
                wide[j, pl.ds(start + tap, count, stride=2), :] for j in range(wide.shape[0])
            ]
            picked.append(jnp.concatenate(lanes, axis=1).astype(jnp.bfloat16))
        taken = picked[0] if len(picked) == 1 else jnp.concatenate(picked, axis=0)
        term = reduce_operands(taken, weight_ref[tap])
        total = term if total is None else total + term
    return total


FIRST = EDGE - KW // 2


def conv_middle_kernel(dna_ref, weight_ref, h1_ref, sent_ref, wide, rows, weights, sems):
    first = pltpu.make_async_copy(dna_ref.at[pl.ds(0, rows.shape[0]), :], rows, sems.at[KW])
    copies = [
        pltpu.make_async_copy(weight_ref.at[tap], weights.at[tap], sems.at[tap])
        for tap in range(KW)
    ]
    for copy in (first, *copies):
        copy.start()
    first.wait()
    store_wide(wide, 0, rows[...])
    total = taps_sum(wide, weights, [(FIRST, sent_ref.shape[0])], copies)
    h1_ref[...] = total
    sent_ref[...] = total.astype(jnp.bfloat16)


def conv_edge_kernel(dna_ref, low_ref, high_ref, weight_ref, h1_ref, sent_ref, wide):
    rows = dna_ref.shape[0]
    upper = sent_ref.shape[0] - EDGE
    first = rows - 2 * upper
    zeros = jnp.zeros((EDGE, dna_ref.shape[1]), jnp.bfloat16)
    store_wide(wide, 0, zeros)
    store_wide(wide, EDGE, low_ref[...])
    store_wide(wide, 2 * EDGE, dna_ref[pl.ds(0, 2 * EDGE), :])
    store_wide(wide, 4 * EDGE, dna_ref[pl.ds(first, rows - first), :])
    store_wide(wide, 4 * EDGE + rows - first, high_ref[...])
    store_wide(wide, 5 * EDGE + rows - first, zeros)
    total = taps_sum(wide, weight_ref, [(FIRST, EDGE), (4 * EDGE + FIRST, upper)])
    h1_ref[...] = total
    sent_ref[...] = total.astype(jnp.bfloat16)


def first_conv(kernel, operands, weight, count, deep, name, streamed=False):
    width, out = weight.shape[2], weight.shape[1]
    kept = jax.ShapeDtypeStruct((count, out), jnp.float32)
    sent = jax.ShapeDtypeStruct((count, out), jnp.bfloat16)
    scratch = [pltpu.VMEM((width // 128, deep, 128), jnp.float32)]
    place = pltpu.VMEM
    if streamed:
        place = pltpu.HBM
        operands = [pltpu.with_memory_space_constraint(a, place) for a in operands]
        weight = pltpu.with_memory_space_constraint(weight, place)
        scratch += [
            pltpu.VMEM((deep, width), jnp.bfloat16),
            pltpu.VMEM(weight.shape, jnp.bfloat16),
            pltpu.SemaphoreType.DMA((KW + 1,)),
        ]
    return pl.pallas_call(
        kernel,
        out_shape=(kept, sent),
        in_specs=[pl.BlockSpec(memory_space=place)] * (len(operands) + 1),
        scratch_shapes=scratch,
        compiler_params=pltpu.CompilerParams(vmem_limit_bytes=24 * MIB),
        cost_estimate=cost(2 * count * out * width * KW, (*operands, weight, kept, sent)),
        name=name,
    )(*operands, weight)


def inverse_norm(blocks):
    squares = None
    for block in blocks:
        term = jnp.sum(block * block, axis=1, keepdims=True)
        squares = term if squares is None else squares + term
    return lax.rsqrt(squares / C + EPS)


def wide_blocks(parts, start, count):
    return [part[pl.ds(start, count), :].astype(jnp.float32) for part in parts]


def gelu(value):
    return jax.nn.gelu(value, approximate=True)


def columns_of(mask, width):
    return pl.ds(pl.multiple_of(owner(mask) * width, LANES), width)


def dilated_middle_kernel(a0, a1, a2, a3, h1_ref, weight_ref, h2_ref, sent_ref, act):
    parts = (a0, a1, a2, a3)
    count, width = a0.shape
    rows = h2_ref.shape[0]
    blocks = wide_blocks(parts, 0, count)
    inverse = inverse_norm(blocks)
    total = h1_ref[pl.ds(8, rows), :]
    for slot, (block, mask) in enumerate(zip(blocks, MASKS)):
        act[slot] = gelu(block * inverse)
        for tap in range(3):
            taken = act[slot, pl.ds((tap + 1) * DILATION_STEP, rows), :].astype(jnp.bfloat16)
            total = total + reduce_operands(taken, weight_ref[tap, :, columns_of(mask, width)])
    h2_ref[...] = total
    sent_ref[...] = total.astype(jnp.bfloat16)


def dilated_edge_kernel(
    m0, m1, m2, m3, e0, e1, e2, e3, hm_ref, he_ref, h2m_ref, weight_ref, h2_ref, sent_ref, act
):
    middle, edge = (m0, m1, m2, m3), (e0, e1, e2, e3)
    inner, width = m0.shape
    outer = e0.shape[0]
    rows = h2_ref.shape[0]
    upper = outer - EDGE
    position = lax.axis_index("seq") * rows + lax.broadcasted_iota(jnp.int32, (outer, 1), 0)
    place = lax.broadcasted_iota(jnp.int32, (outer, 1), 0)
    position = position + jnp.where(place < EDGE, -8, inner - 8)
    inside = (position >= 0) & (position < rows * lax.axis_size("seq"))
    outer_blocks = wide_blocks(edge, 0, outer)
    outer_inverse = jnp.where(inside, inverse_norm(outer_blocks), 0.0)
    low_blocks = wide_blocks(middle, 0, EDGE)
    low_inverse = inverse_norm(low_blocks)
    high_blocks = wide_blocks(middle, inner - EDGE, EDGE)
    high_inverse = inverse_norm(high_blocks)
    last = rows - (outer - EDGE)
    total = jnp.concatenate(
        [
            he_ref[pl.ds(8, 8), :],
            hm_ref[pl.ds(0, 8), :],
            hm_ref[pl.ds(inner - 8, 8), :],
            he_ref[pl.ds(EDGE, upper - 8), :],
        ],
        axis=0,
    )
    tail = 2 * EDGE
    for slot, mask in enumerate(MASKS):
        full = gelu(outer_blocks[slot] * outer_inverse)
        act[slot, pl.ds(0, EDGE), :] = full[:EDGE]
        act[slot, pl.ds(EDGE, EDGE), :] = gelu(low_blocks[slot] * low_inverse)
        act[slot, pl.ds(tail, EDGE), :] = gelu(high_blocks[slot] * high_inverse)
        act[slot, pl.ds(tail + EDGE, upper), :] = full[EDGE:]
        for tap in range(3):
            shifted = (tap + 1) * DILATION_STEP
            taken = jnp.concatenate(
                [
                    act[slot, pl.ds(shifted, EDGE), :],
                    act[slot, pl.ds(tail + shifted, upper), :],
                ],
                axis=0,
            ).astype(jnp.bfloat16)
            total = total + reduce_operands(taken, weight_ref[tap, :, columns_of(mask, width)])
    h2_ref[pl.ds(0, EDGE), :] = total[:EDGE]
    h2_ref[pl.ds(EDGE, last - EDGE), :] = h2m_ref[...]
    h2_ref[pl.ds(last, rows - last), :] = total[EDGE:]
    sent_ref[...] = total.astype(jnp.bfloat16)


def second_conv(kernel, operands, weight, kept_rows, sent_rows, deep, name):
    out, width = weight.shape[1], operands[0].shape[1]
    kept = jax.ShapeDtypeStruct((kept_rows, out), jnp.float32)
    sent = jax.ShapeDtypeStruct((sent_rows, out), jnp.bfloat16)
    return pl.pallas_call(
        kernel,
        out_shape=(kept, sent),
        scratch_shapes=[pltpu.VMEM((4, deep, width), jnp.float32)],
        compiler_params=pltpu.CompilerParams(vmem_limit_bytes=24 * MIB),
        cost_estimate=cost(
            2 * sent_rows * out * weight.shape[2] * 3,
            (*operands, weight, kept, sent),
            deep * weight.shape[2],
        ),
        name=name,
    )(*operands, weight)


def projections(parts, wq, wk, wv, kv_ref):
    width = parts[0].shape[1]
    rows, out = parts[0].shape[0], wq.shape[0]
    blocks = [part[...].astype(jnp.float32) for part in parts]
    inverse = inverse_norm(blocks)
    normed = [(block * inverse).astype(jnp.bfloat16) for block in blocks]

    def product(weight_ref, start=0, stop=rows, weight_first=False):
        total = None
        for part, mask in zip(normed, MASKS):
            weight = weight_ref[:, columns_of(mask, width)]
            taken = part[start:stop]
            pair = (weight, taken) if weight_first else (taken, weight)
            term = reduce_operands(*pair)
            total = term if total is None else total + term
        return total

    kv_ref[:, :out] = product(wk).astype(jnp.bfloat16)
    turned = rows - rows % LANES
    value = product(wv, 0, turned, True).astype(jnp.bfloat16)
    for row in range(0, turned, LANES):
        for lane in range(0, out, LANES):
            kv_ref[pl.ds(row, LANES), pl.ds(out + lane, LANES)] = value[
                lane : lane + LANES, row : row + LANES
            ]
    if turned < rows:
        value = product(wv, turned, rows)
        kv_ref[pl.ds(turned, rows - turned), out:] = value.astype(jnp.bfloat16)
    scale = LOG2E / math.sqrt(HEAD_DIM)
    return (product(wq) * scale).astype(jnp.bfloat16)


def project_middle_kernel(a0, a1, a2, a3, wq, wk, wv, q_ref, kv_ref):
    q_ref[...] = projections((a0, a1, a2, a3), wq, wk, wv, kv_ref)


def project_edge_kernel(a0, a1, a2, a3, qm_ref, wq, wk, wv, q_ref, kv_ref):
    query = projections((a0, a1, a2, a3), wq, wk, wv, kv_ref)
    inner, rows = qm_ref.shape[0], q_ref.shape[0]
    q_ref[pl.ds(0, EDGE), :] = query[:EDGE]
    q_ref[pl.ds(EDGE, inner), :] = qm_ref[...]
    q_ref[pl.ds(EDGE + inner, rows - EDGE - inner), :] = query[EDGE:]


def project(kernel, operands, weights, q_rows, name):
    rows, out = operands[0].shape[0], weights[0].shape[0]
    q = jax.ShapeDtypeStruct((q_rows, out), jnp.bfloat16)
    kv = jax.ShapeDtypeStruct((rows, 2 * out), jnp.bfloat16)
    return pl.pallas_call(
        kernel,
        out_shape=(q, kv),
        compiler_params=pltpu.CompilerParams(vmem_limit_bytes=20 * MIB),
        cost_estimate=cost(6 * rows * out * C, (*operands, *weights, q, kv)),
        name=name,
    )(*operands, *weights)


TILE = 32


def split_rows(block):
    turned = block.shape[0] - block.shape[0] % LANES
    return turned, block.shape[0] - turned


def turned_values(blocks, width, pair):
    lanes = pl.ds(width + pair * LANES, LANES)
    values = []
    for block in blocks:
        for row in range(0, split_rows(block)[0], LANES):
            values.append(block[pl.ds(row, LANES), lanes])
    rest = []
    for block in blocks:
        start, count = split_rows(block)
        if count:
            rest.append(block[pl.ds(start, count), lanes].astype(jnp.float32))
    if rest:
        values.append(jnp.transpose(jnp.concatenate(rest, axis=0)).astype(jnp.bfloat16))
    return jnp.concatenate(values, axis=1)


def ordered_keys(blocks, pair):
    lanes = pl.ds(pair * LANES, LANES)
    keys = [block[pl.ds(0, split_rows(block)[0]), lanes] for block in blocks]
    for block in blocks:
        start, count = split_rows(block)
        if count:
            keys.append(block[pl.ds(start, count), lanes])
    return jnp.concatenate(keys, axis=0)


def partial_attention(query, keys, values, scores, weights, head, lane):
    pair, half = divmod(head, 2)
    mine = query[:, pair * LANES : (pair + 1) * LANES]
    mine = jnp.where((lane // HEAD_DIM) == half, mine, jnp.zeros_like(mine))
    scores[...] = reduce_operands(keys, mine)
    columns = scores.shape[1]
    top = None
    for start in range(0, scores.shape[0], TILE):
        tile = jnp.max(scores[pl.ds(start, TILE), :].reshape(-1, 8, columns), axis=0)
        top = tile if top is None else jnp.maximum(top, tile)
    top = jnp.max(top, axis=0, keepdims=True)
    total = None
    for start in range(0, scores.shape[0], TILE):
        weight = jnp.exp2(scores[pl.ds(start, TILE), :] - top)
        tile = jnp.sum(weight.reshape(-1, 8, columns), axis=0)
        total = tile if total is None else total + tile
        weights[pl.ds(start, TILE), :] = weight.astype(jnp.bfloat16)
    values = values[half * HEAD_DIM : (half + 1) * HEAD_DIM]
    out = jnp.dot(values, weights[...], preferred_element_type=jnp.float32)
    return out, top, jnp.sum(total, axis=0, keepdims=True)


def state_parts(state, head, width, columns):
    return (
        state[pl.ds(head * HEAD_DIM, HEAD_DIM), columns],
        state[pl.ds(width + head, 1), columns],
        state[pl.ds(width + 8 + head, 1), columns],
    )


def merged_parts(one, other):
    top = jnp.maximum(one[1], other[1])
    first, second = jnp.exp2(one[1] - top), jnp.exp2(other[1] - top)
    return first * one[0] + second * other[0], top, first * one[2] + second * other[2]


def attend_kernel(first_column, q_refs, blocks, state, out_ref, scores, weights):
    width = q_refs[0].shape[1]
    query = jnp.concatenate([ref[...] for ref in q_refs], axis=0)
    columns = query.shape[0]
    lane = lax.broadcasted_iota(jnp.int32, (columns, LANES), 1)
    out_ref[pl.ds(width, 16), :] = jnp.zeros((16, columns), jnp.float32)
    for head in range(width // HEAD_DIM):
        if head % 2 == 0:
            keys = ordered_keys(blocks, head // 2)
            values = turned_values(blocks, width, head // 2)
        part = partial_attention(
            query, keys, values, scores.at[head % 2], weights.at[head % 2], head, lane
        )
        if state is not None:
            part = merged_parts(
                part, state_parts(state, head, width, pl.ds(first_column, columns))
            )
        out_ref[pl.ds(head * HEAD_DIM, HEAD_DIM), :] = part[0]
        out_ref[pl.ds(width + head, 1), :] = part[1]
        out_ref[pl.ds(width + 8 + head, 1), :] = part[2]


def attend(queries, blocks, state, first_column, name):
    rows, width = queries[0].shape
    columns = rows * len(queries)
    extent = sum(block.shape[0] for block in blocks)
    out = jax.ShapeDtypeStruct((width + 16, columns), jnp.float32)
    operands = (*queries, *blocks) + (() if state is None else (state,))

    def kernel(*refs):
        q_refs, block_refs = refs[: len(queries)], refs[len(queries) :][: len(blocks)]
        state_ref = None if state is None else refs[len(operands) - 1]
        attend_kernel(
            first_column, q_refs, block_refs, state_ref, *refs[len(operands) :]
        )

    return pl.pallas_call(
        kernel,
        out_shape=out,
        scratch_shapes=[
            pltpu.VMEM((2, extent, columns), jnp.float32),
            pltpu.VMEM((2, extent, columns), jnp.bfloat16),
        ],
        compiler_params=pltpu.CompilerParams(vmem_limit_bytes=24 * MIB),
        cost_estimate=cost(
            4 * columns * width * extent, (*operands, out), columns * extent * width // HEAD_DIM
        ),
        name=name,
    )(*operands)


def mix_kernel(own_state, other_state, w_ref, h2_ref, own_ref, p1, p2, p3, attended):
    rows, width = h2_ref.shape
    for pair in range(width // LANES):
        halves = []
        for head in (2 * pair, 2 * pair + 1):
            out, _, total = merged_parts(
                state_parts(own_state, head, width, pl.ds(0, rows)),
                state_parts(other_state, head, width, pl.ds(0, rows)),
            )
            halves.append(out / total)
        merged = jnp.transpose(jnp.concatenate(halves, axis=0))
        attended[:, pl.ds(pair * LANES, LANES)] = merged.astype(jnp.bfloat16)

    def product(mask):
        return jnp.dot(
            attended[...], w_ref[:, columns_of(mask, width)], preferred_element_type=jnp.float32
        )

    for ref, mask in ((p3, 3), (p2, 2), (p1, 1)):
        ref[...] = product(mask).astype(jnp.bfloat16)
    own_ref[...] = product(0) + h2_ref[...]


def mix(own_state, other_state, w_out, h2):
    rows, width = h2.shape
    own = jax.ShapeDtypeStruct((rows, width), jnp.float32)
    part = jax.ShapeDtypeStruct((rows, width), jnp.bfloat16)
    operands = (own_state, other_state, w_out, h2)
    return pl.pallas_call(
        mix_kernel,
        out_shape=(own, part, part, part),
        scratch_shapes=[pltpu.VMEM((rows, width), jnp.bfloat16)],
        compiler_params=pltpu.CompilerParams(vmem_limit_bytes=16 * MIB),
        cost_estimate=cost(
            2 * rows * width * w_out.shape[1], (*operands, own, part, part, part)
        ),
        name="mix",
    )(*operands)


def exchanged(block, mask):
    count = lax.axis_size("seq")
    return lax.ppermute(block, "seq", [(i, i ^ mask) for i in range(count)])


def on_device(dna, conv_in, dilated_kernel_weight, w_query, w_key, w_value, w_out):
    count = lax.axis_size("seq")
    rows = dna.shape[0] // 2
    inner = rows // 2 - 2 * EDGE
    outer = rows - inner
    low = lax.ppermute(dna[-EDGE:], "seq", [(i, i + 1) for i in range(count - 1)])
    high = lax.ppermute(dna[:EDGE], "seq", [(i + 1, i) for i in range(count - 1)])
    h1_m, sent = first_conv(
        conv_middle_kernel,
        (dna,),
        conv_in,
        inner + EDGE,
        2 * (inner + 2 * EDGE),
        "conv_middle",
        True,
    )
    wide_m = forwarded(shared(sent))
    h1_e, sent = first_conv(
        conv_edge_kernel, (dna, after(low, *wide_m[1:3]), high), conv_in, outer, 2 * (outer + 2 * EDGE), "conv_edge"
    )
    wide_e = shared(sent)
    h2_m, sent = second_conv(
        dilated_middle_kernel,
        (*wide_m, after(h1_m, sent)),
        dilated_kernel_weight,
        inner,
        inner,
        inner + EDGE,
        "dilated_middle",
    )
    normed_m = forwarded(shared(sent, wide_e))
    wide_e = forwarded(wide_e, sent)
    h2, sent = second_conv(
        dilated_edge_kernel,
        (*wide_m, *wide_e, h1_m, h1_e, h2_m),
        dilated_kernel_weight,
        rows,
        outer,
        outer + 2 * EDGE,
        "dilated_edge",
    )
    normed_e = shared(sent, normed_m)
    normed_m[0] = after(normed_m[0], sent)
    weights = (w_query, w_key, w_value)
    q_m, kv_m = project(project_middle_kernel, normed_m, weights, inner, "project_middle")
    x_m, y_m, d_m = (exchanged(kv_m, mask) for mask in (2, 4, 6))
    normed_e = forwarded(normed_e, kv_m)
    q, kv_e = project(project_edge_kernel, (*normed_e, q_m), weights, rows, "project_edge")
    q_other, x_e, y_e, d_e = exchanged(q, 1), *(exchanged(kv_e, mask) for mask in (2, 4, 6))
    state = attend((q, q_other), (kv_m, kv_e, x_m, y_m, d_m), None, 0, "attend_m")
    state = attend((q, q_other), (x_e,), state, 0, "attend_x")
    late = (y_e, d_e)
    state_other = attend((q_other,), late, state, rows, "attend_other")
    given = exchanged(state_other, 1)
    state_own = attend((q,), late, state, 0, "attend_own")
    own, p1, p2, p3 = mix(state_own, given, w_out, h2)
    inward = swapped(p3, 1)
    joined = (p2.astype(jnp.float32) + inward.astype(jnp.float32)).astype(jnp.bfloat16)
    beside = swapped(after(p1, joined), 1)
    total = own + swapped(joined, 2).astype(jnp.float32)
    total = after(total) + beside.astype(jnp.float32)
    return total.astype(jnp.bfloat16)


def solution(mesh):
    in_specs = (
        P("seq", None),
        P(None, "head", None),
        P(None, "head", None),
        P("head", None),
        P("head", None),
        P("head", None),
        P("head", None),
    )
    out_specs = P("seq", "head")
    seq, head = mesh.shape["seq"], mesh.shape["head"]
    aligned = (C // head) % 128 == 0
    body = on_device if head == 4 and seq == 8 and aligned else general_form
    return jax.shard_map(body, mesh=mesh, in_specs=in_specs, out_specs=out_specs, check_vma=False)
```

```python
import functools
import math

import jax
import jax.numpy as jnp
from jax import lax
from jax.experimental import pallas as pl
from jax.experimental.pallas import tpu as pltpu
from jax.sharding import PartitionSpec as P

C = 1536
HEAD_DIM = 64
KW = 5
DILATION_STEP = 4
EPS = 1e-06
EDGE = 16
LOG2E = math.log2(math.e)
MIB = 1 << 20
LANES = 128


def padded_2(block, sides, width):
    for axis, dim in sides:
        count = lax.axis_size(axis)
        forward = [(i, i + 1) for i in range(count - 1)]
        backward = [(target, source) for source, target in forward]
        low = lax.ppermute(
            lax.slice_in_dim(block, block.shape[dim] - width, None, axis=dim), axis, forward
        )
        high = lax.ppermute(lax.slice_in_dim(block, 0, width, axis=dim), axis, backward)
        block = jnp.concatenate([low, block, high], axis=dim)
    return block


def row_scale(hidden):
    squares = lax.psum(jnp.sum(hidden * hidden, axis=1), "head")
    return hidden * lax.rsqrt(squares / C + EPS)[:, None]


def reduce_operands(left, right):
    return lax.dot_general(
        left, right, (((1,), (1,)), ((), ())), preferred_element_type=jnp.float32
    )


def general_form(dna, conv_in, dilated_kernel_weight, w_query, w_key, w_value, w_out):
    local_row_count = dna.shape[0] // 2
    half = (KW - 1) // 2
    padded = padded_2(dna, (("seq", 0),), half)
    h1 = jnp.zeros((local_row_count, conv_in.shape[1]), jnp.float32)
    for kernel_offset in range(KW):
        rows = lax.slice(
            padded,
            (kernel_offset, 0),
            (kernel_offset + 2 * local_row_count - 1, padded.shape[1]),
            (2, 1),
        )
        h1 = h1 + reduce_operands(rows, conv_in[kernel_offset])
    gelu_output = jax.nn.gelu(row_scale(h1), approximate=True).astype(jnp.bfloat16)
    complete_output = lax.all_gather(gelu_output, "head", axis=1, tiled=True)
    broad_input = padded_2(complete_output, (("seq", 0),), DILATION_STEP)
    second_hidden = h1
    for kernel_offset in range(3):
        second_hidden = second_hidden + reduce_operands(
            broad_input[
                DILATION_STEP * kernel_offset : DILATION_STEP * kernel_offset + local_row_count
            ],
            dilated_kernel_weight[kernel_offset],
        )
    normed = row_scale(second_hidden).astype(jnp.bfloat16)
    local_width = w_query.shape[0]
    heads_here = local_width // HEAD_DIM
    piece = lax.all_gather(normed, "head", axis=1, tiled=True)
    q_acc, k_acc, v_acc = (reduce_operands(piece, w) for w in (w_query, w_key, w_value))
    query = q_acc.astype(jnp.bfloat16).reshape(local_row_count, heads_here, HEAD_DIM)
    keys = k_acc.astype(jnp.bfloat16)
    values = v_acc.astype(jnp.bfloat16)
    scale = 1.0 / math.sqrt(HEAD_DIM)
    start_state = (
        jnp.full((heads_here, local_row_count), -1e30, jnp.float32),
        jnp.zeros((heads_here, local_row_count), jnp.float32),
        jnp.zeros((local_row_count, heads_here, HEAD_DIM), jnp.float32),
    )
    key_rows = lax.all_gather(keys, "seq", axis=0, tiled=True)
    value_rows = lax.all_gather(values, "seq", axis=0, tiled=True)
    count = key_rows.shape[0]
    width = 512 if count % 512 == 0 else count
    blocks = count // width
    key_blocks = key_rows.reshape(blocks, width, heads_here, HEAD_DIM)
    value_blocks = value_rows.reshape(blocks, width, heads_here, HEAD_DIM)

    def step(state, operands):
        running, total, acc = state
        key_block, value_block = operands
        scores = (
            jnp.einsum("qhd,khd->hqk", query, key_block, preferred_element_type=jnp.float32) * scale
        )
        newest = jnp.maximum(running, jnp.max(scores, axis=2))
        factor = jnp.exp(running - newest)
        weights = jnp.exp(scores - newest[:, :, None])
        total = total * factor + jnp.sum(weights, axis=2)
        update = jnp.einsum(
            "hqk,khd->qhd",
            weights.astype(jnp.bfloat16),
            value_block,
            preferred_element_type=jnp.float32,
        )
        acc = acc * jnp.transpose(factor)[:, :, None] + update
        return ((newest, total, acc), None)

    state, _ = lax.scan(step, start_state, (key_blocks, value_blocks))
    running, total, acc = state
    attended = (
        (acc / jnp.transpose(total)[:, :, None])
        .reshape(local_row_count, local_width)
        .astype(jnp.bfloat16)
    )
    partial_out = jnp.dot(attended, w_out, preferred_element_type=jnp.float32)
    mixed = lax.psum_scatter(
        partial_out.astype(jnp.bfloat16), "head", scatter_dimension=1, tiled=True
    ).astype(jnp.float32)
    return (second_hidden + mixed).astype(jnp.bfloat16)


def nbytes(*arrays):
    return sum(math.prod(a.shape) * jnp.dtype(a.dtype).itemsize for a in arrays)


def cost(flops, arrays, transcendentals=0):
    return pl.CostEstimate(
        flops=int(flops), bytes_accessed=int(nbytes(*arrays)), transcendentals=int(transcendentals)
    )


def after(value, *others):
    return lax.optimization_barrier((value, *others))[0]


def swapped(block, mask):
    count = lax.axis_size("head")
    return lax.ppermute(block, "head", [(i, i ^ mask) for i in range(count)])


def shared(block, earlier=None):
    near = far = block
    if earlier is not None:
        near, far = after(block, earlier[1]), after(block, earlier[2])
    far = swapped(far, 2)
    near = swapped(near, 1)
    return [block, near, far]


def forwarded(parts, gate=None):
    far = parts[2] if gate is None else after(parts[2], gate)
    return [*parts, swapped(far, 1)]


def owner(mask):
    return jnp.bitwise_xor(lax.axis_index("head"), mask)


MASKS = (0, 1, 2, 3)


def store_wide(wide, start, block):
    for j in range(wide.shape[0]):
        rows = pl.ds(start, block.shape[0])
        wide[j, rows, :] = block[:, 128 * j : 128 * (j + 1)].astype(jnp.float32)


def taps_sum(wide, weight_ref, groups, copies=None):
    total = None
    for tap in range(KW):
        if copies is not None:
            copies[tap].wait()
        picked = []
        for start, count in groups:
            lanes = [
                wide[j, pl.ds(start + tap, count, stride=2), :] for j in range(wide.shape[0])
            ]
            picked.append(jnp.concatenate(lanes, axis=1).astype(jnp.bfloat16))
        taken = picked[0] if len(picked) == 1 else jnp.concatenate(picked, axis=0)
        term = reduce_operands(taken, weight_ref[tap])
        total = term if total is None else total + term
    return total


FIRST = EDGE - KW // 2


def conv_middle_kernel(dna_ref, weight_ref, h1_ref, sent_ref, wide, rows, weights, sems):
    first = pltpu.make_async_copy(dna_ref.at[pl.ds(0, rows.shape[0]), :], rows, sems.at[KW])
    copies = [
        pltpu.make_async_copy(weight_ref.at[tap], weights.at[tap], sems.at[tap])
        for tap in range(KW)
    ]
    for copy in (first, *copies):
        copy.start()
    first.wait()
    store_wide(wide, 0, rows[...])
    total = taps_sum(wide, weights, [(FIRST, sent_ref.shape[0])], copies)
    h1_ref[...] = total
    sent_ref[...] = total.astype(jnp.bfloat16)


def conv_edge_kernel(dna_ref, low_ref, high_ref, weight_ref, h1_ref, sent_ref, wide):
    rows = dna_ref.shape[0]
    upper = sent_ref.shape[0] - EDGE
    first = rows - 2 * upper
    zeros = jnp.zeros((EDGE, dna_ref.shape[1]), jnp.bfloat16)
    store_wide(wide, 0, zeros)
    store_wide(wide, EDGE, low_ref[...])
    store_wide(wide, 2 * EDGE, dna_ref[pl.ds(0, 2 * EDGE), :])
    store_wide(wide, 4 * EDGE, dna_ref[pl.ds(first, rows - first), :])
    store_wide(wide, 4 * EDGE + rows - first, high_ref[...])
    store_wide(wide, 5 * EDGE + rows - first, zeros)
    total = taps_sum(wide, weight_ref, [(FIRST, EDGE), (4 * EDGE + FIRST, upper)])
    h1_ref[...] = total
    sent_ref[...] = total.astype(jnp.bfloat16)


def first_conv(kernel, operands, weight, count, deep, name, streamed=False):
    width, out = weight.shape[2], weight.shape[1]
    kept = jax.ShapeDtypeStruct((count, out), jnp.float32)
    sent = jax.ShapeDtypeStruct((count, out), jnp.bfloat16)
    scratch = [pltpu.VMEM((width // 128, deep, 128), jnp.float32)]
    place = pltpu.VMEM
    if streamed:
        place = pltpu.HBM
        operands = [pltpu.with_memory_space_constraint(a, place) for a in operands]
        weight = pltpu.with_memory_space_constraint(weight, place)
        scratch += [
            pltpu.VMEM((deep, width), jnp.bfloat16),
            pltpu.VMEM(weight.shape, jnp.bfloat16),
            pltpu.SemaphoreType.DMA((KW + 1,)),
        ]
    return pl.pallas_call(
        kernel,
        out_shape=(kept, sent),
        in_specs=[pl.BlockSpec(memory_space=place)] * (len(operands) + 1),
        scratch_shapes=scratch,
        compiler_params=pltpu.CompilerParams(vmem_limit_bytes=24 * MIB),
        cost_estimate=cost(2 * count * out * width * KW, (*operands, weight, kept, sent)),
        name=name,
    )(*operands, weight)


def inverse_norm(blocks):
    squares = None
    for block in blocks:
        term = jnp.sum(block * block, axis=1, keepdims=True)
        squares = term if squares is None else squares + term
    return lax.rsqrt(squares / C + EPS)


def wide_blocks(parts, start, count):
    return [part[pl.ds(start, count), :].astype(jnp.float32) for part in parts]


def gelu(value):
    return jax.nn.gelu(value, approximate=True)


def columns_of(mask, width):
    return pl.ds(pl.multiple_of(owner(mask) * width, LANES), width)


def dilated_middle_kernel(a0, a1, a2, a3, h1_ref, weight_ref, h2_ref, sent_ref, act):
    parts = (a0, a1, a2, a3)
    count, width = a0.shape
    rows = h2_ref.shape[0]
    blocks = wide_blocks(parts, 0, count)
    inverse = inverse_norm(blocks)
    total = h1_ref[pl.ds(8, rows), :]
    for slot, (block, mask) in enumerate(zip(blocks, MASKS)):
        act[slot] = gelu(block * inverse)
        for tap in range(3):
            taken = act[slot, pl.ds((tap + 1) * DILATION_STEP, rows), :].astype(jnp.bfloat16)
            total = total + reduce_operands(taken, weight_ref[tap, :, columns_of(mask, width)])
    h2_ref[...] = total
    sent_ref[...] = total.astype(jnp.bfloat16)


def dilated_edge_kernel(
    m0, m1, m2, m3, e0, e1, e2, e3, hm_ref, he_ref, h2m_ref, weight_ref, h2_ref, sent_ref, act
):
    middle, edge = (m0, m1, m2, m3), (e0, e1, e2, e3)
    inner, width = m0.shape
    outer = e0.shape[0]
    rows = h2_ref.shape[0]
    upper = outer - EDGE
    position = lax.axis_index("seq") * rows + lax.broadcasted_iota(jnp.int32, (outer, 1), 0)
    place = lax.broadcasted_iota(jnp.int32, (outer, 1), 0)
    position = position + jnp.where(place < EDGE, -8, inner - 8)
    inside = (position >= 0) & (position < rows * lax.axis_size("seq"))
    outer_blocks = wide_blocks(edge, 0, outer)
    outer_inverse = jnp.where(inside, inverse_norm(outer_blocks), 0.0)
    low_blocks = wide_blocks(middle, 0, EDGE)
    low_inverse = inverse_norm(low_blocks)
    high_blocks = wide_blocks(middle, inner - EDGE, EDGE)
    high_inverse = inverse_norm(high_blocks)
    last = rows - (outer - EDGE)
    total = jnp.concatenate(
        [
            he_ref[pl.ds(8, 8), :],
            hm_ref[pl.ds(0, 8), :],
            hm_ref[pl.ds(inner - 8, 8), :],
            he_ref[pl.ds(EDGE, upper - 8), :],
        ],
        axis=0,
    )
    tail = 2 * EDGE
    for slot, mask in enumerate(MASKS):
        full = gelu(outer_blocks[slot] * outer_inverse)
        act[slot, pl.ds(0, EDGE), :] = full[:EDGE]
        act[slot, pl.ds(EDGE, EDGE), :] = gelu(low_blocks[slot] * low_inverse)
        act[slot, pl.ds(tail, EDGE), :] = gelu(high_blocks[slot] * high_inverse)
        act[slot, pl.ds(tail + EDGE, upper), :] = full[EDGE:]
        for tap in range(3):
            shifted = (tap + 1) * DILATION_STEP
            taken = jnp.concatenate(
                [
                    act[slot, pl.ds(shifted, EDGE), :],
                    act[slot, pl.ds(tail + shifted, upper), :],
                ],
                axis=0,
            ).astype(jnp.bfloat16)
            total = total + reduce_operands(taken, weight_ref[tap, :, columns_of(mask, width)])
    h2_ref[pl.ds(0, EDGE), :] = total[:EDGE]
    h2_ref[pl.ds(EDGE, last - EDGE), :] = h2m_ref[...]
    h2_ref[pl.ds(last, rows - last), :] = total[EDGE:]
    sent_ref[...] = total.astype(jnp.bfloat16)


def second_conv(kernel, operands, weight, kept_rows, sent_rows, deep, name):
    out, width = weight.shape[1], operands[0].shape[1]
    kept = jax.ShapeDtypeStruct((kept_rows, out), jnp.float32)
    sent = jax.ShapeDtypeStruct((sent_rows, out), jnp.bfloat16)
    return pl.pallas_call(
        kernel,
        out_shape=(kept, sent),
        scratch_shapes=[pltpu.VMEM((4, deep, width), jnp.float32)],
        compiler_params=pltpu.CompilerParams(vmem_limit_bytes=24 * MIB),
        cost_estimate=cost(
            2 * sent_rows * out * weight.shape[2] * 3,
            (*operands, weight, kept, sent),
            deep * weight.shape[2],
        ),
        name=name,
    )(*operands, weight)


def projections(parts, wq, wk, wv, kv_ref):
    width = parts[0].shape[1]
    rows, out = parts[0].shape[0], wq.shape[0]
    blocks = [part[...].astype(jnp.float32) for part in parts]
    inverse = inverse_norm(blocks)
    normed = [(block * inverse).astype(jnp.bfloat16) for block in blocks]

    def product(weight_ref, start=0, stop=rows, weight_first=False):
        total = None
        for part, mask in zip(normed, MASKS):
            weight = weight_ref[:, columns_of(mask, width)]
            taken = part[start:stop]
            pair = (weight, taken) if weight_first else (taken, weight)
            term = reduce_operands(*pair)
            total = term if total is None else total + term
        return total

    kv_ref[:, :out] = product(wk).astype(jnp.bfloat16)
    turned = rows - rows % LANES
    value = product(wv, 0, turned, True).astype(jnp.bfloat16)
    for row in range(0, turned, LANES):
        for lane in range(0, out, LANES):
            kv_ref[pl.ds(row, LANES), pl.ds(out + lane, LANES)] = value[
                lane : lane + LANES, row : row + LANES
            ]
    if turned < rows:
        value = product(wv, turned, rows)
        kv_ref[pl.ds(turned, rows - turned), out:] = value.astype(jnp.bfloat16)
    scale = LOG2E / math.sqrt(HEAD_DIM)
    return (product(wq) * scale).astype(jnp.bfloat16)


def project_middle_kernel(a0, a1, a2, a3, wq, wk, wv, q_ref, kv_ref):
    q_ref[...] = projections((a0, a1, a2, a3), wq, wk, wv, kv_ref)


def project_edge_kernel(a0, a1, a2, a3, qm_ref, wq, wk, wv, q_ref, kv_ref):
    query = projections((a0, a1, a2, a3), wq, wk, wv, kv_ref)
    inner, rows = qm_ref.shape[0], q_ref.shape[0]
    q_ref[pl.ds(0, EDGE), :] = query[:EDGE]
    q_ref[pl.ds(EDGE, inner), :] = qm_ref[...]
    q_ref[pl.ds(EDGE + inner, rows - EDGE - inner), :] = query[EDGE:]


def project(kernel, operands, weights, q_rows, name):
    rows, out = operands[0].shape[0], weights[0].shape[0]
    q = jax.ShapeDtypeStruct((q_rows, out), jnp.bfloat16)
    kv = jax.ShapeDtypeStruct((rows, 2 * out), jnp.bfloat16)
    return pl.pallas_call(
        kernel,
        out_shape=(q, kv),
        compiler_params=pltpu.CompilerParams(vmem_limit_bytes=20 * MIB),
        cost_estimate=cost(6 * rows * out * C, (*operands, *weights, q, kv)),
        name=name,
    )(*operands, *weights)


TILE = 64


def split_rows(block):
    turned = block.shape[0] - block.shape[0] % LANES
    return turned, block.shape[0] - turned


def turned_values(blocks, width, pair):
    lanes = pl.ds(width + pair * LANES, LANES)
    values = []
    for block in blocks:
        for row in range(0, split_rows(block)[0], LANES):
            values.append(block[pl.ds(row, LANES), lanes])
    rest = []
    for block in blocks:
        start, count = split_rows(block)
        if count:
            rest.append(block[pl.ds(start, count), lanes].astype(jnp.float32))
    if rest:
        values.append(jnp.transpose(jnp.concatenate(rest, axis=0)).astype(jnp.bfloat16))
    return jnp.concatenate(values, axis=1)


def ordered_keys(blocks, pair):
    lanes = pl.ds(pair * LANES, LANES)
    keys = [block[pl.ds(0, split_rows(block)[0]), lanes] for block in blocks]
    for block in blocks:
        start, count = split_rows(block)
        if count:
            keys.append(block[pl.ds(start, count), lanes])
    return jnp.concatenate(keys, axis=0)


def partial_attention(query, keys, values, scores, weights, head, lane):
    pair, half = divmod(head, 2)
    mine = query[:, pair * LANES : (pair + 1) * LANES]
    mine = jnp.where((lane // HEAD_DIM) == half, mine, jnp.zeros_like(mine))
    scores[...] = reduce_operands(keys, mine)
    columns = scores.shape[1]
    top = None
    for start in range(0, scores.shape[0], TILE):
        tile = jnp.max(scores[pl.ds(start, TILE), :].reshape(-1, 8, columns), axis=0)
        top = tile if top is None else jnp.maximum(top, tile)
    top = jnp.max(top, axis=0, keepdims=True)
    total = None
    for start in range(0, scores.shape[0], TILE):
        weight = jnp.exp2(scores[pl.ds(start, TILE), :] - top)
        tile = jnp.sum(weight.reshape(-1, 8, columns), axis=0)
        total = tile if total is None else total + tile
        weights[pl.ds(start, TILE), :] = weight.astype(jnp.bfloat16)
    values = values[half * HEAD_DIM : (half + 1) * HEAD_DIM]
    out = jnp.dot(values, weights[...], preferred_element_type=jnp.float32)
    return out, top, jnp.sum(total, axis=0, keepdims=True)


def state_parts(state, head, width, columns):
    return (
        state[pl.ds(head * HEAD_DIM, HEAD_DIM), columns],
        state[pl.ds(width + head, 1), columns],
        state[pl.ds(width + 8 + head, 1), columns],
    )


def merged_parts(one, other):
    top = jnp.maximum(one[1], other[1])
    first, second = jnp.exp2(one[1] - top), jnp.exp2(other[1] - top)
    return first * one[0] + second * other[0], top, first * one[2] + second * other[2]


def attend_kernel(first_column, q_refs, blocks, state, out_ref, scores, weights):
    width = q_refs[0].shape[1]
    query = jnp.concatenate([ref[...] for ref in q_refs], axis=0)
    columns = query.shape[0]
    lane = lax.broadcasted_iota(jnp.int32, (columns, LANES), 1)
    out_ref[pl.ds(width, 16), :] = jnp.zeros((16, columns), jnp.float32)
    for head in range(width // HEAD_DIM):
        if head % 2 == 0:
            keys = ordered_keys(blocks, head // 2)
            values = turned_values(blocks, width, head // 2)
        part = partial_attention(
            query, keys, values, scores.at[head % 2], weights.at[head % 2], head, lane
        )
        if state is not None:
            part = merged_parts(
                part, state_parts(state, head, width, pl.ds(first_column, columns))
            )
        out_ref[pl.ds(head * HEAD_DIM, HEAD_DIM), :] = part[0]
        out_ref[pl.ds(width + head, 1), :] = part[1]
        out_ref[pl.ds(width + 8 + head, 1), :] = part[2]


def attend(queries, blocks, state, first_column, name):
    rows, width = queries[0].shape
    columns = rows * len(queries)
    extent = sum(block.shape[0] for block in blocks)
    out = jax.ShapeDtypeStruct((width + 16, columns), jnp.float32)
    operands = (*queries, *blocks) + (() if state is None else (state,))

    def kernel(*refs):
        q_refs, block_refs = refs[: len(queries)], refs[len(queries) :][: len(blocks)]
        state_ref = None if state is None else refs[len(operands) - 1]
        attend_kernel(
            first_column, q_refs, block_refs, state_ref, *refs[len(operands) :]
        )

    return pl.pallas_call(
        kernel,
        out_shape=out,
        scratch_shapes=[
            pltpu.VMEM((2, extent, columns), jnp.float32),
            pltpu.VMEM((2, extent, columns), jnp.bfloat16),
        ],
        compiler_params=pltpu.CompilerParams(vmem_limit_bytes=24 * MIB),
        cost_estimate=cost(
            4 * columns * width * extent, (*operands, out), columns * extent * width // HEAD_DIM
        ),
        name=name,
    )(*operands)


def mix_kernel(own_state, other_state, w_ref, h2_ref, own_ref, p1, p2, p3, attended):
    rows, width = h2_ref.shape
    for pair in range(width // LANES):
        halves = []
        for head in (2 * pair, 2 * pair + 1):
            out, _, total = merged_parts(
                state_parts(own_state, head, width, pl.ds(0, rows)),
                state_parts(other_state, head, width, pl.ds(0, rows)),
            )
            halves.append(out / total)
        merged = jnp.transpose(jnp.concatenate(halves, axis=0))
        attended[:, pl.ds(pair * LANES, LANES)] = merged.astype(jnp.bfloat16)

    def product(mask):
        return jnp.dot(
            attended[...], w_ref[:, columns_of(mask, width)], preferred_element_type=jnp.float32
        )

    for ref, mask in ((p3, 3), (p2, 2), (p1, 1)):
        ref[...] = product(mask).astype(jnp.bfloat16)
    own_ref[...] = product(0) + h2_ref[...]


def mix(own_state, other_state, w_out, h2):
    rows, width = h2.shape
    own = jax.ShapeDtypeStruct((rows, width), jnp.float32)
    part = jax.ShapeDtypeStruct((rows, width), jnp.bfloat16)
    operands = (own_state, other_state, w_out, h2)
    return pl.pallas_call(
        mix_kernel,
        out_shape=(own, part, part, part),
        scratch_shapes=[pltpu.VMEM((rows, width), jnp.bfloat16)],
        compiler_params=pltpu.CompilerParams(vmem_limit_bytes=16 * MIB),
        cost_estimate=cost(
            2 * rows * width * w_out.shape[1], (*operands, own, part, part, part)
        ),
        name="mix",
    )(*operands)


def exchanged(block, mask):
    count = lax.axis_size("seq")
    return lax.ppermute(block, "seq", [(i, i ^ mask) for i in range(count)])


def on_device(dna, conv_in, dilated_kernel_weight, w_query, w_key, w_value, w_out):
    count = lax.axis_size("seq")
    rows = dna.shape[0] // 2
    inner = rows // 2
    outer = rows - inner
    low = lax.ppermute(dna[-EDGE:], "seq", [(i, i + 1) for i in range(count - 1)])
    high = lax.ppermute(dna[:EDGE], "seq", [(i + 1, i) for i in range(count - 1)])
    h1_m, sent = first_conv(
        conv_middle_kernel,
        (dna,),
        conv_in,
        inner + EDGE,
        2 * (inner + 2 * EDGE),
        "conv_middle",
        True,
    )
    wide_m = forwarded(shared(sent))
    h1_e, sent = first_conv(
        conv_edge_kernel, (dna, after(low, *wide_m[1:3]), high), conv_in, outer, 2 * (outer + 2 * EDGE), "conv_edge"
    )
    wide_e = shared(sent)
    h2_m, sent = second_conv(
        dilated_middle_kernel,
        (*wide_m, after(h1_m, sent)),
        dilated_kernel_weight,
        inner,
        inner,
        inner + EDGE,
        "dilated_middle",
    )
    normed_m = forwarded(shared(sent))
    wide_e = forwarded(wide_e, sent)
    h2, sent = second_conv(
        dilated_edge_kernel,
        (*wide_m, *wide_e, h1_m, h1_e, h2_m),
        dilated_kernel_weight,
        rows,
        outer,
        outer + 2 * EDGE,
        "dilated_edge",
    )
    normed_e = shared(sent, normed_m)
    normed_m[0] = after(normed_m[0], sent)
    weights = (w_query, w_key, w_value)
    q_m, kv_m = project(project_middle_kernel, normed_m, weights, inner, "project_middle")
    x_m, y_m, d_m = (exchanged(kv_m, mask) for mask in (2, 4, 6))
    normed_e = forwarded(normed_e, kv_m)
    q, kv_e = project(project_edge_kernel, (*normed_e, q_m), weights, rows, "project_edge")
    q_other, x_e, y_e, d_e = exchanged(q, 1), *(exchanged(kv_e, mask) for mask in (2, 4, 6))
    state = attend((q, q_other), (kv_m, kv_e, x_m, y_m, d_m), None, 0, "attend_m")
    state = attend((q, q_other), (x_e,), state, 0, "attend_x")
    late = (y_e, d_e)
    state_other = attend((q_other,), late, state, rows, "attend_other")
    given = exchanged(state_other, 1)
    state_own = attend((q,), late, state, 0, "attend_own")
    own, p1, p2, p3 = mix(state_own, given, w_out, h2)
    inward = swapped(p3, 1)
    joined = (p2.astype(jnp.float32) + inward.astype(jnp.float32)).astype(jnp.bfloat16)
    beside = swapped(after(p1, joined), 1)
    total = own + swapped(joined, 2).astype(jnp.float32)
    total = after(total) + beside.astype(jnp.float32)
    return total.astype(jnp.bfloat16)


def solution(mesh):
    in_specs = (
        P("seq", None),
        P(None, "head", None),
        P(None, "head", None),
        P("head", None),
        P("head", None),
        P("head", None),
        P("head", None),
    )
    out_specs = P("seq", "head")
    seq, head = mesh.shape["seq"], mesh.shape["head"]
    aligned = (C // head) % 128 == 0
    body = on_device if head == 4 and seq == 8 and aligned else general_form
    return jax.shard_map(body, mesh=mesh, in_specs=in_specs, out_specs=out_specs, check_vma=False)
```

```python
import functools
import math

import jax
import jax.numpy as jnp
from jax import lax
from jax.experimental import pallas as pl
from jax.experimental.pallas import tpu as pltpu
from jax.sharding import PartitionSpec as P

C = 1536
HEAD_DIM = 64
KW = 5
DILATION_STEP = 4
EPS = 1e-06
EDGE = 16
LOG2E = math.log2(math.e)
MIB = 1 << 20
LANES = 128


def padded_2(block, sides, width):
    for axis, dim in sides:
        count = lax.axis_size(axis)
        forward = [(i, i + 1) for i in range(count - 1)]
        backward = [(target, source) for source, target in forward]
        low = lax.ppermute(
            lax.slice_in_dim(block, block.shape[dim] - width, None, axis=dim), axis, forward
        )
        high = lax.ppermute(lax.slice_in_dim(block, 0, width, axis=dim), axis, backward)
        block = jnp.concatenate([low, block, high], axis=dim)
    return block


def row_scale(hidden):
    squares = lax.psum(jnp.sum(hidden * hidden, axis=1), "head")
    return hidden * lax.rsqrt(squares / C + EPS)[:, None]


def reduce_operands(left, right):
    return lax.dot_general(
        left, right, (((1,), (1,)), ((), ())), preferred_element_type=jnp.float32
    )


def general_form(dna, conv_in, dilated_kernel_weight, w_query, w_key, w_value, w_out):
    local_row_count = dna.shape[0] // 2
    half = (KW - 1) // 2
    padded = padded_2(dna, (("seq", 0),), half)
    h1 = jnp.zeros((local_row_count, conv_in.shape[1]), jnp.float32)
    for kernel_offset in range(KW):
        rows = lax.slice(
            padded,
            (kernel_offset, 0),
            (kernel_offset + 2 * local_row_count - 1, padded.shape[1]),
            (2, 1),
        )
        h1 = h1 + reduce_operands(rows, conv_in[kernel_offset])
    gelu_output = jax.nn.gelu(row_scale(h1), approximate=True).astype(jnp.bfloat16)
    complete_output = lax.all_gather(gelu_output, "head", axis=1, tiled=True)
    broad_input = padded_2(complete_output, (("seq", 0),), DILATION_STEP)
    second_hidden = h1
    for kernel_offset in range(3):
        second_hidden = second_hidden + reduce_operands(
            broad_input[
                DILATION_STEP * kernel_offset : DILATION_STEP * kernel_offset + local_row_count
            ],
            dilated_kernel_weight[kernel_offset],
        )
    normed = row_scale(second_hidden).astype(jnp.bfloat16)
    local_width = w_query.shape[0]
    heads_here = local_width // HEAD_DIM
    piece = lax.all_gather(normed, "head", axis=1, tiled=True)
    q_acc, k_acc, v_acc = (reduce_operands(piece, w) for w in (w_query, w_key, w_value))
    query = q_acc.astype(jnp.bfloat16).reshape(local_row_count, heads_here, HEAD_DIM)
    keys = k_acc.astype(jnp.bfloat16)
    values = v_acc.astype(jnp.bfloat16)
    scale = 1.0 / math.sqrt(HEAD_DIM)
    start_state = (
        jnp.full((heads_here, local_row_count), -1e30, jnp.float32),
        jnp.zeros((heads_here, local_row_count), jnp.float32),
        jnp.zeros((local_row_count, heads_here, HEAD_DIM), jnp.float32),
    )
    key_rows = lax.all_gather(keys, "seq", axis=0, tiled=True)
    value_rows = lax.all_gather(values, "seq", axis=0, tiled=True)
    count = key_rows.shape[0]
    width = 512 if count % 512 == 0 else count
    blocks = count // width
    key_blocks = key_rows.reshape(blocks, width, heads_here, HEAD_DIM)
    value_blocks = value_rows.reshape(blocks, width, heads_here, HEAD_DIM)

    def step(state, operands):
        running, total, acc = state
        key_block, value_block = operands
        scores = (
            jnp.einsum("qhd,khd->hqk", query, key_block, preferred_element_type=jnp.float32) * scale
        )
        newest = jnp.maximum(running, jnp.max(scores, axis=2))
        factor = jnp.exp(running - newest)
        weights = jnp.exp(scores - newest[:, :, None])
        total = total * factor + jnp.sum(weights, axis=2)
        update = jnp.einsum(
            "hqk,khd->qhd",
            weights.astype(jnp.bfloat16),
            value_block,
            preferred_element_type=jnp.float32,
        )
        acc = acc * jnp.transpose(factor)[:, :, None] + update
        return ((newest, total, acc), None)

    state, _ = lax.scan(step, start_state, (key_blocks, value_blocks))
    running, total, acc = state
    attended = (
        (acc / jnp.transpose(total)[:, :, None])
        .reshape(local_row_count, local_width)
        .astype(jnp.bfloat16)
    )
    partial_out = jnp.dot(attended, w_out, preferred_element_type=jnp.float32)
    mixed = lax.psum_scatter(
        partial_out.astype(jnp.bfloat16), "head", scatter_dimension=1, tiled=True
    ).astype(jnp.float32)
    return (second_hidden + mixed).astype(jnp.bfloat16)


def nbytes(*arrays):
    return sum(math.prod(a.shape) * jnp.dtype(a.dtype).itemsize for a in arrays)


def cost(flops, arrays, transcendentals=0):
    return pl.CostEstimate(
        flops=int(flops), bytes_accessed=int(nbytes(*arrays)), transcendentals=int(transcendentals)
    )


def after(value, *others):
    return lax.optimization_barrier((value, *others))[0]


def swapped(block, mask):
    count = lax.axis_size("head")
    return lax.ppermute(block, "head", [(i, i ^ mask) for i in range(count)])


def shared(block, earlier=None):
    near = far = block
    if earlier is not None:
        near, far = after(block, earlier[1]), after(block, earlier[2])
    far = swapped(far, 2)
    near = swapped(near, 1)
    return [block, near, far]


def forwarded(parts, gate=None):
    far = parts[2] if gate is None else after(parts[2], gate)
    return [*parts, swapped(far, 1)]


def owner(mask):
    return jnp.bitwise_xor(lax.axis_index("head"), mask)


MASKS = (0, 1, 2, 3)


def store_wide(wide, start, block):
    for j in range(wide.shape[0]):
        rows = pl.ds(start, block.shape[0])
        wide[j, rows, :] = block[:, 128 * j : 128 * (j + 1)].astype(jnp.float32)


def taps_sum(wide, weight_ref, groups, copies=None):
    total = None
    for tap in range(KW):
        if copies is not None:
            copies[tap].wait()
        picked = []
        for start, count in groups:
            lanes = [
                wide[j, pl.ds(start + tap, count, stride=2), :] for j in range(wide.shape[0])
            ]
            picked.append(jnp.concatenate(lanes, axis=1).astype(jnp.bfloat16))
        taken = picked[0] if len(picked) == 1 else jnp.concatenate(picked, axis=0)
        term = reduce_operands(taken, weight_ref[tap])
        total = term if total is None else total + term
    return total


FIRST = EDGE - KW // 2


def conv_middle_kernel(dna_ref, weight_ref, h1_ref, sent_ref, wide, rows, weights, sems):
    first = pltpu.make_async_copy(dna_ref.at[pl.ds(0, rows.shape[0]), :], rows, sems.at[KW])
    copies = [
        pltpu.make_async_copy(weight_ref.at[tap], weights.at[tap], sems.at[tap])
        for tap in range(KW)
    ]
    for copy in (first, *copies):
        copy.start()
    first.wait()
    store_wide(wide, 0, rows[...])
    total = taps_sum(wide, weights, [(FIRST, sent_ref.shape[0])], copies)
    h1_ref[...] = total
    sent_ref[...] = total.astype(jnp.bfloat16)


def conv_edge_kernel(dna_ref, low_ref, high_ref, weight_ref, h1_ref, sent_ref, wide):
    rows = dna_ref.shape[0]
    upper = sent_ref.shape[0] - EDGE
    first = rows - 2 * upper
    zeros = jnp.zeros((EDGE, dna_ref.shape[1]), jnp.bfloat16)
    store_wide(wide, 0, zeros)
    store_wide(wide, EDGE, low_ref[...])
    store_wide(wide, 2 * EDGE, dna_ref[pl.ds(0, 2 * EDGE), :])
    store_wide(wide, 4 * EDGE, dna_ref[pl.ds(first, rows - first), :])
    store_wide(wide, 4 * EDGE + rows - first, high_ref[...])
    store_wide(wide, 5 * EDGE + rows - first, zeros)
    total = taps_sum(wide, weight_ref, [(FIRST, EDGE), (4 * EDGE + FIRST, upper)])
    h1_ref[...] = total
    sent_ref[...] = total.astype(jnp.bfloat16)


def first_conv(kernel, operands, weight, count, deep, name, streamed=False):
    width, out = weight.shape[2], weight.shape[1]
    kept = jax.ShapeDtypeStruct((count, out), jnp.float32)
    sent = jax.ShapeDtypeStruct((count, out), jnp.bfloat16)
    scratch = [pltpu.VMEM((width // 128, deep, 128), jnp.float32)]
    place = pltpu.VMEM
    if streamed:
        place = pltpu.HBM
        operands = [pltpu.with_memory_space_constraint(a, place) for a in operands]
        weight = pltpu.with_memory_space_constraint(weight, place)
        scratch += [
            pltpu.VMEM((deep, width), jnp.bfloat16),
            pltpu.VMEM(weight.shape, jnp.bfloat16),
            pltpu.SemaphoreType.DMA((KW + 1,)),
        ]
    return pl.pallas_call(
        kernel,
        out_shape=(kept, sent),
        in_specs=[pl.BlockSpec(memory_space=place)] * (len(operands) + 1),
        scratch_shapes=scratch,
        compiler_params=pltpu.CompilerParams(vmem_limit_bytes=24 * MIB),
        cost_estimate=cost(2 * count * out * width * KW, (*operands, weight, kept, sent)),
        name=name,
    )(*operands, weight)


def inverse_norm(blocks):
    squares = None
    for block in blocks:
        term = jnp.sum(block * block, axis=1, keepdims=True)
        squares = term if squares is None else squares + term
    return lax.rsqrt(squares / C + EPS)


def wide_blocks(parts, start, count):
    return [part[pl.ds(start, count), :].astype(jnp.float32) for part in parts]


def gelu(value):
    return jax.nn.gelu(value, approximate=True)


def columns_of(mask, width):
    return pl.ds(pl.multiple_of(owner(mask) * width, LANES), width)


def dilated_middle_kernel(a0, a1, a2, a3, h1_ref, weight_ref, h2_ref, sent_ref, act):
    parts = (a0, a1, a2, a3)
    count, width = a0.shape
    rows = h2_ref.shape[0]
    blocks = wide_blocks(parts, 0, count)
    inverse = inverse_norm(blocks)
    total = h1_ref[pl.ds(8, rows), :]
    for slot, (block, mask) in enumerate(zip(blocks, MASKS)):
        act[slot] = gelu(block * inverse)
        for tap in range(3):
            taken = act[slot, pl.ds((tap + 1) * DILATION_STEP, rows), :].astype(jnp.bfloat16)
            total = total + reduce_operands(taken, weight_ref[tap, :, columns_of(mask, width)])
    h2_ref[...] = total
    sent_ref[...] = total.astype(jnp.bfloat16)


def dilated_edge_kernel(
    m0, m1, m2, m3, e0, e1, e2, e3, hm_ref, he_ref, h2m_ref, weight_ref, h2_ref, sent_ref, act
):
    middle, edge = (m0, m1, m2, m3), (e0, e1, e2, e3)
    inner, width = m0.shape
    outer = e0.shape[0]
    rows = h2_ref.shape[0]
    upper = outer - EDGE
    position = lax.axis_index("seq") * rows + lax.broadcasted_iota(jnp.int32, (outer, 1), 0)
    place = lax.broadcasted_iota(jnp.int32, (outer, 1), 0)
    position = position + jnp.where(place < EDGE, -8, inner - 8)
    inside = (position >= 0) & (position < rows * lax.axis_size("seq"))
    outer_blocks = wide_blocks(edge, 0, outer)
    outer_inverse = jnp.where(inside, inverse_norm(outer_blocks), 0.0)
    low_blocks = wide_blocks(middle, 0, EDGE)
    low_inverse = inverse_norm(low_blocks)
    high_blocks = wide_blocks(middle, inner - EDGE, EDGE)
    high_inverse = inverse_norm(high_blocks)
    last = rows - (outer - EDGE)
    total = jnp.concatenate(
        [
            he_ref[pl.ds(8, 8), :],
            hm_ref[pl.ds(0, 8), :],
            hm_ref[pl.ds(inner - 8, 8), :],
            he_ref[pl.ds(EDGE, upper - 8), :],
        ],
        axis=0,
    )
    tail = 2 * EDGE
    for slot, mask in enumerate(MASKS):
        full = gelu(outer_blocks[slot] * outer_inverse)
        act[slot, pl.ds(0, EDGE), :] = full[:EDGE]
        act[slot, pl.ds(EDGE, EDGE), :] = gelu(low_blocks[slot] * low_inverse)
        act[slot, pl.ds(tail, EDGE), :] = gelu(high_blocks[slot] * high_inverse)
        act[slot, pl.ds(tail + EDGE, upper), :] = full[EDGE:]
        for tap in range(3):
            shifted = (tap + 1) * DILATION_STEP
            taken = jnp.concatenate(
                [
                    act[slot, pl.ds(shifted, EDGE), :],
                    act[slot, pl.ds(tail + shifted, upper), :],
                ],
                axis=0,
            ).astype(jnp.bfloat16)
            total = total + reduce_operands(taken, weight_ref[tap, :, columns_of(mask, width)])
    h2_ref[pl.ds(0, EDGE), :] = total[:EDGE]
    h2_ref[pl.ds(EDGE, last - EDGE), :] = h2m_ref[...]
    h2_ref[pl.ds(last, rows - last), :] = total[EDGE:]
    sent_ref[...] = total.astype(jnp.bfloat16)


def second_conv(kernel, operands, weight, kept_rows, sent_rows, deep, name):
    out, width = weight.shape[1], operands[0].shape[1]
    kept = jax.ShapeDtypeStruct((kept_rows, out), jnp.float32)
    sent = jax.ShapeDtypeStruct((sent_rows, out), jnp.bfloat16)
    return pl.pallas_call(
        kernel,
        out_shape=(kept, sent),
        scratch_shapes=[pltpu.VMEM((4, deep, width), jnp.float32)],
        compiler_params=pltpu.CompilerParams(vmem_limit_bytes=24 * MIB),
        cost_estimate=cost(
            2 * sent_rows * out * weight.shape[2] * 3,
            (*operands, weight, kept, sent),
            deep * weight.shape[2],
        ),
        name=name,
    )(*operands, weight)


def projections(parts, wq, wk, wv, kv_ref):
    width = parts[0].shape[1]
    rows, out = parts[0].shape[0], wq.shape[0]
    blocks = [part[...].astype(jnp.float32) for part in parts]
    inverse = inverse_norm(blocks)
    normed = [(block * inverse).astype(jnp.bfloat16) for block in blocks]

    def product(weight_ref, start=0, stop=rows, weight_first=False):
        total = None
        for part, mask in zip(normed, MASKS):
            weight = weight_ref[:, columns_of(mask, width)]
            taken = part[start:stop]
            pair = (weight, taken) if weight_first else (taken, weight)
            term = reduce_operands(*pair)
            total = term if total is None else total + term
        return total

    kv_ref[:, :out] = product(wk).astype(jnp.bfloat16)
    turned = rows - rows % LANES
    value = product(wv, 0, turned, True).astype(jnp.bfloat16)
    for row in range(0, turned, LANES):
        for lane in range(0, out, LANES):
            kv_ref[pl.ds(row, LANES), pl.ds(out + lane, LANES)] = value[
                lane : lane + LANES, row : row + LANES
            ]
    if turned < rows:
        value = product(wv, turned, rows)
        kv_ref[pl.ds(turned, rows - turned), out:] = value.astype(jnp.bfloat16)
    scale = LOG2E / math.sqrt(HEAD_DIM)
    return (product(wq) * scale).astype(jnp.bfloat16)


def project_middle_kernel(a0, a1, a2, a3, wq, wk, wv, q_ref, kv_ref):
    q_ref[...] = projections((a0, a1, a2, a3), wq, wk, wv, kv_ref)


def project_edge_kernel(a0, a1, a2, a3, qm_ref, wq, wk, wv, q_ref, kv_ref):
    query = projections((a0, a1, a2, a3), wq, wk, wv, kv_ref)
    inner, rows = qm_ref.shape[0], q_ref.shape[0]
    q_ref[pl.ds(0, EDGE), :] = query[:EDGE]
    q_ref[pl.ds(EDGE, inner), :] = qm_ref[...]
    q_ref[pl.ds(EDGE + inner, rows - EDGE - inner), :] = query[EDGE:]


def project(kernel, operands, weights, q_rows, name):
    rows, out = operands[0].shape[0], weights[0].shape[0]
    q = jax.ShapeDtypeStruct((q_rows, out), jnp.bfloat16)
    kv = jax.ShapeDtypeStruct((rows, 2 * out), jnp.bfloat16)
    return pl.pallas_call(
        kernel,
        out_shape=(q, kv),
        compiler_params=pltpu.CompilerParams(vmem_limit_bytes=20 * MIB),
        cost_estimate=cost(6 * rows * out * C, (*operands, *weights, q, kv)),
        name=name,
    )(*operands, *weights)


TILE = 64


def split_rows(block):
    turned = block.shape[0] - block.shape[0] % LANES
    return turned, block.shape[0] - turned


def turned_values(blocks, width, pair):
    lanes = pl.ds(width + pair * LANES, LANES)
    values = []
    for block in blocks:
        for row in range(0, split_rows(block)[0], LANES):
            values.append(block[pl.ds(row, LANES), lanes])
    rest = []
    for block in blocks:
        start, count = split_rows(block)
        if count:
            rest.append(block[pl.ds(start, count), lanes].astype(jnp.float32))
    if rest:
        values.append(jnp.transpose(jnp.concatenate(rest, axis=0)).astype(jnp.bfloat16))
    return jnp.concatenate(values, axis=1)


def ordered_keys(blocks, pair):
    lanes = pl.ds(pair * LANES, LANES)
    keys = [block[pl.ds(0, split_rows(block)[0]), lanes] for block in blocks]
    for block in blocks:
        start, count = split_rows(block)
        if count:
            keys.append(block[pl.ds(start, count), lanes])
    return jnp.concatenate(keys, axis=0)


def partial_attention(query, keys, values, scores, weights, head, lane):
    pair, half = divmod(head, 2)
    mine = query[:, pair * LANES : (pair + 1) * LANES]
    mine = jnp.where((lane // HEAD_DIM) == half, mine, jnp.zeros_like(mine))
    scores[...] = reduce_operands(keys, mine)
    columns = scores.shape[1]
    top = None
    for start in range(0, scores.shape[0], TILE):
        tile = jnp.max(scores[pl.ds(start, TILE), :].reshape(-1, 8, columns), axis=0)
        top = tile if top is None else jnp.maximum(top, tile)
    top = jnp.max(top, axis=0, keepdims=True)
    total = None
    for start in range(0, scores.shape[0], TILE):
        weight = jnp.exp2(scores[pl.ds(start, TILE), :] - top)
        tile = jnp.sum(weight.reshape(-1, 8, columns), axis=0)
        total = tile if total is None else total + tile
        weights[pl.ds(start, TILE), :] = weight.astype(jnp.bfloat16)
    values = values[half * HEAD_DIM : (half + 1) * HEAD_DIM]
    out = jnp.dot(values, weights[...], preferred_element_type=jnp.float32)
    return out, top, jnp.sum(total, axis=0, keepdims=True)


def state_parts(state, head, width, columns):
    return (
        state[pl.ds(head * HEAD_DIM, HEAD_DIM), columns],
        state[pl.ds(width + head, 1), columns],
        state[pl.ds(width + 8 + head, 1), columns],
    )


def merged_parts(one, other):
    top = jnp.maximum(one[1], other[1])
    first, second = jnp.exp2(one[1] - top), jnp.exp2(other[1] - top)
    return first * one[0] + second * other[0], top, first * one[2] + second * other[2]


def attend_kernel(first_column, q_refs, blocks, state, out_ref, scores, weights):
    width = q_refs[0].shape[1]
    query = jnp.concatenate([ref[...] for ref in q_refs], axis=0)
    columns = query.shape[0]
    lane = lax.broadcasted_iota(jnp.int32, (columns, LANES), 1)
    out_ref[pl.ds(width, 16), :] = jnp.zeros((16, columns), jnp.float32)
    for head in range(width // HEAD_DIM):
        if head % 2 == 0:
            keys = ordered_keys(blocks, head // 2)
            values = turned_values(blocks, width, head // 2)
        part = partial_attention(
            query, keys, values, scores.at[head % 2], weights.at[head % 2], head, lane
        )
        if state is not None:
            part = merged_parts(
                part, state_parts(state, head, width, pl.ds(first_column, columns))
            )
        out_ref[pl.ds(head * HEAD_DIM, HEAD_DIM), :] = part[0]
        out_ref[pl.ds(width + head, 1), :] = part[1]
        out_ref[pl.ds(width + 8 + head, 1), :] = part[2]


def attend(queries, blocks, state, first_column, name):
    rows, width = queries[0].shape
    columns = rows * len(queries)
    extent = sum(block.shape[0] for block in blocks)
    out = jax.ShapeDtypeStruct((width + 16, columns), jnp.float32)
    operands = (*queries, *blocks) + (() if state is None else (state,))

    def kernel(*refs):
        q_refs, block_refs = refs[: len(queries)], refs[len(queries) :][: len(blocks)]
        state_ref = None if state is None else refs[len(operands) - 1]
        attend_kernel(
            first_column, q_refs, block_refs, state_ref, *refs[len(operands) :]
        )

    return pl.pallas_call(
        kernel,
        out_shape=out,
        scratch_shapes=[
            pltpu.VMEM((2, extent, columns), jnp.float32),
            pltpu.VMEM((2, extent, columns), jnp.bfloat16),
        ],
        compiler_params=pltpu.CompilerParams(vmem_limit_bytes=24 * MIB),
        cost_estimate=cost(
            4 * columns * width * extent, (*operands, out), columns * extent * width // HEAD_DIM
        ),
        name=name,
    )(*operands)


def mix_kernel(own_state, other_state, w_ref, h2_ref, own_ref, p1, p2, p3, attended):
    rows, width = h2_ref.shape
    for pair in range(width // LANES):
        halves = []
        for head in (2 * pair, 2 * pair + 1):
            out, _, total = merged_parts(
                state_parts(own_state, head, width, pl.ds(0, rows)),
                state_parts(other_state, head, width, pl.ds(0, rows)),
            )
            halves.append(out / total)
        merged = jnp.transpose(jnp.concatenate(halves, axis=0))
        attended[:, pl.ds(pair * LANES, LANES)] = merged.astype(jnp.bfloat16)

    def product(mask):
        return jnp.dot(
            attended[...], w_ref[:, columns_of(mask, width)], preferred_element_type=jnp.float32
        )

    for ref, mask in ((p3, 3), (p2, 2), (p1, 1)):
        ref[...] = product(mask).astype(jnp.bfloat16)
    own_ref[...] = product(0) + h2_ref[...]


def mix(own_state, other_state, w_out, h2):
    rows, width = h2.shape
    own = jax.ShapeDtypeStruct((rows, width), jnp.float32)
    part = jax.ShapeDtypeStruct((rows, width), jnp.bfloat16)
    operands = (own_state, other_state, w_out, h2)
    return pl.pallas_call(
        mix_kernel,
        out_shape=(own, part, part, part),
        scratch_shapes=[pltpu.VMEM((rows, width), jnp.bfloat16)],
        compiler_params=pltpu.CompilerParams(vmem_limit_bytes=16 * MIB),
        cost_estimate=cost(
            2 * rows * width * w_out.shape[1], (*operands, own, part, part, part)
        ),
        name="mix",
    )(*operands)


def exchanged(block, mask):
    count = lax.axis_size("seq")
    return lax.ppermute(block, "seq", [(i, i ^ mask) for i in range(count)])


def on_device(dna, conv_in, dilated_kernel_weight, w_query, w_key, w_value, w_out):
    count = lax.axis_size("seq")
    rows = dna.shape[0] // 2
    inner = rows // 2
    outer = rows - inner
    low = lax.ppermute(dna[-EDGE:], "seq", [(i, i + 1) for i in range(count - 1)])
    high = lax.ppermute(dna[:EDGE], "seq", [(i + 1, i) for i in range(count - 1)])
    h1_m, sent = first_conv(
        conv_middle_kernel,
        (dna,),
        conv_in,
        inner + EDGE,
        2 * (inner + 2 * EDGE),
        "conv_middle",
        True,
    )
    wide_m = forwarded(shared(sent))
    h1_e, sent = first_conv(
        conv_edge_kernel, (dna, after(low, *wide_m[1:3]), high), conv_in, outer, 2 * (outer + 2 * EDGE), "conv_edge"
    )
    wide_e = shared(sent)
    h2_m, sent = second_conv(
        dilated_middle_kernel,
        (*wide_m, after(h1_m, sent)),
        dilated_kernel_weight,
        inner,
        inner,
        inner + EDGE,
        "dilated_middle",
    )
    normed_m = shared(sent)
    wide_e = forwarded(wide_e, sent)
    h2, sent = second_conv(
        dilated_edge_kernel,
        (*wide_m, *wide_e, h1_m, h1_e, h2_m),
        dilated_kernel_weight,
        rows,
        outer,
        outer + 2 * EDGE,
        "dilated_edge",
    )
    normed_e = shared(sent, normed_m)
    normed_m = forwarded(normed_m, sent)
    weights = (w_query, w_key, w_value)
    q_m, kv_m = project(project_middle_kernel, normed_m, weights, inner, "project_middle")
    x_m, y_m, d_m = (exchanged(kv_m, mask) for mask in (2, 4, 6))
    normed_e = forwarded(normed_e, kv_m)
    q, kv_e = project(project_edge_kernel, (*normed_e, q_m), weights, rows, "project_edge")
    q_other, x_e, y_e, d_e = exchanged(q, 1), *(exchanged(kv_e, mask) for mask in (2, 4, 6))
    state = attend((q, q_other), (kv_m, kv_e, x_m, y_m, d_m), None, 0, "attend_m")
    state = attend((q, q_other), (x_e,), state, 0, "attend_x")
    late = (y_e, d_e)
    state_other = attend((q_other,), late, state, rows, "attend_other")
    given = exchanged(state_other, 1)
    state_own = attend((q,), late, state, 0, "attend_own")
    own, p1, p2, p3 = mix(state_own, given, w_out, h2)
    inward = swapped(p3, 1)
    joined = (p2.astype(jnp.float32) + inward.astype(jnp.float32)).astype(jnp.bfloat16)
    beside = swapped(after(p1, joined), 1)
    total = own + swapped(joined, 2).astype(jnp.float32)
    total = after(total) + beside.astype(jnp.float32)
    return total.astype(jnp.bfloat16)


def solution(mesh):
    in_specs = (
        P("seq", None),
        P(None, "head", None),
        P(None, "head", None),
        P("head", None),
        P("head", None),
        P("head", None),
        P("head", None),
    )
    out_specs = P("seq", "head")
    seq, head = mesh.shape["seq"], mesh.shape["head"]
    aligned = (C // head) % 128 == 0
    body = on_device if head == 4 and seq == 8 and aligned else general_form
    return jax.shard_map(body, mesh=mesh, in_specs=in_specs, out_specs=out_specs, check_vma=False)
```
